32 devices in a mesh: dp: 16 (over z, y, x), tensor: 2 (over core).
Axes of the slice: x: 2, y: 2, z: 4, core: 2. Of those that a mesh axis runs over, the one named last changes fastest.
Arguments:
- tokens: bfloat16 [2048, 1536], P('dp'), may hold values from -8 to 8
- attn_norm_gain: bfloat16 [1536], P('dp'), may hold values from 0.5 to 1.5
- w_query: bfloat16 [1536, 1536], P('dp', 'tensor'), may hold values from -1 to 1
- key_projection: bfloat16 [1536, 512], P('dp', 'tensor'), may hold values from -0.625 to 0.625
- value_projection: bfloat16 [1536, 512], P('dp', 'tensor'), may hold values from -0.15625 to 0.15625
- w_out: bfloat16 [1536, 1536], P('dp', 'tensor'), may hold values from -2 to 2
- moe_norm_gain: bfloat16 [1536], P('dp'), may hold values from 0.5 to 1.5
- w_gate: bfloat16 [16, 1536, 512], P('dp', None, 'tensor'), may hold values from -0.15625 to 0.15625
- w_up: bfloat16 [16, 1536, 512], P('dp', None, 'tensor'), may hold values from -0.15625 to 0.15625
- w_down: bfloat16 [16, 1536, 512], P('dp', None, 'tensor'), may hold values from -4 to 4
- router_logits: float32 [2048, 8], P('dp'), may hold values from -3 to 3
- expert_ids: int32 [2048, 8], P('dp'), may hold values from 0 to 15, all different within a row; in each aligned block of 128 rows (0 to 127, 128 to 255, ...) at most 72 rows name the same one
- segment_ids: int32 [16, 128], P('dp'), may hold values from 0 to 12, never falling along the last dimension, each value on 1 to 32 neighbouring positions
- parents: int32 [16, 13], P('dp'), may hold values from 0 to 4, as said below
- cotangent: bfloat16 [2048, 1536], P('dp'), may hold values from -6 to 6
Outputs:
- output: bfloat16 [2048, 1536], P('dp')
- input_grad: float32 [2048, 1536], P('dp')
- grad_attn_norm_gain: float32 [1536], P('dp')
- grad_w_query: float32 [1536, 1536], P('dp', 'tensor')
- grad_w_key: float32 [1536, 512], P('dp', 'tensor')
- grad_w_value: float32 [1536, 512], P('dp', 'tensor')
- grad_w_out: float32 [1536, 1536], P('dp', 'tensor')
- grad_moe_norm_gain: float32 [1536], P('dp')
- grad_w_gate: float32 [16, 1536, 512], P('dp', None, 'tensor')
- grad_w_up: float32 [16, 1536, 512], P('dp', None, 'tensor')
- grad_w_down: float32 [16, 1536, 512], P('dp', None, 'tensor')
- clipped_w_query: float32 [1536, 1536], P('dp', 'tensor')
- clipped_w_key: float32 [1536, 512], P('dp', 'tensor')
The draws below stay inside these ranges and needn't reach their ends.
Inputs may be any that keep to these rules, and one draw needn't show every extreme that they name: `expert_ids`: each row names 8 different experts; within the rows of one tree no expert is named by more than 72 rows, a bound that some block reaches. `segment_ids`: along a tree the segment numbers never fall; each segment has 1 to 32 tokens, one exactly 32. `parents`: segment 0 is the trunk and its own parent; segments 1 to 4 have parent 0; every later segment has a parent among 1 to 4.
All inputs are finite; a program needn't handle non-finite values.
Results may differ from the reference program's by a relative error of at most 0.017.
Values may be sent and summed in bfloat16 or wider, within the bound.
A program may use at most 384 MiB of HBM per device.

```python
import math
import jax
import jax.numpy as jnp
import numpy as np
from jax import lax

MODEL_DIMENSION = 1536
QUERY_HEAD_COUNT = 24
KEY_VALUE_HEADS = 8
HEAD_SIZE = 64
FFE = 512
TOP = 8
BRANCHES = 4
SEGS = 13
TREE = 128
TREES = 16
TOKENS = 2048
EXPERTS = 16
REPL = 1
CAP = 72


def draw_tokens(key, part):
    noise_key, common_key = jax.random.split(key)
    noise_vals = jax.random.normal(noise_key, (TOKENS, MODEL_DIMENSION), jnp.float32)
    common = jax.random.normal(common_key, (MODEL_DIMENSION,), jnp.float32)
    ramp_rows = 3.0 * jnp.arange(TOKENS, dtype=jnp.float32) / TOKENS
    return jnp.clip(noise_vals + ramp_rows[:, None] * common[None, :], -8.0, 8.0).astype(jnp.bfloat16)


def draw_w_query(key, part):
    base_key, head_key = jax.random.split(key)
    base_vals = jnp.clip(jax.random.normal(base_key, (MODEL_DIMENSION, QUERY_HEAD_COUNT * HEAD_SIZE), jnp.float32), -6.0, 6.0)
    head_scale = jnp.exp(jax.random.uniform(head_key, (QUERY_HEAD_COUNT,), jnp.float32, math.log(0.6), math.log(1.5)))
    column_scale = jnp.repeat(head_scale, HEAD_SIZE) * (4.0 / math.sqrt(MODEL_DIMENSION))
    return jnp.clip(base_vals * column_scale[None, :], -1.0, 1.0).astype(jnp.bfloat16)


def draw_parents(key, part):
    trunk_cols = jnp.zeros((TREES, 1 + BRANCHES), jnp.int32)
    leaf_cols = jax.random.randint(key, (TREES, SEGS - 1 - BRANCHES), 1, BRANCHES + 1, dtype=jnp.int32)
    return jnp.concatenate([trunk_cols, leaf_cols], axis=1)


def raised(entries, rng, source, target, parts, factor):
    owner, partner = [(jnp.arange(entries.shape[axis_at]) // (entries.shape[axis_at] // parts)).reshape([-1 if axis == axis_at else 1 for axis in range(entries.ndim)]) for axis_at in (source, target)]
    chosen = jax.random.permutation(rng, parts)[partner]
    strong = (owner == chosen) | (owner == (partner + parts // 2) % parts)
    return jnp.where(strong, factor * entries, entries)


def steps_of(key, extent, shards, smallest, high):
    level, own = 1.0, jax.random.fold_in(key, 6)
    for axis_at, shards_of in shards:
        steps = jnp.exp(jax.random.uniform(jax.random.fold_in(own, axis_at), (shards_of,), jnp.float32, smallest / len(shards), high / len(shards)))
        level = level * jnp.repeat(steps, extent[axis_at] // shards_of).reshape([-1 if axis == axis_at else 1 for axis in range(len(extent))])
    return level


def length_profile(number_of, total, most, lean):
    weights = [(1 << 20) // math.isqrt(rank ** lean) + 1 for rank in range(2, number_of + 1)]
    spare, counts = total - most - (number_of - 1), [1] * (number_of - 1)
    while spare > 0:
        free = [i for i in range(number_of - 1) if counts[i] < most]
        mass, left = sum([weights[i] for i in free]), spare
        for i in free:
            more = min(most - counts[i], max(1, left * weights[i] // mass), spare)
            counts[i] = counts[i] + more
            spare = spare - more
    return np.array([most] + counts)


def ragged(rng, amount, total, limit, skew):
    if amount == 2:
        one = jax.random.randint(rng, (), max(1, total - limit), min(limit, total - 1) + 1)
        return jnp.stack([one, total - one])
    lengths = jnp.asarray(length_profile(amount, total, limit, skew), jnp.int32)
    couples = (amount - 1) // 2
    giver, sink = lengths[1:1 + 2 * couples:2], lengths[2:2 + 2 * couples:2]
    margin = jnp.minimum(giver - 1, limit - sink)
    shifted = jax.random.randint(jax.random.fold_in(rng, 1), (couples,), 0, 1 << 20) % (margin + 1)
    lengths = lengths.at[1:1 + 2 * couples:2].set(giver - shifted).at[2:2 + 2 * couples:2].set(sink + shifted)
    return lengths[jax.random.permutation(jax.random.fold_in(rng, 2), amount)]


def shared_out(stream_key, own, number, rows, count, top, most, lean):
    ranking = jax.random.permutation(stream_key, count)
    crowded, ordinary = shares(count, rows * top, most, lean, True), shares(count, rows * top, most, lean, False)
    places = jnp.arange(count)

    def named(tallies, rotation):
        used = int((tallies > 0).sum())
        fixed = max(1, used // 4)
        passed = fixed + (places - fixed + rotation * (used - fixed)) % max(1, count - fixed)
        return jnp.zeros((count,), jnp.int32).at[ranking[jnp.where(places < fixed, places, passed)]].set(jnp.asarray(tallies, jnp.int32))

    tallies = jnp.where(number % 4 == 0, named(crowded, number // 4), named(ordinary, number - number // 4 - 1))
    mixed = jax.random.permutation(jax.random.fold_in(own, 3), count)
    giver, receiver = mixed[0:count // 2 * 2:2], mixed[1:count // 2 * 2:2]
    slack = jnp.minimum(tallies[giver] - 1, most - tallies[receiver]) // 2
    slack = jnp.where((giver == ranking[0]) | (receiver == ranking[0]) | (tallies[receiver] == 0), 0, jnp.maximum(slack, 0))
    passed = jax.random.randint(jax.random.fold_in(own, 4), (count // 2,), 0, 1 << 20) % (slack + 1)
    tallies = tallies.at[giver].add(-passed).at[receiver].add(passed)
    labels = jnp.searchsorted(jnp.cumsum(tallies), jnp.arange(rows * top), side="right").astype(jnp.int32)
    grid = labels.reshape(top, rows).T
    grid = grid[jax.random.permutation(jax.random.fold_in(own, 1), rows)]
    rotation = jax.random.randint(jax.random.fold_in(own, 2), (rows, 1), 0, top)
    return jnp.take_along_axis(grid, (jnp.arange(top)[None, :] + rotation) % top, axis=1)


def shares(count, total, reach, skew, full):
    loads = [(1 << 20) // math.isqrt(standing ** skew) + 1 for standing in range(1, count + 1)]
    largest = reach if full else min(reach, max(-(-total // count), total * loads[0] // sum(loads)))
    least = 1 if total - largest >= count - 1 else 0
    counts, surplus = [largest] + [least] * (count - 1), total - largest - least * (count - 1)
    while surplus > 0:
        movable = [i for i in range(1, count) if counts[i] < largest] or [i for i in range(1, count) if counts[i] < reach]
        whole, left = sum([loads[i] for i in movable]), surplus
        for i in movable:
            addition = min(reach - counts[i], max(1, left * loads[i] // whole), surplus)
            counts[i] = counts[i] + addition
            surplus = surplus - addition
    return np.array(counts)


def gaussian(stream_key, shape, scale, most, shards=(), kind=jnp.bfloat16):
    entries = jax.random.normal(stream_key, shape, jnp.float32) * scale
    if len(shards) > 0:
        entries = steps_of(stream_key, shape, shards, -0.22, 0.18) * entries
    return jnp.clip(entries, min=-most, max=most).astype(kind)


def heavy_noise(own_key, dims, scale, most, cuts, heavy, kind=jnp.bfloat16):
    result = scale * jax.random.normal(own_key, dims, jnp.float32)
    if cuts:
        result = result * steps_of(own_key, dims, cuts, -0.22, 0.18)
    return jnp.clip(raised(result, jax.random.fold_in(own_key, 3), *heavy), -most, most).astype(kind)


def setup_inputs(seed: int = 0) -> dict:
    splits = jax.random.split(jax.random.key(seed), 16)
    tokens = draw_tokens(jax.random.fold_in(splits[15], 71), 0)
    attn_norm_gain = jnp.clip(1.0 + 0.1 * jax.random.normal(splits[1], (MODEL_DIMENSION,), jnp.float32), 0.5, 1.5).astype(jnp.bfloat16)
    w_query = draw_w_query(jax.random.fold_in(splits[15], 71), 0)
    key_projection = gaussian(splits[3], (MODEL_DIMENSION, KEY_VALUE_HEADS * HEAD_SIZE), (MODEL_DIMENSION // 16) ** -0.5, 0.625, ((0, 16), (1, 2)))
    value_projection = gaussian(splits[4], (MODEL_DIMENSION, KEY_VALUE_HEADS * HEAD_SIZE), MODEL_DIMENSION ** -0.5, 0.15625, ((0, 16), (1, 2)))
    w_out = gaussian(splits[5], (MODEL_DIMENSION, QUERY_HEAD_COUNT * HEAD_SIZE), 8 ** -0.5, 2.0, ((0, 16), (1, 2)))
    moe_norm_gain = jnp.clip(1.0 + 0.1 * jax.random.normal(splits[6], (MODEL_DIMENSION,), jnp.float32), 0.5, 1.5).astype(jnp.bfloat16)
    w_gate = gaussian(splits[7], (EXPERTS * REPL, MODEL_DIMENSION, FFE // REPL), MODEL_DIMENSION ** -0.5, 0.15625, ((0, 16), (2, 2)))
    w_up = gaussian(splits[8], (EXPERTS * REPL, MODEL_DIMENSION, FFE // REPL), MODEL_DIMENSION ** -0.5, 0.15625, ((0, 16), (2, 2)))
    w_down = gaussian(splits[9], (EXPERTS * REPL, MODEL_DIMENSION, FFE // REPL), 2 ** -0.5, 4.0, ((0, 16), (2, 2)))
    router_logits = gaussian(splits[10], (TOKENS, TOP), 0.5, 3.0, ((0, 16),), jnp.float32)
    expert_ids_keys = jax.random.split(jax.random.fold_in(splits[11], 1), TOKENS // TREE)
    expert_ids_turns = jax.random.permutation(jax.random.fold_in(splits[11], 3), TOKENS // TREE)
    expert_ids = jax.vmap(lambda own, number: shared_out(jax.random.fold_in(splits[11], 2), own, number, TREE, EXPERTS, TOP, CAP, 2))(expert_ids_keys, expert_ids_turns).reshape((TOKENS, TOP))
    segment_ids = jax.vmap(lambda own: jnp.searchsorted(jnp.cumsum(ragged(own, SEGS, TREE, TREE // 4, 1)), jnp.arange(TREE), side="right"))(jax.random.split(splits[12], TREES)).reshape((TREES, TREE)).astype(jnp.int32)
    parents = draw_parents(jax.random.fold_in(splits[15], 71), 0)
    cotangent = heavy_noise(splits[14], (TOKENS, MODEL_DIMENSION), 1.0, 6.0, ((0, 16),), (0, 1, 16, 2.0))
    return {"tokens": tokens, "attn_norm_gain": attn_norm_gain, "w_query": w_query, "key_projection": key_projection, "value_projection": value_projection, "w_out": w_out, "moe_norm_gain": moe_norm_gain, "w_gate": w_gate, "w_up": w_up, "w_down": w_down, "router_logits": router_logits, "expert_ids": expert_ids, "segment_ids": segment_ids, "parents": parents, "cotangent": cotangent}


EPSILON = 1e-06
SCORE_SCALE = 1.0 / 64.0
RESIDUAL = 0.22
THETA = 10000.0
CLIP_LIMIT = 2.0
NEGATIVE = -1e+30
EXACT_PRECISION = lax.Precision.HIGHEST

@jax.custom_vjp
def low(v):
    return lax.optimization_barrier(v.astype(jnp.bfloat16)).astype(jnp.float32)

@jax.custom_vjp
def low_back(v):
    return v

def low_keep(v):
    return (low(v), None)

def low_pass(kept, grad):
    return (grad,)

def back_keep(v):
    return (v, None)

def back_low(kept, grad):
    return (low(grad),)
low.defvjp(low_keep, low_pass)
low_back.defvjp(back_keep, back_low)

def tree_layout(seg_row, par_row):
    tree_length = seg_row.shape[0]
    seg_count = par_row.shape[0]
    seg_index = jnp.arange(seg_count, dtype=jnp.int32)
    member = (seg_row[:, None] == seg_index[None, :]).astype(jnp.int32)
    seg_len = lax.optimization_barrier(jnp.sum(member, axis=0)).astype(jnp.int32)
    seg_start = (jnp.cumsum(seg_len) - seg_len).astype(jnp.int32)
    parent_hot = (par_row[:, None] == seg_index[None, :]).astype(jnp.int32)
    grand_parent = lax.optimization_barrier(jnp.sum(parent_hot * par_row[None, :], axis=1)).astype(jnp.int32)
    grand_hot = (grand_parent[:, None] == seg_index[None, :]).astype(jnp.int32)
    parent_len = lax.optimization_barrier(jnp.sum(parent_hot * seg_len[None, :], axis=1)).astype(jnp.int32)
    grand_len = lax.optimization_barrier(jnp.sum(grand_hot * seg_len[None, :], axis=1)).astype(jnp.int32)
    offset = jnp.where(seg_index != 0, parent_len, 0) + jnp.where(par_row != 0, grand_len, 0)
    tok_start = lax.optimization_barrier(jnp.sum(member * seg_start[None, :], axis=1)).astype(jnp.int32)
    tok_offset = lax.optimization_barrier(jnp.sum(member * offset[None, :], axis=1)).astype(jnp.int32)
    places = jnp.arange(tree_length, dtype=jnp.int32)
    position = (places - tok_start + tok_offset).astype(jnp.float32)
    identity = (seg_index[:, None] == seg_index[None, :]).astype(jnp.int32)
    ancestor = jnp.minimum(identity + parent_hot + grand_hot, 1)
    reached = jnp.dot(member, ancestor)
    linked = jnp.dot(reached, member.T) > 0
    allowed = linked & (places[None, :] <= places[:, None])
    return (position, allowed)

def rope_tables(position, head_dim):
    half_dim = head_dim // 2
    frequency = THETA ** (-2.0 * jnp.arange(half_dim, dtype=jnp.float32) / head_dim)
    angles = position[:, None] * frequency[None, :]
    return (jnp.cos(angles)[:, None, :], jnp.sin(angles)[:, None, :])

def apply_rotary(values_in, cosine_table, sine_values):
    half_dim = values_in.shape[-1] // 2
    first_half = values_in[..., :half_dim]
    second_half = values_in[..., half_dim:]
    return jnp.concatenate([first_half * cosine_table - second_half * sine_values, second_half * cosine_table + first_half * sine_values], axis=-1)

def slot_tables(routes, experts, capacity):
    flat_ids = routes.reshape(-1).astype(jnp.int32)
    row_count = flat_ids.shape[0]
    member = (flat_ids[:, None] == jnp.arange(experts, dtype=jnp.int32)[None, :]).astype(jnp.int32)
    before = (jnp.cumsum(member, axis=0) - member).astype(jnp.int32)
    slot_index = lax.optimization_barrier(jnp.sum(before * member, axis=1)).astype(jnp.int32)
    target = (flat_ids * capacity + slot_index).astype(jnp.int32)
    source = jnp.full((experts * capacity,), -1, jnp.int32).at[target].set(jnp.arange(row_count, dtype=jnp.int32))
    return (slot_index, target, source)

def expert_whole(weight_in):
    return weight_in.reshape(EXPERTS, REPL, MODEL_DIMENSION, FFE // REPL).transpose(0, 2, 1, 3).reshape(EXPERTS, MODEL_DIMENSION, FFE)

def tree_forward(weights, pieces):
    attn_gain, query_w, key_weight, value_weight, out_w, moe_gain, gate_parts, up_parts, down_parts = weights
    gate_w = expert_whole(gate_parts)
    up_w = expert_whole(up_parts)
    down_w = expert_whole(down_parts)
    inputs, seg_row, par_row, routes, logits = pieces
    tree_length = inputs.shape[0]
    inv_attn = lax.rsqrt(lax.optimization_barrier(jnp.mean(inputs * inputs, axis=1, keepdims=True)) + EPSILON)
    normalized_rows = low(inputs * inv_attn * attn_gain)
    position, allowed = tree_layout(seg_row, par_row)
    cosine_table, sine_values = rope_tables(position, HEAD_SIZE)
    query_linear = low_back(jnp.dot(normalized_rows, query_w, precision=EXACT_PRECISION)).reshape(tree_length, QUERY_HEAD_COUNT, HEAD_SIZE)
    key_linear = low_back(jnp.dot(normalized_rows, key_weight, precision=EXACT_PRECISION)).reshape(tree_length, KEY_VALUE_HEADS, HEAD_SIZE)
    query_rows = low(apply_rotary(query_linear, cosine_table, sine_values)).reshape(tree_length, KEY_VALUE_HEADS, QUERY_HEAD_COUNT // KEY_VALUE_HEADS, HEAD_SIZE)
    keys_all = low(apply_rotary(key_linear, cosine_table, sine_values))
    value_rows_full = low(low_back(jnp.dot(normalized_rows, value_weight, precision=EXACT_PRECISION))).reshape(tree_length, KEY_VALUE_HEADS, HEAD_SIZE)
    scores = low_back(jnp.einsum('qhgd,khd->hgqk', query_rows, keys_all, precision=EXACT_PRECISION) * SCORE_SCALE)
    scores = jnp.where(allowed[None, None], scores, NEGATIVE)
    head_peak = lax.optimization_barrier(jnp.max(scores, axis=(2, 3))).reshape(QUERY_HEAD_COUNT)
    row_max = lax.optimization_barrier(jnp.max(scores, axis=3, keepdims=True))
    expo = jnp.exp(scores - row_max)
    prob_low = low(expo / lax.optimization_barrier(jnp.sum(expo, axis=3, keepdims=True)))
    head_out = low_back(low(jnp.einsum('hgqk,khd->qhgd', prob_low, value_rows_full, precision=EXACT_PRECISION))).reshape(tree_length, QUERY_HEAD_COUNT * HEAD_SIZE)
    attn_mix = low_back(jnp.dot(head_out, out_w.T, precision=EXACT_PRECISION))
    hidden = inputs + RESIDUAL * attn_mix
    inv_moe = lax.rsqrt(lax.optimization_barrier(jnp.mean(hidden * hidden, axis=1, keepdims=True)) + EPSILON)
    moe_in = low(hidden * inv_moe * moe_gain)
    logit_max = lax.optimization_barrier(jnp.max(logits, axis=1, keepdims=True))
    logit_exp = jnp.exp(logits - logit_max)
    gate_probs = logit_exp / lax.optimization_barrier(jnp.sum(logit_exp, axis=1, keepdims=True))
    slot_index, target, source = slot_tables(routes, EXPERTS, CAP)
    filled = source >= 0
    source_token = jnp.maximum(source, 0) // TOP
    buffer = low_back(jnp.where(filled[:, None], moe_in[source_token], 0.0)).reshape(EXPERTS, CAP, MODEL_DIMENSION)
    gate_pre = low_back(jnp.einsum('ecd,edf->ecf', buffer, gate_w, precision=EXACT_PRECISION))
    up_pre = low_back(jnp.einsum('ecd,edf->ecf', buffer, up_w, precision=EXACT_PRECISION))
    active = low(gate_pre / (1.0 + jnp.exp(-gate_pre)) * up_pre)
    expert_out = low_back(low(jnp.einsum('ecf,edf->ecd', active, down_w, precision=EXACT_PRECISION))).reshape(EXPERTS * CAP, MODEL_DIMENSION)
    picked = expert_out[target].reshape(tree_length, TOP, MODEL_DIMENSION)
    expert_mix = lax.optimization_barrier(jnp.sum(gate_probs[:, :, None] * picked, axis=1))
    output = low(hidden + RESIDUAL * expert_mix)
    return (output, head_peak)

def reference(tokens, attn_norm_gain, w_query, key_projection, value_projection, w_out, moe_norm_gain, w_gate, w_up, w_down, router_logits, expert_ids, segment_ids, parents, cotangent):
    weights = tuple((item.astype(jnp.float32) for item in (attn_norm_gain, w_query, key_projection, value_projection, w_out, moe_norm_gain, w_gate, w_up, w_down)))
    inputs = tokens.astype(jnp.float32).reshape(TREES, TREE, MODEL_DIMENSION)
    routes = expert_ids.reshape(TREES, TREE, TOP)
    logits = router_logits.astype(jnp.float32).reshape(TREES, TREE, TOP)
    tree_step = jax.checkpoint(tree_forward)

    def forward(inputs_all, weights_all):

        def one_tree(pieces):
            return tree_step(weights_all, pieces)
        return lax.map(one_tree, (inputs_all, segment_ids, parents, routes, logits))
    output, backward, peaks = jax.vjp(forward, inputs, weights, has_aux=True)
    grad_inputs, grad_weights = backward(cotangent.astype(jnp.float32).reshape(TREES, TREE, MODEL_DIMENSION))
    head_peak = lax.optimization_barrier(jnp.max(peaks, axis=0))
    scale_factor = CLIP_LIMIT / jnp.maximum(head_peak, CLIP_LIMIT)
    query_scale = jnp.repeat(jnp.sqrt(scale_factor), HEAD_SIZE)
    key_clip_scale = jnp.repeat(jnp.sqrt(lax.optimization_barrier(jnp.min(scale_factor.reshape(KEY_VALUE_HEADS, QUERY_HEAD_COUNT // KEY_VALUE_HEADS), axis=1))), HEAD_SIZE)
    clipped_query = weights[1] * query_scale[None, :]
    clipped_key = weights[2] * key_clip_scale[None, :]
    return (output.reshape(TOKENS, MODEL_DIMENSION).astype(jnp.bfloat16), grad_inputs.reshape(TOKENS, MODEL_DIMENSION), grad_weights[0], grad_weights[1], grad_weights[2], grad_weights[3], grad_weights[4], grad_weights[5], grad_weights[6], grad_weights[7], grad_weights[8], clipped_query, clipped_key)
```

```python
import functools

import jax
import jax.numpy as jnp
from jax import lax
from jax.experimental import pallas as pl
from jax.experimental.pallas import tpu as pltpu
from jax.sharding import PartitionSpec as P

HEAD_SIZE = 64
FFE = 512
TOP = 8


EPSILON = 1e-06
SCORE_SCALE = 1.0 / 64.0
RESIDUAL = 0.22
THETA = 10000.0
CLIP_LIMIT = 2.0
NEGATIVE = -1e30


def tree_layout(seg_row, par_row):
    tree_length = seg_row.shape[0]
    seg_count = par_row.shape[0]
    seg_index = jnp.arange(seg_count, dtype=jnp.int32)
    member = (seg_row[:, None] == seg_index[None, :]).astype(jnp.int32)
    seg_len = jnp.sum(member, axis=0)
    seg_start = jnp.sum(jnp.where(seg_index[:, None] > seg_index[None, :], seg_len[None, :], 0), axis=1)
    parent_hot = (par_row[:, None] == seg_index[None, :]).astype(jnp.int32)
    grand_parent = jnp.sum(parent_hot * par_row[None, :], axis=1)
    grand_hot = (grand_parent[:, None] == seg_index[None, :]).astype(jnp.int32)
    parent_len = jnp.sum(parent_hot * seg_len[None, :], axis=1)
    grand_len = jnp.sum(grand_hot * seg_len[None, :], axis=1)
    offset = jnp.where(seg_index != 0, parent_len, 0) + jnp.where(par_row != 0, grand_len, 0)
    tok_start = jnp.sum(member * seg_start[None, :], axis=1)
    tok_offset = jnp.sum(member * offset[None, :], axis=1)
    places = jnp.arange(tree_length, dtype=jnp.int32)
    position = (places - tok_start + tok_offset).astype(jnp.float32)
    identity = (seg_index[:, None] == seg_index[None, :]).astype(jnp.int32)
    ancestor = jnp.minimum(identity + parent_hot + grand_hot, 1)
    reached = jnp.dot(member, ancestor)
    linked = jnp.dot(reached, member.T) > 0
    allowed = linked & (places[None, :] <= places[:, None])
    return (position, allowed)


def rope_tables(position, head_dim):
    half_dim = head_dim // 2
    frequency = THETA ** (-2.0 * jnp.arange(half_dim, dtype=jnp.float32) / head_dim)
    angles = position[:, None] * frequency[None, :]
    return (jnp.cos(angles)[:, None, :], jnp.sin(angles)[:, None, :])


def apply_rotary(values_in, cosine_table, sine_values):
    half_dim = values_in.shape[-1] // 2
    first_half = values_in[..., :half_dim]
    second_half = values_in[..., half_dim:]
    return jnp.concatenate(
        [
            first_half * cosine_table - second_half * sine_values,
            second_half * cosine_table + first_half * sine_values,
        ],
        axis=-1,
    )


def rotate_back(grads_in, cosine_table, sine_values):
    half_dim = grads_in.shape[-1] // 2
    first_half = grads_in[..., :half_dim]
    second_half = grads_in[..., half_dim:]
    return jnp.concatenate(
        [
            first_half * cosine_table + second_half * sine_values,
            second_half * cosine_table - first_half * sine_values,
        ],
        axis=-1,
    )


def slot_tables(routes, experts, capacity):
    flat_ids = routes.reshape(-1)
    row_count = flat_ids.shape[0]
    member = (flat_ids[:, None] == jnp.arange(experts, dtype=jnp.int32)[None, :]).astype(jnp.int32)
    row_total = flat_ids.shape[0]
    before = jnp.dot((jnp.arange(row_total)[:, None] > jnp.arange(row_total)[None, :]).astype(jnp.float32), member.astype(jnp.float32), precision=lax.Precision.HIGHEST).astype(jnp.int32)
    slot_index = jnp.sum(before * member, axis=1)
    target = flat_ids * capacity + slot_index
    source = (
        jnp.full((experts * capacity,), -1, jnp.int32)
        .at[target]
        .set(jnp.arange(row_count, dtype=jnp.int32))
    )
    return (flat_ids, slot_index, source)


def contract_rows(left, right):
    return lax.dot_general(
        left, right, (((0,), (0,)), ((), ())), preferred_element_type=jnp.float32
    )


def contract_cols(left, right):
    return lax.dot_general(
        left, right, (((1,), (1,)), ((), ())), preferred_element_type=jnp.float32
    )


def expert_forward(inputs, gate_w, up_w, down_w):
    gate_pre = jnp.dot(inputs, gate_w, preferred_element_type=jnp.float32)
    up_pre = jnp.dot(inputs, up_w, preferred_element_type=jnp.float32)
    active = (gate_pre / (1.0 + jnp.exp(-gate_pre)) * up_pre).astype(jnp.bfloat16)
    return (contract_cols(active, down_w), (gate_pre, up_pre, active))


def expert_backward(inputs, grads_out, gate_w, up_w, down_w, kept_acts):
    gate_pre, up_pre, active = kept_acts
    d_active = jnp.dot(grads_out, down_w, preferred_element_type=jnp.float32)
    grad_down = contract_rows(grads_out, active)
    sigmoid_val = 1.0 / (1.0 + jnp.exp(-gate_pre))
    d_gate = (d_active * up_pre * sigmoid_val * (1.0 + gate_pre * (1.0 - sigmoid_val))).astype(
        jnp.bfloat16
    )
    d_up = (d_active * gate_pre * sigmoid_val).astype(jnp.bfloat16)
    grad_gate = contract_rows(inputs, d_gate)
    grad_up = contract_rows(inputs, d_up)
    d_inputs = contract_cols(d_gate, gate_w) + contract_cols(d_up, up_w)
    return (d_inputs, grad_gate, grad_up, grad_down)


def send_rows(rows_in):
    return lax.all_to_all(rows_in, "dp", split_axis=0, concat_axis=0, tiled=True)


def return_rows(rows_in):
    return lax.all_to_all(
        rows_in.astype(jnp.bfloat16), "dp", split_axis=0, concat_axis=0, tiled=True
    ).astype(rows_in.dtype)


def send_grads(rows_in):
    return lax.all_to_all(rows_in, "dp", split_axis=0, concat_axis=0, tiled=True)


def return_grads(rows_in):
    return lax.all_to_all(
        rows_in.astype(jnp.bfloat16), "dp", split_axis=0, concat_axis=0, tiled=True
    ).astype(rows_in.dtype)


def share_slots(partial_rows):
    return lax.psum_scatter(partial_rows, "tensor", scatter_dimension=1, tiled=True)


def on_device_general(
    tokens,
    attn_norm_gain,
    w_query,
    key_projection,
    value_projection,
    w_out,
    moe_norm_gain,
    w_gate,
    w_up,
    w_down,
    router_logits,
    expert_ids,
    segment_ids,
    parents,
    cotangent,
):
    length = tokens.shape[0]
    model_width = tokens.shape[1]
    q_cols = w_query.shape[1]
    kv_cols = key_projection.shape[1]
    q_heads = q_cols // HEAD_SIZE
    kv_heads = kv_cols // HEAD_SIZE
    group_size = q_heads // kv_heads
    dp_size = lax.axis_size("dp")
    tensor_ranks = lax.axis_size("tensor")
    replicas = FFE // (w_gate.shape[2] * tensor_ranks)
    experts = dp_size // replicas
    capacity = 4 * (9 * length * TOP // (32 * experts))
    share_rows = capacity // tensor_ranks
    first_slot = lax.axis_index("tensor") * share_rows
    block_rows = min(length, 512)
    attn_gain, moe_gain, query_w, key_weight, value_weight, out_w = (
        lax.all_gather(attn_norm_gain, "dp", axis=0, tiled=True),
        lax.all_gather(moe_norm_gain, "dp", axis=0, tiled=True),
        lax.all_gather(w_query, "dp", axis=0, tiled=True),
        lax.all_gather(key_projection, "dp", axis=0, tiled=True),
        lax.all_gather(value_projection, "dp", axis=0, tiled=True),
        lax.all_gather(w_out, "dp", axis=0, tiled=True),
    )
    attn_gain_f = attn_gain.astype(jnp.float32)
    moe_gain_f = moe_gain.astype(jnp.float32)
    inputs = tokens.astype(jnp.float32)
    inv_attn = lax.rsqrt(jnp.mean(inputs * inputs, axis=1, keepdims=True) + EPSILON)
    unit_attn = inputs * inv_attn
    normalized_rows = (unit_attn * attn_gain_f).astype(jnp.bfloat16)
    position, allowed = tree_layout(segment_ids[0], parents[0])
    cosine_table, sine_values = rope_tables(position, HEAD_SIZE)
    query_linear = jnp.dot(normalized_rows, query_w, preferred_element_type=jnp.float32).reshape(
        length, q_heads, HEAD_SIZE
    )
    key_linear = jnp.dot(normalized_rows, key_weight, preferred_element_type=jnp.float32).reshape(
        length, kv_heads, HEAD_SIZE
    )
    query_heads = (
        apply_rotary(query_linear, cosine_table, sine_values)
        .astype(jnp.bfloat16)
        .reshape(length, kv_heads, group_size, HEAD_SIZE)
    )
    key_heads = apply_rotary(key_linear, cosine_table, sine_values).astype(jnp.bfloat16)
    value_heads = (
        jnp.dot(normalized_rows, value_weight, preferred_element_type=jnp.float32)
        .astype(jnp.bfloat16)
        .reshape(length, kv_heads, HEAD_SIZE)
    )
    q_block = query_heads
    mask_rows = allowed[None, None]
    scores = (
        jnp.einsum("qhgd,khd->hgqk", q_block, key_heads, preferred_element_type=jnp.float32)
        * SCORE_SCALE
    )
    scores = jnp.where(mask_rows, scores, NEGATIVE)
    peak_parts = [jnp.max(scores, axis=(2, 3))]
    row_max = jnp.max(scores, axis=3, keepdims=True)
    expo = jnp.exp(scores - row_max)
    row_total = jnp.sum(expo, axis=3, keepdims=True)
    lse_parts = [row_max + jnp.log(row_total)]
    prob_low = (expo / row_total).astype(jnp.bfloat16)
    block_outs = jnp.einsum(
        "hgqk,khd->qhgd", prob_low, value_heads, preferred_element_type=jnp.float32
    )
    head_out = block_outs.reshape(length, q_cols).astype(jnp.bfloat16)
    attn_mix = lax.psum(contract_cols(head_out, out_w), "tensor")
    hidden = inputs + RESIDUAL * attn_mix
    head_peak = lax.pmax(jnp.max(jnp.stack(peak_parts), axis=0).reshape(q_heads), "dp")
    inv_moe = lax.rsqrt(jnp.mean(hidden * hidden, axis=1, keepdims=True) + EPSILON)
    unit_moe = hidden * inv_moe
    moe_in = (unit_moe * moe_gain_f).astype(jnp.bfloat16)
    logit_max = jnp.max(router_logits, axis=1, keepdims=True)
    logit_exp = jnp.exp(router_logits - logit_max)
    gate_probs = logit_exp / jnp.sum(logit_exp, axis=1, keepdims=True)
    flat_ids, slot_index, source = slot_tables(expert_ids, experts, capacity)
    filled = source >= 0
    source_row = jnp.maximum(source, 0)
    source_token = source_row // TOP
    dispatch_rows = jnp.where(
        filled[:, None], moe_in[source_token], jnp.zeros((), jnp.bfloat16)
    ).reshape(experts, capacity, model_width)
    arrived = send_rows(jnp.repeat(dispatch_rows, replicas, axis=0))
    gate_w, up_w, down_w = (w_gate[0], w_up[0], w_down[0])
    expert_in = arrived.reshape(dp_size * capacity, model_width)
    expert_out, kept_acts = expert_forward(expert_in, gate_w, up_w, down_w)
    partial_out = share_slots(expert_out.reshape(dp_size, capacity, model_width))
    back_parts = return_rows(partial_out).reshape(experts, replicas, share_rows, model_width)
    back_rows = (
        jnp.sum(back_parts, axis=1).astype(jnp.bfloat16).reshape(experts * share_rows, model_width)
    )
    own_slot = ((slot_index >= first_slot) & (slot_index < first_slot + share_rows)).reshape(
        length, TOP
    )
    local_index = (
        flat_ids * share_rows + jnp.clip(slot_index - first_slot, 0, share_rows - 1)
    ).reshape(length, TOP)
    mix_part = jnp.zeros((length, model_width), jnp.float32)
    for column in range(TOP):
        gate_weight = jnp.where(own_slot[:, column], gate_probs[:, column], 0.0)
        mix_part = mix_part + gate_weight[:, None] * back_rows[local_index[:, column]].astype(
            jnp.float32
        )
    expert_mix = lax.psum(mix_part.astype(jnp.bfloat16), "tensor").astype(jnp.float32)
    output = (hidden + RESIDUAL * expert_mix).astype(jnp.bfloat16)
    grad_output = cotangent.astype(jnp.float32)
    mix_grad = RESIDUAL * grad_output
    row_gate = gate_probs.reshape(-1)[source_row]
    grad_rows = (
        jnp.where(filled[:, None], row_gate[:, None] * mix_grad[source_token], 0.0)
        .astype(jnp.bfloat16)
        .reshape(experts, capacity, model_width)
    )
    grad_arrived = send_grads(jnp.repeat(grad_rows, replicas, axis=0)).reshape(
        dp_size * capacity, model_width
    )
    d_inputs, grad_gate, grad_up, grad_down = expert_backward(
        expert_in, grad_arrived, gate_w, up_w, down_w, kept_acts
    )
    d_back = share_slots(d_inputs.reshape(dp_size, capacity, model_width))
    grad_gate, grad_up, grad_down = (grad_gate[None], grad_up[None], grad_down[None])
    d_parts = return_grads(d_back).reshape(experts, replicas, share_rows, model_width)
    d_returned = (
        jnp.sum(d_parts, axis=1).astype(jnp.bfloat16).reshape(experts * share_rows, model_width)
    )
    d_mix_part = jnp.zeros((length, model_width), jnp.float32)
    for column in range(TOP):
        d_mix_part = d_mix_part + jnp.where(
            own_slot[:, column][:, None],
            d_returned[local_index[:, column]].astype(jnp.float32),
            0.0,
        )
    d_moe_in = lax.psum(d_mix_part, "tensor")
    scaled_moe = d_moe_in * moe_gain_f
    grad_moe_gain = jnp.sum(d_moe_in * unit_moe, axis=0)
    d_hidden = grad_output + inv_moe * (
        scaled_moe - unit_moe * jnp.mean(scaled_moe * unit_moe, axis=1, keepdims=True)
    )
    d_attn = (RESIDUAL * d_hidden).astype(jnp.bfloat16)
    grad_out_w = contract_rows(d_attn, head_out)
    d_heads = (
        jnp.dot(d_attn, out_w, preferred_element_type=jnp.float32)
        .astype(jnp.bfloat16)
        .reshape(length, kv_heads, group_size, HEAD_SIZE)
    )
    d_query_parts = []
    d_key = jnp.zeros((length, kv_heads, HEAD_SIZE), jnp.float32)
    d_value = jnp.zeros((length, kv_heads, HEAD_SIZE), jnp.float32)
    for block_number, row_begin in enumerate(range(0, length, block_rows)):
        q_block = query_heads
        mask_rows = allowed[None, None]
        scores = (
            jnp.einsum("qhgd,khd->hgqk", q_block, key_heads, preferred_element_type=jnp.float32)
            * SCORE_SCALE
        )
        scores = jnp.where(mask_rows, scores, NEGATIVE)
        prob_full = jnp.exp(scores - lse_parts[block_number])
        prob_low = prob_full.astype(jnp.bfloat16)
        d_value = jnp.einsum(
            "hgqk,qhgd->khd", prob_low, d_heads, preferred_element_type=jnp.float32
        )
        d_prob = jnp.einsum(
            "qhgd,khd->hgqk", d_heads, value_heads, preferred_element_type=jnp.float32
        )
        inner = jnp.sum(prob_full * d_prob, axis=3, keepdims=True)
        d_scores = (prob_full * (d_prob - inner)).astype(jnp.bfloat16)
        d_query_parts.append(
            jnp.einsum("hgqk,khd->qhgd", d_scores, key_heads, preferred_element_type=jnp.float32)
            * SCORE_SCALE
        )
        d_key = (
            jnp.einsum("hgqk,qhgd->khd", d_scores, q_block, preferred_element_type=jnp.float32)
            * SCORE_SCALE
        )
    d_query_all = d_query_parts[0].reshape(length, q_heads, HEAD_SIZE)
    d_query_lin = (
        rotate_back(d_query_all, cosine_table, sine_values)
        .astype(jnp.bfloat16)
        .reshape(length, q_cols)
    )
    d_key_lin = (
        rotate_back(d_key, cosine_table, sine_values).astype(jnp.bfloat16).reshape(length, kv_cols)
    )
    d_value_lin = d_value.astype(jnp.bfloat16).reshape(length, kv_cols)
    grad_query_w = contract_rows(normalized_rows, d_query_lin)
    grad_key_w = contract_rows(normalized_rows, d_key_lin)
    grad_value_w = contract_rows(normalized_rows, d_value_lin)
    d_normed_part = (
        contract_cols(d_query_lin, query_w)
        + contract_cols(d_key_lin, key_weight)
        + contract_cols(d_value_lin, value_weight)
    )
    d_normed = lax.psum(d_normed_part.astype(jnp.bfloat16), "tensor").astype(jnp.float32)
    scaled_attn = d_normed * attn_gain_f
    grad_attn_gain = jnp.sum(d_normed * unit_attn, axis=0)
    input_grad = d_hidden + inv_attn * (
        scaled_attn - unit_attn * jnp.mean(scaled_attn * unit_attn, axis=1, keepdims=True)
    )
    reduced = (
        lax.psum_scatter(grad_attn_gain, "dp", scatter_dimension=0, tiled=True),
        lax.psum_scatter(grad_moe_gain, "dp", scatter_dimension=0, tiled=True),
        lax.psum_scatter(grad_query_w, "dp", scatter_dimension=0, tiled=True),
        lax.psum_scatter(grad_key_w, "dp", scatter_dimension=0, tiled=True),
        lax.psum_scatter(grad_value_w, "dp", scatter_dimension=0, tiled=True),
        lax.psum_scatter(grad_out_w, "dp", scatter_dimension=0, tiled=True),
    )
    scale_factor = CLIP_LIMIT / jnp.maximum(head_peak, CLIP_LIMIT)
    query_scale = jnp.repeat(jnp.sqrt(scale_factor), HEAD_SIZE)
    key_clip_scale = jnp.repeat(
        jnp.sqrt(jnp.min(scale_factor.reshape(kv_heads, group_size), axis=1)), HEAD_SIZE
    )
    clipped_query = w_query.astype(jnp.float32) * query_scale[None, :]
    clipped_key = key_projection.astype(jnp.float32) * key_clip_scale[None, :]
    return (
        output,
        input_grad,
        reduced[0],
        reduced[2],
        reduced[3],
        reduced[4],
        reduced[5],
        reduced[1],
        grad_gate,
        grad_up,
        grad_down,
        clipped_query,
        clipped_key,
    )


MESH_IDS = pl.DeviceIdType.MESH
F32 = jnp.float32
BF16 = jnp.bfloat16


class Place:
    def __init__(self, line):
        self.line = line
        self.count = 4 * line
        me = lax.axis_index("dp")
        self.core = lax.axis_index("tensor")
        self.me = me
        self.z = me // 4
        y, x = (me // 2) % 2, me % 2
        self.step_a, self.step_b = 2 - self.core, 1 + self.core
        self.a = y * (1 - self.core) + x * self.core
        self.b = x * (1 - self.core) + y * self.core

    def part(self, z, a, b):
        return z * 4 + a * self.step_a + b * self.step_b

    def up(self):
        return (self.me + 4, self.core)

    def down(self):
        return (self.me - 4, self.core)

    def beside_a(self):
        return (self.me + self.step_a * (1 - 2 * self.a), self.core)

    def beside_b(self):
        return (self.me + self.step_b * (1 - 2 * self.b), self.core)

    def twin(self):
        return (self.me, 1 - self.core)

    def peer(self, offset):
        return lax.rem(self.me + offset, self.count)


def enter(place):
    barrier = pltpu.get_barrier_semaphore()

    def greet(offset, carry):
        pl.semaphore_signal(
            barrier, inc=1, device_id=(place.peer(offset), place.core), device_id_type=MESH_IDS
        )
        return carry

    lax.fori_loop(1, place.count, greet, 0)
    pl.semaphore_signal(barrier, inc=1, device_id=place.twin(), device_id_type=MESH_IDS)
    pl.semaphore_wait(barrier, place.count)


def remote(src, dst, send_sem, recv_sem, device):
    return pltpu.make_async_remote_copy(
        src_ref=src,
        dst_ref=dst,
        send_sem=send_sem,
        recv_sem=recv_sem,
        device_id=device,
        device_id_type=MESH_IDS,
    )


class Notes:
    def __init__(self, place, src, dst, send_sem, recv_sem, alike):
        self.place, self.src, self.dst = place, src, dst
        self.send_sem, self.recv_sem, self.alike = send_sem, recv_sem, alike

    def _copy(self, offset, source):
        place = self.place
        to = place.peer(offset)
        return remote(
            self.src if self.alike else self.src.at[to],
            self.dst.at[source],
            self.send_sem.at[offset],
            self.recv_sem.at[source],
            (to, place.core),
        )

    def start(self):
        def send(offset, carry):
            self._copy(offset, self.place.me).start()
            return carry

        lax.fori_loop(1, self.place.count, send, 0)
        me = self.place.me
        self.dst[me] = self.src[...] if self.alike else self.src[me]

    def finish(self):
        def settle(offset, carry):
            self._copy(offset, self.place.peer(offset)).wait_recv()
            self._copy(offset, self.place.me).wait_send()
            return carry

        lax.fori_loop(1, self.place.count, settle, 0)


class Gather:
    def __init__(self, place, view, send_sem, recv_sem):
        self.place, self.view = place, view
        self.send_sem, self.recv_sem = send_sem, recv_sem

    def _copy(self, part, way):
        place, line = self.place, self.place.line
        z = part // 4
        if way == "up":
            slot, device = z, place.up()
        elif way == "down":
            slot, device = line + z, place.down()
        elif way == "a":
            slot, device = 2 * line + z, place.beside_a()
        else:
            slot, device = 3 * line + part - place.b * place.step_b, place.beside_b()
        ref = self.view(part)
        return remote(ref, ref, self.send_sem.at[slot], self.recv_sem.at[part], device)

    def _await(self, part):
        self._copy(part, "b").wait_recv()

    def start(self):
        place = self.place
        me, last = place.me, place.line - 1

        @pl.when(place.z < last)
        def _():
            self._copy(me, "up").start()

        @pl.when(place.z > 0)
        def _():
            self._copy(me, "down").start()

        self._copy(me, "a").start()
        self._copy(me, "b").start()

    def along(self, step):
        place = self.place
        last = place.line - 1
        below = place.part(place.z - step, place.a, place.b)
        above = place.part(place.z + step, place.a, place.b)

        @pl.when(place.z >= step)
        def _():
            self._await(below)

            @pl.when(place.z < last)
            def _():
                self._copy(below, "up").start()

            self._copy(below, "a").start()
            self._copy(below, "b").start()

        @pl.when(place.z + step <= last)
        def _():
            self._await(above)

            @pl.when(place.z > 0)
            def _():
                self._copy(above, "down").start()

            self._copy(above, "a").start()
            self._copy(above, "b").start()

    def across(self, step):
        place = self.place

        def take(z):
            part = place.part(z, 1 - place.a, place.b)
            self._await(part)
            self._copy(part, "b").start()

        if step == 0:
            take(place.z)
        else:
            pl.when(place.z >= step)(lambda: take(place.z - step))
            pl.when(place.z + step < place.line)(lambda: take(place.z + step))

    def finish(self):
        place, last = self.place, self.place.line - 1

        def settle(z, carry):
            for a in (0, 1):
                self._await(place.part(z, a, 1 - place.b))
                self._copy(place.part(z, a, place.b), "b").wait_send()
            self._copy(place.part(z, place.a, place.b), "a").wait_send()
            own = place.part(z, place.a, place.b)

            @pl.when(jnp.logical_and(z <= place.z, place.z < last))
            def _():
                self._copy(own, "up").wait_send()

            @pl.when(jnp.logical_and(z >= place.z, place.z > 0))
            def _():
                self._copy(own, "down").wait_send()

            return carry

        lax.fori_loop(0, place.line, settle, 0)


def gather_all(gathers):
    line = gathers[0].place.line
    for g in gathers:
        g.start()
    for step in range(1, line + 1):
        for g in gathers:
            if step < line:
                g.along(step)
            g.across(step - 1)
    for g in gathers:
        g.finish()


class Reduce:
    def __init__(self, place, parts, from_b, from_a, from_z, sems):
        self.place, self.parts = place, parts
        self.from_b, self.from_a, self.from_z = from_b, from_a, from_z
        self.send_sem, self.recv_sem = sems

    def _to_b(self, z, a, slot=None):
        place, line = self.place, self.place.line
        slot = z * 2 + a
        return remote(
            self.parts.at[place.part(z, a, 1 - place.b)],
            self.from_b.at[slot],
            self.send_sem.at[slot],
            self.recv_sem.at[slot],
            place.beside_b(),
        )

    def _to_a(self, z):
        place, line = self.place, self.place.line
        return remote(
            self.parts.at[place.part(z, 1 - place.a, place.b)],
            self.from_a.at[z],
            self.send_sem.at[2 * line + z],
            self.recv_sem.at[2 * line + z],
            place.beside_a(),
        )

    def _along(self, z, way):
        place, line = self.place, self.place.line
        slot = way * line + z
        return remote(
            self.parts.at[place.part(z, place.a, place.b)],
            self.from_z.at[slot],
            self.send_sem.at[3 * line + slot],
            self.recv_sem.at[3 * line + slot],
            place.up() if way == 0 else place.down(),
        )

    def _add(self, part, block):
        self.parts[part] = (self.parts[part].astype(F32) + block.astype(F32)).astype(BF16)

    def send_b(self, z, a):
        self._to_b(z, a).start()

    def fold_b(self, z, a):
        self._to_b(z, a).wait_recv()
        self._add(self.place.part(z, a, self.place.b), self.from_b[z * 2 + a])

    def send_a(self, z):
        self._to_a(z).start()

    def fold_a(self, z):
        self._to_a(z).wait_recv()
        self._add(self.place.part(z, self.place.a, self.place.b), self.from_a[z])

    def pass_up(self, z):
        place = self.place

        @pl.when(place.z < z)
        def _():
            @pl.when(place.z > 0)
            def _():
                self._along(z, 0).wait_recv()
                self._add(place.part(z, place.a, place.b), self.from_z[z])

            self._along(z, 0).start()

    def pass_down(self, z):
        place, line = self.place, self.place.line

        @pl.when(place.z > z)
        def _():
            @pl.when(place.z < line - 1)
            def _():
                self._along(z, 1).wait_recv()
                self._add(place.part(z, place.a, place.b), self.from_z[line + z])

            self._along(z, 1).start()

    def result(self, out):
        place, line = self.place, self.place.line
        me, z = place.me, place.z
        out[...] = self.parts[me].astype(F32)

        @pl.when(z > 0)
        def _():
            self._along(z, 0).wait_recv()
            out[...] += self.from_z[z].astype(F32)

        @pl.when(z < line - 1)
        def _():
            self._along(z, 1).wait_recv()
            out[...] += self.from_z[line + z].astype(F32)

    def settle(self):
        place, line = self.place, self.place.line

        def wait(z, carry):
            for a in (0, 1):
                self._to_b(z, a).wait_send()
            self._to_a(z).wait_send()

            @pl.when(place.z < z)
            def _():
                self._along(z, 0).wait_send()

            @pl.when(place.z > z)
            def _():
                self._along(z, 1).wait_send()

            return carry

        lax.fori_loop(0, line, wait, 0)


def ends_first(line):
    order = []
    for i in range((line + 1) // 2):
        order += [i] if i == line - 1 - i else [i, line - 1 - i]
    return order


def reduce_rest(reduces):
    line = reduces[0].place.line
    place = reduces[0].place
    for r in reduces:
        for z in ends_first(line):
            r.fold_b(z, 1 - place.a)
            r.send_a(z)
        for z in ends_first(line):
            r.fold_b(z, place.a)
        for z in ends_first(line):
            r.fold_a(z)
        for k in range(line):
            r.pass_up(line - 1 - k)
            r.pass_down(k)


def weights_kernel(
    line,
    query_ref,
    key_ref,
    value_ref,
    out_ref,
    cot_ref,
    note_ref,
    query_all,
    key_all,
    value_all,
    out_all,
    cot_all,
    notes,
    sends,
    recvs,
    note_send,
    note_recv,
    twin_sems,
    local_sems,
):
    place = Place(line)
    half = cot_ref.shape[1] // 2
    span = pl.ds(pl.multiple_of(place.core * half, 128), half)
    own = []
    for i, (src, dst) in enumerate(
        ((query_ref, query_all), (key_ref, key_all), (value_ref, value_all), (out_ref, out_all), (cot_ref, cot_all))
    ):
        own.append(pltpu.make_async_copy(src, dst.at[place.me], local_sems.at[i]))
        own[-1].start()
    enter(place)
    note = Notes(place, note_ref, notes, note_send, note_recv, False)
    note.start()
    for c in own:
        c.wait()
    gathers = [
        Gather(place, lambda p, ref=ref: ref.at[p], sends.at[i], recvs.at[i])
        for i, ref in enumerate((query_all, key_all, value_all, out_all))
    ]
    gathers.append(Gather(place, lambda p: cot_all.at[p, :, span], sends.at[4], recvs.at[4]))
    gather_all(gathers)
    swap_halves(place, cot_all, span, twin_sems)
    note.finish()


def swap_halves(place, ref, span, sems):
    def twin(part):
        view = ref.at[part, :, span]
        return remote(view, view, sems.at[0, part], sems.at[1, part], place.twin())

    def begin(offset, carry):
        twin(place.peer(offset)).start()
        return carry

    def end(offset, carry):
        copy = twin(place.peer(offset))
        copy.wait_send()
        copy.wait_recv()
        return carry

    lax.fori_loop(1, place.count, begin, 0)
    lax.fori_loop(1, place.count, end, 0)


ANY = pl.BlockSpec(memory_space=pl.ANY)
IN_VMEM = pl.BlockSpec(memory_space=pltpu.VMEM)


def params(number):
    return pltpu.CompilerParams(
        collective_id=number, has_side_effects=True, vmem_limit_bytes=56 * 2**20
    )


def gather_weights(line, query, key, value, out, cotangent, note):
    count = 4 * line
    shapes = [query.shape, key.shape, value.shape, out.shape, cotangent.shape]
    return pl.pallas_call(
        functools.partial(weights_kernel, line),
        out_shape=[jax.ShapeDtypeStruct((count, *s), BF16) for s in shapes]
        + [jax.ShapeDtypeStruct(note.shape, F32)],
        in_specs=[ANY] * 5 + [IN_VMEM],
        out_specs=[ANY] * 5 + [IN_VMEM],
        scratch_shapes=[
            pltpu.SemaphoreType.DMA((5, 3 * line + count)),
            pltpu.SemaphoreType.DMA((5, count)),
            pltpu.SemaphoreType.DMA((count,)),
            pltpu.SemaphoreType.DMA((count,)),
            pltpu.SemaphoreType.DMA((2, count)),
            pltpu.SemaphoreType.DMA((5,)),
        ],
        compiler_params=params(0),
        name="gather_weights",
    )(query, key, value, out, cotangent, note)


def rows_kernel(line, rows_ref, rows_all, send, recv, twin_sems, local_sem):
    place = Place(line)
    half = rows_ref.shape[1] // 2
    span = pl.ds(pl.multiple_of(place.core * half, 128), half)
    own = pltpu.make_async_copy(rows_ref, rows_all.at[place.me], local_sem)
    own.start()
    enter(place)
    own.wait()
    gather_all([Gather(place, lambda p: rows_all.at[p, :, span], send, recv)])
    swap_halves(place, rows_all, span, twin_sems)


def gather_rows(line, rows):
    count = 4 * line
    return pl.pallas_call(
        functools.partial(rows_kernel, line),
        out_shape=jax.ShapeDtypeStruct((count, *rows.shape), BF16),
        in_specs=[ANY],
        out_specs=ANY,
        scratch_shapes=[
            pltpu.SemaphoreType.DMA((3 * line + count,)),
            pltpu.SemaphoreType.DMA((count,)),
            pltpu.SemaphoreType.DMA((2, count)),
            pltpu.SemaphoreType.DMA,
        ],
        compiler_params=params(1),
        name="gather_rows",
    )(rows)


def swap_kernel(line, mine_ref, sum_ref, other, sems):
    place = Place(line)
    barrier = pltpu.get_barrier_semaphore()
    pl.semaphore_signal(barrier, inc=1, device_id=place.twin(), device_id_type=MESH_IDS)
    pl.semaphore_wait(barrier, 1)
    copy = remote(mine_ref, other, sems.at[0], sems.at[1], place.twin())
    copy.start()
    copy.wait()
    sum_ref[...] = mine_ref[...].astype(F32) + other[...].astype(F32)


def twin_sum(line, number, mine):
    return pl.pallas_call(
        functools.partial(swap_kernel, line),
        out_shape=jax.ShapeDtypeStruct(mine.shape, F32),
        in_specs=[IN_VMEM],
        out_specs=IN_VMEM,
        scratch_shapes=[pltpu.VMEM(mine.shape, mine.dtype), pltpu.SemaphoreType.DMA((2,))],
        compiler_params=params(number),
        name="twin_sum",
    )(mine)


def experts_kernel(
    line,
    grads_ref,
    outs_ref,
    grads_sum,
    outs_sum,
    parts,
    arrived,
    from_b,
    from_a,
    from_z,
    total,
    sends,
    recvs,
    twin_sems,
    last_sems,
    local_sems,
):
    place = Place(line)
    width = grads_ref.shape[2]
    half = width // 2
    mine = pl.ds(pl.multiple_of(place.core * half, 128), half)
    theirs = pl.ds(pl.multiple_of((1 - place.core) * half, 128), half)
    enter(place)
    order = [(z, a, b) for b in (1, 0) for a in (1, 0) for z in ends_first(line)]

    def at(spot):
        z, a, b = spot
        flip = lambda own, other: own + other * (1 - 2 * own)
        return place.part(z, flip(place.a, a), flip(place.b, b))

    def load(i, ref, spot):
        part = at(spot)
        return pltpu.make_async_copy(ref.at[part, :, mine], parts.at[i, part], local_sems.at[i, part])

    def share(i, ref, spot):
        part = at(spot)
        return remote(
            ref.at[part, :, theirs],
            arrived.at[i, part],
            twin_sems.at[i, 0, part],
            twin_sems.at[i, 1, part],
            place.twin(),
        )

    sources = (grads_ref, outs_ref)
    for i, ref in enumerate(sources):
        for spot in order:
            share(i, ref, spot).start()
            load(i, ref, spot).start()
    reduces = [
        Reduce(place, parts.at[i], from_b.at[i], from_a.at[i], from_z.at[i], (sends.at[i], recvs.at[i]))
        for i in range(2)
    ]
    for i, ref in enumerate(sources):
        for spot in order:
            part = at(spot)
            load(i, ref, spot).wait()
            share(i, ref, spot).wait_recv()
            reduces[i]._add(part, arrived[i, part])
            z, a, b = spot
            if b == 1:
                reduces[i].send_b(z, place.a + a * (1 - 2 * place.a))
    reduce_rest(reduces)
    copies = []
    for i, out in enumerate((grads_sum, outs_sum)):
        reduces[i].result(total.at[i])
        out[:, mine] = total[i]
        copies.append(
            remote(total.at[i], out.at[:, mine], last_sems.at[0, i], last_sems.at[1, i], place.twin())
        )
        copies[-1].start()
    for r in reduces:
        r.settle()
    for i, ref in enumerate(sources):
        for spot in order:
            share(i, ref, spot).wait_send()
    for c in copies:
        c.wait()


def reduce_experts(line, grads, outs):
    count, rows, width = grads.shape
    half = width // 2
    full = jax.ShapeDtypeStruct((rows, width), F32)
    return pl.pallas_call(
        functools.partial(experts_kernel, line),
        out_shape=[full, full],
        in_specs=[ANY, ANY],
        out_specs=[IN_VMEM, IN_VMEM],
        scratch_shapes=[
            pltpu.VMEM((2, count, rows, half), BF16),
            pltpu.VMEM((2, count, rows, half), BF16),
            pltpu.VMEM((2, 2 * line, rows, half), BF16),
            pltpu.VMEM((2, line, rows, half), BF16),
            pltpu.VMEM((2, 2 * line, rows, half), BF16),
            pltpu.VMEM((2, rows, half), F32),
            pltpu.SemaphoreType.DMA((2, 5 * line)),
            pltpu.SemaphoreType.DMA((2, 5 * line)),
            pltpu.SemaphoreType.DMA((2, 2, count)),
            pltpu.SemaphoreType.DMA((2, 2)),
            pltpu.SemaphoreType.DMA((2, count)),
        ],
        compiler_params=params(2),
        name="reduce_experts",
    )(grads, outs)


def grads_kernel(
    line,
    query_ref,
    key_ref,
    value_ref,
    out_ref,
    peak_ref,
    gain_ref,
    query_sum,
    key_sum,
    value_sum,
    out_sum,
    peaks,
    gains,
    *scratch,
):
    place = Place(line)
    from_b, from_a, from_z = scratch[0:4], scratch[4:8], scratch[8:12]
    work = scratch[12:16]
    sends, recvs, note_sends, note_recvs, local_sems = scratch[16:]
    loads = [
        pltpu.make_async_copy(src, dst, local_sems.at[i])
        for i, (src, dst) in enumerate(zip((query_ref, key_ref, value_ref, out_ref), work))
    ]
    for c in loads:
        c.start()
    enter(place)
    notes = [
        Notes(place, peak_ref, peaks, note_sends.at[0], note_recvs.at[0], True),
        Notes(place, gain_ref, gains, note_sends.at[1], note_recvs.at[1], False),
    ]
    for n in notes:
        n.start()
    for c in loads:
        c.wait()
    reduces = [
        Reduce(place, work[i], from_b[i], from_a[i], from_z[i], (sends.at[i], recvs.at[i]))
        for i in (3, 0, 1, 2)
    ]
    for r in reduces:
        for a in (1 - place.a, place.a):
            for z in ends_first(line):
                r.send_b(z, a)
    reduce_rest(reduces)
    for r, out in zip(reduces, (out_sum, query_sum, key_sum, value_sum)):
        r.result(out)
    for r in reduces:
        r.settle()
    for n in notes:
        n.finish()


def reduce_grads(line, grads, peak, gain):
    count = 4 * line
    blocks = [g.shape[1:] for g in grads]
    many = lambda n: [pltpu.VMEM((n, *s), BF16) for s in blocks]
    return pl.pallas_call(
        functools.partial(grads_kernel, line),
        out_shape=[jax.ShapeDtypeStruct(s, F32) for s in blocks]
        + [jax.ShapeDtypeStruct((count, *peak.shape), F32), jax.ShapeDtypeStruct(gain.shape, F32)],
        in_specs=[ANY] * 4 + [IN_VMEM] * 2,
        out_specs=[IN_VMEM] * 6,
        scratch_shapes=many(2 * line)
        + many(line)
        + many(2 * line)
        + many(count)
        + [
            pltpu.SemaphoreType.DMA((4, 5 * line)),
            pltpu.SemaphoreType.DMA((4, 5 * line)),
            pltpu.SemaphoreType.DMA((2, count)),
            pltpu.SemaphoreType.DMA((2, count)),
            pltpu.SemaphoreType.DMA((4,)),
        ],
        compiler_params=params(3),
        name="reduce_grads",
    )(*grads, peak, gain)


def note_tiles(*rows):
    tiles = [jnp.pad(r.astype(F32), ((0, 0), (0, 128 - r.shape[1]))) for r in rows]
    tiles += [jnp.zeros_like(tiles[0])] * (8 - len(tiles))
    return jnp.stack(tiles, axis=1)


def on_device_dense(
    tokens,
    attn_norm_gain,
    w_query,
    key_projection,
    value_projection,
    w_out,
    moe_norm_gain,
    w_gate,
    w_up,
    w_down,
    router_logits,
    expert_ids,
    segment_ids,
    parents,
    cotangent,
):
    length, model_width = tokens.shape
    q_cols, kv_cols = w_query.shape[1], key_projection.shape[1]
    q_heads, kv_heads = q_cols // HEAD_SIZE, kv_cols // HEAD_SIZE
    group_size = q_heads // kv_heads
    count = lax.axis_size("dp")
    line = count // 4
    shard = attn_norm_gain.shape[0]
    logit_max = jnp.max(router_logits, axis=1, keepdims=True)
    logit_exp = jnp.exp(router_logits - logit_max)
    gate_probs = logit_exp / jnp.sum(logit_exp, axis=1, keepdims=True)
    expert_index = jnp.arange(count, dtype=jnp.int32)
    named = expert_ids[None, :, :] == expert_index[:, None, None]
    gate_rows = jnp.sum(jnp.where(named, gate_probs[None], 0.0), axis=2)
    own_gains = [jnp.broadcast_to(g[None], (count, shard)) for g in (attn_norm_gain, moe_norm_gain)]
    query_all, key_all, value_all, out_all, cot_all, notes = gather_weights(
        line,
        w_query,
        key_projection,
        value_projection,
        w_out,
        cotangent,
        note_tiles(gate_rows, *own_gains),
    )
    query_w = query_all.reshape(model_width, q_cols)
    key_weight = key_all.reshape(model_width, kv_cols)
    value_weight = value_all.reshape(model_width, kv_cols)
    out_w = out_all.reshape(model_width, q_cols)
    expert_gate = notes[:, 0, :length].reshape(count * length, 1)
    attn_gain_f = notes[:, 1, :shard].reshape(model_width)
    moe_gain_f = notes[:, 2, :shard].reshape(model_width)
    inputs = tokens.astype(F32)
    inv_attn = lax.rsqrt(jnp.mean(inputs * inputs, axis=1, keepdims=True) + EPSILON)
    unit_attn = inputs * inv_attn
    normalized_rows = (unit_attn * attn_gain_f).astype(BF16)
    position, allowed = tree_layout(segment_ids[0], parents[0])
    cosine_table, sine_values = rope_tables(position, HEAD_SIZE)
    query_linear = jnp.dot(normalized_rows, query_w, preferred_element_type=F32).reshape(
        length, q_heads, HEAD_SIZE
    )
    key_linear = jnp.dot(normalized_rows, key_weight, preferred_element_type=F32).reshape(
        length, kv_heads, HEAD_SIZE
    )
    query_heads = (
        apply_rotary(query_linear, cosine_table, sine_values)
        .astype(BF16)
        .reshape(length, kv_heads, group_size, HEAD_SIZE)
    )
    key_heads = apply_rotary(key_linear, cosine_table, sine_values).astype(BF16)
    value_heads = (
        jnp.dot(normalized_rows, value_weight, preferred_element_type=F32)
        .astype(BF16)
        .reshape(length, kv_heads, HEAD_SIZE)
    )
    scores = (
        jnp.einsum("qhgd,khd->hgqk", query_heads, key_heads, preferred_element_type=F32)
        * SCORE_SCALE
    )
    scores = jnp.where(allowed[None, None], scores, NEGATIVE)
    own_peak = jnp.max(scores, axis=(2, 3)).reshape(1, q_heads)
    row_max = jnp.max(scores, axis=3, keepdims=True)
    expo = jnp.exp(scores - row_max)
    prob_full = expo / jnp.sum(expo, axis=3, keepdims=True)
    prob_low = prob_full.astype(BF16)
    head_out = (
        jnp.einsum("hgqk,khd->qhgd", prob_low, value_heads, preferred_element_type=F32)
        .reshape(length, q_cols)
        .astype(BF16)
    )
    attn_mix = twin_sum(line, 4, contract_cols(head_out, out_w))
    hidden = inputs + RESIDUAL * attn_mix
    inv_moe = lax.rsqrt(jnp.mean(hidden * hidden, axis=1, keepdims=True) + EPSILON)
    unit_moe = hidden * inv_moe
    moe_in = (unit_moe * moe_gain_f).astype(BF16)
    expert_in = gather_rows(line, moe_in).reshape(count * length, model_width)
    gate_w, up_w, down_w = (w_gate[0], w_up[0], w_down[0])
    expert_out, kept_acts = expert_forward(expert_in, gate_w, up_w, down_w)
    grad_rows = (
        expert_gate * (RESIDUAL * cot_all.reshape(count * length, model_width).astype(F32))
    ).astype(BF16)
    d_inputs, grad_gate, grad_up, grad_down = expert_backward(
        expert_in, grad_rows, gate_w, up_w, down_w, kept_acts
    )
    mix_out = (expert_gate * expert_out).astype(BF16).reshape(count, length, model_width)
    d_moe_in, expert_mix = reduce_experts(
        line, d_inputs.astype(BF16).reshape(count, length, model_width), mix_out
    )
    output = (hidden + RESIDUAL * expert_mix).astype(BF16)
    grad_output = cotangent.astype(F32)
    scaled_moe = d_moe_in * moe_gain_f
    grad_moe_gain = jnp.sum(d_moe_in * unit_moe, axis=0)
    d_hidden = grad_output + inv_moe * (
        scaled_moe - unit_moe * jnp.mean(scaled_moe * unit_moe, axis=1, keepdims=True)
    )
    d_attn = (RESIDUAL * d_hidden).astype(BF16)
    grad_out_w = contract_rows(d_attn, head_out)
    d_heads = (
        jnp.dot(d_attn, out_w, preferred_element_type=F32)
        .astype(BF16)
        .reshape(length, kv_heads, group_size, HEAD_SIZE)
    )
    d_value = jnp.einsum("hgqk,qhgd->khd", prob_low, d_heads, preferred_element_type=F32)
    d_prob = jnp.einsum("qhgd,khd->hgqk", d_heads, value_heads, preferred_element_type=F32)
    inner = jnp.sum(prob_full * d_prob, axis=3, keepdims=True)
    d_scores = (prob_full * (d_prob - inner)).astype(BF16)
    d_query_all = (
        jnp.einsum("hgqk,khd->qhgd", d_scores, key_heads, preferred_element_type=F32) * SCORE_SCALE
    ).reshape(length, q_heads, HEAD_SIZE)
    d_key = (
        jnp.einsum("hgqk,qhgd->khd", d_scores, query_heads, preferred_element_type=F32)
        * SCORE_SCALE
    )
    d_query_lin = (
        rotate_back(d_query_all, cosine_table, sine_values).astype(BF16).reshape(length, q_cols)
    )
    d_key_lin = rotate_back(d_key, cosine_table, sine_values).astype(BF16).reshape(length, kv_cols)
    d_value_lin = d_value.astype(BF16).reshape(length, kv_cols)
    grads = [
        contract_rows(normalized_rows, g).astype(BF16).reshape(count, shard, g.shape[1])
        for g in (d_query_lin, d_key_lin, d_value_lin)
    ] + [grad_out_w.astype(BF16).reshape(count, shard, q_cols)]
    d_normed_part = (
        contract_cols(d_query_lin, query_w)
        + contract_cols(d_key_lin, key_weight)
        + contract_cols(d_value_lin, value_weight)
    )
    d_normed = twin_sum(line, 5, d_normed_part.astype(BF16))
    scaled_attn = d_normed * attn_gain_f
    grad_attn_gain = jnp.sum(d_normed * unit_attn, axis=0)
    input_grad = d_hidden + inv_attn * (
        scaled_attn - unit_attn * jnp.mean(scaled_attn * unit_attn, axis=1, keepdims=True)
    )
    peak_tile = note_tiles(own_peak)[0]
    gain_tiles = note_tiles(grad_attn_gain.reshape(count, shard), grad_moe_gain.reshape(count, shard))
    grad_query, grad_key, grad_value, grad_out, peaks, gains = reduce_grads(
        line, grads, peak_tile, gain_tiles
    )
    head_peak = jnp.max(peaks[:, 0, :q_heads], axis=0)
    gain_sums = jnp.sum(gains, axis=0)
    scale_factor = CLIP_LIMIT / jnp.maximum(head_peak, CLIP_LIMIT)
    query_scale = jnp.repeat(jnp.sqrt(scale_factor), HEAD_SIZE)
    key_clip_scale = jnp.repeat(
        jnp.sqrt(jnp.min(scale_factor.reshape(kv_heads, group_size), axis=1)), HEAD_SIZE
    )
    clipped_query = w_query.astype(F32) * query_scale[None, :]
    clipped_key = key_projection.astype(F32) * key_clip_scale[None, :]
    return (
        output,
        input_grad,
        gain_sums[0, :shard],
        grad_query,
        grad_key,
        grad_value,
        grad_out,
        gain_sums[1, :shard],
        grad_gate[None],
        grad_up[None],
        grad_down[None],
        clipped_query,
        clipped_key,
    )


DENSE_BYTES = 8 * 2**20


def on_device(*args):
    tokens, w_gate = args[0], args[7]
    count, ranks = lax.axis_size("dp"), lax.axis_size("tensor")
    rows_bytes = count * tokens.shape[0] * tokens.shape[1] * 2
    whole_experts = w_gate.shape[2] * ranks == FFE
    dense = whole_experts and ranks == 2 and count % 4 == 0 and rows_bytes <= DENSE_BYTES
    return on_device_dense(*args) if dense else on_device_general(*args)


def solution(mesh):
    in_specs = (
        P("dp", None),
        P("dp"),
        P("dp", "tensor"),
        P("dp", "tensor"),
        P("dp", "tensor"),
        P("dp", "tensor"),
        P("dp"),
        P("dp", None, "tensor"),
        P("dp", None, "tensor"),
        P("dp", None, "tensor"),
        P("dp", None),
        P("dp", None),
        P("dp", None),
        P("dp", None),
        P("dp", None),
    )
    out_specs = (
        P("dp", None),
        P("dp", None),
        P("dp"),
        P("dp", "tensor"),
        P("dp", "tensor"),
        P("dp", "tensor"),
        P("dp", "tensor"),
        P("dp"),
        P("dp", None, "tensor"),
        P("dp", None, "tensor"),
        P("dp", None, "tensor"),
        P("dp", "tensor"),
        P("dp", "tensor"),
    )
    return jax.shard_map(
        on_device, mesh=mesh, in_specs=in_specs, out_specs=out_specs, check_vma=False
    )
```

```python
import functools

import jax
import jax.numpy as jnp
from jax import lax
from jax.experimental import pallas as pl
from jax.experimental.pallas import tpu as pltpu
from jax.sharding import PartitionSpec as P

HEAD_SIZE = 64
FFE = 512
TOP = 8


EPSILON = 1e-06
SCORE_SCALE = 1.0 / 64.0
RESIDUAL = 0.22
THETA = 10000.0
CLIP_LIMIT = 2.0
NEGATIVE = -1e30


def tree_layout(seg_row, par_row):
    tree_length = seg_row.shape[0]
    seg_count = par_row.shape[0]
    seg_index = jnp.arange(seg_count, dtype=jnp.int32)
    member = (seg_row[:, None] == seg_index[None, :]).astype(jnp.int32)
    seg_len = jnp.sum(member, axis=0)
    seg_start = jnp.sum(jnp.where(seg_index[:, None] > seg_index[None, :], seg_len[None, :], 0), axis=1)
    parent_hot = (par_row[:, None] == seg_index[None, :]).astype(jnp.int32)
    grand_parent = jnp.sum(parent_hot * par_row[None, :], axis=1)
    grand_hot = (grand_parent[:, None] == seg_index[None, :]).astype(jnp.int32)
    parent_len = jnp.sum(parent_hot * seg_len[None, :], axis=1)
    grand_len = jnp.sum(grand_hot * seg_len[None, :], axis=1)
    offset = jnp.where(seg_index != 0, parent_len, 0) + jnp.where(par_row != 0, grand_len, 0)
    tok_start = jnp.sum(member * seg_start[None, :], axis=1)
    tok_offset = jnp.sum(member * offset[None, :], axis=1)
    places = jnp.arange(tree_length, dtype=jnp.int32)
    position = (places - tok_start + tok_offset).astype(jnp.float32)
    identity = (seg_index[:, None] == seg_index[None, :]).astype(jnp.int32)
    ancestor = jnp.minimum(identity + parent_hot + grand_hot, 1)
    reached = jnp.dot(member, ancestor)
    linked = jnp.dot(reached, member.T) > 0
    allowed = linked & (places[None, :] <= places[:, None])
    return (position, allowed)


def rope_tables(position, head_dim):
    half_dim = head_dim // 2
    frequency = THETA ** (-2.0 * jnp.arange(half_dim, dtype=jnp.float32) / head_dim)
    angles = position[:, None] * frequency[None, :]
    return (jnp.cos(angles)[:, None, :], jnp.sin(angles)[:, None, :])


def apply_rotary(values_in, cosine_table, sine_values):
    half_dim = values_in.shape[-1] // 2
    first_half = values_in[..., :half_dim]
    second_half = values_in[..., half_dim:]
    return jnp.concatenate(
        [
            first_half * cosine_table - second_half * sine_values,
            second_half * cosine_table + first_half * sine_values,
        ],
        axis=-1,
    )


def rotate_back(grads_in, cosine_table, sine_values):
    half_dim = grads_in.shape[-1] // 2
    first_half = grads_in[..., :half_dim]
    second_half = grads_in[..., half_dim:]
    return jnp.concatenate(
        [
            first_half * cosine_table + second_half * sine_values,
            second_half * cosine_table - first_half * sine_values,
        ],
        axis=-1,
    )


def slot_tables(routes, experts, capacity):
    flat_ids = routes.reshape(-1)
    row_count = flat_ids.shape[0]
    member = (flat_ids[:, None] == jnp.arange(experts, dtype=jnp.int32)[None, :]).astype(jnp.int32)
    row_total = flat_ids.shape[0]
    before = jnp.dot((jnp.arange(row_total)[:, None] > jnp.arange(row_total)[None, :]).astype(jnp.float32), member.astype(jnp.float32), precision=lax.Precision.HIGHEST).astype(jnp.int32)
    slot_index = jnp.sum(before * member, axis=1)
    target = flat_ids * capacity + slot_index
    source = (
        jnp.full((experts * capacity,), -1, jnp.int32)
        .at[target]
        .set(jnp.arange(row_count, dtype=jnp.int32))
    )
    return (flat_ids, slot_index, source)


def contract_rows(left, right):
    return lax.dot_general(
        left, right, (((0,), (0,)), ((), ())), preferred_element_type=jnp.float32
    )


def contract_cols(left, right):
    return lax.dot_general(
        left, right, (((1,), (1,)), ((), ())), preferred_element_type=jnp.float32
    )


def expert_forward(inputs, gate_w, up_w, down_w):
    gate_pre = jnp.dot(inputs, gate_w, preferred_element_type=jnp.float32)
    up_pre = jnp.dot(inputs, up_w, preferred_element_type=jnp.float32)
    active = (gate_pre / (1.0 + jnp.exp(-gate_pre)) * up_pre).astype(jnp.bfloat16)
    return (contract_cols(active, down_w), (gate_pre, up_pre, active))


def expert_backward(inputs, grads_out, gate_w, up_w, down_w, kept_acts):
    gate_pre, up_pre, active = kept_acts
    d_active = jnp.dot(grads_out, down_w, preferred_element_type=jnp.float32)
    grad_down = contract_rows(grads_out, active)
    sigmoid_val = 1.0 / (1.0 + jnp.exp(-gate_pre))
    d_gate = (d_active * up_pre * sigmoid_val * (1.0 + gate_pre * (1.0 - sigmoid_val))).astype(
        jnp.bfloat16
    )
    d_up = (d_active * gate_pre * sigmoid_val).astype(jnp.bfloat16)
    grad_gate = contract_rows(inputs, d_gate)
    grad_up = contract_rows(inputs, d_up)
    d_inputs = contract_cols(d_gate, gate_w) + contract_cols(d_up, up_w)
    return (d_inputs, grad_gate, grad_up, grad_down)


def send_rows(rows_in):
    return lax.all_to_all(rows_in, "dp", split_axis=0, concat_axis=0, tiled=True)


def return_rows(rows_in):
    return lax.all_to_all(
        rows_in.astype(jnp.bfloat16), "dp", split_axis=0, concat_axis=0, tiled=True
    ).astype(rows_in.dtype)


def send_grads(rows_in):
    return lax.all_to_all(rows_in, "dp", split_axis=0, concat_axis=0, tiled=True)


def return_grads(rows_in):
    return lax.all_to_all(
        rows_in.astype(jnp.bfloat16), "dp", split_axis=0, concat_axis=0, tiled=True
    ).astype(rows_in.dtype)


def share_slots(partial_rows):
    return lax.psum_scatter(partial_rows, "tensor", scatter_dimension=1, tiled=True)


def on_device_general(
    tokens,
    attn_norm_gain,
    w_query,
    key_projection,
    value_projection,
    w_out,
    moe_norm_gain,
    w_gate,
    w_up,
    w_down,
    router_logits,
    expert_ids,
    segment_ids,
    parents,
    cotangent,
):
    length = tokens.shape[0]
    model_width = tokens.shape[1]
    q_cols = w_query.shape[1]
    kv_cols = key_projection.shape[1]
    q_heads = q_cols // HEAD_SIZE
    kv_heads = kv_cols // HEAD_SIZE
    group_size = q_heads // kv_heads
    dp_size = lax.axis_size("dp")
    tensor_ranks = lax.axis_size("tensor")
    replicas = FFE // (w_gate.shape[2] * tensor_ranks)
    experts = dp_size // replicas
    capacity = 4 * (9 * length * TOP // (32 * experts))
    share_rows = capacity // tensor_ranks
    first_slot = lax.axis_index("tensor") * share_rows
    block_rows = min(length, 512)
    attn_gain, moe_gain, query_w, key_weight, value_weight, out_w = (
        lax.all_gather(attn_norm_gain, "dp", axis=0, tiled=True),
        lax.all_gather(moe_norm_gain, "dp", axis=0, tiled=True),
        lax.all_gather(w_query, "dp", axis=0, tiled=True),
        lax.all_gather(key_projection, "dp", axis=0, tiled=True),
        lax.all_gather(value_projection, "dp", axis=0, tiled=True),
        lax.all_gather(w_out, "dp", axis=0, tiled=True),
    )
    attn_gain_f = attn_gain.astype(jnp.float32)
    moe_gain_f = moe_gain.astype(jnp.float32)
    inputs = tokens.astype(jnp.float32)
    inv_attn = lax.rsqrt(jnp.mean(inputs * inputs, axis=1, keepdims=True) + EPSILON)
    unit_attn = inputs * inv_attn
    normalized_rows = (unit_attn * attn_gain_f).astype(jnp.bfloat16)
    position, allowed = tree_layout(segment_ids[0], parents[0])
    cosine_table, sine_values = rope_tables(position, HEAD_SIZE)
    query_linear = jnp.dot(normalized_rows, query_w, preferred_element_type=jnp.float32).reshape(
        length, q_heads, HEAD_SIZE
    )
    key_linear = jnp.dot(normalized_rows, key_weight, preferred_element_type=jnp.float32).reshape(
        length, kv_heads, HEAD_SIZE
    )
    query_heads = (
        apply_rotary(query_linear, cosine_table, sine_values)
        .astype(jnp.bfloat16)
        .reshape(length, kv_heads, group_size, HEAD_SIZE)
    )
    key_heads = apply_rotary(key_linear, cosine_table, sine_values).astype(jnp.bfloat16)
    value_heads = (
        jnp.dot(normalized_rows, value_weight, preferred_element_type=jnp.float32)
        .astype(jnp.bfloat16)
        .reshape(length, kv_heads, HEAD_SIZE)
    )
    q_block = query_heads
    mask_rows = allowed[None, None]
    scores = (
        jnp.einsum("qhgd,khd->hgqk", q_block, key_heads, preferred_element_type=jnp.float32)
        * SCORE_SCALE
    )
    scores = jnp.where(mask_rows, scores, NEGATIVE)
    peak_parts = [jnp.max(scores, axis=(2, 3))]
    row_max = jnp.max(scores, axis=3, keepdims=True)
    expo = jnp.exp(scores - row_max)
    row_total = jnp.sum(expo, axis=3, keepdims=True)
    lse_parts = [row_max + jnp.log(row_total)]
    prob_low = (expo / row_total).astype(jnp.bfloat16)
    block_outs = jnp.einsum(
        "hgqk,khd->qhgd", prob_low, value_heads, preferred_element_type=jnp.float32
    )
    head_out = block_outs.reshape(length, q_cols).astype(jnp.bfloat16)
    attn_mix = lax.psum(contract_cols(head_out, out_w), "tensor")
    hidden = inputs + RESIDUAL * attn_mix
    head_peak = lax.pmax(jnp.max(jnp.stack(peak_parts), axis=0).reshape(q_heads), "dp")
    inv_moe = lax.rsqrt(jnp.mean(hidden * hidden, axis=1, keepdims=True) + EPSILON)
    unit_moe = hidden * inv_moe
    moe_in = (unit_moe * moe_gain_f).astype(jnp.bfloat16)
    logit_max = jnp.max(router_logits, axis=1, keepdims=True)
    logit_exp = jnp.exp(router_logits - logit_max)
    gate_probs = logit_exp / jnp.sum(logit_exp, axis=1, keepdims=True)
    flat_ids, slot_index, source = slot_tables(expert_ids, experts, capacity)
    filled = source >= 0
    source_row = jnp.maximum(source, 0)
    source_token = source_row // TOP
    dispatch_rows = jnp.where(
        filled[:, None], moe_in[source_token], jnp.zeros((), jnp.bfloat16)
    ).reshape(experts, capacity, model_width)
    arrived = send_rows(jnp.repeat(dispatch_rows, replicas, axis=0))
    gate_w, up_w, down_w = (w_gate[0], w_up[0], w_down[0])
    expert_in = arrived.reshape(dp_size * capacity, model_width)
    expert_out, kept_acts = expert_forward(expert_in, gate_w, up_w, down_w)
    partial_out = share_slots(expert_out.reshape(dp_size, capacity, model_width))
    back_parts = return_rows(partial_out).reshape(experts, replicas, share_rows, model_width)
    back_rows = (
        jnp.sum(back_parts, axis=1).astype(jnp.bfloat16).reshape(experts * share_rows, model_width)
    )
    own_slot = ((slot_index >= first_slot) & (slot_index < first_slot + share_rows)).reshape(
        length, TOP
    )
    local_index = (
        flat_ids * share_rows + jnp.clip(slot_index - first_slot, 0, share_rows - 1)
    ).reshape(length, TOP)
    mix_part = jnp.zeros((length, model_width), jnp.float32)
    for column in range(TOP):
        gate_weight = jnp.where(own_slot[:, column], gate_probs[:, column], 0.0)
        mix_part = mix_part + gate_weight[:, None] * back_rows[local_index[:, column]].astype(
            jnp.float32
        )
    expert_mix = lax.psum(mix_part.astype(jnp.bfloat16), "tensor").astype(jnp.float32)
    output = (hidden + RESIDUAL * expert_mix).astype(jnp.bfloat16)
    grad_output = cotangent.astype(jnp.float32)
    mix_grad = RESIDUAL * grad_output
    row_gate = gate_probs.reshape(-1)[source_row]
    grad_rows = (
        jnp.where(filled[:, None], row_gate[:, None] * mix_grad[source_token], 0.0)
        .astype(jnp.bfloat16)
        .reshape(experts, capacity, model_width)
    )
    grad_arrived = send_grads(jnp.repeat(grad_rows, replicas, axis=0)).reshape(
        dp_size * capacity, model_width
    )
    d_inputs, grad_gate, grad_up, grad_down = expert_backward(
        expert_in, grad_arrived, gate_w, up_w, down_w, kept_acts
    )
    d_back = share_slots(d_inputs.reshape(dp_size, capacity, model_width))
    grad_gate, grad_up, grad_down = (grad_gate[None], grad_up[None], grad_down[None])
    d_parts = return_grads(d_back).reshape(experts, replicas, share_rows, model_width)
    d_returned = (
        jnp.sum(d_parts, axis=1).astype(jnp.bfloat16).reshape(experts * share_rows, model_width)
    )
    d_mix_part = jnp.zeros((length, model_width), jnp.float32)
    for column in range(TOP):
        d_mix_part = d_mix_part + jnp.where(
            own_slot[:, column][:, None],
            d_returned[local_index[:, column]].astype(jnp.float32),
            0.0,
        )
    d_moe_in = lax.psum(d_mix_part, "tensor")
    scaled_moe = d_moe_in * moe_gain_f
    grad_moe_gain = jnp.sum(d_moe_in * unit_moe, axis=0)
    d_hidden = grad_output + inv_moe * (
        scaled_moe - unit_moe * jnp.mean(scaled_moe * unit_moe, axis=1, keepdims=True)
    )
    d_attn = (RESIDUAL * d_hidden).astype(jnp.bfloat16)
    grad_out_w = contract_rows(d_attn, head_out)
    d_heads = (
        jnp.dot(d_attn, out_w, preferred_element_type=jnp.float32)
        .astype(jnp.bfloat16)
        .reshape(length, kv_heads, group_size, HEAD_SIZE)
    )
    d_query_parts = []
    d_key = jnp.zeros((length, kv_heads, HEAD_SIZE), jnp.float32)
    d_value = jnp.zeros((length, kv_heads, HEAD_SIZE), jnp.float32)
    for block_number, row_begin in enumerate(range(0, length, block_rows)):
        q_block = query_heads
        mask_rows = allowed[None, None]
        scores = (
            jnp.einsum("qhgd,khd->hgqk", q_block, key_heads, preferred_element_type=jnp.float32)
            * SCORE_SCALE
        )
        scores = jnp.where(mask_rows, scores, NEGATIVE)
        prob_full = jnp.exp(scores - lse_parts[block_number])
        prob_low = prob_full.astype(jnp.bfloat16)
        d_value = jnp.einsum(
            "hgqk,qhgd->khd", prob_low, d_heads, preferred_element_type=jnp.float32
        )
        d_prob = jnp.einsum(
            "qhgd,khd->hgqk", d_heads, value_heads, preferred_element_type=jnp.float32
        )
        inner = jnp.sum(prob_full * d_prob, axis=3, keepdims=True)
        d_scores = (prob_full * (d_prob - inner)).astype(jnp.bfloat16)
        d_query_parts.append(
            jnp.einsum("hgqk,khd->qhgd", d_scores, key_heads, preferred_element_type=jnp.float32)
            * SCORE_SCALE
        )
        d_key = (
            jnp.einsum("hgqk,qhgd->khd", d_scores, q_block, preferred_element_type=jnp.float32)
            * SCORE_SCALE
        )
    d_query_all = d_query_parts[0].reshape(length, q_heads, HEAD_SIZE)
    d_query_lin = (
        rotate_back(d_query_all, cosine_table, sine_values)
        .astype(jnp.bfloat16)
        .reshape(length, q_cols)
    )
    d_key_lin = (
        rotate_back(d_key, cosine_table, sine_values).astype(jnp.bfloat16).reshape(length, kv_cols)
    )
    d_value_lin = d_value.astype(jnp.bfloat16).reshape(length, kv_cols)
    grad_query_w = contract_rows(normalized_rows, d_query_lin)
    grad_key_w = contract_rows(normalized_rows, d_key_lin)
    grad_value_w = contract_rows(normalized_rows, d_value_lin)
    d_normed_part = (
        contract_cols(d_query_lin, query_w)
        + contract_cols(d_key_lin, key_weight)
        + contract_cols(d_value_lin, value_weight)
    )
    d_normed = lax.psum(d_normed_part.astype(jnp.bfloat16), "tensor").astype(jnp.float32)
    scaled_attn = d_normed * attn_gain_f
    grad_attn_gain = jnp.sum(d_normed * unit_attn, axis=0)
    input_grad = d_hidden + inv_attn * (
        scaled_attn - unit_attn * jnp.mean(scaled_attn * unit_attn, axis=1, keepdims=True)
    )
    reduced = (
        lax.psum_scatter(grad_attn_gain, "dp", scatter_dimension=0, tiled=True),
        lax.psum_scatter(grad_moe_gain, "dp", scatter_dimension=0, tiled=True),
        lax.psum_scatter(grad_query_w, "dp", scatter_dimension=0, tiled=True),
        lax.psum_scatter(grad_key_w, "dp", scatter_dimension=0, tiled=True),
        lax.psum_scatter(grad_value_w, "dp", scatter_dimension=0, tiled=True),
        lax.psum_scatter(grad_out_w, "dp", scatter_dimension=0, tiled=True),
    )
    scale_factor = CLIP_LIMIT / jnp.maximum(head_peak, CLIP_LIMIT)
    query_scale = jnp.repeat(jnp.sqrt(scale_factor), HEAD_SIZE)
    key_clip_scale = jnp.repeat(
        jnp.sqrt(jnp.min(scale_factor.reshape(kv_heads, group_size), axis=1)), HEAD_SIZE
    )
    clipped_query = w_query.astype(jnp.float32) * query_scale[None, :]
    clipped_key = key_projection.astype(jnp.float32) * key_clip_scale[None, :]
    return (
        output,
        input_grad,
        reduced[0],
        reduced[2],
        reduced[3],
        reduced[4],
        reduced[5],
        reduced[1],
        grad_gate,
        grad_up,
        grad_down,
        clipped_query,
        clipped_key,
    )


MESH_IDS = pl.DeviceIdType.MESH
F32 = jnp.float32
BF16 = jnp.bfloat16


class Place:
    def __init__(self, line):
        self.line = line
        self.count = 4 * line
        me = lax.axis_index("dp")
        self.core = lax.axis_index("tensor")
        self.me = me
        self.z = me // 4
        y, x = (me // 2) % 2, me % 2
        self.step_a, self.step_b = 2 - self.core, 1 + self.core
        self.a = y * (1 - self.core) + x * self.core
        self.b = x * (1 - self.core) + y * self.core

    def part(self, z, a, b):
        return z * 4 + a * self.step_a + b * self.step_b

    def up(self):
        return (self.me + 4, self.core)

    def down(self):
        return (self.me - 4, self.core)

    def beside_a(self):
        return (self.me + self.step_a * (1 - 2 * self.a), self.core)

    def beside_b(self):
        return (self.me + self.step_b * (1 - 2 * self.b), self.core)

    def twin(self):
        return (self.me, 1 - self.core)

    def peer(self, offset):
        return lax.rem(self.me + offset, self.count)


def enter(place):
    barrier = pltpu.get_barrier_semaphore()

    def greet(offset, carry):
        pl.semaphore_signal(
            barrier, inc=1, device_id=(place.peer(offset), place.core), device_id_type=MESH_IDS
        )
        return carry

    lax.fori_loop(1, place.count, greet, 0)
    pl.semaphore_signal(barrier, inc=1, device_id=place.twin(), device_id_type=MESH_IDS)
    pl.semaphore_wait(barrier, place.count)


def remote(src, dst, send_sem, recv_sem, device):
    return pltpu.make_async_remote_copy(
        src_ref=src,
        dst_ref=dst,
        send_sem=send_sem,
        recv_sem=recv_sem,
        device_id=device,
        device_id_type=MESH_IDS,
    )


class Notes:
    def __init__(self, place, src, dst, send_sem, recv_sem, alike):
        self.place, self.src, self.dst = place, src, dst
        self.send_sem, self.recv_sem, self.alike = send_sem, recv_sem, alike

    def _copy(self, offset, source):
        place = self.place
        to = place.peer(offset)
        return remote(
            self.src if self.alike else self.src.at[to],
            self.dst.at[source],
            self.send_sem.at[offset],
            self.recv_sem.at[source],
            (to, place.core),
        )

    def start(self):
        def send(offset, carry):
            self._copy(offset, self.place.me).start()
            return carry

        lax.fori_loop(1, self.place.count, send, 0)
        me = self.place.me
        self.dst[me] = self.src[...] if self.alike else self.src[me]

    def finish(self):
        def settle(offset, carry):
            self._copy(offset, self.place.peer(offset)).wait_recv()
            self._copy(offset, self.place.me).wait_send()
            return carry

        lax.fori_loop(1, self.place.count, settle, 0)


class Gather:
    def __init__(self, place, view, send_sem, recv_sem, fixed=False):
        self.place, self.view, self.fixed = place, view, fixed
        self.send_sem, self.recv_sem = send_sem, recv_sem

    def _copy(self, source, target, sem, device):
        there = self.view(source if self.fixed else target)
        return remote(self.view(source), there, self.send_sem.at[sem], self.recv_sem.at[target], device)

    def _to_z(self, step):
        place = self.place
        own = place.z
        return self._copy(own, own, step + place.line - 1, (place.me + 4 * step, place.core))

    def _to_a(self, z):
        line = self.place.line
        return self._copy(z, line + z, 2 * line - 1 + z, self.place.beside_a())

    def _to_b(self, slot):
        line = self.place.line
        return self._copy(slot, 2 * line + slot, 3 * line - 1 + slot, self.place.beside_b())

    def take(self, slot):
        self._copy(slot, slot, 0, self.place.beside_b()).wait_recv()

    def near(self, step, action):
        place = self.place
        if step == 0:
            action(place.z)
        else:
            pl.when(place.z >= step)(lambda: action(place.z - step))
            pl.when(place.z + step < place.line)(lambda: action(place.z + step))

    def start(self):
        place = self.place

        def reach(step):
            pl.when(place.z >= step)(lambda: self._to_z(-step).start())
            pl.when(place.z + step < place.line)(lambda: self._to_z(step).start())

        reach(1)
        self._to_a(place.z).start()
        self._to_b(place.z).start()
        for step in range(2, place.line):
            reach(step)

    def along(self, step, then=None):
        def pass_on(z):
            self.take(z)
            self._to_a(z).start()
            self._to_b(z).start()
            if then is not None:
                then(z)

        self.near(step, pass_on)

    def across(self, step, then=None):
        line = self.place.line

        def pass_on(z):
            self.take(line + z)
            self._to_b(line + z).start()
            if then is not None:
                then(line + z)

        self.near(step, pass_on)

    def settle(self):
        place = self.place
        line = place.line

        def wait(z, carry):
            self._to_a(z).wait_send()
            self._to_b(z).wait_send()
            self._to_b(line + z).wait_send()
            pl.when(z != place.z)(lambda: self._to_z(z - place.z).wait_send())
            return carry

        lax.fori_loop(0, line, wait, 0)

    def take_rest(self):
        line = self.place.line

        def wait(k, carry):
            self.take(2 * line + k)
            return carry

        lax.fori_loop(0, 2 * line, wait, 0)


def gather_all(gathers, thens=None):
    line = gathers[0].place.line
    thens = thens or [None] * len(gathers)
    for g in gathers:
        g.start()
    for step in range(1, line + 1):
        for g, then in zip(gathers, thens):
            if step < line:
                g.along(step, then)
            g.across(step - 1, then)


class Twin:
    def __init__(self, place, source, target, send_sem, recv_sem):
        self.place, self.source, self.target = place, source, target
        self.send_sem, self.recv_sem = send_sem, recv_sem

    def copy(self, slot):
        line = self.place.line
        group = slot // line
        there = slot + line * ((group % 2) - (group // 2))
        return remote(
            self.source(slot),
            self.target(there),
            self.send_sem.at[slot],
            self.recv_sem.at[there],
            self.place.twin(),
        )

    def start(self, slot):
        self.copy(slot).start()

    def take(self, slot):
        remote(
            self.source(slot),
            self.target(slot),
            self.send_sem.at[slot],
            self.recv_sem.at[slot],
            self.place.twin(),
        ).wait_recv()

    def wait_send(self, slot):
        self.copy(slot).wait_send()


class Reduce:
    def __init__(self, place, parts, from_b, from_a, from_z, send_sem, recv_sem):
        self.place, self.parts = place, parts
        self.from_b, self.from_a, self.from_z = from_b, from_a, from_z
        self.send_sem, self.recv_sem = send_sem, recv_sem

    def _copy(self, source, target, sem, device):
        return remote(source, target, self.send_sem.at[sem], self.recv_sem.at[sem], device)

    def _to_b(self, k):
        line = self.place.line
        return self._copy(self.parts.at[2 * line + k], self.from_b.at[k], k, self.place.beside_b())

    def _to_a(self, z):
        line = self.place.line
        return self._copy(self.parts.at[line + z], self.from_a.at[z], 2 * line + z, self.place.beside_a())

    def _along(self, z, way):
        place = self.place
        slot = way * place.line + z
        device = place.up() if way == 0 else place.down()
        return self._copy(self.parts.at[z], self.from_z.at[slot], 3 * place.line + slot, device)

    def _add(self, slot, block):
        self.parts[slot] = (self.parts[slot].astype(F32) + block.astype(F32)).astype(BF16)

    def send_b(self, k):
        self._to_b(k).start()

    def fold_b(self, k):
        self._to_b(k).wait_recv()
        self._add(k, self.from_b[k])

    def send_a(self, z):
        self._to_a(z).start()

    def fold_a(self, z):
        self._to_a(z).wait_recv()
        self._add(z, self.from_a[z])

    def pass_up(self, z):
        place = self.place

        @pl.when(place.z < z)
        def _():
            @pl.when(place.z > 0)
            def _():
                self._along(z, 0).wait_recv()
                self._add(z, self.from_z[z])

            self._along(z, 0).start()

    def pass_down(self, z):
        place, line = self.place, self.place.line

        @pl.when(place.z > z)
        def _():
            @pl.when(place.z < line - 1)
            def _():
                self._along(z, 1).wait_recv()
                self._add(z, self.from_z[line + z])

            self._along(z, 1).start()

    def fold_line_a(self):
        line = self.place.line
        for z in ends_first(line):
            self.fold_b(line + z)
            self.send_a(z)

    def fold_line_own(self):
        for z in ends_first(self.place.line):
            self.fold_b(z)

    def finish_line(self):
        line = self.place.line
        for z in ends_first(line):
            self.fold_a(z)
        for k in range(line):
            self.pass_up(line - 1 - k)
            self.pass_down(k)

    def result(self, out):
        place, line = self.place, self.place.line
        z = place.z
        out[...] = self.parts[z].astype(F32)

        @pl.when(z > 0)
        def _():
            self._along(z, 0).wait_recv()
            out[...] += self.from_z[z].astype(F32)

        @pl.when(z < line - 1)
        def _():
            self._along(z, 1).wait_recv()
            out[...] += self.from_z[line + z].astype(F32)

    def settle(self):
        place, line = self.place, self.place.line

        def wait(z, carry):
            self._to_b(z).wait_send()
            self._to_b(line + z).wait_send()
            self._to_a(z).wait_send()
            pl.when(place.z < z)(lambda: self._along(z, 0).wait_send())
            pl.when(place.z > z)(lambda: self._along(z, 1).wait_send())
            return carry

        lax.fori_loop(0, line, wait, 0)


def reduce_scratch(line, block):
    return [
        pltpu.VMEM((2 * line, *block), BF16),
        pltpu.VMEM((line, *block), BF16),
        pltpu.VMEM((2 * line, *block), BF16),
        pltpu.SemaphoreType.DMA((5 * line,)),
        pltpu.SemaphoreType.DMA((5 * line,)),
    ]


def ends_first(line):
    order = []
    for i in range((line + 1) // 2):
        order += [i] if i == line - 1 - i else [i, line - 1 - i]
    return order


def part_of(place, slot):
    line = place.line
    group, z = slot // line, slot % line
    flip_a, flip_b = group % 2, group // 2
    a = place.a + flip_a * (1 - 2 * place.a)
    b = place.b + flip_b * (1 - 2 * place.b)
    return place.part(z, a, b)


def halves(place, width):
    half = width // 2
    mine = pl.ds(pl.multiple_of(place.core * half, 128), half)
    theirs = pl.ds(pl.multiple_of((1 - place.core) * half, 128), half)
    return mine, theirs


def weights_kernel(
    line,
    query_ref,
    key_ref,
    value_ref,
    out_ref,
    cot_ref,
    note_ref,
    query_all,
    key_all,
    value_all,
    out_all,
    cot_all,
    notes,
    sends,
    recvs,
    note_send,
    note_recv,
    twin_sems,
    local_sems,
):
    place = Place(line)
    span, _ = halves(place, cot_ref.shape[1])
    own = []
    blocks = ((query_ref, query_all), (key_ref, key_all), (value_ref, value_all), (out_ref, out_all))
    for i, (src, dst) in enumerate(blocks):
        own.append(pltpu.make_async_copy(src, dst.at[place.me], local_sems.at[i]))
    own.append(pltpu.make_async_copy(cot_ref, cot_all.at[place.z], local_sems.at[4]))
    for c in own:
        c.start()
    enter(place)
    note = Notes(place, note_ref, notes, note_send, note_recv, False)
    note.start()
    for c in own:
        c.wait()
    gathers = [
        Gather(place, lambda s, ref=ref: ref.at[part_of(place, s)], sends.at[i], recvs.at[i], True)
        for i, ref in enumerate((query_all, key_all, value_all, out_all))
    ]
    cot_view = lambda s: cot_all.at[s, :, span]
    cot_gather = Gather(place, cot_view, sends.at[4], recvs.at[4])
    twin = Twin(place, cot_view, cot_view, twin_sems.at[0], twin_sems.at[1])
    gathers.append(cot_gather)
    gather_all(gathers, [None] * 4 + [twin.start])
    for g in gathers[:4]:
        g.take_rest()

    def rest(slot, carry):
        cot_gather.take(slot)
        twin.start(slot)
        return carry

    lax.fori_loop(2 * line, 4 * line, rest, 0)
    for g in gathers:
        g.settle()

    def other(slot, carry):
        @pl.when(slot != place.z)
        def _():
            twin.wait_send(slot)
            twin.take(slot)

        return carry

    lax.fori_loop(0, 4 * line, other, 0)
    note.finish()


ANY = pl.BlockSpec(memory_space=pl.ANY)
IN_VMEM = pl.BlockSpec(memory_space=pltpu.VMEM)


def params(number):
    return pltpu.CompilerParams(
        collective_id=number, has_side_effects=True, vmem_limit_bytes=56 * 2**20
    )


def gather_weights(line, query, key, value, out, cotangent, note):
    count = 4 * line
    shapes = [query.shape, key.shape, value.shape, out.shape, cotangent.shape]
    return pl.pallas_call(
        functools.partial(weights_kernel, line),
        out_shape=[jax.ShapeDtypeStruct((count, *s), BF16) for s in shapes]
        + [jax.ShapeDtypeStruct(note.shape, F32)],
        in_specs=[ANY] * 5 + [IN_VMEM],
        out_specs=[ANY] * 5 + [IN_VMEM],
        scratch_shapes=[
            pltpu.SemaphoreType.DMA((5, 5 * line)),
            pltpu.SemaphoreType.DMA((5, count)),
            pltpu.SemaphoreType.DMA((count,)),
            pltpu.SemaphoreType.DMA((count,)),
            pltpu.SemaphoreType.DMA((2, count)),
            pltpu.SemaphoreType.DMA((5,)),
        ],
        compiler_params=params(0),
        name="gather_weights",
    )(query, key, value, out, cotangent, note)


def swap_kernel(line, mine_ref, sum_ref, other, sems):
    place = Place(line)
    barrier = pltpu.get_barrier_semaphore()
    pl.semaphore_signal(barrier, inc=1, device_id=place.twin(), device_id_type=MESH_IDS)
    pl.semaphore_wait(barrier, 1)
    copy = remote(mine_ref, other, sems.at[0], sems.at[1], place.twin())
    copy.start()
    copy.wait()
    sum_ref[...] = mine_ref[...].astype(F32) + other[...].astype(F32)


def twin_sum(line, number, mine):
    return pl.pallas_call(
        functools.partial(swap_kernel, line),
        out_shape=jax.ShapeDtypeStruct(mine.shape, F32),
        in_specs=[IN_VMEM],
        out_specs=IN_VMEM,
        scratch_shapes=[pltpu.VMEM(mine.shape, mine.dtype), pltpu.SemaphoreType.DMA((2,))],
        compiler_params=params(number),
        name="twin_sum",
    )(mine)


def experts_kernel(
    line,
    rows_ref,
    cot_ref,
    notes_ref,
    gate_ref,
    up_ref,
    down_ref,
    d_rows_ref,
    mix_ref,
    grad_gate_ref,
    grad_up_ref,
    grad_down_ref,
    rows,
    cots,
    active,
    d_gate,
    d_up,
    grad_stage,
    mix_stage,
    grad_parts,
    mix_parts,
    grads,
    total,
    from_b,
    from_a,
    from_z,
    reduce_send,
    reduce_recv,
    gather_send,
    gather_recv,
    twin_sems,
    load_sems,
    last_sems,
    store_sems,
):
    place = Place(line)
    count = 4 * line
    length, width = rows_ref.shape
    hidden = gate_ref.shape[1]
    mine, theirs = halves(place, width)

    def load(slot):
        return pltpu.make_async_copy(cot_ref.at[slot], cots.at[slot], load_sems.at[slot])

    def begin(slot, carry):
        load(slot).start()
        return carry

    lax.fori_loop(0, count, begin, 0)
    rows[place.z] = rows_ref[...]
    enter(place)
    view = lambda s: rows.at[s, :, mine]
    gather = Gather(place, view, gather_send, gather_recv)
    row_twin = Twin(place, view, view, twin_sems.at[0], twin_sems.at[1])
    grad_twin = Twin(
        place, lambda s: grad_stage.at[s, :, theirs], lambda s: grad_parts.at[s], twin_sems.at[2], twin_sems.at[3]
    )
    mix_twin = Twin(
        place, lambda s: mix_stage.at[s, :, theirs], lambda s: mix_parts.at[s], twin_sems.at[4], twin_sems.at[5]
    )
    reduce = Reduce(place, grad_parts, from_b, from_a, from_z, reduce_send, reduce_recv)
    gather_all([gather], [row_twin.start])

    def fold(slot):
        grad_twin.take(slot)
        reduce._add(slot, grad_stage[slot, :, mine])
        pl.when(slot >= 2 * line)(lambda: reduce.send_b(slot - 2 * line))

    def column(slot):
        return jnp.transpose(notes_ref[part_of(place, slot)])[:, 0:1]

    def step(tile, carry):
        first = 2 * tile
        pair = (first, first + 1)
        two = pl.ds(first, 2)
        flat = pl.ds(pl.multiple_of(first * length, 2 * length), 2 * length)
        for slot in pair:
            pl.when(slot != place.z)(lambda slot=slot: row_twin.take(slot))
            load(slot).wait()
        x = rows[two].reshape(2 * length, width)
        gate = jnp.concatenate([column(slot) for slot in pair], axis=0)
        gate_pre = jnp.dot(x, gate_ref[...], preferred_element_type=F32)
        up_pre = jnp.dot(x, up_ref[...], preferred_element_type=F32)
        sigmoid = 1.0 / (1.0 + jnp.exp(-gate_pre))
        silu = gate_pre * sigmoid
        act = (silu * up_pre).astype(BF16)
        active[flat, :] = act
        mix = contract_cols(act, down_ref[...])
        mix_stage[two] = (gate * mix).astype(BF16).reshape(2, length, width)
        d_out = (gate * (RESIDUAL * cots[two].reshape(2 * length, width).astype(F32))).astype(BF16)
        cots[two] = d_out.reshape(2, length, width)
        d_act = jnp.dot(d_out, down_ref[...], preferred_element_type=F32)
        d_g = (d_act * up_pre * sigmoid * (1.0 + gate_pre * (1.0 - sigmoid))).astype(BF16)
        d_u = (d_act * silu).astype(BF16)
        d_gate[flat, :] = d_g
        d_up[flat, :] = d_u
        d_in = contract_cols(d_g, gate_ref[...]) + contract_cols(d_u, up_ref[...])
        grad_stage[two] = d_in.astype(BF16).reshape(2, length, width)
        for slot in pair:
            grad_twin.start(slot)
            mix_twin.start(slot)

        group = (tile + 1) // (line // 2)

        @pl.when(jnp.logical_or(group == 1, group == 3))
        def _():
            for slot in (first + 2, first + 3):
                slot = slot + line * (3 - group) // 2
                gather.take(slot)
                row_twin.start(slot)

        @pl.when(jnp.logical_and(tile > 0, (first - 1) // line != 1))
        def _():
            for slot in (first - 2, first - 1):
                fold(slot)

        return carry

    lax.fori_loop(0, 2 * line, step, 0)
    for slot in (count - 2, count - 1):
        fold(slot)

    def fold_late(slot, carry):
        fold(slot)
        return carry

    lax.fori_loop(line, 2 * line, fold_late, 0)

    def weight_grad(number, left, right, out_ref):
        left = left.reshape(count * length, left.shape[2]) if len(left.shape) == 3 else left

        def some(i, carry):
            span = pl.ds(pl.multiple_of(i * 512, 512), 512)
            grads[number, span, :] = contract_rows(left[:, span], right[...])
            return carry

        lax.fori_loop(0, width // 512, some, 0)
        store = pltpu.make_async_copy(grads.at[number], out_ref, store_sems.at[number])
        store.start()
        return store

    stores = [weight_grad(0, cots, active, grad_down_ref)]
    reduce.fold_line_own()
    stores.append(weight_grad(1, rows, d_gate, grad_gate_ref))
    reduce.fold_line_a()
    stores.append(weight_grad(2, rows, d_up, grad_up_ref))
    reduce.finish_line()

    def mix_fold(slot, carry):
        mix_twin.take(slot)
        mix_parts[slot] = (mix_parts[slot].astype(F32) + mix_stage[slot, :, mine].astype(F32)).astype(BF16)
        return carry

    lax.fori_loop(0, count, mix_fold, 0)
    stores.append(pltpu.make_async_copy(mix_parts, mix_ref, store_sems.at[3]))
    stores[-1].start()
    reduce.result(total)
    d_rows_ref[:, mine] = total[...]
    last = remote(total, d_rows_ref.at[:, mine], last_sems.at[0], last_sems.at[1], place.twin())
    last.start()
    reduce.settle()
    gather.settle()

    def settle(slot, carry):
        pl.when(slot != place.z)(lambda: row_twin.wait_send(slot))
        grad_twin.wait_send(slot)
        mix_twin.wait_send(slot)
        return carry

    lax.fori_loop(0, count, settle, 0)
    for c in stores:
        c.wait()
    last.wait()


def run_experts(line, rows, cots, notes, gate, up, down):
    count = 4 * line
    length, width = rows.shape
    half, hidden = width // 2, gate.shape[1]
    grad = jax.ShapeDtypeStruct((width, hidden), F32)
    return pl.pallas_call(
        functools.partial(experts_kernel, line),
        out_shape=[
            jax.ShapeDtypeStruct((length, width), F32),
            jax.ShapeDtypeStruct((count, length, half), BF16),
            grad,
            grad,
            grad,
        ],
        in_specs=[IN_VMEM, ANY, IN_VMEM, IN_VMEM, IN_VMEM, IN_VMEM],
        out_specs=[IN_VMEM, ANY, ANY, ANY, ANY],
        scratch_shapes=[
            pltpu.VMEM((count, length, width), BF16),
            pltpu.VMEM((count, length, width), BF16),
            pltpu.VMEM((count * length, hidden), BF16),
            pltpu.VMEM((count * length, hidden), BF16),
            pltpu.VMEM((count * length, hidden), BF16),
            pltpu.VMEM((count, length, width), BF16),
            pltpu.VMEM((count, length, width), BF16),
            pltpu.VMEM((count, length, half), BF16),
            pltpu.VMEM((count, length, half), BF16),
            pltpu.VMEM((3, width, hidden), F32),
            pltpu.VMEM((length, half), F32),
        ]
        + reduce_scratch(line, (length, half))
        + [
            pltpu.SemaphoreType.DMA((5 * line,)),
            pltpu.SemaphoreType.DMA((count,)),
            pltpu.SemaphoreType.DMA((6, count)),
            pltpu.SemaphoreType.DMA((count,)),
            pltpu.SemaphoreType.DMA((2,)),
            pltpu.SemaphoreType.DMA((4,)),
        ],
        compiler_params=params(2),
        name="run_experts",
    )(rows, cots, notes, gate, up, down)


def grads_kernel(
    line,
    query_ref,
    key_ref,
    value_ref,
    out_ref,
    mix_ref,
    peak_ref,
    gain_ref,
    query_sum,
    key_sum,
    value_sum,
    out_sum,
    mix_sum,
    peaks,
    gains,
    *scratch,
):
    place = Place(line)
    count = 4 * line
    work, rest = scratch[:5], scratch[5:30]
    total, last_sems, note_sends, note_recvs, local_sems = scratch[30:]
    reduces = [Reduce(place, work[i], *rest[5 * i : 5 * i + 5]) for i in range(5)]

    def loads(i, slot):
        source = mix_ref.at[slot] if i == 4 else (query_ref, key_ref, value_ref, out_ref)[i].at[part_of(place, slot)]
        return pltpu.make_async_copy(source, work[i].at[slot], local_sems.at[i, slot])

    def begin(slot, carry):
        for i in range(5):
            loads(i, slot).start()
        return carry

    lax.fori_loop(0, count, begin, 0)
    enter(place)
    notes = [
        Notes(place, peak_ref, peaks, note_sends.at[0], note_recvs.at[0], True),
        Notes(place, gain_ref, gains, note_sends.at[1], note_recvs.at[1], False),
    ]
    for n in notes:
        n.start()

    def loaded(slot, carry):
        for i in range(5):
            loads(i, slot).wait()
        return carry

    lax.fori_loop(0, count, loaded, 0)
    order = [reduces[i] for i in (4, 3, 0, 1, 2)]
    mine, _ = halves(place, mix_sum.shape[1])
    for r in order:
        for k in [line + z for z in ends_first(line)] + ends_first(line):
            r.send_b(k)
    for r in order:
        r.fold_line_a()
        r.fold_line_own()
        r.finish_line()
    outs = (query_sum, key_sum, value_sum, out_sum, total)
    reduces[4].result(total)
    mix_sum[:, mine] = total[...]
    last = remote(total, mix_sum.at[:, mine], last_sems.at[0], last_sems.at[1], place.twin())
    last.start()
    for i in (3, 0, 1, 2):
        reduces[i].result(outs[i])
    for r in reduces:
        r.settle()
    for n in notes:
        n.finish()
    last.wait()


def reduce_grads(line, grads, mix, peak, gain):
    count = 4 * line
    blocks = [g.shape[1:] for g in grads] + [mix.shape[1:]]
    rows, half = blocks[4]
    return pl.pallas_call(
        functools.partial(grads_kernel, line),
        out_shape=[jax.ShapeDtypeStruct(s, F32) for s in blocks[:4]]
        + [
            jax.ShapeDtypeStruct((rows, 2 * half), F32),
            jax.ShapeDtypeStruct((count, *peak.shape), F32),
            jax.ShapeDtypeStruct(gain.shape, F32),
        ],
        in_specs=[ANY] * 5 + [IN_VMEM] * 2,
        out_specs=[IN_VMEM] * 7,
        scratch_shapes=[pltpu.VMEM((count, *s), BF16) for s in blocks]
        + [x for s in blocks for x in reduce_scratch(line, s)]
        + [
            pltpu.VMEM((rows, half), F32),
            pltpu.SemaphoreType.DMA((2,)),
            pltpu.SemaphoreType.DMA((2, count)),
            pltpu.SemaphoreType.DMA((2, count)),
            pltpu.SemaphoreType.DMA((5, count)),
        ],
        compiler_params=params(3),
        name="reduce_grads",
    )(*grads, mix, peak, gain)


def note_tiles(*rows):
    tiles = [jnp.pad(r.astype(F32), ((0, 0), (0, 128 - r.shape[1]))) for r in rows]
    tiles += [jnp.zeros_like(tiles[0])] * (8 - len(tiles))
    return jnp.stack(tiles, axis=1)


def on_device_dense(
    tokens,
    attn_norm_gain,
    w_query,
    key_projection,
    value_projection,
    w_out,
    moe_norm_gain,
    w_gate,
    w_up,
    w_down,
    router_logits,
    expert_ids,
    segment_ids,
    parents,
    cotangent,
):
    length, model_width = tokens.shape
    q_cols, kv_cols = w_query.shape[1], key_projection.shape[1]
    q_heads, kv_heads = q_cols // HEAD_SIZE, kv_cols // HEAD_SIZE
    group_size = q_heads // kv_heads
    count = lax.axis_size("dp")
    line = count // 4
    shard = attn_norm_gain.shape[0]
    logit_max = jnp.max(router_logits, axis=1, keepdims=True)
    logit_exp = jnp.exp(router_logits - logit_max)
    gate_probs = logit_exp / jnp.sum(logit_exp, axis=1, keepdims=True)
    expert_index = jnp.arange(count, dtype=jnp.int32)
    named = expert_ids[None, :, :] == expert_index[:, None, None]
    gate_rows = jnp.sum(jnp.where(named, gate_probs[None], 0.0), axis=2)
    own_gains = [jnp.broadcast_to(g[None], (count, shard)) for g in (attn_norm_gain, moe_norm_gain)]
    query_all, key_all, value_all, out_all, cot_all, notes = gather_weights(
        line,
        w_query,
        key_projection,
        value_projection,
        w_out,
        cotangent,
        note_tiles(gate_rows, *own_gains),
    )
    query_w = query_all.reshape(model_width, q_cols)
    key_weight = key_all.reshape(model_width, kv_cols)
    value_weight = value_all.reshape(model_width, kv_cols)
    out_w = out_all.reshape(model_width, q_cols)
    attn_gain_f = notes[:, 1, :shard].reshape(model_width)
    moe_gain_f = notes[:, 2, :shard].reshape(model_width)
    inputs = tokens.astype(F32)
    inv_attn = lax.rsqrt(jnp.mean(inputs * inputs, axis=1, keepdims=True) + EPSILON)
    unit_attn = inputs * inv_attn
    normalized_rows = (unit_attn * attn_gain_f).astype(BF16)
    position, allowed = tree_layout(segment_ids[0], parents[0])
    cosine_table, sine_values = rope_tables(position, HEAD_SIZE)
    query_linear = jnp.dot(normalized_rows, query_w, preferred_element_type=F32).reshape(
        length, q_heads, HEAD_SIZE
    )
    key_linear = jnp.dot(normalized_rows, key_weight, preferred_element_type=F32).reshape(
        length, kv_heads, HEAD_SIZE
    )
    query_heads = (
        apply_rotary(query_linear, cosine_table, sine_values)
        .astype(BF16)
        .reshape(length, kv_heads, group_size, HEAD_SIZE)
    )
    key_heads = apply_rotary(key_linear, cosine_table, sine_values).astype(BF16)
    value_heads = (
        jnp.dot(normalized_rows, value_weight, preferred_element_type=F32)
        .astype(BF16)
        .reshape(length, kv_heads, HEAD_SIZE)
    )
    scores = (
        jnp.einsum("qhgd,khd->hgqk", query_heads, key_heads, preferred_element_type=F32)
        * SCORE_SCALE
    )
    scores = jnp.where(allowed[None, None], scores, NEGATIVE)
    own_peak = jnp.max(scores, axis=(2, 3)).reshape(1, q_heads)
    row_max = jnp.max(scores, axis=3, keepdims=True)
    expo = jnp.exp(scores - row_max)
    prob_full = expo / jnp.sum(expo, axis=3, keepdims=True)
    prob_low = prob_full.astype(BF16)
    head_out = (
        jnp.einsum("hgqk,khd->qhgd", prob_low, value_heads, preferred_element_type=F32)
        .reshape(length, q_cols)
        .astype(BF16)
    )
    attn_mix = twin_sum(line, 4, contract_cols(head_out, out_w))
    hidden = inputs + RESIDUAL * attn_mix
    inv_moe = lax.rsqrt(jnp.mean(hidden * hidden, axis=1, keepdims=True) + EPSILON)
    unit_moe = hidden * inv_moe
    moe_in = (unit_moe * moe_gain_f).astype(BF16)
    d_moe_in, mix_parts, grad_gate, grad_up, grad_down = run_experts(
        line, moe_in, cot_all, notes, w_gate[0], w_up[0], w_down[0]
    )
    grad_output = cotangent.astype(F32)
    scaled_moe = d_moe_in * moe_gain_f
    grad_moe_gain = jnp.sum(d_moe_in * unit_moe, axis=0)
    d_hidden = grad_output + inv_moe * (
        scaled_moe - unit_moe * jnp.mean(scaled_moe * unit_moe, axis=1, keepdims=True)
    )
    d_attn = (RESIDUAL * d_hidden).astype(BF16)
    grad_out_w = contract_rows(d_attn, head_out)
    d_heads = (
        jnp.dot(d_attn, out_w, preferred_element_type=F32)
        .astype(BF16)
        .reshape(length, kv_heads, group_size, HEAD_SIZE)
    )
    d_value = jnp.einsum("hgqk,qhgd->khd", prob_low, d_heads, preferred_element_type=F32)
    d_prob = jnp.einsum("qhgd,khd->hgqk", d_heads, value_heads, preferred_element_type=F32)
    inner = jnp.sum(prob_full * d_prob, axis=3, keepdims=True)
    d_scores = (prob_full * (d_prob - inner)).astype(BF16)
    d_query_all = (
        jnp.einsum("hgqk,khd->qhgd", d_scores, key_heads, preferred_element_type=F32) * SCORE_SCALE
    ).reshape(length, q_heads, HEAD_SIZE)
    d_key = (
        jnp.einsum("hgqk,qhgd->khd", d_scores, query_heads, preferred_element_type=F32)
        * SCORE_SCALE
    )
    d_query_lin = (
        rotate_back(d_query_all, cosine_table, sine_values).astype(BF16).reshape(length, q_cols)
    )
    d_key_lin = rotate_back(d_key, cosine_table, sine_values).astype(BF16).reshape(length, kv_cols)
    d_value_lin = d_value.astype(BF16).reshape(length, kv_cols)
    grads = [
        contract_rows(normalized_rows, g).astype(BF16).reshape(count, shard, g.shape[1])
        for g in (d_query_lin, d_key_lin, d_value_lin)
    ] + [grad_out_w.astype(BF16).reshape(count, shard, q_cols)]
    d_normed_part = (
        contract_cols(d_query_lin, query_w)
        + contract_cols(d_key_lin, key_weight)
        + contract_cols(d_value_lin, value_weight)
    )
    d_normed = twin_sum(line, 5, d_normed_part.astype(BF16))
    scaled_attn = d_normed * attn_gain_f
    grad_attn_gain = jnp.sum(d_normed * unit_attn, axis=0)
    input_grad = d_hidden + inv_attn * (
        scaled_attn - unit_attn * jnp.mean(scaled_attn * unit_attn, axis=1, keepdims=True)
    )
    peak_tile = note_tiles(own_peak)[0]
    gain_tiles = note_tiles(grad_attn_gain.reshape(count, shard), grad_moe_gain.reshape(count, shard))
    grad_query, grad_key, grad_value, grad_out, expert_mix, peaks, gains = reduce_grads(
        line, grads, mix_parts, peak_tile, gain_tiles
    )
    output = (hidden + RESIDUAL * expert_mix).astype(BF16)
    head_peak = jnp.max(peaks[:, 0, :q_heads], axis=0)
    gain_sums = jnp.sum(gains, axis=0)
    scale_factor = CLIP_LIMIT / jnp.maximum(head_peak, CLIP_LIMIT)
    query_scale = jnp.repeat(jnp.sqrt(scale_factor), HEAD_SIZE)
    key_clip_scale = jnp.repeat(
        jnp.sqrt(jnp.min(scale_factor.reshape(kv_heads, group_size), axis=1)), HEAD_SIZE
    )
    clipped_query = w_query.astype(F32) * query_scale[None, :]
    clipped_key = key_projection.astype(F32) * key_clip_scale[None, :]
    return (
        output,
        input_grad,
        gain_sums[0, :shard],
        grad_query,
        grad_key,
        grad_value,
        grad_out,
        gain_sums[1, :shard],
        grad_gate[None],
        grad_up[None],
        grad_down[None],
        clipped_query,
        clipped_key,
    )


DENSE_BYTES = 8 * 2**20


def on_device(*args):
    tokens, w_gate = args[0], args[7]
    count, ranks = lax.axis_size("dp"), lax.axis_size("tensor")
    rows_bytes = count * tokens.shape[0] * tokens.shape[1] * 2
    whole_experts = w_gate.shape[2] * ranks == FFE
    dense = whole_experts and ranks == 2 and count % 8 == 0 and rows_bytes <= DENSE_BYTES
    return on_device_dense(*args) if dense else on_device_general(*args)


def solution(mesh):
    in_specs = (
        P("dp", None),
        P("dp"),
        P("dp", "tensor"),
        P("dp", "tensor"),
        P("dp", "tensor"),
        P("dp", "tensor"),
        P("dp"),
        P("dp", None, "tensor"),
        P("dp", None, "tensor"),
        P("dp", None, "tensor"),
        P("dp", None),
        P("dp", None),
        P("dp", None),
        P("dp", None),
        P("dp", None),
    )
    out_specs = (
        P("dp", None),
        P("dp", None),
        P("dp"),
        P("dp", "tensor"),
        P("dp", "tensor"),
        P("dp", "tensor"),
        P("dp", "tensor"),
        P("dp"),
        P("dp", None, "tensor"),
        P("dp", None, "tensor"),
        P("dp", None, "tensor"),
        P("dp", "tensor"),
        P("dp", "tensor"),
    )
    return jax.shard_map(
        on_device, mesh=mesh, in_specs=in_specs, out_specs=out_specs, check_vma=False
    )
```

```python
import functools

import jax
import jax.numpy as jnp
from jax import lax
from jax.experimental import pallas as pl
from jax.experimental.pallas import tpu as pltpu
from jax.sharding import PartitionSpec as P

HEAD_SIZE = 64
FFE = 512
TOP = 8


EPSILON = 1e-06
SCORE_SCALE = 1.0 / 64.0
RESIDUAL = 0.22
THETA = 10000.0
CLIP_LIMIT = 2.0
NEGATIVE = -1e30


def tree_layout(seg_row, par_row):
    tree_length = seg_row.shape[0]
    seg_count = par_row.shape[0]
    seg_index = jnp.arange(seg_count, dtype=jnp.int32)
    member = (seg_row[:, None] == seg_index[None, :]).astype(jnp.int32)
    seg_len = jnp.sum(member, axis=0)
    seg_start = jnp.sum(jnp.where(seg_index[:, None] > seg_index[None, :], seg_len[None, :], 0), axis=1)
    parent_hot = (par_row[:, None] == seg_index[None, :]).astype(jnp.int32)
    grand_parent = jnp.sum(parent_hot * par_row[None, :], axis=1)
    grand_hot = (grand_parent[:, None] == seg_index[None, :]).astype(jnp.int32)
    parent_len = jnp.sum(parent_hot * seg_len[None, :], axis=1)
    grand_len = jnp.sum(grand_hot * seg_len[None, :], axis=1)
    offset = jnp.where(seg_index != 0, parent_len, 0) + jnp.where(par_row != 0, grand_len, 0)
    tok_start = jnp.sum(member * seg_start[None, :], axis=1)
    tok_offset = jnp.sum(member * offset[None, :], axis=1)
    places = jnp.arange(tree_length, dtype=jnp.int32)
    position = (places - tok_start + tok_offset).astype(jnp.float32)
    identity = (seg_index[:, None] == seg_index[None, :]).astype(jnp.int32)
    ancestor = jnp.minimum(identity + parent_hot + grand_hot, 1)
    reached = jnp.dot(member, ancestor)
    linked = jnp.dot(reached, member.T) > 0
    allowed = linked & (places[None, :] <= places[:, None])
    return (position, allowed)


def rope_tables(position, head_dim):
    half_dim = head_dim // 2
    frequency = THETA ** (-2.0 * jnp.arange(half_dim, dtype=jnp.float32) / head_dim)
    angles = position[:, None] * frequency[None, :]
    return (jnp.cos(angles)[:, None, :], jnp.sin(angles)[:, None, :])


def apply_rotary(values_in, cosine_table, sine_values):
    half_dim = values_in.shape[-1] // 2
    first_half = values_in[..., :half_dim]
    second_half = values_in[..., half_dim:]
    return jnp.concatenate(
        [
            first_half * cosine_table - second_half * sine_values,
            second_half * cosine_table + first_half * sine_values,
        ],
        axis=-1,
    )


def rotate_back(grads_in, cosine_table, sine_values):
    half_dim = grads_in.shape[-1] // 2
    first_half = grads_in[..., :half_dim]
    second_half = grads_in[..., half_dim:]
    return jnp.concatenate(
        [
            first_half * cosine_table + second_half * sine_values,
            second_half * cosine_table - first_half * sine_values,
        ],
        axis=-1,
    )


def slot_tables(routes, experts, capacity):
    flat_ids = routes.reshape(-1)
    row_count = flat_ids.shape[0]
    member = (flat_ids[:, None] == jnp.arange(experts, dtype=jnp.int32)[None, :]).astype(jnp.int32)
    row_total = flat_ids.shape[0]
    before = jnp.dot((jnp.arange(row_total)[:, None] > jnp.arange(row_total)[None, :]).astype(jnp.float32), member.astype(jnp.float32), precision=lax.Precision.HIGHEST).astype(jnp.int32)
    slot_index = jnp.sum(before * member, axis=1)
    target = flat_ids * capacity + slot_index
    source = (
        jnp.full((experts * capacity,), -1, jnp.int32)
        .at[target]
        .set(jnp.arange(row_count, dtype=jnp.int32))
    )
    return (flat_ids, slot_index, source)


def contract_rows(left, right):
    return lax.dot_general(
        left, right, (((0,), (0,)), ((), ())), preferred_element_type=jnp.float32
    )


def contract_cols(left, right):
    return lax.dot_general(
        left, right, (((1,), (1,)), ((), ())), preferred_element_type=jnp.float32
    )


def expert_forward(inputs, gate_w, up_w, down_w):
    gate_pre = jnp.dot(inputs, gate_w, preferred_element_type=jnp.float32)
    up_pre = jnp.dot(inputs, up_w, preferred_element_type=jnp.float32)
    active = (gate_pre / (1.0 + jnp.exp(-gate_pre)) * up_pre).astype(jnp.bfloat16)
    return (contract_cols(active, down_w), (gate_pre, up_pre, active))


def expert_backward(inputs, grads_out, gate_w, up_w, down_w, kept_acts):
    gate_pre, up_pre, active = kept_acts
    d_active = jnp.dot(grads_out, down_w, preferred_element_type=jnp.float32)
    grad_down = contract_rows(grads_out, active)
    sigmoid_val = 1.0 / (1.0 + jnp.exp(-gate_pre))
    d_gate = (d_active * up_pre * sigmoid_val * (1.0 + gate_pre * (1.0 - sigmoid_val))).astype(
        jnp.bfloat16
    )
    d_up = (d_active * gate_pre * sigmoid_val).astype(jnp.bfloat16)
    grad_gate = contract_rows(inputs, d_gate)
    grad_up = contract_rows(inputs, d_up)
    d_inputs = contract_cols(d_gate, gate_w) + contract_cols(d_up, up_w)
    return (d_inputs, grad_gate, grad_up, grad_down)


def send_rows(rows_in):
    return lax.all_to_all(rows_in, "dp", split_axis=0, concat_axis=0, tiled=True)


def return_rows(rows_in):
    return lax.all_to_all(
        rows_in.astype(jnp.bfloat16), "dp", split_axis=0, concat_axis=0, tiled=True
    ).astype(rows_in.dtype)


def send_grads(rows_in):
    return lax.all_to_all(rows_in, "dp", split_axis=0, concat_axis=0, tiled=True)


def return_grads(rows_in):
    return lax.all_to_all(
        rows_in.astype(jnp.bfloat16), "dp", split_axis=0, concat_axis=0, tiled=True
    ).astype(rows_in.dtype)


def share_slots(partial_rows):
    return lax.psum_scatter(partial_rows, "tensor", scatter_dimension=1, tiled=True)


def on_device_general(
    tokens,
    attn_norm_gain,
    w_query,
    key_projection,
    value_projection,
    w_out,
    moe_norm_gain,
    w_gate,
    w_up,
    w_down,
    router_logits,
    expert_ids,
    segment_ids,
    parents,
    cotangent,
):
    length = tokens.shape[0]
    model_width = tokens.shape[1]
    q_cols = w_query.shape[1]
    kv_cols = key_projection.shape[1]
    q_heads = q_cols // HEAD_SIZE
    kv_heads = kv_cols // HEAD_SIZE
    group_size = q_heads // kv_heads
    dp_size = lax.axis_size("dp")
    tensor_ranks = lax.axis_size("tensor")
    replicas = FFE // (w_gate.shape[2] * tensor_ranks)
    experts = dp_size // replicas
    capacity = 4 * (9 * length * TOP // (32 * experts))
    share_rows = capacity // tensor_ranks
    first_slot = lax.axis_index("tensor") * share_rows
    block_rows = min(length, 512)
    attn_gain, moe_gain, query_w, key_weight, value_weight, out_w = (
        lax.all_gather(attn_norm_gain, "dp", axis=0, tiled=True),
        lax.all_gather(moe_norm_gain, "dp", axis=0, tiled=True),
        lax.all_gather(w_query, "dp", axis=0, tiled=True),
        lax.all_gather(key_projection, "dp", axis=0, tiled=True),
        lax.all_gather(value_projection, "dp", axis=0, tiled=True),
        lax.all_gather(w_out, "dp", axis=0, tiled=True),
    )
    attn_gain_f = attn_gain.astype(jnp.float32)
    moe_gain_f = moe_gain.astype(jnp.float32)
    inputs = tokens.astype(jnp.float32)
    inv_attn = lax.rsqrt(jnp.mean(inputs * inputs, axis=1, keepdims=True) + EPSILON)
    unit_attn = inputs * inv_attn
    normalized_rows = (unit_attn * attn_gain_f).astype(jnp.bfloat16)
    position, allowed = tree_layout(segment_ids[0], parents[0])
    cosine_table, sine_values = rope_tables(position, HEAD_SIZE)
    query_linear = jnp.dot(normalized_rows, query_w, preferred_element_type=jnp.float32).reshape(
        length, q_heads, HEAD_SIZE
    )
    key_linear = jnp.dot(normalized_rows, key_weight, preferred_element_type=jnp.float32).reshape(
        length, kv_heads, HEAD_SIZE
    )
    query_heads = (
        apply_rotary(query_linear, cosine_table, sine_values)
        .astype(jnp.bfloat16)
        .reshape(length, kv_heads, group_size, HEAD_SIZE)
    )
    key_heads = apply_rotary(key_linear, cosine_table, sine_values).astype(jnp.bfloat16)
    value_heads = (
        jnp.dot(normalized_rows, value_weight, preferred_element_type=jnp.float32)
        .astype(jnp.bfloat16)
        .reshape(length, kv_heads, HEAD_SIZE)
    )
    q_block = query_heads
    mask_rows = allowed[None, None]
    scores = (
        jnp.einsum("qhgd,khd->hgqk", q_block, key_heads, preferred_element_type=jnp.float32)
        * SCORE_SCALE
    )
    scores = jnp.where(mask_rows, scores, NEGATIVE)
    peak_parts = [jnp.max(scores, axis=(2, 3))]
    row_max = jnp.max(scores, axis=3, keepdims=True)
    expo = jnp.exp(scores - row_max)
    row_total = jnp.sum(expo, axis=3, keepdims=True)
    lse_parts = [row_max + jnp.log(row_total)]
    prob_low = (expo / row_total).astype(jnp.bfloat16)
    block_outs = jnp.einsum(
        "hgqk,khd->qhgd", prob_low, value_heads, preferred_element_type=jnp.float32
    )
    head_out = block_outs.reshape(length, q_cols).astype(jnp.bfloat16)
    attn_mix = lax.psum(contract_cols(head_out, out_w), "tensor")
    hidden = inputs + RESIDUAL * attn_mix
    head_peak = lax.pmax(jnp.max(jnp.stack(peak_parts), axis=0).reshape(q_heads), "dp")
    inv_moe = lax.rsqrt(jnp.mean(hidden * hidden, axis=1, keepdims=True) + EPSILON)
    unit_moe = hidden * inv_moe
    moe_in = (unit_moe * moe_gain_f).astype(jnp.bfloat16)
    logit_max = jnp.max(router_logits, axis=1, keepdims=True)
    logit_exp = jnp.exp(router_logits - logit_max)
    gate_probs = logit_exp / jnp.sum(logit_exp, axis=1, keepdims=True)
    flat_ids, slot_index, source = slot_tables(expert_ids, experts, capacity)
    filled = source >= 0
    source_row = jnp.maximum(source, 0)
    source_token = source_row // TOP
    dispatch_rows = jnp.where(
        filled[:, None], moe_in[source_token], jnp.zeros((), jnp.bfloat16)
    ).reshape(experts, capacity, model_width)
    arrived = send_rows(jnp.repeat(dispatch_rows, replicas, axis=0))
    gate_w, up_w, down_w = (w_gate[0], w_up[0], w_down[0])
    expert_in = arrived.reshape(dp_size * capacity, model_width)
    expert_out, kept_acts = expert_forward(expert_in, gate_w, up_w, down_w)
    partial_out = share_slots(expert_out.reshape(dp_size, capacity, model_width))
    back_parts = return_rows(partial_out).reshape(experts, replicas, share_rows, model_width)
    back_rows = (
        jnp.sum(back_parts, axis=1).astype(jnp.bfloat16).reshape(experts * share_rows, model_width)
    )
    own_slot = ((slot_index >= first_slot) & (slot_index < first_slot + share_rows)).reshape(
        length, TOP
    )
    local_index = (
        flat_ids * share_rows + jnp.clip(slot_index - first_slot, 0, share_rows - 1)
    ).reshape(length, TOP)
    mix_part = jnp.zeros((length, model_width), jnp.float32)
    for column in range(TOP):
        gate_weight = jnp.where(own_slot[:, column], gate_probs[:, column], 0.0)
        mix_part = mix_part + gate_weight[:, None] * back_rows[local_index[:, column]].astype(
            jnp.float32
        )
    expert_mix = lax.psum(mix_part.astype(jnp.bfloat16), "tensor").astype(jnp.float32)
    output = (hidden + RESIDUAL * expert_mix).astype(jnp.bfloat16)
    grad_output = cotangent.astype(jnp.float32)
    mix_grad = RESIDUAL * grad_output
    row_gate = gate_probs.reshape(-1)[source_row]
    grad_rows = (
        jnp.where(filled[:, None], row_gate[:, None] * mix_grad[source_token], 0.0)
        .astype(jnp.bfloat16)
        .reshape(experts, capacity, model_width)
    )
    grad_arrived = send_grads(jnp.repeat(grad_rows, replicas, axis=0)).reshape(
        dp_size * capacity, model_width
    )
    d_inputs, grad_gate, grad_up, grad_down = expert_backward(
        expert_in, grad_arrived, gate_w, up_w, down_w, kept_acts
    )
    d_back = share_slots(d_inputs.reshape(dp_size, capacity, model_width))
    grad_gate, grad_up, grad_down = (grad_gate[None], grad_up[None], grad_down[None])
    d_parts = return_grads(d_back).reshape(experts, replicas, share_rows, model_width)
    d_returned = (
        jnp.sum(d_parts, axis=1).astype(jnp.bfloat16).reshape(experts * share_rows, model_width)
    )
    d_mix_part = jnp.zeros((length, model_width), jnp.float32)
    for column in range(TOP):
        d_mix_part = d_mix_part + jnp.where(
            own_slot[:, column][:, None],
            d_returned[local_index[:, column]].astype(jnp.float32),
            0.0,
        )
    d_moe_in = lax.psum(d_mix_part, "tensor")
    scaled_moe = d_moe_in * moe_gain_f
    grad_moe_gain = jnp.sum(d_moe_in * unit_moe, axis=0)
    d_hidden = grad_output + inv_moe * (
        scaled_moe - unit_moe * jnp.mean(scaled_moe * unit_moe, axis=1, keepdims=True)
    )
    d_attn = (RESIDUAL * d_hidden).astype(jnp.bfloat16)
    grad_out_w = contract_rows(d_attn, head_out)
    d_heads = (
        jnp.dot(d_attn, out_w, preferred_element_type=jnp.float32)
        .astype(jnp.bfloat16)
        .reshape(length, kv_heads, group_size, HEAD_SIZE)
    )
    d_query_parts = []
    d_key = jnp.zeros((length, kv_heads, HEAD_SIZE), jnp.float32)
    d_value = jnp.zeros((length, kv_heads, HEAD_SIZE), jnp.float32)
    for block_number, row_begin in enumerate(range(0, length, block_rows)):
        q_block = query_heads
        mask_rows = allowed[None, None]
        scores = (
            jnp.einsum("qhgd,khd->hgqk", q_block, key_heads, preferred_element_type=jnp.float32)
            * SCORE_SCALE
        )
        scores = jnp.where(mask_rows, scores, NEGATIVE)
        prob_full = jnp.exp(scores - lse_parts[block_number])
        prob_low = prob_full.astype(jnp.bfloat16)
        d_value = jnp.einsum(
            "hgqk,qhgd->khd", prob_low, d_heads, preferred_element_type=jnp.float32
        )
        d_prob = jnp.einsum(
            "qhgd,khd->hgqk", d_heads, value_heads, preferred_element_type=jnp.float32
        )
        inner = jnp.sum(prob_full * d_prob, axis=3, keepdims=True)
        d_scores = (prob_full * (d_prob - inner)).astype(jnp.bfloat16)
        d_query_parts.append(
            jnp.einsum("hgqk,khd->qhgd", d_scores, key_heads, preferred_element_type=jnp.float32)
            * SCORE_SCALE
        )
        d_key = (
            jnp.einsum("hgqk,qhgd->khd", d_scores, q_block, preferred_element_type=jnp.float32)
            * SCORE_SCALE
        )
    d_query_all = d_query_parts[0].reshape(length, q_heads, HEAD_SIZE)
    d_query_lin = (
        rotate_back(d_query_all, cosine_table, sine_values)
        .astype(jnp.bfloat16)
        .reshape(length, q_cols)
    )
    d_key_lin = (
        rotate_back(d_key, cosine_table, sine_values).astype(jnp.bfloat16).reshape(length, kv_cols)
    )
    d_value_lin = d_value.astype(jnp.bfloat16).reshape(length, kv_cols)
    grad_query_w = contract_rows(normalized_rows, d_query_lin)
    grad_key_w = contract_rows(normalized_rows, d_key_lin)
    grad_value_w = contract_rows(normalized_rows, d_value_lin)
    d_normed_part = (
        contract_cols(d_query_lin, query_w)
        + contract_cols(d_key_lin, key_weight)
        + contract_cols(d_value_lin, value_weight)
    )
    d_normed = lax.psum(d_normed_part.astype(jnp.bfloat16), "tensor").astype(jnp.float32)
    scaled_attn = d_normed * attn_gain_f
    grad_attn_gain = jnp.sum(d_normed * unit_attn, axis=0)
    input_grad = d_hidden + inv_attn * (
        scaled_attn - unit_attn * jnp.mean(scaled_attn * unit_attn, axis=1, keepdims=True)
    )
    reduced = (
        lax.psum_scatter(grad_attn_gain, "dp", scatter_dimension=0, tiled=True),
        lax.psum_scatter(grad_moe_gain, "dp", scatter_dimension=0, tiled=True),
        lax.psum_scatter(grad_query_w, "dp", scatter_dimension=0, tiled=True),
        lax.psum_scatter(grad_key_w, "dp", scatter_dimension=0, tiled=True),
        lax.psum_scatter(grad_value_w, "dp", scatter_dimension=0, tiled=True),
        lax.psum_scatter(grad_out_w, "dp", scatter_dimension=0, tiled=True),
    )
    scale_factor = CLIP_LIMIT / jnp.maximum(head_peak, CLIP_LIMIT)
    query_scale = jnp.repeat(jnp.sqrt(scale_factor), HEAD_SIZE)
    key_clip_scale = jnp.repeat(
        jnp.sqrt(jnp.min(scale_factor.reshape(kv_heads, group_size), axis=1)), HEAD_SIZE
    )
    clipped_query = w_query.astype(jnp.float32) * query_scale[None, :]
    clipped_key = key_projection.astype(jnp.float32) * key_clip_scale[None, :]
    return (
        output,
        input_grad,
        reduced[0],
        reduced[2],
        reduced[3],
        reduced[4],
        reduced[5],
        reduced[1],
        grad_gate,
        grad_up,
        grad_down,
        clipped_query,
        clipped_key,
    )


MESH_IDS = pl.DeviceIdType.MESH
F32 = jnp.float32
BF16 = jnp.bfloat16


class Place:
    def __init__(self, line):
        self.line = line
        self.count = 4 * line
        me = lax.axis_index("dp")
        self.core = lax.axis_index("tensor")
        self.me = me
        self.z = me // 4
        y, x = (me // 2) % 2, me % 2
        self.step_a, self.step_b = 2 - self.core, 1 + self.core
        self.a = y * (1 - self.core) + x * self.core
        self.b = x * (1 - self.core) + y * self.core

    def part(self, z, a, b):
        return z * 4 + a * self.step_a + b * self.step_b

    def up(self):
        return (self.me + 4, self.core)

    def down(self):
        return (self.me - 4, self.core)

    def beside_a(self):
        return (self.me + self.step_a * (1 - 2 * self.a), self.core)

    def beside_b(self):
        return (self.me + self.step_b * (1 - 2 * self.b), self.core)

    def twin(self):
        return (self.me, 1 - self.core)

    def peer(self, offset):
        return lax.rem(self.me + offset, self.count)


def enter(place):
    barrier = pltpu.get_barrier_semaphore()

    def greet(offset, carry):
        pl.semaphore_signal(
            barrier, inc=1, device_id=(place.peer(offset), place.core), device_id_type=MESH_IDS
        )
        return carry

    lax.fori_loop(1, place.count, greet, 0)
    pl.semaphore_signal(barrier, inc=1, device_id=place.twin(), device_id_type=MESH_IDS)
    pl.semaphore_wait(barrier, place.count)


def remote(src, dst, send_sem, recv_sem, device):
    return pltpu.make_async_remote_copy(
        src_ref=src,
        dst_ref=dst,
        send_sem=send_sem,
        recv_sem=recv_sem,
        device_id=device,
        device_id_type=MESH_IDS,
    )


class Notes:
    def __init__(self, place, src, dst, send_sem, recv_sem, alike):
        self.place, self.src, self.dst = place, src, dst
        self.send_sem, self.recv_sem, self.alike = send_sem, recv_sem, alike

    def _copy(self, offset, source):
        place = self.place
        to = place.peer(offset)
        return remote(
            self.src if self.alike else self.src.at[to],
            self.dst.at[source],
            self.send_sem.at[offset],
            self.recv_sem.at[source],
            (to, place.core),
        )

    def start(self):
        def send(offset, carry):
            self._copy(offset, self.place.me).start()
            return carry

        lax.fori_loop(1, self.place.count, send, 0)
        me = self.place.me
        self.dst[me] = self.src[...] if self.alike else self.src[me]

    def finish(self):
        def settle(offset, carry):
            self._copy(offset, self.place.peer(offset)).wait_recv()
            self._copy(offset, self.place.me).wait_send()
            return carry

        lax.fori_loop(1, self.place.count, settle, 0)


class Gather:
    def __init__(self, place, view, send_sem, recv_sem, fixed=False):
        self.place, self.view, self.fixed = place, view, fixed
        self.send_sem, self.recv_sem = send_sem, recv_sem

    def _copy(self, source, target, sem, device):
        there = self.view(source if self.fixed else target)
        return remote(self.view(source), there, self.send_sem.at[sem], self.recv_sem.at[target], device)

    def _to_z(self, step):
        place = self.place
        own = place.z
        return self._copy(own, own, step + place.line - 1, (place.me + 4 * step, place.core))

    def _to_a(self, z):
        line = self.place.line
        return self._copy(z, line + z, 2 * line - 1 + z, self.place.beside_a())

    def _to_b(self, slot):
        line = self.place.line
        return self._copy(slot, 2 * line + slot, 3 * line - 1 + slot, self.place.beside_b())

    def take(self, slot):
        self._copy(slot, slot, 0, self.place.beside_b()).wait_recv()

    def near(self, step, action):
        place = self.place
        if step == 0:
            action(place.z)
        else:
            pl.when(place.z >= step)(lambda: action(place.z - step))
            pl.when(place.z + step < place.line)(lambda: action(place.z + step))

    def start(self):
        place = self.place

        def reach(step):
            pl.when(place.z >= step)(lambda: self._to_z(-step).start())
            pl.when(place.z + step < place.line)(lambda: self._to_z(step).start())

        reach(1)
        self._to_a(place.z).start()
        self._to_b(place.z).start()
        for step in range(2, place.line):
            reach(step)

    def along(self, step, then=None):
        def pass_on(z):
            self.take(z)
            self._to_a(z).start()
            self._to_b(z).start()
            if then is not None:
                then(z)

        self.near(step, pass_on)

    def across(self, step, then=None):
        line = self.place.line

        def pass_on(z):
            self.take(line + z)
            self._to_b(line + z).start()
            if then is not None:
                then(line + z)

        self.near(step, pass_on)

    def settle(self):
        place = self.place
        line = place.line

        def wait(z, carry):
            self._to_a(z).wait_send()
            self._to_b(z).wait_send()
            self._to_b(line + z).wait_send()
            pl.when(z != place.z)(lambda: self._to_z(z - place.z).wait_send())
            return carry

        lax.fori_loop(0, line, wait, 0)

    def take_rest(self):
        line = self.place.line

        def wait(k, carry):
            self.take(2 * line + k)
            return carry

        lax.fori_loop(0, 2 * line, wait, 0)


def gather_all(gathers, thens=None):
    line = gathers[0].place.line
    thens = thens or [None] * len(gathers)
    gathers[0].start()
    for i, (g, then) in enumerate(zip(gathers, thens)):
        for step in range(1, line + 1):
            if step < line:
                g.along(step, then)
            if step == line - 1 and i + 1 < len(gathers):
                gathers[i + 1].start()
            g.across(step - 1, then)


class Twin:
    def __init__(self, place, source, target, send_sem, recv_sem):
        self.place, self.source, self.target = place, source, target
        self.send_sem, self.recv_sem = send_sem, recv_sem

    def copy(self, slot):
        line = self.place.line
        group = slot // line
        there = slot + line * ((group % 2) - (group // 2))
        return remote(
            self.source(slot),
            self.target(there),
            self.send_sem.at[slot],
            self.recv_sem.at[there],
            self.place.twin(),
        )

    def start(self, slot):
        self.copy(slot).start()

    def take(self, slot):
        remote(
            self.source(slot),
            self.target(slot),
            self.send_sem.at[slot],
            self.recv_sem.at[slot],
            self.place.twin(),
        ).wait_recv()

    def wait_send(self, slot):
        self.copy(slot).wait_send()


class Reduce:
    def __init__(self, place, parts, from_b, from_a, from_z, send_sem, recv_sem):
        self.place, self.parts = place, parts
        self.from_b, self.from_a, self.from_z = from_b, from_a, from_z
        self.send_sem, self.recv_sem = send_sem, recv_sem

    def _copy(self, source, target, sem, device):
        return remote(source, target, self.send_sem.at[sem], self.recv_sem.at[sem], device)

    def _to_b(self, k):
        line = self.place.line
        return self._copy(self.parts.at[2 * line + k], self.from_b.at[k], k, self.place.beside_b())

    def _to_a(self, z):
        line = self.place.line
        return self._copy(self.parts.at[line + z], self.from_a.at[z], 2 * line + z, self.place.beside_a())

    def _to_z(self, target):
        place, line = self.place, self.place.line
        return remote(
            self.parts.at[target],
            self.from_z.at[place.z],
            self.send_sem.at[3 * line + target],
            self.recv_sem.at[3 * line + place.z],
            (place.me + 4 * (target - place.z), place.core),
        )

    def _add(self, slot, block):
        self.parts[slot] = (self.parts[slot].astype(F32) + block.astype(F32)).astype(BF16)

    def send_b(self, k):
        self._to_b(k).start()

    def fold_b(self, k):
        self._to_b(k).wait_recv()
        self._add(k, self.from_b[k])

    def send_a(self, z):
        self._to_a(z).start()

    def fold_a(self, z):
        self._to_a(z).wait_recv()
        self._add(z, self.from_a[z])

    def send_line(self):
        place = self.place
        for z in ends_first(place.line):
            pl.when(place.z != z)(lambda z=z: self._to_z(z).start())

    def fold_line_a(self):
        line = self.place.line
        for z in ends_first(line):
            self.fold_b(line + z)
            self.send_a(z)

    def fold_line_own(self):
        for z in ends_first(self.place.line):
            self.fold_b(z)

    def finish_line(self):
        for z in ends_first(self.place.line):
            self.fold_a(z)
        self.send_line()

    def result(self, out):
        place, line = self.place, self.place.line
        out[...] = self.parts[place.z].astype(F32)

        def add(z, carry):
            @pl.when(z != place.z)
            def _():
                remote(
                    self.parts.at[z], self.from_z.at[z], self.send_sem.at[0], self.recv_sem.at[3 * line + z], place.up()
                ).wait_recv()
                out[...] += self.from_z[z].astype(F32)

            return carry

        lax.fori_loop(0, line, add, 0)

    def settle(self):
        place, line = self.place, self.place.line

        def wait(z, carry):
            self._to_b(z).wait_send()
            self._to_b(line + z).wait_send()
            self._to_a(z).wait_send()
            pl.when(place.z != z)(lambda: self._to_z(z).wait_send())
            return carry

        lax.fori_loop(0, line, wait, 0)


AHEAD = 4


def reduce_all(reduces, finish):
    line = reduces[0].place.line
    ks = [line + z for z in ends_first(line)] + ends_first(line)
    steps = [(i, k) for i in range(len(reduces)) for k in ks]
    for i, k in steps[:AHEAD]:
        reduces[i].send_b(k)
    for at, (i, k) in enumerate(steps):
        if at + AHEAD < len(steps):
            ahead, block = steps[at + AHEAD]
            reduces[ahead].send_b(block)
        reduces[i].fold_b(k)
        if k >= line:
            reduces[i].send_a(k - line)
        if k == ks[line - 1] and i > 0:
            reduces[i - 1].finish_line()
        if k == ks[-1] and i > 0:
            finish(i - 1)
    reduces[-1].finish_line()
    finish(len(reduces) - 1)


def reduce_scratch(line, block):
    return [
        pltpu.VMEM((2 * line, *block), BF16),
        pltpu.VMEM((line, *block), BF16),
        pltpu.VMEM((line, *block), BF16),
        pltpu.SemaphoreType.DMA((4 * line,)),
        pltpu.SemaphoreType.DMA((4 * line,)),
    ]


def ends_first(line):
    order = []
    for i in range((line + 1) // 2):
        order += [i] if i == line - 1 - i else [i, line - 1 - i]
    return order


def part_of(place, slot):
    line = place.line
    group, z = slot // line, slot % line
    flip_a, flip_b = group % 2, group // 2
    a = place.a + flip_a * (1 - 2 * place.a)
    b = place.b + flip_b * (1 - 2 * place.b)
    return place.part(z, a, b)


def halves(place, width):
    half = width // 2
    mine = pl.ds(pl.multiple_of(place.core * half, 128), half)
    theirs = pl.ds(pl.multiple_of((1 - place.core) * half, 128), half)
    return mine, theirs


def weights_kernel(
    line,
    query_ref,
    key_ref,
    value_ref,
    out_ref,
    cot_ref,
    note_ref,
    query_all,
    key_all,
    value_all,
    out_all,
    cot_all,
    notes,
    sends,
    recvs,
    note_send,
    note_recv,
    twin_sems,
    local_sems,
):
    place = Place(line)
    span, _ = halves(place, cot_ref.shape[1])
    own = []
    blocks = ((query_ref, query_all), (key_ref, key_all), (value_ref, value_all), (out_ref, out_all))
    for i, (src, dst) in enumerate(blocks):
        own.append(pltpu.make_async_copy(src, dst.at[place.me], local_sems.at[i]))
    own.append(pltpu.make_async_copy(cot_ref, cot_all.at[place.z], local_sems.at[4]))
    for c in own:
        c.start()
    enter(place)
    note = Notes(place, note_ref, notes, note_send, note_recv, False)
    note.start()
    for c in own:
        c.wait()
    gathers = [
        Gather(place, lambda s, ref=ref: ref.at[part_of(place, s)], sends.at[i], recvs.at[i], True)
        for i, ref in enumerate((query_all, key_all, value_all, out_all))
    ]
    cot_view = lambda s: cot_all.at[s, :, span]
    cot_gather = Gather(place, cot_view, sends.at[4], recvs.at[4])
    twin = Twin(place, cot_view, cot_view, twin_sems.at[0], twin_sems.at[1])
    gathers.append(cot_gather)
    gather_all(gathers, [None] * 4 + [twin.start])
    for g in gathers[:4]:
        g.take_rest()

    def rest(slot, carry):
        cot_gather.take(slot)
        twin.start(slot)
        return carry

    lax.fori_loop(2 * line, 4 * line, rest, 0)
    for g in gathers:
        g.settle()

    def other(slot, carry):
        @pl.when(slot != place.z)
        def _():
            twin.wait_send(slot)
            twin.take(slot)

        return carry

    lax.fori_loop(0, 4 * line, other, 0)
    note.finish()


ANY = pl.BlockSpec(memory_space=pl.ANY)
IN_VMEM = pl.BlockSpec(memory_space=pltpu.VMEM)


def params(number):
    return pltpu.CompilerParams(
        collective_id=number, has_side_effects=True, vmem_limit_bytes=56 * 2**20
    )


def gather_weights(line, query, key, value, out, cotangent, note):
    count = 4 * line
    shapes = [query.shape, key.shape, value.shape, out.shape, cotangent.shape]
    return pl.pallas_call(
        functools.partial(weights_kernel, line),
        out_shape=[jax.ShapeDtypeStruct((count, *s), BF16) for s in shapes]
        + [jax.ShapeDtypeStruct(note.shape, F32)],
        in_specs=[ANY] * 5 + [IN_VMEM],
        out_specs=[ANY] * 5 + [IN_VMEM],
        scratch_shapes=[
            pltpu.SemaphoreType.DMA((5, 5 * line)),
            pltpu.SemaphoreType.DMA((5, count)),
            pltpu.SemaphoreType.DMA((count,)),
            pltpu.SemaphoreType.DMA((count,)),
            pltpu.SemaphoreType.DMA((2, count)),
            pltpu.SemaphoreType.DMA((5,)),
        ],
        compiler_params=params(0),
        name="gather_weights",
    )(query, key, value, out, cotangent, note)


def swap_kernel(line, mine_ref, sum_ref, other, sems):
    place = Place(line)
    barrier = pltpu.get_barrier_semaphore()
    pl.semaphore_signal(barrier, inc=1, device_id=place.twin(), device_id_type=MESH_IDS)
    pl.semaphore_wait(barrier, 1)
    copy = remote(mine_ref, other, sems.at[0], sems.at[1], place.twin())
    copy.start()
    copy.wait()
    sum_ref[...] = mine_ref[...].astype(F32) + other[...].astype(F32)


def twin_sum(line, number, mine):
    return pl.pallas_call(
        functools.partial(swap_kernel, line),
        out_shape=jax.ShapeDtypeStruct(mine.shape, F32),
        in_specs=[IN_VMEM],
        out_specs=IN_VMEM,
        scratch_shapes=[pltpu.VMEM(mine.shape, mine.dtype), pltpu.SemaphoreType.DMA((2,))],
        compiler_params=params(number),
        name="twin_sum",
    )(mine)


def experts_kernel(
    line,
    rows_ref,
    cot_ref,
    notes_ref,
    gate_ref,
    up_ref,
    down_ref,
    d_rows_ref,
    mix_ref,
    grad_gate_ref,
    grad_up_ref,
    grad_down_ref,
    rows,
    cots,
    active,
    d_gate,
    d_up,
    grad_stage,
    mix_stage,
    grad_parts,
    mix_parts,
    grads,
    total,
    from_b,
    from_a,
    from_z,
    reduce_send,
    reduce_recv,
    gather_send,
    gather_recv,
    twin_sems,
    load_sems,
    last_sems,
    store_sems,
):
    place = Place(line)
    count = 4 * line
    length, width = rows_ref.shape
    hidden = gate_ref.shape[1]
    mine, theirs = halves(place, width)

    def load(slot):
        return pltpu.make_async_copy(cot_ref.at[slot], cots.at[slot], load_sems.at[slot])

    def begin(slot, carry):
        load(slot).start()
        return carry

    lax.fori_loop(0, count, begin, 0)
    rows[place.z] = rows_ref[...]
    enter(place)
    view = lambda s: rows.at[s, :, mine]
    gather = Gather(place, view, gather_send, gather_recv)
    row_twin = Twin(place, view, view, twin_sems.at[0], twin_sems.at[1])
    grad_twin = Twin(
        place, lambda s: grad_stage.at[s, :, theirs], lambda s: grad_parts.at[s], twin_sems.at[2], twin_sems.at[3]
    )
    mix_twin = Twin(
        place, lambda s: mix_stage.at[s, :, theirs], lambda s: mix_parts.at[s], twin_sems.at[4], twin_sems.at[5]
    )
    reduce = Reduce(place, grad_parts, from_b, from_a, from_z, reduce_send, reduce_recv)
    gather_all([gather], [row_twin.start])

    def fold(slot):
        grad_twin.take(slot)
        reduce._add(slot, grad_stage[slot, :, mine])
        pl.when(slot >= 2 * line)(lambda: reduce.send_b(slot - 2 * line))

    def column(slot):
        return jnp.transpose(notes_ref[part_of(place, slot)])[:, 0:1]

    def step(tile, carry):
        first = 2 * tile
        pair = (first, first + 1)
        two = pl.ds(first, 2)
        flat = pl.ds(pl.multiple_of(first * length, 2 * length), 2 * length)
        for slot in pair:
            pl.when(slot != place.z)(lambda slot=slot: row_twin.take(slot))
            load(slot).wait()
        x = rows[two].reshape(2 * length, width)
        gate = jnp.concatenate([column(slot) for slot in pair], axis=0)
        gate_pre = jnp.dot(x, gate_ref[...], preferred_element_type=F32)
        up_pre = jnp.dot(x, up_ref[...], preferred_element_type=F32)
        sigmoid = 1.0 / (1.0 + jnp.exp(-gate_pre))
        silu = gate_pre * sigmoid
        act = (silu * up_pre).astype(BF16)
        active[flat, :] = act
        mix = contract_cols(act, down_ref[...])
        mix_stage[two] = (gate * mix).astype(BF16).reshape(2, length, width)
        d_out = (gate * (RESIDUAL * cots[two].reshape(2 * length, width).astype(F32))).astype(BF16)
        cots[two] = d_out.reshape(2, length, width)
        d_act = jnp.dot(d_out, down_ref[...], preferred_element_type=F32)
        d_g = (d_act * up_pre * sigmoid * (1.0 + gate_pre * (1.0 - sigmoid))).astype(BF16)
        d_u = (d_act * silu).astype(BF16)
        d_gate[flat, :] = d_g
        d_up[flat, :] = d_u
        d_in = contract_cols(d_g, gate_ref[...]) + contract_cols(d_u, up_ref[...])
        grad_stage[two] = d_in.astype(BF16).reshape(2, length, width)
        for slot in pair:
            grad_twin.start(slot)
            mix_twin.start(slot)

        group = (tile + 1) // (line // 2)

        @pl.when(jnp.logical_or(group == 1, group == 3))
        def _():
            for slot in (first + 2, first + 3):
                slot = slot + line * (3 - group) // 2
                gather.take(slot)
                row_twin.start(slot)

        @pl.when(jnp.logical_and(tile > 0, (first - 1) // line != 1))
        def _():
            for slot in (first - 2, first - 1):
                fold(slot)

        return carry

    lax.fori_loop(0, 2 * line, step, 0)
    for slot in (count - 2, count - 1):
        fold(slot)

    def fold_late(slot, carry):
        fold(slot)
        return carry

    lax.fori_loop(line, 2 * line, fold_late, 0)

    def weight_grad(number, left, right, out_ref):
        left = left.reshape(count * length, left.shape[2]) if len(left.shape) == 3 else left

        def some(i, carry):
            span = pl.ds(pl.multiple_of(i * 512, 512), 512)
            grads[number, span, :] = contract_rows(left[:, span], right[...])
            return carry

        lax.fori_loop(0, width // 512, some, 0)
        store = pltpu.make_async_copy(grads.at[number], out_ref, store_sems.at[number])
        store.start()
        return store

    stores = [weight_grad(0, cots, active, grad_down_ref)]
    reduce.fold_line_own()
    stores.append(weight_grad(1, rows, d_gate, grad_gate_ref))
    reduce.fold_line_a()
    stores.append(weight_grad(2, rows, d_up, grad_up_ref))
    reduce.finish_line()

    def mix_fold(slot, carry):
        mix_twin.take(slot)
        mix_parts[slot] = (mix_parts[slot].astype(F32) + mix_stage[slot, :, mine].astype(F32)).astype(BF16)
        return carry

    lax.fori_loop(0, count, mix_fold, 0)
    stores.append(pltpu.make_async_copy(mix_parts, mix_ref, store_sems.at[3]))
    stores[-1].start()
    reduce.result(total)
    d_rows_ref[:, mine] = total[...]
    last = remote(total, d_rows_ref.at[:, mine], last_sems.at[0], last_sems.at[1], place.twin())
    last.start()
    reduce.settle()
    gather.settle()

    def settle(slot, carry):
        pl.when(slot != place.z)(lambda: row_twin.wait_send(slot))
        grad_twin.wait_send(slot)
        mix_twin.wait_send(slot)
        return carry

    lax.fori_loop(0, count, settle, 0)
    for c in stores:
        c.wait()
    last.wait()


def run_experts(line, rows, cots, notes, gate, up, down):
    count = 4 * line
    length, width = rows.shape
    half, hidden = width // 2, gate.shape[1]
    grad = jax.ShapeDtypeStruct((width, hidden), F32)
    return pl.pallas_call(
        functools.partial(experts_kernel, line),
        out_shape=[
            jax.ShapeDtypeStruct((length, width), F32),
            jax.ShapeDtypeStruct((count, length, half), BF16),
            grad,
            grad,
            grad,
        ],
        in_specs=[IN_VMEM, ANY, IN_VMEM, IN_VMEM, IN_VMEM, IN_VMEM],
        out_specs=[IN_VMEM, ANY, ANY, ANY, ANY],
        scratch_shapes=[
            pltpu.VMEM((count, length, width), BF16),
            pltpu.VMEM((count, length, width), BF16),
            pltpu.VMEM((count * length, hidden), BF16),
            pltpu.VMEM((count * length, hidden), BF16),
            pltpu.VMEM((count * length, hidden), BF16),
            pltpu.VMEM((count, length, width), BF16),
            pltpu.VMEM((count, length, width), BF16),
            pltpu.VMEM((count, length, half), BF16),
            pltpu.VMEM((count, length, half), BF16),
            pltpu.VMEM((3, width, hidden), F32),
            pltpu.VMEM((length, half), F32),
        ]
        + reduce_scratch(line, (length, half))
        + [
            pltpu.SemaphoreType.DMA((5 * line,)),
            pltpu.SemaphoreType.DMA((count,)),
            pltpu.SemaphoreType.DMA((6, count)),
            pltpu.SemaphoreType.DMA((count,)),
            pltpu.SemaphoreType.DMA((2,)),
            pltpu.SemaphoreType.DMA((4,)),
        ],
        compiler_params=params(2),
        name="run_experts",
    )(rows, cots, notes, gate, up, down)


def grads_kernel(
    line,
    query_ref,
    key_ref,
    value_ref,
    out_ref,
    mix_ref,
    peak_ref,
    gain_ref,
    query_sum,
    key_sum,
    value_sum,
    out_sum,
    mix_sum,
    peaks,
    gains,
    *scratch,
):
    place = Place(line)
    count = 4 * line
    work, rest = scratch[:5], scratch[5:30]
    total, last_sems, note_sends, note_recvs, local_sems = scratch[30:]
    reduces = [Reduce(place, work[i], *rest[5 * i : 5 * i + 5]) for i in range(5)]

    def loads(i, slot):
        source = mix_ref.at[slot] if i == 4 else (query_ref, key_ref, value_ref, out_ref)[i].at[part_of(place, slot)]
        return pltpu.make_async_copy(source, work[i].at[slot], local_sems.at[i, slot])

    def begin(slot, carry):
        for i in range(5):
            loads(i, slot).start()
        return carry

    lax.fori_loop(0, count, begin, 0)
    enter(place)
    notes = [
        Notes(place, peak_ref, peaks, note_sends.at[0], note_recvs.at[0], True),
        Notes(place, gain_ref, gains, note_sends.at[1], note_recvs.at[1], False),
    ]
    for n in notes:
        n.start()

    def loaded(slot, carry):
        for i in range(5):
            loads(i, slot).wait()
        return carry

    lax.fori_loop(0, count, loaded, 0)
    mine, _ = halves(place, mix_sum.shape[1])
    outs = (query_sum, key_sum, value_sum, out_sum, total)
    order = (4, 3, 0, 1, 2)
    last = remote(total, mix_sum.at[:, mine], last_sems.at[0], last_sems.at[1], place.twin())

    def finish(at):
        i = order[at]
        reduces[i].result(outs[i])
        if i == 4:
            mix_sum[:, mine] = total[...]
            last.start()

    reduce_all([reduces[i] for i in order], finish)
    for r in reduces:
        r.settle()
    for n in notes:
        n.finish()
    last.wait()


def reduce_grads(line, grads, mix, peak, gain):
    count = 4 * line
    blocks = [g.shape[1:] for g in grads] + [mix.shape[1:]]
    rows, half = blocks[4]
    return pl.pallas_call(
        functools.partial(grads_kernel, line),
        out_shape=[jax.ShapeDtypeStruct(s, F32) for s in blocks[:4]]
        + [
            jax.ShapeDtypeStruct((rows, 2 * half), F32),
            jax.ShapeDtypeStruct((count, *peak.shape), F32),
            jax.ShapeDtypeStruct(gain.shape, F32),
        ],
        in_specs=[ANY] * 5 + [IN_VMEM] * 2,
        out_specs=[IN_VMEM] * 7,
        scratch_shapes=[pltpu.VMEM((count, *s), BF16) for s in blocks]
        + [x for s in blocks for x in reduce_scratch(line, s)]
        + [
            pltpu.VMEM((rows, half), F32),
            pltpu.SemaphoreType.DMA((2,)),
            pltpu.SemaphoreType.DMA((2, count)),
            pltpu.SemaphoreType.DMA((2, count)),
            pltpu.SemaphoreType.DMA((5, count)),
        ],
        compiler_params=params(3),
        name="reduce_grads",
    )(*grads, mix, peak, gain)


def note_tiles(*rows):
    tiles = [jnp.pad(r.astype(F32), ((0, 0), (0, 128 - r.shape[1]))) for r in rows]
    tiles += [jnp.zeros_like(tiles[0])] * (8 - len(tiles))
    return jnp.stack(tiles, axis=1)


def on_device_dense(
    tokens,
    attn_norm_gain,
    w_query,
    key_projection,
    value_projection,
    w_out,
    moe_norm_gain,
    w_gate,
    w_up,
    w_down,
    router_logits,
    expert_ids,
    segment_ids,
    parents,
    cotangent,
):
    length, model_width = tokens.shape
    q_cols, kv_cols = w_query.shape[1], key_projection.shape[1]
    q_heads, kv_heads = q_cols // HEAD_SIZE, kv_cols // HEAD_SIZE
    group_size = q_heads // kv_heads
    count = lax.axis_size("dp")
    line = count // 4
    shard = attn_norm_gain.shape[0]
    logit_max = jnp.max(router_logits, axis=1, keepdims=True)
    logit_exp = jnp.exp(router_logits - logit_max)
    gate_probs = logit_exp / jnp.sum(logit_exp, axis=1, keepdims=True)
    expert_index = jnp.arange(count, dtype=jnp.int32)
    named = expert_ids[None, :, :] == expert_index[:, None, None]
    gate_rows = jnp.sum(jnp.where(named, gate_probs[None], 0.0), axis=2)
    own_gains = [jnp.broadcast_to(g[None], (count, shard)) for g in (attn_norm_gain, moe_norm_gain)]
    query_all, key_all, value_all, out_all, cot_all, notes = gather_weights(
        line,
        w_query,
        key_projection,
        value_projection,
        w_out,
        cotangent,
        note_tiles(gate_rows, *own_gains),
    )
    query_w = query_all.reshape(model_width, q_cols)
    key_weight = key_all.reshape(model_width, kv_cols)
    value_weight = value_all.reshape(model_width, kv_cols)
    out_w = out_all.reshape(model_width, q_cols)
    attn_gain_f = notes[:, 1, :shard].reshape(model_width)
    moe_gain_f = notes[:, 2, :shard].reshape(model_width)
    inputs = tokens.astype(F32)
    inv_attn = lax.rsqrt(jnp.mean(inputs * inputs, axis=1, keepdims=True) + EPSILON)
    unit_attn = inputs * inv_attn
    normalized_rows = (unit_attn * attn_gain_f).astype(BF16)
    position, allowed = tree_layout(segment_ids[0], parents[0])
    cosine_table, sine_values = rope_tables(position, HEAD_SIZE)
    query_linear = jnp.dot(normalized_rows, query_w, preferred_element_type=F32).reshape(
        length, q_heads, HEAD_SIZE
    )
    key_linear = jnp.dot(normalized_rows, key_weight, preferred_element_type=F32).reshape(
        length, kv_heads, HEAD_SIZE
    )
    query_heads = (
        apply_rotary(query_linear, cosine_table, sine_values)
        .astype(BF16)
        .reshape(length, kv_heads, group_size, HEAD_SIZE)
    )
    key_heads = apply_rotary(key_linear, cosine_table, sine_values).astype(BF16)
    value_heads = (
        jnp.dot(normalized_rows, value_weight, preferred_element_type=F32)
        .astype(BF16)
        .reshape(length, kv_heads, HEAD_SIZE)
    )
    scores = (
        jnp.einsum("qhgd,khd->hgqk", query_heads, key_heads, preferred_element_type=F32)
        * SCORE_SCALE
    )
    scores = jnp.where(allowed[None, None], scores, NEGATIVE)
    own_peak = jnp.max(scores, axis=(2, 3)).reshape(1, q_heads)
    row_max = jnp.max(scores, axis=3, keepdims=True)
    expo = jnp.exp(scores - row_max)
    prob_full = expo / jnp.sum(expo, axis=3, keepdims=True)
    prob_low = prob_full.astype(BF16)
    head_out = (
        jnp.einsum("hgqk,khd->qhgd", prob_low, value_heads, preferred_element_type=F32)
        .reshape(length, q_cols)
        .astype(BF16)
    )
    attn_mix = twin_sum(line, 4, contract_cols(head_out, out_w))
    hidden = inputs + RESIDUAL * attn_mix
    inv_moe = lax.rsqrt(jnp.mean(hidden * hidden, axis=1, keepdims=True) + EPSILON)
    unit_moe = hidden * inv_moe
    moe_in = (unit_moe * moe_gain_f).astype(BF16)
    d_moe_in, mix_parts, grad_gate, grad_up, grad_down = run_experts(
        line, moe_in, cot_all, notes, w_gate[0], w_up[0], w_down[0]
    )
    grad_output = cotangent.astype(F32)
    scaled_moe = d_moe_in * moe_gain_f
    grad_moe_gain = jnp.sum(d_moe_in * unit_moe, axis=0)
    d_hidden = grad_output + inv_moe * (
        scaled_moe - unit_moe * jnp.mean(scaled_moe * unit_moe, axis=1, keepdims=True)
    )
    d_attn = (RESIDUAL * d_hidden).astype(BF16)
    grad_out_w = contract_rows(d_attn, head_out)
    d_heads = (
        jnp.dot(d_attn, out_w, preferred_element_type=F32)
        .astype(BF16)
        .reshape(length, kv_heads, group_size, HEAD_SIZE)
    )
    d_value = jnp.einsum("hgqk,qhgd->khd", prob_low, d_heads, preferred_element_type=F32)
    d_prob = jnp.einsum("qhgd,khd->hgqk", d_heads, value_heads, preferred_element_type=F32)
    inner = jnp.sum(prob_full * d_prob, axis=3, keepdims=True)
    d_scores = (prob_full * (d_prob - inner)).astype(BF16)
    d_query_all = (
        jnp.einsum("hgqk,khd->qhgd", d_scores, key_heads, preferred_element_type=F32) * SCORE_SCALE
    ).reshape(length, q_heads, HEAD_SIZE)
    d_key = (
        jnp.einsum("hgqk,qhgd->khd", d_scores, query_heads, preferred_element_type=F32)
        * SCORE_SCALE
    )
    d_query_lin = (
        rotate_back(d_query_all, cosine_table, sine_values).astype(BF16).reshape(length, q_cols)
    )
    d_key_lin = rotate_back(d_key, cosine_table, sine_values).astype(BF16).reshape(length, kv_cols)
    d_value_lin = d_value.astype(BF16).reshape(length, kv_cols)
    grads = [
        contract_rows(normalized_rows, g).astype(BF16).reshape(count, shard, g.shape[1])
        for g in (d_query_lin, d_key_lin, d_value_lin)
    ] + [grad_out_w.astype(BF16).reshape(count, shard, q_cols)]
    d_normed_part = (
        contract_cols(d_query_lin, query_w)
        + contract_cols(d_key_lin, key_weight)
        + contract_cols(d_value_lin, value_weight)
    )
    d_normed = twin_sum(line, 5, d_normed_part.astype(BF16))
    scaled_attn = d_normed * attn_gain_f
    grad_attn_gain = jnp.sum(d_normed * unit_attn, axis=0)
    input_grad = d_hidden + inv_attn * (
        scaled_attn - unit_attn * jnp.mean(scaled_attn * unit_attn, axis=1, keepdims=True)
    )
    peak_tile = note_tiles(own_peak)[0]
    gain_tiles = note_tiles(grad_attn_gain.reshape(count, shard), grad_moe_gain.reshape(count, shard))
    grad_query, grad_key, grad_value, grad_out, expert_mix, peaks, gains = reduce_grads(
        line, grads, mix_parts, peak_tile, gain_tiles
    )
    output = (hidden + RESIDUAL * expert_mix).astype(BF16)
    head_peak = jnp.max(peaks[:, 0, :q_heads], axis=0)
    gain_sums = jnp.sum(gains, axis=0)
    scale_factor = CLIP_LIMIT / jnp.maximum(head_peak, CLIP_LIMIT)
    query_scale = jnp.repeat(jnp.sqrt(scale_factor), HEAD_SIZE)
    key_clip_scale = jnp.repeat(
        jnp.sqrt(jnp.min(scale_factor.reshape(kv_heads, group_size), axis=1)), HEAD_SIZE
    )
    clipped_query = w_query.astype(F32) * query_scale[None, :]
    clipped_key = key_projection.astype(F32) * key_clip_scale[None, :]
    return (
        output,
        input_grad,
        gain_sums[0, :shard],
        grad_query,
        grad_key,
        grad_value,
        grad_out,
        gain_sums[1, :shard],
        grad_gate[None],
        grad_up[None],
        grad_down[None],
        clipped_query,
        clipped_key,
    )


DENSE_BYTES = 8 * 2**20


def on_device(*args):
    tokens, w_gate = args[0], args[7]
    count, ranks = lax.axis_size("dp"), lax.axis_size("tensor")
    rows_bytes = count * tokens.shape[0] * tokens.shape[1] * 2
    whole_experts = w_gate.shape[2] * ranks == FFE
    dense = whole_experts and ranks == 2 and count % 8 == 0 and rows_bytes <= DENSE_BYTES
    return on_device_dense(*args) if dense else on_device_general(*args)


def solution(mesh):
    in_specs = (
        P("dp", None),
        P("dp"),
        P("dp", "tensor"),
        P("dp", "tensor"),
        P("dp", "tensor"),
        P("dp", "tensor"),
        P("dp"),
        P("dp", None, "tensor"),
        P("dp", None, "tensor"),
        P("dp", None, "tensor"),
        P("dp", None),
        P("dp", None),
        P("dp", None),
        P("dp", None),
        P("dp", None),
    )
    out_specs = (
        P("dp", None),
        P("dp", None),
        P("dp"),
        P("dp", "tensor"),
        P("dp", "tensor"),
        P("dp", "tensor"),
        P("dp", "tensor"),
        P("dp"),
        P("dp", None, "tensor"),
        P("dp", None, "tensor"),
        P("dp", None, "tensor"),
        P("dp", "tensor"),
        P("dp", "tensor"),
    )
    return jax.shard_map(
        on_device, mesh=mesh, in_specs=in_specs, out_specs=out_specs, check_vma=False
    )
```

```python
import functools

import jax
import jax.numpy as jnp
from jax import lax
from jax.experimental import pallas as pl
from jax.experimental.pallas import tpu as pltpu
from jax.sharding import PartitionSpec as P

HEAD_SIZE = 64
FFE = 512
TOP = 8


EPSILON = 1e-06
SCORE_SCALE = 1.0 / 64.0
RESIDUAL = 0.22
THETA = 10000.0
CLIP_LIMIT = 2.0
NEGATIVE = -1e30


def tree_layout(seg_row, par_row):
    tree_length = seg_row.shape[0]
    seg_count = par_row.shape[0]
    seg_index = jnp.arange(seg_count, dtype=jnp.int32)
    member = (seg_row[:, None] == seg_index[None, :]).astype(jnp.int32)
    seg_len = jnp.sum(member, axis=0)
    seg_start = jnp.sum(jnp.where(seg_index[:, None] > seg_index[None, :], seg_len[None, :], 0), axis=1)
    parent_hot = (par_row[:, None] == seg_index[None, :]).astype(jnp.int32)
    grand_parent = jnp.sum(parent_hot * par_row[None, :], axis=1)
    grand_hot = (grand_parent[:, None] == seg_index[None, :]).astype(jnp.int32)
    parent_len = jnp.sum(parent_hot * seg_len[None, :], axis=1)
    grand_len = jnp.sum(grand_hot * seg_len[None, :], axis=1)
    offset = jnp.where(seg_index != 0, parent_len, 0) + jnp.where(par_row != 0, grand_len, 0)
    tok_start = jnp.sum(member * seg_start[None, :], axis=1)
    tok_offset = jnp.sum(member * offset[None, :], axis=1)
    places = jnp.arange(tree_length, dtype=jnp.int32)
    position = (places - tok_start + tok_offset).astype(jnp.float32)
    identity = (seg_index[:, None] == seg_index[None, :]).astype(jnp.int32)
    ancestor = jnp.minimum(identity + parent_hot + grand_hot, 1)
    reached = jnp.dot(member, ancestor)
    linked = jnp.dot(reached, member.T) > 0
    allowed = linked & (places[None, :] <= places[:, None])
    return (position, allowed)


def rope_tables(position, head_dim):
    half_dim = head_dim // 2
    frequency = THETA ** (-2.0 * jnp.arange(half_dim, dtype=jnp.float32) / head_dim)
    angles = position[:, None] * frequency[None, :]
    return (jnp.cos(angles)[:, None, :], jnp.sin(angles)[:, None, :])


def apply_rotary(values_in, cosine_table, sine_values):
    half_dim = values_in.shape[-1] // 2
    first_half = values_in[..., :half_dim]
    second_half = values_in[..., half_dim:]
    return jnp.concatenate(
        [
            first_half * cosine_table - second_half * sine_values,
            second_half * cosine_table + first_half * sine_values,
        ],
        axis=-1,
    )


def rotate_back(grads_in, cosine_table, sine_values):
    half_dim = grads_in.shape[-1] // 2
    first_half = grads_in[..., :half_dim]
    second_half = grads_in[..., half_dim:]
    return jnp.concatenate(
        [
            first_half * cosine_table + second_half * sine_values,
            second_half * cosine_table - first_half * sine_values,
        ],
        axis=-1,
    )


def slot_tables(routes, experts, capacity):
    flat_ids = routes.reshape(-1)
    row_count = flat_ids.shape[0]
    member = (flat_ids[:, None] == jnp.arange(experts, dtype=jnp.int32)[None, :]).astype(jnp.int32)
    row_total = flat_ids.shape[0]
    before = jnp.dot((jnp.arange(row_total)[:, None] > jnp.arange(row_total)[None, :]).astype(jnp.float32), member.astype(jnp.float32), precision=lax.Precision.HIGHEST).astype(jnp.int32)
    slot_index = jnp.sum(before * member, axis=1)
    target = flat_ids * capacity + slot_index
    source = (
        jnp.full((experts * capacity,), -1, jnp.int32)
        .at[target]
        .set(jnp.arange(row_count, dtype=jnp.int32))
    )
    return (flat_ids, slot_index, source)


def contract_rows(left, right):
    return lax.dot_general(
        left, right, (((0,), (0,)), ((), ())), preferred_element_type=jnp.float32
    )


def contract_cols(left, right):
    return lax.dot_general(
        left, right, (((1,), (1,)), ((), ())), preferred_element_type=jnp.float32
    )


def expert_forward(inputs, gate_w, up_w, down_w):
    gate_pre = jnp.dot(inputs, gate_w, preferred_element_type=jnp.float32)
    up_pre = jnp.dot(inputs, up_w, preferred_element_type=jnp.float32)
    active = (gate_pre / (1.0 + jnp.exp(-gate_pre)) * up_pre).astype(jnp.bfloat16)
    return (contract_cols(active, down_w), (gate_pre, up_pre, active))


def expert_backward(inputs, grads_out, gate_w, up_w, down_w, kept_acts):
    gate_pre, up_pre, active = kept_acts
    d_active = jnp.dot(grads_out, down_w, preferred_element_type=jnp.float32)
    grad_down = contract_rows(grads_out, active)
    sigmoid_val = 1.0 / (1.0 + jnp.exp(-gate_pre))
    d_gate = (d_active * up_pre * sigmoid_val * (1.0 + gate_pre * (1.0 - sigmoid_val))).astype(
        jnp.bfloat16
    )
    d_up = (d_active * gate_pre * sigmoid_val).astype(jnp.bfloat16)
    grad_gate = contract_rows(inputs, d_gate)
    grad_up = contract_rows(inputs, d_up)
    d_inputs = contract_cols(d_gate, gate_w) + contract_cols(d_up, up_w)
    return (d_inputs, grad_gate, grad_up, grad_down)


def send_rows(rows_in):
    return lax.all_to_all(rows_in, "dp", split_axis=0, concat_axis=0, tiled=True)


def return_rows(rows_in):
    return lax.all_to_all(
        rows_in.astype(jnp.bfloat16), "dp", split_axis=0, concat_axis=0, tiled=True
    ).astype(rows_in.dtype)


def send_grads(rows_in):
    return lax.all_to_all(rows_in, "dp", split_axis=0, concat_axis=0, tiled=True)


def return_grads(rows_in):
    return lax.all_to_all(
        rows_in.astype(jnp.bfloat16), "dp", split_axis=0, concat_axis=0, tiled=True
    ).astype(rows_in.dtype)


def share_slots(partial_rows):
    return lax.psum_scatter(partial_rows, "tensor", scatter_dimension=1, tiled=True)


def on_device_general(
    tokens,
    attn_norm_gain,
    w_query,
    key_projection,
    value_projection,
    w_out,
    moe_norm_gain,
    w_gate,
    w_up,
    w_down,
    router_logits,
    expert_ids,
    segment_ids,
    parents,
    cotangent,
):
    length = tokens.shape[0]
    model_width = tokens.shape[1]
    q_cols = w_query.shape[1]
    kv_cols = key_projection.shape[1]
    q_heads = q_cols // HEAD_SIZE
    kv_heads = kv_cols // HEAD_SIZE
    group_size = q_heads // kv_heads
    dp_size = lax.axis_size("dp")
    tensor_ranks = lax.axis_size("tensor")
    replicas = FFE // (w_gate.shape[2] * tensor_ranks)
    experts = dp_size // replicas
    capacity = 4 * (9 * length * TOP // (32 * experts))
    share_rows = capacity // tensor_ranks
    first_slot = lax.axis_index("tensor") * share_rows
    block_rows = min(length, 512)
    attn_gain, moe_gain, query_w, key_weight, value_weight, out_w = (
        lax.all_gather(attn_norm_gain, "dp", axis=0, tiled=True),
        lax.all_gather(moe_norm_gain, "dp", axis=0, tiled=True),
        lax.all_gather(w_query, "dp", axis=0, tiled=True),
        lax.all_gather(key_projection, "dp", axis=0, tiled=True),
        lax.all_gather(value_projection, "dp", axis=0, tiled=True),
        lax.all_gather(w_out, "dp", axis=0, tiled=True),
    )
    attn_gain_f = attn_gain.astype(jnp.float32)
    moe_gain_f = moe_gain.astype(jnp.float32)
    inputs = tokens.astype(jnp.float32)
    inv_attn = lax.rsqrt(jnp.mean(inputs * inputs, axis=1, keepdims=True) + EPSILON)
    unit_attn = inputs * inv_attn
    normalized_rows = (unit_attn * attn_gain_f).astype(jnp.bfloat16)
    position, allowed = tree_layout(segment_ids[0], parents[0])
    cosine_table, sine_values = rope_tables(position, HEAD_SIZE)
    query_linear = jnp.dot(normalized_rows, query_w, preferred_element_type=jnp.float32).reshape(
        length, q_heads, HEAD_SIZE
    )
    key_linear = jnp.dot(normalized_rows, key_weight, preferred_element_type=jnp.float32).reshape(
        length, kv_heads, HEAD_SIZE
    )
    query_heads = (
        apply_rotary(query_linear, cosine_table, sine_values)
        .astype(jnp.bfloat16)
        .reshape(length, kv_heads, group_size, HEAD_SIZE)
    )
    key_heads = apply_rotary(key_linear, cosine_table, sine_values).astype(jnp.bfloat16)
    value_heads = (
        jnp.dot(normalized_rows, value_weight, preferred_element_type=jnp.float32)
        .astype(jnp.bfloat16)
        .reshape(length, kv_heads, HEAD_SIZE)
    )
    q_block = query_heads
    mask_rows = allowed[None, None]
    scores = (
        jnp.einsum("qhgd,khd->hgqk", q_block, key_heads, preferred_element_type=jnp.float32)
        * SCORE_SCALE
    )
    scores = jnp.where(mask_rows, scores, NEGATIVE)
    peak_parts = [jnp.max(scores, axis=(2, 3))]
    row_max = jnp.max(scores, axis=3, keepdims=True)
    expo = jnp.exp(scores - row_max)
    row_total = jnp.sum(expo, axis=3, keepdims=True)
    lse_parts = [row_max + jnp.log(row_total)]
    prob_low = (expo / row_total).astype(jnp.bfloat16)
    block_outs = jnp.einsum(
        "hgqk,khd->qhgd", prob_low, value_heads, preferred_element_type=jnp.float32
    )
    head_out = block_outs.reshape(length, q_cols).astype(jnp.bfloat16)
    attn_mix = lax.psum(contract_cols(head_out, out_w), "tensor")
    hidden = inputs + RESIDUAL * attn_mix
    head_peak = lax.pmax(jnp.max(jnp.stack(peak_parts), axis=0).reshape(q_heads), "dp")
    inv_moe = lax.rsqrt(jnp.mean(hidden * hidden, axis=1, keepdims=True) + EPSILON)
    unit_moe = hidden * inv_moe
    moe_in = (unit_moe * moe_gain_f).astype(jnp.bfloat16)
    logit_max = jnp.max(router_logits, axis=1, keepdims=True)
    logit_exp = jnp.exp(router_logits - logit_max)
    gate_probs = logit_exp / jnp.sum(logit_exp, axis=1, keepdims=True)
    flat_ids, slot_index, source = slot_tables(expert_ids, experts, capacity)
    filled = source >= 0
    source_row = jnp.maximum(source, 0)
    source_token = source_row // TOP
    dispatch_rows = jnp.where(
        filled[:, None], moe_in[source_token], jnp.zeros((), jnp.bfloat16)
    ).reshape(experts, capacity, model_width)
    arrived = send_rows(jnp.repeat(dispatch_rows, replicas, axis=0))
    gate_w, up_w, down_w = (w_gate[0], w_up[0], w_down[0])
    expert_in = arrived.reshape(dp_size * capacity, model_width)
    expert_out, kept_acts = expert_forward(expert_in, gate_w, up_w, down_w)
    partial_out = share_slots(expert_out.reshape(dp_size, capacity, model_width))
    back_parts = return_rows(partial_out).reshape(experts, replicas, share_rows, model_width)
    back_rows = (
        jnp.sum(back_parts, axis=1).astype(jnp.bfloat16).reshape(experts * share_rows, model_width)
    )
    own_slot = ((slot_index >= first_slot) & (slot_index < first_slot + share_rows)).reshape(
        length, TOP
    )
    local_index = (
        flat_ids * share_rows + jnp.clip(slot_index - first_slot, 0, share_rows - 1)
    ).reshape(length, TOP)
    mix_part = jnp.zeros((length, model_width), jnp.float32)
    for column in range(TOP):
        gate_weight = jnp.where(own_slot[:, column], gate_probs[:, column], 0.0)
        mix_part = mix_part + gate_weight[:, None] * back_rows[local_index[:, column]].astype(
            jnp.float32
        )
    expert_mix = lax.psum(mix_part.astype(jnp.bfloat16), "tensor").astype(jnp.float32)
    output = (hidden + RESIDUAL * expert_mix).astype(jnp.bfloat16)
    grad_output = cotangent.astype(jnp.float32)
    mix_grad = RESIDUAL * grad_output
    row_gate = gate_probs.reshape(-1)[source_row]
    grad_rows = (
        jnp.where(filled[:, None], row_gate[:, None] * mix_grad[source_token], 0.0)
        .astype(jnp.bfloat16)
        .reshape(experts, capacity, model_width)
    )
    grad_arrived = send_grads(jnp.repeat(grad_rows, replicas, axis=0)).reshape(
        dp_size * capacity, model_width
    )
    d_inputs, grad_gate, grad_up, grad_down = expert_backward(
        expert_in, grad_arrived, gate_w, up_w, down_w, kept_acts
    )
    d_back = share_slots(d_inputs.reshape(dp_size, capacity, model_width))
    grad_gate, grad_up, grad_down = (grad_gate[None], grad_up[None], grad_down[None])
    d_parts = return_grads(d_back).reshape(experts, replicas, share_rows, model_width)
    d_returned = (
        jnp.sum(d_parts, axis=1).astype(jnp.bfloat16).reshape(experts * share_rows, model_width)
    )
    d_mix_part = jnp.zeros((length, model_width), jnp.float32)
    for column in range(TOP):
        d_mix_part = d_mix_part + jnp.where(
            own_slot[:, column][:, None],
            d_returned[local_index[:, column]].astype(jnp.float32),
            0.0,
        )
    d_moe_in = lax.psum(d_mix_part, "tensor")
    scaled_moe = d_moe_in * moe_gain_f
    grad_moe_gain = jnp.sum(d_moe_in * unit_moe, axis=0)
    d_hidden = grad_output + inv_moe * (
        scaled_moe - unit_moe * jnp.mean(scaled_moe * unit_moe, axis=1, keepdims=True)
    )
    d_attn = (RESIDUAL * d_hidden).astype(jnp.bfloat16)
    grad_out_w = contract_rows(d_attn, head_out)
    d_heads = (
        jnp.dot(d_attn, out_w, preferred_element_type=jnp.float32)
        .astype(jnp.bfloat16)
        .reshape(length, kv_heads, group_size, HEAD_SIZE)
    )
    d_query_parts = []
    d_key = jnp.zeros((length, kv_heads, HEAD_SIZE), jnp.float32)
    d_value = jnp.zeros((length, kv_heads, HEAD_SIZE), jnp.float32)
    for block_number, row_begin in enumerate(range(0, length, block_rows)):
        q_block = query_heads
        mask_rows = allowed[None, None]
        scores = (
            jnp.einsum("qhgd,khd->hgqk", q_block, key_heads, preferred_element_type=jnp.float32)
            * SCORE_SCALE
        )
        scores = jnp.where(mask_rows, scores, NEGATIVE)
        prob_full = jnp.exp(scores - lse_parts[block_number])
        prob_low = prob_full.astype(jnp.bfloat16)
        d_value = jnp.einsum(
            "hgqk,qhgd->khd", prob_low, d_heads, preferred_element_type=jnp.float32
        )
        d_prob = jnp.einsum(
            "qhgd,khd->hgqk", d_heads, value_heads, preferred_element_type=jnp.float32
        )
        inner = jnp.sum(prob_full * d_prob, axis=3, keepdims=True)
        d_scores = (prob_full * (d_prob - inner)).astype(jnp.bfloat16)
        d_query_parts.append(
            jnp.einsum("hgqk,khd->qhgd", d_scores, key_heads, preferred_element_type=jnp.float32)
            * SCORE_SCALE
        )
        d_key = (
            jnp.einsum("hgqk,qhgd->khd", d_scores, q_block, preferred_element_type=jnp.float32)
            * SCORE_SCALE
        )
    d_query_all = d_query_parts[0].reshape(length, q_heads, HEAD_SIZE)
    d_query_lin = (
        rotate_back(d_query_all, cosine_table, sine_values)
        .astype(jnp.bfloat16)
        .reshape(length, q_cols)
    )
    d_key_lin = (
        rotate_back(d_key, cosine_table, sine_values).astype(jnp.bfloat16).reshape(length, kv_cols)
    )
    d_value_lin = d_value.astype(jnp.bfloat16).reshape(length, kv_cols)
    grad_query_w = contract_rows(normalized_rows, d_query_lin)
    grad_key_w = contract_rows(normalized_rows, d_key_lin)
    grad_value_w = contract_rows(normalized_rows, d_value_lin)
    d_normed_part = (
        contract_cols(d_query_lin, query_w)
        + contract_cols(d_key_lin, key_weight)
        + contract_cols(d_value_lin, value_weight)
    )
    d_normed = lax.psum(d_normed_part.astype(jnp.bfloat16), "tensor").astype(jnp.float32)
    scaled_attn = d_normed * attn_gain_f
    grad_attn_gain = jnp.sum(d_normed * unit_attn, axis=0)
    input_grad = d_hidden + inv_attn * (
        scaled_attn - unit_attn * jnp.mean(scaled_attn * unit_attn, axis=1, keepdims=True)
    )
    reduced = (
        lax.psum_scatter(grad_attn_gain, "dp", scatter_dimension=0, tiled=True),
        lax.psum_scatter(grad_moe_gain, "dp", scatter_dimension=0, tiled=True),
        lax.psum_scatter(grad_query_w, "dp", scatter_dimension=0, tiled=True),
        lax.psum_scatter(grad_key_w, "dp", scatter_dimension=0, tiled=True),
        lax.psum_scatter(grad_value_w, "dp", scatter_dimension=0, tiled=True),
        lax.psum_scatter(grad_out_w, "dp", scatter_dimension=0, tiled=True),
    )
    scale_factor = CLIP_LIMIT / jnp.maximum(head_peak, CLIP_LIMIT)
    query_scale = jnp.repeat(jnp.sqrt(scale_factor), HEAD_SIZE)
    key_clip_scale = jnp.repeat(
        jnp.sqrt(jnp.min(scale_factor.reshape(kv_heads, group_size), axis=1)), HEAD_SIZE
    )
    clipped_query = w_query.astype(jnp.float32) * query_scale[None, :]
    clipped_key = key_projection.astype(jnp.float32) * key_clip_scale[None, :]
    return (
        output,
        input_grad,
        reduced[0],
        reduced[2],
        reduced[3],
        reduced[4],
        reduced[5],
        reduced[1],
        grad_gate,
        grad_up,
        grad_down,
        clipped_query,
        clipped_key,
    )


MESH_IDS = pl.DeviceIdType.MESH
F32 = jnp.float32
BF16 = jnp.bfloat16


class Place:
    def __init__(self, line):
        self.line = line
        self.count = 4 * line
        me = lax.axis_index("dp")
        self.core = lax.axis_index("tensor")
        self.me = me
        self.z = me // 4
        y, x = (me // 2) % 2, me % 2
        self.step_a, self.step_b = 2 - self.core, 1 + self.core
        self.a = y * (1 - self.core) + x * self.core
        self.b = x * (1 - self.core) + y * self.core

    def part(self, z, a, b):
        return z * 4 + a * self.step_a + b * self.step_b

    def up(self):
        return (self.me + 4, self.core)

    def down(self):
        return (self.me - 4, self.core)

    def beside_a(self):
        return (self.me + self.step_a * (1 - 2 * self.a), self.core)

    def beside_b(self):
        return (self.me + self.step_b * (1 - 2 * self.b), self.core)

    def twin(self):
        return (self.me, 1 - self.core)

    def peer(self, offset):
        return lax.rem(self.me + offset, self.count)


def enter(place):
    barrier = pltpu.get_barrier_semaphore()

    def greet(offset, carry):
        pl.semaphore_signal(
            barrier, inc=1, device_id=(place.peer(offset), place.core), device_id_type=MESH_IDS
        )
        return carry

    lax.fori_loop(1, place.count, greet, 0)
    pl.semaphore_signal(barrier, inc=1, device_id=place.twin(), device_id_type=MESH_IDS)
    pl.semaphore_wait(barrier, place.count)


def remote(src, dst, send_sem, recv_sem, device):
    return pltpu.make_async_remote_copy(
        src_ref=src,
        dst_ref=dst,
        send_sem=send_sem,
        recv_sem=recv_sem,
        device_id=device,
        device_id_type=MESH_IDS,
    )


class Notes:
    def __init__(self, place, src, dst, send_sem, recv_sem, alike):
        self.place, self.src, self.dst = place, src, dst
        self.send_sem, self.recv_sem, self.alike = send_sem, recv_sem, alike

    def _copy(self, offset, source):
        place = self.place
        to = place.peer(offset)
        return remote(
            self.src if self.alike else self.src.at[to],
            self.dst.at[source],
            self.send_sem.at[offset],
            self.recv_sem.at[source],
            (to, place.core),
        )

    def start(self):
        def send(offset, carry):
            self._copy(offset, self.place.me).start()
            return carry

        lax.fori_loop(1, self.place.count, send, 0)
        me = self.place.me
        self.dst[me] = self.src[...] if self.alike else self.src[me]

    def finish(self):
        def settle(offset, carry):
            self._copy(offset, self.place.peer(offset)).wait_recv()
            self._copy(offset, self.place.me).wait_send()
            return carry

        lax.fori_loop(1, self.place.count, settle, 0)


class Gather:
    def __init__(self, place, view, send_sem, recv_sem, fixed=False):
        self.place, self.view, self.fixed = place, view, fixed
        self.send_sem, self.recv_sem = send_sem, recv_sem

    def _copy(self, source, target, sem, device):
        there = self.view(source if self.fixed else target)
        return remote(self.view(source), there, self.send_sem.at[sem], self.recv_sem.at[target], device)

    def _to_z(self, step):
        place = self.place
        own = place.z
        return self._copy(own, own, step + place.line - 1, (place.me + 4 * step, place.core))

    def _to_a(self, z):
        line = self.place.line
        return self._copy(z, line + z, 2 * line - 1 + z, self.place.beside_a())

    def _to_b(self, slot):
        line = self.place.line
        return self._copy(slot, 2 * line + slot, 3 * line - 1 + slot, self.place.beside_b())

    def take(self, slot):
        self._copy(slot, slot, 0, self.place.beside_b()).wait_recv()

    def near(self, step, action):
        place = self.place
        if step == 0:
            action(place.z)
        else:
            pl.when(place.z >= step)(lambda: action(place.z - step))
            pl.when(place.z + step < place.line)(lambda: action(place.z + step))

    def start(self):
        place = self.place

        def reach(step):
            pl.when(place.z >= step)(lambda: self._to_z(-step).start())
            pl.when(place.z + step < place.line)(lambda: self._to_z(step).start())

        reach(1)
        self._to_a(place.z).start()
        self._to_b(place.z).start()
        for step in range(2, place.line):
            reach(step)

    def along(self, step, then=None):
        def pass_on(z):
            self.take(z)
            self._to_a(z).start()
            self._to_b(z).start()
            if then is not None:
                then(z)

        self.near(step, pass_on)

    def across(self, step, then=None):
        line = self.place.line

        def pass_on(z):
            self.take(line + z)
            self._to_b(line + z).start()
            if then is not None:
                then(line + z)

        self.near(step, pass_on)

    def settle(self):
        place = self.place
        line = place.line

        def wait(z, carry):
            self._to_a(z).wait_send()
            self._to_b(z).wait_send()
            self._to_b(line + z).wait_send()
            pl.when(z != place.z)(lambda: self._to_z(z - place.z).wait_send())
            return carry

        lax.fori_loop(0, line, wait, 0)

    def take_rest(self):
        line = self.place.line

        def wait(k, carry):
            self.take(2 * line + k)
            return carry

        lax.fori_loop(0, 2 * line, wait, 0)


def gather_all(gathers, thens=None):
    line = gathers[0].place.line
    thens = thens or [None] * len(gathers)
    gathers[0].start()
    for i, (g, then) in enumerate(zip(gathers, thens)):
        for step in range(1, line + 1):
            if step < line:
                g.along(step, then)
            if step == line - 1 and i + 1 < len(gathers):
                gathers[i + 1].start()
            g.across(step - 1, then)


class Twin:
    def __init__(self, place, source, target, send_sem, recv_sem):
        self.place, self.source, self.target = place, source, target
        self.send_sem, self.recv_sem = send_sem, recv_sem

    def copy(self, slot):
        line = self.place.line
        group = slot // line
        there = slot + line * ((group % 2) - (group // 2))
        return remote(
            self.source(slot),
            self.target(there),
            self.send_sem.at[slot],
            self.recv_sem.at[there],
            self.place.twin(),
        )

    def start(self, slot):
        self.copy(slot).start()

    def take(self, slot):
        remote(
            self.source(slot),
            self.target(slot),
            self.send_sem.at[slot],
            self.recv_sem.at[slot],
            self.place.twin(),
        ).wait_recv()

    def wait_send(self, slot):
        self.copy(slot).wait_send()


class Reduce:
    def __init__(self, place, parts, from_b, from_a, from_z, send_sem, recv_sem, index=lambda slot: slot):
        self.place, self.parts, self.index = place, parts, index
        self.from_b, self.from_a, self.from_z = from_b, from_a, from_z
        self.send_sem, self.recv_sem = send_sem, recv_sem

    def _copy(self, source, target, sem, device):
        return remote(source, target, self.send_sem.at[sem], self.recv_sem.at[sem], device)

    def _to_b(self, k):
        line = self.place.line
        return self._copy(self.parts.at[self.index(2 * line + k)], self.from_b.at[k], k, self.place.beside_b())

    def _to_a(self, z):
        line = self.place.line
        block = self.parts.at[self.index(line + z)]
        return self._copy(block, self.from_a.at[z], 2 * line + z, self.place.beside_a())

    def _to_z(self, target):
        place, line = self.place, self.place.line
        return remote(
            self.parts.at[self.index(target)],
            self.from_z.at[place.z],
            self.send_sem.at[3 * line + target],
            self.recv_sem.at[3 * line + place.z],
            (place.me + 4 * (target - place.z), place.core),
        )

    def _add(self, slot, block):
        at = self.index(slot)
        self.parts[at] = (self.parts[at].astype(F32) + block.astype(F32)).astype(BF16)

    def send_b(self, k):
        self._to_b(k).start()

    def fold_b(self, k):
        self._to_b(k).wait_recv()
        self._add(k, self.from_b[k])

    def send_a(self, z):
        self._to_a(z).start()

    def fold_a(self, z):
        self._to_a(z).wait_recv()
        self._add(z, self.from_a[z])

    def send_line(self):
        place = self.place
        for z in ends_first(place.line):
            pl.when(place.z != z)(lambda z=z: self._to_z(z).start())

    def fold_line_a(self):
        line = self.place.line
        for z in ends_first(line):
            self.fold_b(line + z)
            self.send_a(z)

    def fold_line_own(self):
        for z in ends_first(self.place.line):
            self.fold_b(z)

    def finish_line(self):
        for z in ends_first(self.place.line):
            self.fold_a(z)
        self.send_line()

    def result(self, out):
        place, line = self.place, self.place.line
        out[...] = self.parts[self.index(place.z)].astype(F32)

        def add(z, carry):
            @pl.when(z != place.z)
            def _():
                remote(
                    self.from_z.at[z], self.from_z.at[z], self.send_sem.at[0], self.recv_sem.at[3 * line + z], place.up()
                ).wait_recv()
                out[...] += self.from_z[z].astype(F32)

            return carry

        lax.fori_loop(0, line, add, 0)

    def settle(self):
        place, line = self.place, self.place.line

        def wait(z, carry):
            self._to_b(z).wait_send()
            self._to_b(line + z).wait_send()
            self._to_a(z).wait_send()
            pl.when(place.z != z)(lambda: self._to_z(z).wait_send())
            return carry

        lax.fori_loop(0, line, wait, 0)


AHEAD = 4


class Reductions:
    def __init__(self, reduces, finish):
        self.reduces, self.finish, self.at = reduces, finish, 0
        line = self.line = reduces[0].place.line
        self.ks = [line + z for z in ends_first(line)] + ends_first(line)
        self.steps = [(i, k) for i in range(len(reduces)) for k in self.ks]

    def start(self):
        for i, k in self.steps[:AHEAD]:
            self.reduces[i].send_b(k)

    def run(self, number):
        for _ in range(number):
            self._step()

    def _step(self):
        if self.at + AHEAD < len(self.steps):
            ahead, block = self.steps[self.at + AHEAD]
            self.reduces[ahead].send_b(block)
        i, k = self.steps[self.at]
        self.at += 1
        self.reduces[i].fold_b(k)
        if k >= self.line:
            self.reduces[i].send_a(k - self.line)
        if k == self.ks[self.line - 1] and i > 0:
            self.reduces[i - 1].finish_line()
        if k == self.ks[-1] and i > 0:
            self.finish(i - 1)

    def complete(self):
        self.run(len(self.steps) - self.at)
        self.reduces[-1].finish_line()
        self.finish(len(self.reduces) - 1)


def reduce_scratch(line, block):
    return [
        pltpu.VMEM((2 * line, *block), BF16),
        pltpu.VMEM((line, *block), BF16),
        pltpu.VMEM((line, *block), BF16),
        pltpu.SemaphoreType.DMA((4 * line,)),
        pltpu.SemaphoreType.DMA((4 * line,)),
    ]


def ends_first(line):
    order = []
    for i in range((line + 1) // 2):
        order += [i] if i == line - 1 - i else [i, line - 1 - i]
    return order


def part_of(place, slot):
    line = place.line
    group, z = slot // line, slot % line
    flip_a, flip_b = group % 2, group // 2
    a = place.a + flip_a * (1 - 2 * place.a)
    b = place.b + flip_b * (1 - 2 * place.b)
    return place.part(z, a, b)


def halves(place, width):
    half = width // 2
    mine = pl.ds(pl.multiple_of(place.core * half, 128), half)
    theirs = pl.ds(pl.multiple_of((1 - place.core) * half, 128), half)
    return mine, theirs


def place_half(chunk, have, want, lane):
    chunk = chunk if have == want else pltpu.roll(chunk, HEAD_SIZE, 1)
    return jnp.where(lane // HEAD_SIZE == want, chunk, 0.0)


def rope_chunk(chunk, tables, sign):
    ahead = pltpu.roll(chunk, 128 - HEAD_SIZE // 2, 1)
    behind = pltpu.roll(chunk, HEAD_SIZE // 2, 1)
    return chunk * tables[0] + sign * (ahead * tables[1] + behind * tables[2])


def chunk_of(ref, j):
    return ref[:, 128 * j : 128 * (j + 1)]


def pair_of(ref, j, group_size, lane):
    both = []
    for half in (0, 1):
        group = (2 * j + half) // group_size
        both.append(place_half(chunk_of(ref, group // 2).astype(F32), group % 2, half, lane))
    return jnp.concatenate(both, axis=0).astype(BF16)


def spread_gains(notes, shard, width):
    total = jnp.zeros((8, width), F32)
    for p in range(notes.shape[0]):
        row = jnp.concatenate([notes[p], jnp.zeros((8, width - 128), F32)], axis=1)
        total += pltpu.roll(row, shard * p, 1) if p else row
    return total


def forward_kernel(
    line,
    group_size,
    tokens_ref,
    query_ref,
    key_ref,
    value_ref,
    out_ref,
    cot_ref,
    note_ref,
    tables_ref,
    allowed_ref,
    moe_in_ref,
    hidden_ref,
    normed_ref,
    head_out_ref,
    queries_ref,
    keys_ref,
    values_ref,
    probs_ref,
    peak_ref,
    gains_ref,
    notes,
    query_keep,
    key_keep,
    value_keep,
    out_keep,
    cot_keep,
    query_all,
    key_all,
    value_all,
    out_all,
    cot_all,
    mix_mine,
    mix_other,
    sends,
    recvs,
    note_send,
    note_recv,
    twin_sems,
    local_sems,
    keep_sems,
    mix_sems,
):
    place = Place(line)
    count = 4 * line
    length, width = tokens_ref.shape
    shard, q_cols = query_ref.shape
    chunks = q_cols // 128
    span, _ = halves(place, width)
    own = []
    blocks = ((query_ref, query_all), (key_ref, key_all), (value_ref, value_all), (out_ref, out_all))
    for i, (src, dst) in enumerate(blocks):
        own.append(pltpu.make_async_copy(src, dst.at[place.me], local_sems.at[i]))
    own.append(pltpu.make_async_copy(cot_ref, cot_all.at[place.z], local_sems.at[4]))
    for c in own:
        c.start()
    enter(place)
    note = Notes(place, note_ref, notes, note_send, note_recv, False)
    for c in own:
        c.wait()
    gathers = [
        Gather(place, lambda s, ref=ref: ref.at[part_of(place, s)], sends.at[i], recvs.at[i], True)
        for i, ref in enumerate((query_all, key_all, value_all, out_all))
    ]
    cot_view = lambda s: cot_all.at[s, :, span]
    cot = Gather(place, cot_view, sends.at[4], recvs.at[4])
    twin = Twin(place, cot_view, cot_view, twin_sems.at[0], twin_sems.at[1])
    out = gathers[3]
    for g in gathers[:3]:
        g.start()
    note.start()
    inputs = tokens_ref[...].astype(F32)
    inv_attn = lax.rsqrt(jnp.mean(inputs * inputs, axis=1, keepdims=True) + EPSILON)
    for g in gathers[:3]:
        g.along(1)
    note.finish()
    gains_ref[...] = spread_gains(notes, shard, width)
    normed_ref[...] = (inputs * inv_attn * gains_ref[1:2, :]).astype(BF16)
    for g in gathers[:3]:
        g.across(0)
    for step in range(2, line + 1):
        for g in gathers[:3]:
            if step < line:
                g.along(step)
            g.across(step - 1)
        if step == line - 1:
            out.start()
    for g in gathers[:3]:
        g.take_rest()
    normed = normed_ref[...]
    tables = [tables_ref[i] for i in range(3)]
    query_lin = jnp.dot(normed, query_all[...].reshape(width, q_cols), preferred_element_type=F32)
    for j in range(chunks):
        queries_ref[:, 128 * j : 128 * (j + 1)] = rope_chunk(
            query_lin[:, 128 * j : 128 * (j + 1)], tables, 1.0
        ).astype(BF16)
    out.along(1)
    out.across(0)
    kv_cols = key_ref.shape[1]
    key_lin = jnp.dot(normed, key_all[...].reshape(width, kv_cols), preferred_element_type=F32)
    for j in range(kv_cols // 128):
        keys_ref[:, 128 * j : 128 * (j + 1)] = rope_chunk(
            key_lin[:, 128 * j : 128 * (j + 1)], tables, 1.0
        ).astype(BF16)
    values_ref[...] = jnp.dot(
        normed, value_all[...].reshape(width, kv_cols), preferred_element_type=F32
    ).astype(BF16)
    lane = lax.broadcasted_iota(jnp.int32, (length, 128), 1)
    small_lane = lax.broadcasted_iota(jnp.int32, (8, 128), 1)
    allowed = allowed_ref[...] > 0.0
    peaks = jnp.zeros((8, 128), F32)
    between = {
        0: lambda: (out.along(2), out.across(1)),
        1: lambda: out.along(3) if line > 3 else None,
        2: lambda: (cot.start(), out.across(2)),
        3: lambda: out.across(3) if line > 3 else None,
    }
    for j in range(chunks):
        both = contract_cols(chunk_of(queries_ref, j), pair_of(keys_ref, j, group_size, lane)) * SCORE_SCALE
        low = []
        for half in (0, 1):
            scores = jnp.where(allowed, both[:, length * half : length * (half + 1)], NEGATIVE)
            row_max = jnp.max(scores, axis=1, keepdims=True)
            peak = jnp.max(row_max, axis=0, keepdims=True)
            peaks = jnp.where(small_lane == 2 * j + half, peak, peaks)
            expo = jnp.exp(scores - row_max)
            prob = expo / jnp.sum(expo, axis=1, keepdims=True)
            probs_ref[j, :, length * half : length * (half + 1)] = prob
            low.append(prob.astype(BF16))
        mixed = jnp.dot(
            jnp.concatenate(low, axis=1),
            pair_of(values_ref, j, group_size, lane),
            preferred_element_type=F32,
        )
        head_out_ref[:, 128 * j : 128 * (j + 1)] = mixed.astype(BF16)
        if j in between:
            between[j]()
    peak_ref[...] = peaks
    keeps = [
        pltpu.make_async_copy(src, dst, keep_sems.at[i])
        for i, (src, dst) in enumerate(
            (
                (query_all, query_keep),
                (key_all, key_keep),
                (value_all, value_keep),
                (out_all, out_keep),
                (cot_all, cot_keep),
            )
        )
    ]
    for c in keeps[:3]:
        c.start()
    out.take_rest()
    keeps[3].start()
    mix_mine[...] = contract_cols(head_out_ref[...], out_all[...].reshape(width, q_cols))
    swap = remote(mix_mine, mix_other, mix_sems.at[0], mix_sems.at[1], place.twin())
    swap.start()
    cot.along(1, twin.start)
    cot.across(0, twin.start)
    swap.wait()
    hidden = tokens_ref[...].astype(F32) + RESIDUAL * (mix_mine[...] + mix_other[...])
    hidden_ref[...] = hidden
    inv_moe = lax.rsqrt(jnp.mean(hidden * hidden, axis=1, keepdims=True) + EPSILON)
    moe_in_ref[...] = (hidden * inv_moe * gains_ref[2:3, :]).astype(BF16)
    for step in range(2, line + 1):
        if step < line:
            cot.along(step, twin.start)
        cot.across(step - 1, twin.start)

    def rest(slot, carry):
        cot.take(slot)
        twin.start(slot)
        return carry

    lax.fori_loop(2 * line, count, rest, 0)
    for g in gathers + [cot]:
        g.settle()

    def other(slot, carry):
        @pl.when(slot != place.z)
        def _():
            twin.wait_send(slot)
            twin.take(slot)

        return carry

    lax.fori_loop(0, count, other, 0)
    keeps[4].start()
    for c in keeps:
        c.wait()


ANY = pl.BlockSpec(memory_space=pl.ANY)
IN_VMEM = pl.BlockSpec(memory_space=pltpu.VMEM)


def params(number):
    return pltpu.CompilerParams(
        collective_id=number, has_side_effects=True, vmem_limit_bytes=56 * 2**20
    )


def run_forward(line, group_size, tokens, query, key, value, out, cotangent, note, tables, allowed):
    count = 4 * line
    length, width = tokens.shape
    q_cols, kv_cols = query.shape[1], key.shape[1]
    blocks = [x.shape for x in (query, key, value, out, cotangent)]
    shape = jax.ShapeDtypeStruct
    outs = [
        shape((length, width), BF16),
        shape((length, width), F32),
        shape((length, width), BF16),
        shape((length, q_cols), BF16),
        shape((length, q_cols), BF16),
        shape((length, kv_cols), BF16),
        shape((length, kv_cols), BF16),
        shape((q_cols // 128, length, 2 * length), F32),
        shape((8, 128), F32),
        shape((8, width), F32),
        shape(note.shape, F32),
    ]
    return pl.pallas_call(
        functools.partial(forward_kernel, line, group_size),
        out_shape=outs + [shape((count, *s), BF16) for s in blocks],
        in_specs=[IN_VMEM] + [ANY] * 5 + [IN_VMEM] * 3,
        out_specs=[IN_VMEM] * len(outs) + [ANY] * 5,
        scratch_shapes=[pltpu.VMEM((count, *s), BF16) for s in blocks]
        + [
            pltpu.VMEM((length, width), F32),
            pltpu.VMEM((length, width), F32),
            pltpu.SemaphoreType.DMA((5, 5 * line)),
            pltpu.SemaphoreType.DMA((5, count)),
            pltpu.SemaphoreType.DMA((count,)),
            pltpu.SemaphoreType.DMA((count,)),
            pltpu.SemaphoreType.DMA((2, count)),
            pltpu.SemaphoreType.DMA((5,)),
            pltpu.SemaphoreType.DMA((5,)),
            pltpu.SemaphoreType.DMA((2,)),
        ],
        compiler_params=params(0),
        name="run_forward",
    )(tokens, query, key, value, out, cotangent, note, tables, allowed)


def experts_kernel(
    line,
    rows_ref,
    cot_ref,
    notes_ref,
    gate_ref,
    up_ref,
    down_ref,
    d_rows_ref,
    mix_ref,
    grad_gate_ref,
    grad_up_ref,
    grad_down_ref,
    rows,
    cots,
    active,
    d_gate,
    d_up,
    grad_stage,
    mix_stage,
    grad_parts,
    mix_parts,
    grads,
    total,
    from_b,
    from_a,
    from_z,
    reduce_send,
    reduce_recv,
    gather_send,
    gather_recv,
    twin_sems,
    load_sems,
    last_sems,
    store_sems,
):
    place = Place(line)
    count = 4 * line
    length, width = rows_ref.shape
    hidden = gate_ref.shape[1]
    mine, theirs = halves(place, width)

    def load(slot):
        return pltpu.make_async_copy(cot_ref.at[slot], cots.at[slot], load_sems.at[slot])

    def begin(slot, carry):
        load(slot).start()
        return carry

    lax.fori_loop(0, count, begin, 0)
    rows[place.z] = rows_ref[...]
    enter(place)
    view = lambda s: rows.at[s, :, mine]
    gather = Gather(place, view, gather_send, gather_recv)
    row_twin = Twin(place, view, view, twin_sems.at[0], twin_sems.at[1])
    grad_twin = Twin(
        place, lambda s: grad_stage.at[s, :, theirs], lambda s: grad_parts.at[s], twin_sems.at[2], twin_sems.at[3]
    )
    mix_twin = Twin(
        place, lambda s: mix_stage.at[s, :, theirs], lambda s: mix_parts.at[s], twin_sems.at[4], twin_sems.at[5]
    )
    reduce = Reduce(place, grad_parts, from_b, from_a, from_z, reduce_send, reduce_recv)
    gather_all([gather], [row_twin.start])

    def fold(slot):
        grad_twin.take(slot)
        reduce._add(slot, grad_stage[slot, :, mine])
        pl.when(slot >= 2 * line)(lambda: reduce.send_b(slot - 2 * line))

    def column(slot):
        return jnp.transpose(notes_ref[part_of(place, slot)])[:, 0:1]

    def step(tile, carry):
        first = 2 * tile
        pair = (first, first + 1)
        two = pl.ds(first, 2)
        flat = pl.ds(pl.multiple_of(first * length, 2 * length), 2 * length)
        for slot in pair:
            pl.when(slot != place.z)(lambda slot=slot: row_twin.take(slot))
            load(slot).wait()
        x = rows[two].reshape(2 * length, width)
        gate = jnp.concatenate([column(slot) for slot in pair], axis=0)
        gate_pre = jnp.dot(x, gate_ref[...], preferred_element_type=F32)
        up_pre = jnp.dot(x, up_ref[...], preferred_element_type=F32)
        sigmoid = 1.0 / (1.0 + jnp.exp(-gate_pre))
        silu = gate_pre * sigmoid
        act = (silu * up_pre).astype(BF16)
        active[flat, :] = act
        mix = contract_cols(act, down_ref[...])
        mix_stage[two] = (gate * mix).astype(BF16).reshape(2, length, width)
        d_out = (gate * (RESIDUAL * cots[two].reshape(2 * length, width).astype(F32))).astype(BF16)
        cots[two] = d_out.reshape(2, length, width)
        d_act = jnp.dot(d_out, down_ref[...], preferred_element_type=F32)
        d_g = (d_act * up_pre * sigmoid * (1.0 + gate_pre * (1.0 - sigmoid))).astype(BF16)
        d_u = (d_act * silu).astype(BF16)
        d_gate[flat, :] = d_g
        d_up[flat, :] = d_u
        d_in = contract_cols(d_g, gate_ref[...]) + contract_cols(d_u, up_ref[...])
        grad_stage[two] = d_in.astype(BF16).reshape(2, length, width)
        for slot in pair:
            grad_twin.start(slot)
            mix_twin.start(slot)

        group = (tile + 1) // (line // 2)

        @pl.when(jnp.logical_or(group == 1, group == 3))
        def _():
            for slot in (first + 2, first + 3):
                slot = slot + line * (3 - group) // 2
                gather.take(slot)
                row_twin.start(slot)

        @pl.when(jnp.logical_and(tile > 0, (first - 1) // line != 1))
        def _():
            for slot in (first - 2, first - 1):
                fold(slot)

        return carry

    lax.fori_loop(0, 2 * line, step, 0)
    for slot in (count - 2, count - 1):
        fold(slot)

    def fold_late(slot, carry):
        fold(slot)
        return carry

    lax.fori_loop(line, 2 * line, fold_late, 0)

    def weight_grad(number, left, right, out_ref):
        left = left.reshape(count * length, left.shape[2]) if len(left.shape) == 3 else left

        def some(i, carry):
            span = pl.ds(pl.multiple_of(i * 512, 512), 512)
            grads[number, span, :] = contract_rows(left[:, span], right[...])
            return carry

        lax.fori_loop(0, width // 512, some, 0)
        store = pltpu.make_async_copy(grads.at[number], out_ref, store_sems.at[number])
        store.start()
        return store

    stores = [weight_grad(0, cots, active, grad_down_ref)]
    reduce.fold_line_own()
    stores.append(weight_grad(1, rows, d_gate, grad_gate_ref))
    reduce.fold_line_a()
    stores.append(weight_grad(2, rows, d_up, grad_up_ref))
    reduce.finish_line()

    def mix_fold(slot, carry):
        mix_twin.take(slot)
        mix_parts[slot] = (mix_parts[slot].astype(F32) + mix_stage[slot, :, mine].astype(F32)).astype(BF16)
        return carry

    lax.fori_loop(0, count, mix_fold, 0)
    stores.append(pltpu.make_async_copy(mix_parts, mix_ref, store_sems.at[3]))
    stores[-1].start()
    reduce.result(total)
    d_rows_ref[:, mine] = total[...]
    last = remote(total, d_rows_ref.at[:, mine], last_sems.at[0], last_sems.at[1], place.twin())
    last.start()
    reduce.settle()
    gather.settle()

    def settle(slot, carry):
        pl.when(slot != place.z)(lambda: row_twin.wait_send(slot))
        grad_twin.wait_send(slot)
        mix_twin.wait_send(slot)
        return carry

    lax.fori_loop(0, count, settle, 0)
    for c in stores:
        c.wait()
    last.wait()


def run_experts(line, rows, cots, notes, gate, up, down):
    count = 4 * line
    length, width = rows.shape
    half, hidden = width // 2, gate.shape[1]
    grad = jax.ShapeDtypeStruct((width, hidden), F32)
    return pl.pallas_call(
        functools.partial(experts_kernel, line),
        out_shape=[
            jax.ShapeDtypeStruct((length, width), F32),
            jax.ShapeDtypeStruct((count, length, half), BF16),
            grad,
            grad,
            grad,
        ],
        in_specs=[IN_VMEM, ANY, IN_VMEM, IN_VMEM, IN_VMEM, IN_VMEM],
        out_specs=[IN_VMEM, ANY, ANY, ANY, ANY],
        scratch_shapes=[
            pltpu.VMEM((count, length, width), BF16),
            pltpu.VMEM((count, length, width), BF16),
            pltpu.VMEM((count * length, hidden), BF16),
            pltpu.VMEM((count * length, hidden), BF16),
            pltpu.VMEM((count * length, hidden), BF16),
            pltpu.VMEM((count, length, width), BF16),
            pltpu.VMEM((count, length, width), BF16),
            pltpu.VMEM((count, length, half), BF16),
            pltpu.VMEM((count, length, half), BF16),
            pltpu.VMEM((3, width, hidden), F32),
            pltpu.VMEM((length, half), F32),
        ]
        + reduce_scratch(line, (length, half))
        + [
            pltpu.SemaphoreType.DMA((5 * line,)),
            pltpu.SemaphoreType.DMA((count,)),
            pltpu.SemaphoreType.DMA((6, count)),
            pltpu.SemaphoreType.DMA((count,)),
            pltpu.SemaphoreType.DMA((2,)),
            pltpu.SemaphoreType.DMA((4,)),
        ],
        compiler_params=params(2),
        name="run_experts",
    )(rows, cots, notes, gate, up, down)


def backward_kernel(
    line,
    group_size,
    tokens_ref,
    hidden_ref,
    d_rows_ref,
    cot_ref,
    normed_ref,
    head_out_ref,
    queries_ref,
    keys_ref,
    values_ref,
    probs_ref,
    gains_ref,
    peak_ref,
    tables_ref,
    query_keep,
    key_keep,
    value_keep,
    out_keep,
    mix_ref,
    input_grad_ref,
    output_ref,
    query_sum,
    key_sum,
    value_sum,
    out_sum,
    notes,
    *scratch,
):
    place = Place(line)
    count = 4 * line
    length, width = tokens_ref.shape
    q_cols, kv_cols = queries_ref.shape[1], keys_ref.shape[1]
    shard = width // count
    chunks = q_cols // 128
    (query_all, key_all, value_all, out_all), work = scratch[:4], scratch[4:9]
    rest = scratch[9:34]
    (
        total,
        d_heads,
        d_query,
        d_key,
        d_value,
        part_mine,
        part_other,
        d_hidden_keep,
        mix_total,
        note,
        weight_sems,
        load_sems,
        last_sems,
        part_sems,
        note_sends,
        note_recvs,
    ) = scratch[34:]
    by_part = lambda slot: part_of(place, slot)
    reduces = [
        Reduce(place, work[i], *rest[5 * i : 5 * i + 5], *(() if i == 4 else (by_part,))) for i in range(5)
    ]

    def load(slot):
        return pltpu.make_async_copy(mix_ref.at[slot], work[4].at[slot], load_sems.at[slot])

    def begin(slot, carry):
        load(slot).start()
        return carry

    def loaded(slot, carry):
        load(slot).wait()
        return carry

    lax.fori_loop(0, count, begin, 0)
    weights = [
        pltpu.make_async_copy(src, dst, weight_sems.at[i])
        for i, (src, dst) in enumerate(
            ((out_keep, out_all), (query_keep, query_all), (key_keep, key_all), (value_keep, value_all))
        )
    ]
    for c in weights:
        c.start()
    enter(place)
    lax.fori_loop(0, count, loaded, 0)
    mine, theirs = halves(place, width)
    outs = (query_sum, key_sum, value_sum, out_sum, total)
    order = (4, 3, 0, 1, 2)
    last = remote(total, mix_total.at[:, mine], last_sems.at[0], last_sems.at[1], place.twin())

    def finish(at):
        i = order[at]
        reduces[i].result(outs[i])
        if i == 4:
            mix_total[:, mine] = total[...]
            last.start()

    run = Reductions([reduces[i] for i in order], finish)
    run.start()
    hidden = hidden_ref[...]
    inv_moe = lax.rsqrt(jnp.mean(hidden * hidden, axis=1, keepdims=True) + EPSILON)
    unit_moe = hidden * inv_moe
    d_rows = d_rows_ref[...]
    scaled = d_rows * gains_ref[2:3, :]
    d_hidden = cot_ref[...].astype(F32) + inv_moe * (
        scaled - unit_moe * jnp.mean(scaled * unit_moe, axis=1, keepdims=True)
    )
    d_hidden_keep[...] = d_hidden
    moe_gain = jnp.sum(d_rows * unit_moe, axis=0, keepdims=True)
    d_attn = (RESIDUAL * d_hidden).astype(BF16)
    run.run(2)
    work[3][...] = contract_rows(d_attn, head_out_ref[...]).astype(BF16).reshape(count, shard, q_cols)
    run.run(2)
    weights[0].wait()
    d_heads[...] = jnp.dot(
        d_attn, out_all[...].reshape(width, q_cols), preferred_element_type=F32
    ).astype(BF16)
    run.run(1)
    lane = lax.broadcasted_iota(jnp.int32, (length, 128), 1)
    d_key[...] = jnp.zeros_like(d_key)
    d_value[...] = jnp.zeros_like(d_value)
    tables = [tables_ref[i] for i in range(3)]
    for j in range(chunks):
        d_out = chunk_of(d_heads, j)
        keys = pair_of(keys_ref, j, group_size, lane)
        d_prob = contract_cols(d_out, pair_of(values_ref, j, group_size, lane))
        low, d_scores = [], []
        for half in (0, 1):
            side = slice(length * half, length * (half + 1))
            prob = probs_ref[j, :, side]
            grad = d_prob[:, side]
            inner = jnp.sum(prob * grad, axis=1, keepdims=True)
            d_scores.append((prob * (grad - inner)).astype(BF16))
            low.append(prob.astype(BF16))
        d_scores = jnp.concatenate(d_scores, axis=1)
        d_values = contract_rows(jnp.concatenate(low, axis=1), d_out)
        d_keys = contract_rows(d_scores, chunk_of(queries_ref, j)) * SCORE_SCALE
        turned = rope_chunk(
            jnp.dot(d_scores, keys, preferred_element_type=F32) * SCORE_SCALE, tables, -1.0
        )
        d_query[:, 128 * j : 128 * (j + 1)] = turned.astype(BF16)
        for half in (0, 1):
            group = (2 * j + half) // group_size
            side = slice(length * half, length * (half + 1))
            cols = slice(128 * (group // 2), 128 * (group // 2 + 1))
            d_key[:, cols] += place_half(d_keys[side], half, group % 2, lane)
            d_value[:, cols] += place_half(d_values[side], half, group % 2, lane)
        run.run(1)
    normed = normed_ref[...]
    work[0][...] = contract_rows(normed, d_query[...]).astype(BF16).reshape(count, shard, q_cols)
    d_key_lin = jnp.concatenate(
        [rope_chunk(chunk_of(d_key, j), tables, -1.0) for j in range(kv_cols // 128)], axis=1
    ).astype(BF16)
    d_value_lin = d_value[...].astype(BF16)
    run.run(2)
    work[1][...] = contract_rows(normed, d_key_lin).astype(BF16).reshape(count, shard, kv_cols)
    work[2][...] = contract_rows(normed, d_value_lin).astype(BF16).reshape(count, shard, kv_cols)
    run.run(2)
    for c in weights[1:]:
        c.wait()
    part_mine[...] = (
        contract_cols(d_query[...], query_all[...].reshape(width, q_cols))
        + contract_cols(d_key_lin, key_all[...].reshape(width, kv_cols))
        + contract_cols(d_value_lin, value_all[...].reshape(width, kv_cols))
    )
    swap = remote(part_mine, part_other, part_sems.at[0], part_sems.at[1], place.twin())
    swap.start()
    run.run(2)
    swap.wait()
    d_normed = part_mine[...] + part_other[...]
    inputs = tokens_ref[...].astype(F32)
    inv_attn = lax.rsqrt(jnp.mean(inputs * inputs, axis=1, keepdims=True) + EPSILON)
    unit_attn = inputs * inv_attn
    scaled = d_normed * gains_ref[1:2, :]
    input_grad_ref[...] = d_hidden_keep[...] + inv_attn * (
        scaled - unit_attn * jnp.mean(scaled * unit_attn, axis=1, keepdims=True)
    )
    attn_gain = jnp.sum(d_normed * unit_attn, axis=0, keepdims=True)
    rows = jnp.concatenate([attn_gain, moe_gain, jnp.zeros((6, width), F32)], axis=0)
    row = lax.broadcasted_iota(jnp.int32, (8, 128), 0)
    peaks = jnp.broadcast_to(peak_ref[0:1, :], (8, 128))
    for p in range(count):
        turned = pltpu.roll(rows, width - shard * p, 1) if p else rows
        note[p] = jnp.where(row == 2, peaks, turned[:, :128])
    exchange = Notes(place, note, notes, note_sends, note_recvs, False)
    exchange.start()
    run.complete()
    for r in reduces:
        r.settle()
    last.wait()
    output_ref[...] = (hidden_ref[...] + RESIDUAL * mix_total[...]).astype(BF16)
    exchange.finish()


def run_backward(line, group_size, kept, keeps, mix):
    count = 4 * line
    tokens, queries, keys = kept[0], kept[6], kept[7]
    length, width = tokens.shape
    q_cols, kv_cols = queries.shape[1], keys.shape[1]
    blocks = [x.shape[1:] for x in keeps] + [mix.shape[1:]]
    half = width // 2
    shape = jax.ShapeDtypeStruct
    outs = (
        [shape((length, width), F32), shape((length, width), BF16)]
        + [shape(s, F32) for s in blocks[:4]]
        + [shape((count, 8, 128), F32)]
    )
    return pl.pallas_call(
        functools.partial(backward_kernel, line, group_size),
        out_shape=outs,
        in_specs=[IN_VMEM] * len(kept) + [ANY] * 5,
        out_specs=[IN_VMEM] * len(outs),
        scratch_shapes=[pltpu.VMEM(x.shape, BF16) for x in keeps]
        + [pltpu.VMEM((count, *s), BF16) for s in blocks]
        + [x for s in blocks for x in reduce_scratch(line, s)]
        + [
            pltpu.VMEM((length, half), F32),
            pltpu.VMEM((length, q_cols), BF16),
            pltpu.VMEM((length, q_cols), BF16),
            pltpu.VMEM((length, kv_cols), F32),
            pltpu.VMEM((length, kv_cols), F32),
            pltpu.VMEM((length, width), F32),
            pltpu.VMEM((length, width), F32),
            pltpu.VMEM((length, width), F32),
            pltpu.VMEM((length, width), F32),
            pltpu.VMEM((count, 8, 128), F32),
            pltpu.SemaphoreType.DMA((4,)),
            pltpu.SemaphoreType.DMA((count,)),
            pltpu.SemaphoreType.DMA((2,)),
            pltpu.SemaphoreType.DMA((2,)),
            pltpu.SemaphoreType.DMA((count,)),
            pltpu.SemaphoreType.DMA((count,)),
        ],
        compiler_params=params(3),
        name="run_backward",
    )(*kept, *keeps, mix)


def finish_kernel(
    group_size,
    output_in,
    input_grad_in,
    query_in,
    key_in,
    value_in,
    out_in,
    notes,
    query_ref,
    key_ref,
    gate_in,
    up_in,
    down_in,
    output,
    input_grad,
    grad_query,
    grad_key,
    grad_value,
    grad_out,
    gains,
    clipped_query,
    clipped_key,
    grad_gate,
    grad_up,
    grad_down,
    sems,
):
    pairs = ((gate_in, grad_gate), (up_in, grad_up), (down_in, grad_down))
    copies = [pltpu.make_async_copy(src, dst.at[0], sems.at[i]) for i, (src, dst) in enumerate(pairs)]
    for c in copies:
        c.start()
    output[...] = output_in[...]
    input_grad[...] = input_grad_in[...]
    grad_query[...] = query_in[...]
    grad_key[...] = key_in[...]
    grad_value[...] = value_in[...]
    grad_out[...] = out_in[...]
    total, peaks = notes[0], notes[0]
    for p in range(1, notes.shape[0]):
        total = total + notes[p]
        peaks = jnp.maximum(peaks, notes[p])
    gains[...] = total
    factor = CLIP_LIMIT / jnp.maximum(peaks, CLIP_LIMIT)
    root = jnp.sqrt(factor)
    lane = lax.broadcasted_iota(jnp.int32, (8, 128), 1)

    def scale(h):
        return jnp.max(jnp.where(lane == h, root, 0.0), axis=1, keepdims=True)[2:3, :]

    heads = query_ref.shape[1] // HEAD_SIZE
    wide = lax.broadcasted_iota(jnp.int32, (1, 128), 1)
    scales = [scale(h) for h in range(heads)]
    for j in range(heads // 2):
        row = jnp.where(wide < HEAD_SIZE, scales[2 * j], scales[2 * j + 1])
        cols = slice(128 * j, 128 * (j + 1))
        clipped_query[:, cols] = query_ref[:, cols].astype(F32) * row
    least = [
        functools.reduce(jnp.minimum, scales[group_size * g : group_size * (g + 1)])
        for g in range(heads // group_size)
    ]
    for j in range(len(least) // 2):
        row = jnp.where(wide < HEAD_SIZE, least[2 * j], least[2 * j + 1])
        cols = slice(128 * j, 128 * (j + 1))
        clipped_key[:, cols] = key_ref[:, cols].astype(F32) * row
    for c in copies:
        c.wait()


def finish(group_size, found, notes, query, key, expert_grads):
    shape = jax.ShapeDtypeStruct
    outs = [shape(x.shape, x.dtype) for x in found] + [
        shape((8, 128), F32),
        shape(query.shape, F32),
        shape(key.shape, F32),
    ]
    return pl.pallas_call(
        functools.partial(finish_kernel, group_size),
        out_shape=outs + [shape((1, *g.shape), F32) for g in expert_grads],
        in_specs=[IN_VMEM] * 9 + [ANY] * 3,
        out_specs=[IN_VMEM] * 9 + [ANY] * 3,
        scratch_shapes=[pltpu.SemaphoreType.DMA((3,))],
        compiler_params=pltpu.CompilerParams(vmem_limit_bytes=56 * 2**20),
        name="finish",
    )(*found, notes, query, key, *expert_grads)


def note_tiles(*rows):
    tiles = [jnp.pad(r.astype(F32), ((0, 0), (0, 128 - r.shape[1]))) for r in rows]
    tiles += [jnp.zeros_like(tiles[0])] * (8 - len(tiles))
    return jnp.stack(tiles, axis=1)


def on_device_dense(
    tokens,
    attn_norm_gain,
    w_query,
    key_projection,
    value_projection,
    w_out,
    moe_norm_gain,
    w_gate,
    w_up,
    w_down,
    router_logits,
    expert_ids,
    segment_ids,
    parents,
    cotangent,
):
    length, model_width = tokens.shape
    q_cols, kv_cols = w_query.shape[1], key_projection.shape[1]
    q_heads, kv_heads = q_cols // HEAD_SIZE, kv_cols // HEAD_SIZE
    group_size = q_heads // kv_heads
    count = lax.axis_size("dp")
    line = count // 4
    shard = attn_norm_gain.shape[0]
    logit_max = jnp.max(router_logits, axis=1, keepdims=True)
    logit_exp = jnp.exp(router_logits - logit_max)
    gate_probs = logit_exp / jnp.sum(logit_exp, axis=1, keepdims=True)
    expert_index = jnp.arange(count, dtype=jnp.int32)
    named = expert_ids[None, :, :] == expert_index[:, None, None]
    gate_rows = jnp.sum(jnp.where(named, gate_probs[None], 0.0), axis=2)
    own_gains = [jnp.broadcast_to(g[None], (count, shard)) for g in (attn_norm_gain, moe_norm_gain)]
    note = note_tiles(gate_rows, *own_gains)
    position, allowed = tree_layout(segment_ids[0], parents[0])
    cosine, sine = (jnp.tile(t[:, 0, :], (1, 4)) for t in rope_tables(position, HEAD_SIZE))
    first = (jnp.arange(128) % HEAD_SIZE < HEAD_SIZE // 2)[None, :]
    tables = jnp.stack([cosine, jnp.where(first, -sine, 0.0), jnp.where(first, 0.0, sine)])
    (moe_in, hidden, normed, head_out, queries, keys, values, probs, peak, gains, notes, *keeps, cots) = run_forward(
        line,
        group_size,
        tokens,
        w_query,
        key_projection,
        value_projection,
        w_out,
        cotangent,
        note,
        tables,
        allowed.astype(F32),
    )
    d_moe_in, mix_parts, *expert_grads = run_experts(
        line, moe_in, cots, notes, w_gate[0], w_up[0], w_down[0]
    )
    kept = (tokens, hidden, d_moe_in, cotangent, normed, head_out, queries, keys, values, probs, gains, peak, tables)
    input_grad, output, *grads, sums = run_backward(line, group_size, kept, keeps, mix_parts)
    output, input_grad, gq, gk, gv, go, gains, clipped_query, clipped_key, gg, gu, gd = finish(
        group_size, (output, input_grad, *grads), sums, w_query, key_projection, expert_grads
    )
    return (
        output,
        input_grad,
        gains[0, :shard],
        gq,
        gk,
        gv,
        go,
        gains[1, :shard],
        gg,
        gu,
        gd,
        clipped_query,
        clipped_key,
    )


DENSE_BYTES = 8 * 2**20


def on_device(*args):
    tokens, w_gate = args[0], args[7]
    count, ranks = lax.axis_size("dp"), lax.axis_size("tensor")
    rows_bytes = count * tokens.shape[0] * tokens.shape[1] * 2
    whole_experts = w_gate.shape[2] * ranks == FFE
    dense = whole_experts and ranks == 2 and count % 8 == 0 and rows_bytes <= DENSE_BYTES
    return on_device_dense(*args) if dense else on_device_general(*args)


def solution(mesh):
    in_specs = (
        P("dp", None),
        P("dp"),
        P("dp", "tensor"),
        P("dp", "tensor"),
        P("dp", "tensor"),
        P("dp", "tensor"),
        P("dp"),
        P("dp", None, "tensor"),
        P("dp", None, "tensor"),
        P("dp", None, "tensor"),
        P("dp", None),
        P("dp", None),
        P("dp", None),
        P("dp", None),
        P("dp", None),
    )
    out_specs = (
        P("dp", None),
        P("dp", None),
        P("dp"),
        P("dp", "tensor"),
        P("dp", "tensor"),
        P("dp", "tensor"),
        P("dp", "tensor"),
        P("dp"),
        P("dp", None, "tensor"),
        P("dp", None, "tensor"),
        P("dp", None, "tensor"),
        P("dp", "tensor"),
        P("dp", "tensor"),
    )
    return jax.shard_map(
        on_device, mesh=mesh, in_specs=in_specs, out_specs=out_specs, check_vma=False
    )
```

```python
import functools

import jax
import jax.numpy as jnp
from jax import lax
from jax.experimental import pallas as pl
from jax.experimental.pallas import tpu as pltpu
from jax.sharding import PartitionSpec as P

HEAD_SIZE = 64
FFE = 512
TOP = 8


EPSILON = 1e-06
SCORE_SCALE = 1.0 / 64.0
RESIDUAL = 0.22
THETA = 10000.0
CLIP_LIMIT = 2.0
NEGATIVE = -1e30


def tree_layout(seg_row, par_row):
    tree_length = seg_row.shape[0]
    seg_count = par_row.shape[0]
    seg_index = jnp.arange(seg_count, dtype=jnp.int32)
    member = (seg_row[:, None] == seg_index[None, :]).astype(jnp.int32)
    seg_len = jnp.sum(member, axis=0)
    seg_start = jnp.sum(jnp.where(seg_index[:, None] > seg_index[None, :], seg_len[None, :], 0), axis=1)
    parent_hot = (par_row[:, None] == seg_index[None, :]).astype(jnp.int32)
    grand_parent = jnp.sum(parent_hot * par_row[None, :], axis=1)
    grand_hot = (grand_parent[:, None] == seg_index[None, :]).astype(jnp.int32)
    parent_len = jnp.sum(parent_hot * seg_len[None, :], axis=1)
    grand_len = jnp.sum(grand_hot * seg_len[None, :], axis=1)
    offset = jnp.where(seg_index != 0, parent_len, 0) + jnp.where(par_row != 0, grand_len, 0)
    tok_start = jnp.sum(member * seg_start[None, :], axis=1)
    tok_offset = jnp.sum(member * offset[None, :], axis=1)
    places = jnp.arange(tree_length, dtype=jnp.int32)
    position = (places - tok_start + tok_offset).astype(jnp.float32)
    identity = (seg_index[:, None] == seg_index[None, :]).astype(jnp.int32)
    ancestor = jnp.minimum(identity + parent_hot + grand_hot, 1)
    reached = jnp.dot(member, ancestor)
    linked = jnp.dot(reached, member.T) > 0
    allowed = linked & (places[None, :] <= places[:, None])
    return (position, allowed)


def rope_tables(position, head_dim):
    half_dim = head_dim // 2
    frequency = THETA ** (-2.0 * jnp.arange(half_dim, dtype=jnp.float32) / head_dim)
    angles = position[:, None] * frequency[None, :]
    return (jnp.cos(angles)[:, None, :], jnp.sin(angles)[:, None, :])


def apply_rotary(values_in, cosine_table, sine_values):
    half_dim = values_in.shape[-1] // 2
    first_half = values_in[..., :half_dim]
    second_half = values_in[..., half_dim:]
    return jnp.concatenate(
        [
            first_half * cosine_table - second_half * sine_values,
            second_half * cosine_table + first_half * sine_values,
        ],
        axis=-1,
    )


def rotate_back(grads_in, cosine_table, sine_values):
    half_dim = grads_in.shape[-1] // 2
    first_half = grads_in[..., :half_dim]
    second_half = grads_in[..., half_dim:]
    return jnp.concatenate(
        [
            first_half * cosine_table + second_half * sine_values,
            second_half * cosine_table - first_half * sine_values,
        ],
        axis=-1,
    )


def slot_tables(routes, experts, capacity):
    flat_ids = routes.reshape(-1)
    row_count = flat_ids.shape[0]
    member = (flat_ids[:, None] == jnp.arange(experts, dtype=jnp.int32)[None, :]).astype(jnp.int32)
    row_total = flat_ids.shape[0]
    before = jnp.dot((jnp.arange(row_total)[:, None] > jnp.arange(row_total)[None, :]).astype(jnp.float32), member.astype(jnp.float32), precision=lax.Precision.HIGHEST).astype(jnp.int32)
    slot_index = jnp.sum(before * member, axis=1)
    target = flat_ids * capacity + slot_index
    source = (
        jnp.full((experts * capacity,), -1, jnp.int32)
        .at[target]
        .set(jnp.arange(row_count, dtype=jnp.int32))
    )
    return (flat_ids, slot_index, source)


def contract_rows(left, right):
    return lax.dot_general(
        left, right, (((0,), (0,)), ((), ())), preferred_element_type=jnp.float32
    )


def contract_cols(left, right):
    return lax.dot_general(
        left, right, (((1,), (1,)), ((), ())), preferred_element_type=jnp.float32
    )


def expert_forward(inputs, gate_w, up_w, down_w):
    gate_pre = jnp.dot(inputs, gate_w, preferred_element_type=jnp.float32)
    up_pre = jnp.dot(inputs, up_w, preferred_element_type=jnp.float32)
    active = (gate_pre / (1.0 + jnp.exp(-gate_pre)) * up_pre).astype(jnp.bfloat16)
    return (contract_cols(active, down_w), (gate_pre, up_pre, active))


def expert_backward(inputs, grads_out, gate_w, up_w, down_w, kept_acts):
    gate_pre, up_pre, active = kept_acts
    d_active = jnp.dot(grads_out, down_w, preferred_element_type=jnp.float32)
    grad_down = contract_rows(grads_out, active)
    sigmoid_val = 1.0 / (1.0 + jnp.exp(-gate_pre))
    d_gate = (d_active * up_pre * sigmoid_val * (1.0 + gate_pre * (1.0 - sigmoid_val))).astype(
        jnp.bfloat16
    )
    d_up = (d_active * gate_pre * sigmoid_val).astype(jnp.bfloat16)
    grad_gate = contract_rows(inputs, d_gate)
    grad_up = contract_rows(inputs, d_up)
    d_inputs = contract_cols(d_gate, gate_w) + contract_cols(d_up, up_w)
    return (d_inputs, grad_gate, grad_up, grad_down)


def send_rows(rows_in):
    return lax.all_to_all(rows_in, "dp", split_axis=0, concat_axis=0, tiled=True)


def return_rows(rows_in):
    return lax.all_to_all(
        rows_in.astype(jnp.bfloat16), "dp", split_axis=0, concat_axis=0, tiled=True
    ).astype(rows_in.dtype)


def send_grads(rows_in):
    return lax.all_to_all(rows_in, "dp", split_axis=0, concat_axis=0, tiled=True)


def return_grads(rows_in):
    return lax.all_to_all(
        rows_in.astype(jnp.bfloat16), "dp", split_axis=0, concat_axis=0, tiled=True
    ).astype(rows_in.dtype)


def share_slots(partial_rows):
    return lax.psum_scatter(partial_rows, "tensor", scatter_dimension=1, tiled=True)


def on_device_general(
    tokens,
    attn_norm_gain,
    w_query,
    key_projection,
    value_projection,
    w_out,
    moe_norm_gain,
    w_gate,
    w_up,
    w_down,
    router_logits,
    expert_ids,
    segment_ids,
    parents,
    cotangent,
):
    length = tokens.shape[0]
    model_width = tokens.shape[1]
    q_cols = w_query.shape[1]
    kv_cols = key_projection.shape[1]
    q_heads = q_cols // HEAD_SIZE
    kv_heads = kv_cols // HEAD_SIZE
    group_size = q_heads // kv_heads
    dp_size = lax.axis_size("dp")
    tensor_ranks = lax.axis_size("tensor")
    replicas = FFE // (w_gate.shape[2] * tensor_ranks)
    experts = dp_size // replicas
    capacity = 4 * (9 * length * TOP // (32 * experts))
    share_rows = capacity // tensor_ranks
    first_slot = lax.axis_index("tensor") * share_rows
    block_rows = min(length, 512)
    attn_gain, moe_gain, query_w, key_weight, value_weight, out_w = (
        lax.all_gather(attn_norm_gain, "dp", axis=0, tiled=True),
        lax.all_gather(moe_norm_gain, "dp", axis=0, tiled=True),
        lax.all_gather(w_query, "dp", axis=0, tiled=True),
        lax.all_gather(key_projection, "dp", axis=0, tiled=True),
        lax.all_gather(value_projection, "dp", axis=0, tiled=True),
        lax.all_gather(w_out, "dp", axis=0, tiled=True),
    )
    attn_gain_f = attn_gain.astype(jnp.float32)
    moe_gain_f = moe_gain.astype(jnp.float32)
    inputs = tokens.astype(jnp.float32)
    inv_attn = lax.rsqrt(jnp.mean(inputs * inputs, axis=1, keepdims=True) + EPSILON)
    unit_attn = inputs * inv_attn
    normalized_rows = (unit_attn * attn_gain_f).astype(jnp.bfloat16)
    position, allowed = tree_layout(segment_ids[0], parents[0])
    cosine_table, sine_values = rope_tables(position, HEAD_SIZE)
    query_linear = jnp.dot(normalized_rows, query_w, preferred_element_type=jnp.float32).reshape(
        length, q_heads, HEAD_SIZE
    )
    key_linear = jnp.dot(normalized_rows, key_weight, preferred_element_type=jnp.float32).reshape(
        length, kv_heads, HEAD_SIZE
    )
    query_heads = (
        apply_rotary(query_linear, cosine_table, sine_values)
        .astype(jnp.bfloat16)
        .reshape(length, kv_heads, group_size, HEAD_SIZE)
    )
    key_heads = apply_rotary(key_linear, cosine_table, sine_values).astype(jnp.bfloat16)
    value_heads = (
        jnp.dot(normalized_rows, value_weight, preferred_element_type=jnp.float32)
        .astype(jnp.bfloat16)
        .reshape(length, kv_heads, HEAD_SIZE)
    )
    q_block = query_heads
    mask_rows = allowed[None, None]
    scores = (
        jnp.einsum("qhgd,khd->hgqk", q_block, key_heads, preferred_element_type=jnp.float32)
        * SCORE_SCALE
    )
    scores = jnp.where(mask_rows, scores, NEGATIVE)
    peak_parts = [jnp.max(scores, axis=(2, 3))]
    row_max = jnp.max(scores, axis=3, keepdims=True)
    expo = jnp.exp(scores - row_max)
    row_total = jnp.sum(expo, axis=3, keepdims=True)
    lse_parts = [row_max + jnp.log(row_total)]
    prob_low = (expo / row_total).astype(jnp.bfloat16)
    block_outs = jnp.einsum(
        "hgqk,khd->qhgd", prob_low, value_heads, preferred_element_type=jnp.float32
    )
    head_out = block_outs.reshape(length, q_cols).astype(jnp.bfloat16)
    attn_mix = lax.psum(contract_cols(head_out, out_w), "tensor")
    hidden = inputs + RESIDUAL * attn_mix
    head_peak = lax.pmax(jnp.max(jnp.stack(peak_parts), axis=0).reshape(q_heads), "dp")
    inv_moe = lax.rsqrt(jnp.mean(hidden * hidden, axis=1, keepdims=True) + EPSILON)
    unit_moe = hidden * inv_moe
    moe_in = (unit_moe * moe_gain_f).astype(jnp.bfloat16)
    logit_max = jnp.max(router_logits, axis=1, keepdims=True)
    logit_exp = jnp.exp(router_logits - logit_max)
    gate_probs = logit_exp / jnp.sum(logit_exp, axis=1, keepdims=True)
    flat_ids, slot_index, source = slot_tables(expert_ids, experts, capacity)
    filled = source >= 0
    source_row = jnp.maximum(source, 0)
    source_token = source_row // TOP
    dispatch_rows = jnp.where(
        filled[:, None], moe_in[source_token], jnp.zeros((), jnp.bfloat16)
    ).reshape(experts, capacity, model_width)
    arrived = send_rows(jnp.repeat(dispatch_rows, replicas, axis=0))
    gate_w, up_w, down_w = (w_gate[0], w_up[0], w_down[0])
    expert_in = arrived.reshape(dp_size * capacity, model_width)
    expert_out, kept_acts = expert_forward(expert_in, gate_w, up_w, down_w)
    partial_out = share_slots(expert_out.reshape(dp_size, capacity, model_width))
    back_parts = return_rows(partial_out).reshape(experts, replicas, share_rows, model_width)
    back_rows = (
        jnp.sum(back_parts, axis=1).astype(jnp.bfloat16).reshape(experts * share_rows, model_width)
    )
    own_slot = ((slot_index >= first_slot) & (slot_index < first_slot + share_rows)).reshape(
        length, TOP
    )
    local_index = (
        flat_ids * share_rows + jnp.clip(slot_index - first_slot, 0, share_rows - 1)
    ).reshape(length, TOP)
    mix_part = jnp.zeros((length, model_width), jnp.float32)
    for column in range(TOP):
        gate_weight = jnp.where(own_slot[:, column], gate_probs[:, column], 0.0)
        mix_part = mix_part + gate_weight[:, None] * back_rows[local_index[:, column]].astype(
            jnp.float32
        )
    expert_mix = lax.psum(mix_part.astype(jnp.bfloat16), "tensor").astype(jnp.float32)
    output = (hidden + RESIDUAL * expert_mix).astype(jnp.bfloat16)
    grad_output = cotangent.astype(jnp.float32)
    mix_grad = RESIDUAL * grad_output
    row_gate = gate_probs.reshape(-1)[source_row]
    grad_rows = (
        jnp.where(filled[:, None], row_gate[:, None] * mix_grad[source_token], 0.0)
        .astype(jnp.bfloat16)
        .reshape(experts, capacity, model_width)
    )
    grad_arrived = send_grads(jnp.repeat(grad_rows, replicas, axis=0)).reshape(
        dp_size * capacity, model_width
    )
    d_inputs, grad_gate, grad_up, grad_down = expert_backward(
        expert_in, grad_arrived, gate_w, up_w, down_w, kept_acts
    )
    d_back = share_slots(d_inputs.reshape(dp_size, capacity, model_width))
    grad_gate, grad_up, grad_down = (grad_gate[None], grad_up[None], grad_down[None])
    d_parts = return_grads(d_back).reshape(experts, replicas, share_rows, model_width)
    d_returned = (
        jnp.sum(d_parts, axis=1).astype(jnp.bfloat16).reshape(experts * share_rows, model_width)
    )
    d_mix_part = jnp.zeros((length, model_width), jnp.float32)
    for column in range(TOP):
        d_mix_part = d_mix_part + jnp.where(
            own_slot[:, column][:, None],
            d_returned[local_index[:, column]].astype(jnp.float32),
            0.0,
        )
    d_moe_in = lax.psum(d_mix_part, "tensor")
    scaled_moe = d_moe_in * moe_gain_f
    grad_moe_gain = jnp.sum(d_moe_in * unit_moe, axis=0)
    d_hidden = grad_output + inv_moe * (
        scaled_moe - unit_moe * jnp.mean(scaled_moe * unit_moe, axis=1, keepdims=True)
    )
    d_attn = (RESIDUAL * d_hidden).astype(jnp.bfloat16)
    grad_out_w = contract_rows(d_attn, head_out)
    d_heads = (
        jnp.dot(d_attn, out_w, preferred_element_type=jnp.float32)
        .astype(jnp.bfloat16)
        .reshape(length, kv_heads, group_size, HEAD_SIZE)
    )
    d_query_parts = []
    d_key = jnp.zeros((length, kv_heads, HEAD_SIZE), jnp.float32)
    d_value = jnp.zeros((length, kv_heads, HEAD_SIZE), jnp.float32)
    for block_number, row_begin in enumerate(range(0, length, block_rows)):
        q_block = query_heads
        mask_rows = allowed[None, None]
        scores = (
            jnp.einsum("qhgd,khd->hgqk", q_block, key_heads, preferred_element_type=jnp.float32)
            * SCORE_SCALE
        )
        scores = jnp.where(mask_rows, scores, NEGATIVE)
        prob_full = jnp.exp(scores - lse_parts[block_number])
        prob_low = prob_full.astype(jnp.bfloat16)
        d_value = jnp.einsum(
            "hgqk,qhgd->khd", prob_low, d_heads, preferred_element_type=jnp.float32
        )
        d_prob = jnp.einsum(
            "qhgd,khd->hgqk", d_heads, value_heads, preferred_element_type=jnp.float32
        )
        inner = jnp.sum(prob_full * d_prob, axis=3, keepdims=True)
        d_scores = (prob_full * (d_prob - inner)).astype(jnp.bfloat16)
        d_query_parts.append(
            jnp.einsum("hgqk,khd->qhgd", d_scores, key_heads, preferred_element_type=jnp.float32)
            * SCORE_SCALE
        )
        d_key = (
            jnp.einsum("hgqk,qhgd->khd", d_scores, q_block, preferred_element_type=jnp.float32)
            * SCORE_SCALE
        )
    d_query_all = d_query_parts[0].reshape(length, q_heads, HEAD_SIZE)
    d_query_lin = (
        rotate_back(d_query_all, cosine_table, sine_values)
        .astype(jnp.bfloat16)
        .reshape(length, q_cols)
    )
    d_key_lin = (
        rotate_back(d_key, cosine_table, sine_values).astype(jnp.bfloat16).reshape(length, kv_cols)
    )
    d_value_lin = d_value.astype(jnp.bfloat16).reshape(length, kv_cols)
    grad_query_w = contract_rows(normalized_rows, d_query_lin)
    grad_key_w = contract_rows(normalized_rows, d_key_lin)
    grad_value_w = contract_rows(normalized_rows, d_value_lin)
    d_normed_part = (
        contract_cols(d_query_lin, query_w)
        + contract_cols(d_key_lin, key_weight)
        + contract_cols(d_value_lin, value_weight)
    )
    d_normed = lax.psum(d_normed_part.astype(jnp.bfloat16), "tensor").astype(jnp.float32)
    scaled_attn = d_normed * attn_gain_f
    grad_attn_gain = jnp.sum(d_normed * unit_attn, axis=0)
    input_grad = d_hidden + inv_attn * (
        scaled_attn - unit_attn * jnp.mean(scaled_attn * unit_attn, axis=1, keepdims=True)
    )
    reduced = (
        lax.psum_scatter(grad_attn_gain, "dp", scatter_dimension=0, tiled=True),
        lax.psum_scatter(grad_moe_gain, "dp", scatter_dimension=0, tiled=True),
        lax.psum_scatter(grad_query_w, "dp", scatter_dimension=0, tiled=True),
        lax.psum_scatter(grad_key_w, "dp", scatter_dimension=0, tiled=True),
        lax.psum_scatter(grad_value_w, "dp", scatter_dimension=0, tiled=True),
        lax.psum_scatter(grad_out_w, "dp", scatter_dimension=0, tiled=True),
    )
    scale_factor = CLIP_LIMIT / jnp.maximum(head_peak, CLIP_LIMIT)
    query_scale = jnp.repeat(jnp.sqrt(scale_factor), HEAD_SIZE)
    key_clip_scale = jnp.repeat(
        jnp.sqrt(jnp.min(scale_factor.reshape(kv_heads, group_size), axis=1)), HEAD_SIZE
    )
    clipped_query = w_query.astype(jnp.float32) * query_scale[None, :]
    clipped_key = key_projection.astype(jnp.float32) * key_clip_scale[None, :]
    return (
        output,
        input_grad,
        reduced[0],
        reduced[2],
        reduced[3],
        reduced[4],
        reduced[5],
        reduced[1],
        grad_gate,
        grad_up,
        grad_down,
        clipped_query,
        clipped_key,
    )


MESH_IDS = pl.DeviceIdType.MESH
F32 = jnp.float32
BF16 = jnp.bfloat16


class Place:
    def __init__(self, line):
        self.line = line
        self.count = 4 * line
        me = lax.axis_index("dp")
        self.core = lax.axis_index("tensor")
        self.me = me
        self.z = me // 4
        y, x = (me // 2) % 2, me % 2
        self.step_a, self.step_b = 2 - self.core, 1 + self.core
        self.a = y * (1 - self.core) + x * self.core
        self.b = x * (1 - self.core) + y * self.core

    def part(self, z, a, b):
        return z * 4 + a * self.step_a + b * self.step_b

    def up(self):
        return (self.me + 4, self.core)

    def down(self):
        return (self.me - 4, self.core)

    def beside_a(self):
        return (self.me + self.step_a * (1 - 2 * self.a), self.core)

    def beside_b(self):
        return (self.me + self.step_b * (1 - 2 * self.b), self.core)

    def twin(self):
        return (self.me, 1 - self.core)

    def peer(self, offset):
        return lax.rem(self.me + offset, self.count)


def enter(place):
    barrier = pltpu.get_barrier_semaphore()

    def greet(offset, carry):
        pl.semaphore_signal(
            barrier, inc=1, device_id=(place.peer(offset), place.core), device_id_type=MESH_IDS
        )
        return carry

    lax.fori_loop(1, place.count, greet, 0)
    pl.semaphore_signal(barrier, inc=1, device_id=place.twin(), device_id_type=MESH_IDS)
    pl.semaphore_wait(barrier, place.count)


def remote(src, dst, send_sem, recv_sem, device):
    return pltpu.make_async_remote_copy(
        src_ref=src,
        dst_ref=dst,
        send_sem=send_sem,
        recv_sem=recv_sem,
        device_id=device,
        device_id_type=MESH_IDS,
    )


class Notes:
    def __init__(self, place, src, dst, send_sem, recv_sem, alike):
        self.place, self.src, self.dst = place, src, dst
        self.send_sem, self.recv_sem, self.alike = send_sem, recv_sem, alike

    def _copy(self, offset, source):
        place = self.place
        to = place.peer(offset)
        return remote(
            self.src if self.alike else self.src.at[to],
            self.dst.at[source],
            self.send_sem.at[offset],
            self.recv_sem.at[source],
            (to, place.core),
        )

    def start(self):
        def send(offset, carry):
            self._copy(offset, self.place.me).start()
            return carry

        lax.fori_loop(1, self.place.count, send, 0)
        me = self.place.me
        self.dst[me] = self.src[...] if self.alike else self.src[me]

    def finish(self):
        def settle(offset, carry):
            self._copy(offset, self.place.peer(offset)).wait_recv()
            self._copy(offset, self.place.me).wait_send()
            return carry

        lax.fori_loop(1, self.place.count, settle, 0)


class Gather:
    def __init__(self, place, view, send_sem, recv_sem, fixed=False):
        self.place, self.view, self.fixed = place, view, fixed
        self.send_sem, self.recv_sem = send_sem, recv_sem

    def _copy(self, source, target, sem, device):
        there = self.view(source if self.fixed else target)
        return remote(self.view(source), there, self.send_sem.at[sem], self.recv_sem.at[target], device)

    def _to_z(self, step):
        place = self.place
        own = place.z
        return self._copy(own, own, step + place.line - 1, (place.me + 4 * step, place.core))

    def _to_a(self, z):
        line = self.place.line
        return self._copy(z, line + z, 2 * line - 1 + z, self.place.beside_a())

    def _to_b(self, slot):
        line = self.place.line
        return self._copy(slot, 2 * line + slot, 3 * line - 1 + slot, self.place.beside_b())

    def take(self, slot):
        self._copy(slot, slot, 0, self.place.beside_b()).wait_recv()

    def near(self, step, action):
        place = self.place
        if step == 0:
            action(place.z)
        else:
            pl.when(place.z >= step)(lambda: action(place.z - step))
            pl.when(place.z + step < place.line)(lambda: action(place.z + step))

    def start(self):
        place = self.place

        def reach(step):
            pl.when(place.z >= step)(lambda: self._to_z(-step).start())
            pl.when(place.z + step < place.line)(lambda: self._to_z(step).start())

        reach(1)
        self._to_a(place.z).start()
        self._to_b(place.z).start()
        for step in range(2, place.line):
            reach(step)

    def along(self, step, then=None):
        def pass_on(z):
            self.take(z)
            self._to_a(z).start()
            self._to_b(z).start()
            if then is not None:
                then(z)

        self.near(step, pass_on)

    def across(self, step, then=None):
        line = self.place.line

        def pass_on(z):
            self.take(line + z)
            self._to_b(line + z).start()
            if then is not None:
                then(line + z)

        self.near(step, pass_on)

    def settle(self):
        place = self.place
        line = place.line

        def wait(z, carry):
            self._to_a(z).wait_send()
            self._to_b(z).wait_send()
            self._to_b(line + z).wait_send()
            pl.when(z != place.z)(lambda: self._to_z(z - place.z).wait_send())
            return carry

        lax.fori_loop(0, line, wait, 0)

    def take_rest(self):
        line = self.place.line

        def wait(k, carry):
            self.take(2 * line + k)
            return carry

        lax.fori_loop(0, 2 * line, wait, 0)


def gather_all(gathers, thens=None):
    line = gathers[0].place.line
    thens = thens or [None] * len(gathers)
    gathers[0].start()
    for i, (g, then) in enumerate(zip(gathers, thens)):
        for step in range(1, line + 1):
            if step < line:
                g.along(step, then)
            if step == line - 1 and i + 1 < len(gathers):
                gathers[i + 1].start()
            g.across(step - 1, then)


class Twin:
    def __init__(self, place, source, target, send_sem, recv_sem):
        self.place, self.source, self.target = place, source, target
        self.send_sem, self.recv_sem = send_sem, recv_sem

    def copy(self, slot):
        line = self.place.line
        group = slot // line
        there = slot + line * ((group % 2) - (group // 2))
        return remote(
            self.source(slot),
            self.target(there),
            self.send_sem.at[slot],
            self.recv_sem.at[there],
            self.place.twin(),
        )

    def start(self, slot):
        self.copy(slot).start()

    def take(self, slot):
        remote(
            self.source(slot),
            self.target(slot),
            self.send_sem.at[slot],
            self.recv_sem.at[slot],
            self.place.twin(),
        ).wait_recv()

    def wait_send(self, slot):
        self.copy(slot).wait_send()


class Reduce:
    def __init__(self, place, parts, from_b, from_a, from_z, send_sem, recv_sem, index=lambda slot: slot):
        self.place, self.parts, self.index = place, parts, index
        self.from_b, self.from_a, self.from_z = from_b, from_a, from_z
        self.send_sem, self.recv_sem = send_sem, recv_sem

    def _copy(self, source, target, sem, device):
        return remote(source, target, self.send_sem.at[sem], self.recv_sem.at[sem], device)

    def _to_b(self, k):
        line = self.place.line
        return self._copy(self.parts.at[self.index(2 * line + k)], self.from_b.at[k], k, self.place.beside_b())

    def _to_a(self, z):
        line = self.place.line
        block = self.parts.at[self.index(line + z)]
        return self._copy(block, self.from_a.at[z], 2 * line + z, self.place.beside_a())

    def _to_z(self, target):
        place, line = self.place, self.place.line
        return remote(
            self.parts.at[self.index(target)],
            self.from_z.at[place.z],
            self.send_sem.at[3 * line + target],
            self.recv_sem.at[3 * line + place.z],
            (place.me + 4 * (target - place.z), place.core),
        )

    def _add(self, slot, block):
        at = self.index(slot)
        self.parts[at] = (self.parts[at].astype(F32) + block.astype(F32)).astype(BF16)

    def send_b(self, k):
        self._to_b(k).start()

    def fold_b(self, k):
        self._to_b(k).wait_recv()
        self._add(k, self.from_b[k])

    def send_a(self, z):
        self._to_a(z).start()

    def fold_a(self, z):
        self._to_a(z).wait_recv()
        self._add(z, self.from_a[z])

    def send_line(self):
        place = self.place
        for z in ends_first(place.line):
            pl.when(place.z != z)(lambda z=z: self._to_z(z).start())

    def fold_line_a(self):
        line = self.place.line
        for z in ends_first(line):
            self.fold_b(line + z)
            self.send_a(z)

    def fold_line_own(self):
        for z in ends_first(self.place.line):
            self.fold_b(z)

    def finish_line(self):
        for z in ends_first(self.place.line):
            self.fold_a(z)
        self.send_line()

    def result(self, out):
        place, line = self.place, self.place.line
        out[...] = self.parts[self.index(place.z)].astype(F32)

        def add(z, carry):
            @pl.when(z != place.z)
            def _():
                remote(
                    self.from_z.at[z], self.from_z.at[z], self.send_sem.at[0], self.recv_sem.at[3 * line + z], place.up()
                ).wait_recv()
                out[...] += self.from_z[z].astype(F32)

            return carry

        lax.fori_loop(0, line, add, 0)

    def settle(self):
        place, line = self.place, self.place.line

        def wait(z, carry):
            self._to_b(z).wait_send()
            self._to_b(line + z).wait_send()
            self._to_a(z).wait_send()
            pl.when(place.z != z)(lambda: self._to_z(z).wait_send())
            return carry

        lax.fori_loop(0, line, wait, 0)


AHEAD = 4


class Reductions:
    def __init__(self, reduces, finish):
        self.reduces, self.finish, self.at = reduces, finish, 0
        line = self.line = reduces[0].place.line
        self.ks = [line + z for z in ends_first(line)] + ends_first(line)
        self.steps = [(i, k) for i in range(len(reduces)) for k in self.ks]

    def start(self):
        for i, k in self.steps[:AHEAD]:
            self.reduces[i].send_b(k)

    def run(self, number):
        for _ in range(number):
            self._step()

    def _step(self):
        if self.at + AHEAD < len(self.steps):
            ahead, block = self.steps[self.at + AHEAD]
            self.reduces[ahead].send_b(block)
        i, k = self.steps[self.at]
        self.at += 1
        self.reduces[i].fold_b(k)
        if k >= self.line:
            self.reduces[i].send_a(k - self.line)
        if k == self.ks[self.line - 1] and i > 0:
            self.reduces[i - 1].finish_line()
        if k == self.ks[-1] and i > 0:
            self.finish(i - 1)

    def complete(self):
        self.run(len(self.steps) - self.at)
        self.reduces[-1].finish_line()
        self.finish(len(self.reduces) - 1)


def reduce_scratch(line, block):
    return [
        pltpu.VMEM((2 * line, *block), BF16),
        pltpu.VMEM((line, *block), BF16),
        pltpu.VMEM((line, *block), BF16),
        pltpu.SemaphoreType.DMA((4 * line,)),
        pltpu.SemaphoreType.DMA((4 * line,)),
    ]


def ends_first(line):
    order = []
    for i in range((line + 1) // 2):
        order += [i] if i == line - 1 - i else [i, line - 1 - i]
    return order


def part_of(place, slot):
    line = place.line
    group, z = slot // line, slot % line
    flip_a, flip_b = group % 2, group // 2
    a = place.a + flip_a * (1 - 2 * place.a)
    b = place.b + flip_b * (1 - 2 * place.b)
    return place.part(z, a, b)


def halves(place, width):
    half = width // 2
    mine = pl.ds(pl.multiple_of(place.core * half, 128), half)
    theirs = pl.ds(pl.multiple_of((1 - place.core) * half, 128), half)
    return mine, theirs


def place_half(chunk, have, want, lane):
    chunk = chunk if have == want else pltpu.roll(chunk, HEAD_SIZE, 1)
    return jnp.where(lane // HEAD_SIZE == want, chunk, 0.0)


def rope_chunk(chunk, tables, sign):
    ahead = pltpu.roll(chunk, 128 - HEAD_SIZE // 2, 1)
    behind = pltpu.roll(chunk, HEAD_SIZE // 2, 1)
    return chunk * tables[0] + sign * (ahead * tables[1] + behind * tables[2])


def chunk_of(ref, j):
    return ref[:, 128 * j : 128 * (j + 1)]


def pair_of(ref, j, group_size, lane):
    both = []
    for half in (0, 1):
        group = (2 * j + half) // group_size
        both.append(place_half(chunk_of(ref, group // 2).astype(F32), group % 2, half, lane))
    return jnp.concatenate(both, axis=0).astype(BF16)


def spread_gains(notes, shard, width):
    total = jnp.zeros((8, width), F32)
    for p in range(notes.shape[0]):
        row = jnp.concatenate([notes[p], jnp.zeros((8, width - 128), F32)], axis=1)
        total += pltpu.roll(row, shard * p, 1) if p else row
    return total


def gate_table(logits, ids):
    expo = jnp.exp(logits - jnp.max(logits, axis=1, keepdims=True))
    probs = expo / jnp.sum(expo, axis=1, keepdims=True)
    length, top = logits.shape
    expert = lax.broadcasted_iota(jnp.int32, (length, 128), 1)
    table = jnp.zeros((length, 128), F32)
    for c in range(top):
        table += jnp.where(ids[:, c : c + 1] == expert, probs[:, c : c + 1], 0.0)
    return jnp.transpose(table)


def write_notes(note_ref, gates, gains):
    shard = gains[0].shape[1]
    row = lax.broadcasted_iota(jnp.int32, (8, 128), 0)
    pad = jnp.zeros((1, 128 - shard), F32)
    below = jnp.zeros((8, 128), F32)
    for i, gain in enumerate(gains):
        below = jnp.where(row == i + 1, jnp.concatenate([gain, pad], axis=1), below)
    for p in range(note_ref.shape[0]):
        note_ref[p] = jnp.where(row == 0, gates[p : p + 1, :], below)


def tree_tables(segments, parents, length):
    row = lax.broadcasted_iota(jnp.int32, (length, length), 0)
    lane = lax.broadcasted_iota(jnp.int32, (length, length), 1)

    def total(x):
        return jnp.sum(x.astype(F32), axis=1, keepdims=True)

    own_row = segments.astype(F32)
    own = total(jnp.where(row == lane, own_row, 0.0))
    kinds = parents.shape[1]
    kind = lax.broadcasted_iota(jnp.int32, (length, kinds), 1).astype(F32)
    above = parents.astype(F32)
    parent = total(jnp.where(kind == own, above, 0.0))
    grand = total(jnp.where(kind == parent, above, 0.0))
    in_parent, in_grand = own_row == parent, own_row == grand
    start = total(jnp.where(own_row < own, 1.0, 0.0))
    offset = jnp.where(own != 0.0, total(jnp.where(in_parent, 1.0, 0.0)), 0.0)
    offset += jnp.where(parent != 0.0, total(jnp.where(in_grand, 1.0, 0.0)), 0.0)
    place = lax.broadcasted_iota(jnp.int32, (length, 1), 0).astype(F32)
    linked = jnp.logical_or(own_row == own, jnp.logical_or(in_parent, in_grand))
    return place - start + offset, jnp.logical_and(linked, lane <= row)


def write_tables(tables_ref, position):
    lane = lax.broadcasted_iota(jnp.int32, (1, 128), 1)
    half = HEAD_SIZE // 2
    frequency = THETA ** ((lane % half).astype(F32) * (-2.0 / HEAD_SIZE))
    angles = position * frequency
    sine = jnp.sin(angles)
    first = lane % HEAD_SIZE < half
    tables_ref[0] = jnp.cos(angles)
    tables_ref[1] = jnp.where(first, -sine, 0.0)
    tables_ref[2] = jnp.where(first, 0.0, sine)


def forward_kernel(
    line,
    group_size,
    tokens_ref,
    query_ref,
    key_ref,
    value_ref,
    out_ref,
    cot_ref,
    gain_a_ref,
    gain_m_ref,
    logits_ref,
    ids_ref,
    segments_ref,
    parents_ref,
    moe_in_ref,
    hidden_ref,
    normed_ref,
    head_out_ref,
    queries_ref,
    keys_ref,
    values_ref,
    probs_ref,
    peak_ref,
    tables_ref,
    gains_ref,
    notes,
    query_keep,
    key_keep,
    value_keep,
    out_keep,
    cot_keep,
    query_all,
    key_all,
    value_all,
    out_all,
    cot_all,
    mix_mine,
    mix_other,
    note_ref,
    sends,
    recvs,
    note_send,
    note_recv,
    twin_sems,
    local_sems,
    keep_sems,
    mix_sems,
):
    place = Place(line)
    count = 4 * line
    length, width = tokens_ref.shape
    shard, q_cols = query_ref.shape
    chunks = q_cols // 128
    span, _ = halves(place, width)
    own = []
    blocks = ((query_ref, query_all), (key_ref, key_all), (value_ref, value_all), (out_ref, out_all))
    for i, (src, dst) in enumerate(blocks):
        own.append(pltpu.make_async_copy(src, dst.at[place.me], local_sems.at[i]))
    own.append(pltpu.make_async_copy(cot_ref, cot_all.at[place.z], local_sems.at[4]))
    for c in own:
        c.start()
    enter(place)
    note = Notes(place, note_ref, notes, note_send, note_recv, False)
    for c in own:
        c.wait()
    gathers = [
        Gather(place, lambda s, ref=ref: ref.at[part_of(place, s)], sends.at[i], recvs.at[i], True)
        for i, ref in enumerate((query_all, key_all, value_all, out_all))
    ]
    cot_view = lambda s: cot_all.at[s, :, span]
    cot = Gather(place, cot_view, sends.at[4], recvs.at[4])
    twin = Twin(place, cot_view, cot_view, twin_sems.at[0], twin_sems.at[1])
    out = gathers[3]
    for g in gathers[:3]:
        g.start()
    gains = [g[...].astype(F32) for g in (gain_a_ref, gain_m_ref)]
    write_notes(note_ref, gate_table(logits_ref[...], ids_ref[...]), gains)
    note.start()
    inputs = tokens_ref[...].astype(F32)
    inv_attn = lax.rsqrt(jnp.mean(inputs * inputs, axis=1, keepdims=True) + EPSILON)
    for g in gathers[:3]:
        g.along(1)
    note.finish()
    gains_ref[...] = spread_gains(notes, shard, width)
    normed_ref[...] = (inputs * inv_attn * gains_ref[1:2, :]).astype(BF16)
    for g in gathers[:3]:
        g.across(0)
    position, allowed = tree_tables(segments_ref[...], parents_ref[...], length)
    write_tables(tables_ref, position)
    for step in range(2, line + 1):
        for g in gathers[:3]:
            if step < line:
                g.along(step)
            g.across(step - 1)
        if step == line - 1:
            out.start()
    for g in gathers[:3]:
        g.take_rest()
    normed = normed_ref[...]
    tables = [tables_ref[i] for i in range(3)]
    query_lin = jnp.dot(normed, query_all[...].reshape(width, q_cols), preferred_element_type=F32)
    for j in range(chunks):
        queries_ref[:, 128 * j : 128 * (j + 1)] = rope_chunk(
            query_lin[:, 128 * j : 128 * (j + 1)], tables, 1.0
        ).astype(BF16)
    out.along(1)
    out.across(0)
    kv_cols = key_ref.shape[1]
    key_lin = jnp.dot(normed, key_all[...].reshape(width, kv_cols), preferred_element_type=F32)
    for j in range(kv_cols // 128):
        keys_ref[:, 128 * j : 128 * (j + 1)] = rope_chunk(
            key_lin[:, 128 * j : 128 * (j + 1)], tables, 1.0
        ).astype(BF16)
    values_ref[...] = jnp.dot(
        normed, value_all[...].reshape(width, kv_cols), preferred_element_type=F32
    ).astype(BF16)
    lane = lax.broadcasted_iota(jnp.int32, (length, 128), 1)
    small_lane = lax.broadcasted_iota(jnp.int32, (8, 128), 1)
    peaks = jnp.zeros((8, 128), F32)
    between = {
        0: lambda: (out.along(2), out.across(1)),
        1: lambda: out.along(3) if line > 3 else None,
        2: lambda: (cot.start(), out.across(2)),
        3: lambda: out.across(3) if line > 3 else None,
    }
    for j in range(chunks):
        both = contract_cols(chunk_of(queries_ref, j), pair_of(keys_ref, j, group_size, lane)) * SCORE_SCALE
        low = []
        for half in (0, 1):
            scores = jnp.where(allowed, both[:, length * half : length * (half + 1)], NEGATIVE)
            row_max = jnp.max(scores, axis=1, keepdims=True)
            peak = jnp.max(row_max, axis=0, keepdims=True)
            peaks = jnp.where(small_lane == 2 * j + half, peak, peaks)
            expo = jnp.exp(scores - row_max)
            prob = expo / jnp.sum(expo, axis=1, keepdims=True)
            probs_ref[j, :, length * half : length * (half + 1)] = prob
            low.append(prob.astype(BF16))
        mixed = jnp.dot(
            jnp.concatenate(low, axis=1),
            pair_of(values_ref, j, group_size, lane),
            preferred_element_type=F32,
        )
        head_out_ref[:, 128 * j : 128 * (j + 1)] = mixed.astype(BF16)
        if j in between:
            between[j]()
    peak_ref[...] = peaks
    keeps = [
        pltpu.make_async_copy(src, dst, keep_sems.at[i])
        for i, (src, dst) in enumerate(
            (
                (query_all, query_keep),
                (key_all, key_keep),
                (value_all, value_keep),
                (out_all, out_keep),
                (cot_all, cot_keep),
            )
        )
    ]
    for c in keeps[:3]:
        c.start()
    out.take_rest()
    keeps[3].start()
    mix_mine[...] = contract_cols(head_out_ref[...], out_all[...].reshape(width, q_cols))
    swap = remote(mix_mine, mix_other, mix_sems.at[0], mix_sems.at[1], place.twin())
    swap.start()
    cot.along(1, twin.start)
    cot.across(0, twin.start)
    swap.wait()
    hidden = tokens_ref[...].astype(F32) + RESIDUAL * (mix_mine[...] + mix_other[...])
    hidden_ref[...] = hidden
    inv_moe = lax.rsqrt(jnp.mean(hidden * hidden, axis=1, keepdims=True) + EPSILON)
    moe_in_ref[...] = (hidden * inv_moe * gains_ref[2:3, :]).astype(BF16)
    for step in range(2, line + 1):
        if step < line:
            cot.along(step, twin.start)
        cot.across(step - 1, twin.start)

    def rest(slot, carry):
        cot.take(slot)
        twin.start(slot)
        return carry

    lax.fori_loop(2 * line, count, rest, 0)
    for g in gathers + [cot]:
        g.settle()

    def other(slot, carry):
        @pl.when(slot != place.z)
        def _():
            twin.wait_send(slot)
            twin.take(slot)

        return carry

    lax.fori_loop(0, count, other, 0)
    keeps[4].start()
    for c in keeps:
        c.wait()


ANY = pl.BlockSpec(memory_space=pl.ANY)
IN_VMEM = pl.BlockSpec(memory_space=pltpu.VMEM)


def params(number):
    return pltpu.CompilerParams(
        collective_id=number, has_side_effects=True, vmem_limit_bytes=56 * 2**20
    )


def run_forward(line, group_size, tokens, query, key, value, out, cotangent, *small):
    count = 4 * line
    length, width = tokens.shape
    q_cols, kv_cols = query.shape[1], key.shape[1]
    blocks = [x.shape for x in (query, key, value, out, cotangent)]
    shape = jax.ShapeDtypeStruct
    outs = [
        shape((length, width), BF16),
        shape((length, width), F32),
        shape((length, width), BF16),
        shape((length, q_cols), BF16),
        shape((length, q_cols), BF16),
        shape((length, kv_cols), BF16),
        shape((length, kv_cols), BF16),
        shape((q_cols // 128, length, 2 * length), F32),
        shape((8, 128), F32),
        shape((3, length, 128), F32),
        shape((8, width), F32),
        shape((count, 8, 128), F32),
    ]
    return pl.pallas_call(
        functools.partial(forward_kernel, line, group_size),
        out_shape=outs + [shape((count, *s), BF16) for s in blocks],
        in_specs=[IN_VMEM] + [ANY] * 5 + [IN_VMEM] * len(small),
        out_specs=[IN_VMEM] * len(outs) + [ANY] * 5,
        scratch_shapes=[pltpu.VMEM((count, *s), BF16) for s in blocks]
        + [
            pltpu.VMEM((length, width), F32),
            pltpu.VMEM((length, width), F32),
            pltpu.VMEM((count, 8, 128), F32),
            pltpu.SemaphoreType.DMA((5, 5 * line)),
            pltpu.SemaphoreType.DMA((5, count)),
            pltpu.SemaphoreType.DMA((count,)),
            pltpu.SemaphoreType.DMA((count,)),
            pltpu.SemaphoreType.DMA((2, count)),
            pltpu.SemaphoreType.DMA((5,)),
            pltpu.SemaphoreType.DMA((5,)),
            pltpu.SemaphoreType.DMA((2,)),
        ],
        compiler_params=params(0),
        name="run_forward",
    )(tokens, query, key, value, out, cotangent, *small)


def experts_kernel(
    line,
    rows_ref,
    cot_ref,
    notes_ref,
    gate_ref,
    up_ref,
    down_ref,
    d_rows_ref,
    mix_ref,
    grad_gate_ref,
    grad_up_ref,
    grad_down_ref,
    rows,
    cots,
    active,
    d_gate,
    d_up,
    d_active,
    grad_stage,
    mix_stage,
    grad_parts,
    mix_parts,
    grads,
    total,
    from_b,
    from_a,
    from_z,
    reduce_send,
    reduce_recv,
    gather_send,
    gather_recv,
    twin_sems,
    load_sems,
    last_sems,
    store_sems,
):
    place = Place(line)
    count = 4 * line
    length, width = rows_ref.shape
    hidden = gate_ref.shape[1]
    mine, theirs = halves(place, width)

    def load(slot):
        return pltpu.make_async_copy(cot_ref.at[slot], cots.at[slot], load_sems.at[slot])

    def begin(slot, carry):
        load(slot).start()
        return carry

    lax.fori_loop(0, count, begin, 0)
    rows[place.z] = rows_ref[...]
    enter(place)
    view = lambda s: rows.at[s, :, mine]
    gather = Gather(place, view, gather_send, gather_recv)
    row_twin = Twin(place, view, view, twin_sems.at[0], twin_sems.at[1])
    grad_twin = Twin(
        place, lambda s: grad_stage.at[s, :, theirs], lambda s: grad_parts.at[s], twin_sems.at[2], twin_sems.at[3]
    )
    mix_twin = Twin(
        place, lambda s: mix_stage.at[s, :, theirs], lambda s: mix_parts.at[s], twin_sems.at[4], twin_sems.at[5]
    )
    reduce = Reduce(place, grad_parts, from_b, from_a, from_z, reduce_send, reduce_recv)

    def fold(slot):
        grad_twin.take(slot)
        reduce._add(slot, grad_stage[slot, :, mine])
        pl.when(slot >= 2 * line)(lambda: reduce.send_b(slot - 2 * line))

    def column(slot):
        return jnp.transpose(notes_ref[part_of(place, slot)])[:, 0:1]

    def tile_of(tile):
        first = 2 * tile
        pair = (first, first + 1)
        gate = jnp.concatenate([column(slot) for slot in pair], axis=0)
        return pair, pl.ds(first, 2), pl.ds(pl.multiple_of(first * length, 2 * length), 2 * length), gate

    def ahead(tile, carry):
        pair, two, flat, gate = tile_of(tile)
        for slot in pair:
            load(slot).wait()
        d_out = (gate * (RESIDUAL * cots[two].reshape(2 * length, width).astype(F32))).astype(BF16)
        cots[two] = d_out.reshape(2, length, width)
        d_active[flat, :] = jnp.dot(d_out, down_ref[...], preferred_element_type=F32)
        return carry

    def step(tile, carry):
        first = 2 * tile
        pair = (first, first + 1)
        two = pl.ds(first, 2)
        flat = pl.ds(pl.multiple_of(first * length, 2 * length), 2 * length)
        for slot in pair:
            pl.when(slot != place.z)(lambda slot=slot: row_twin.take(slot))
        x = rows[two].reshape(2 * length, width)
        gate_pre = jnp.dot(x, gate_ref[...], preferred_element_type=F32)
        up_pre = jnp.dot(x, up_ref[...], preferred_element_type=F32)
        sigmoid = 1.0 / (1.0 + jnp.exp(-gate_pre))
        silu = gate_pre * sigmoid
        active[flat, :] = (silu * up_pre).astype(BF16)
        d_act = d_active[flat, :]
        d_g = (d_act * up_pre * sigmoid * (1.0 + gate_pre * (1.0 - sigmoid))).astype(BF16)
        d_u = (d_act * silu).astype(BF16)
        d_gate[flat, :] = d_g
        d_up[flat, :] = d_u
        d_in = contract_cols(d_g, gate_ref[...]) + contract_cols(d_u, up_ref[...])
        grad_stage[two] = d_in.astype(BF16).reshape(2, length, width)
        for slot in pair:
            grad_twin.start(slot)
        group = (tile + 1) // (line // 2)

        @pl.when(jnp.logical_or(group == 1, group == 3))
        def _():
            for slot in (first + 2, first + 3):
                slot = slot + line * (3 - group) // 2
                gather.take(slot)
                row_twin.start(slot)

        @pl.when(jnp.logical_and(tile > 0, (first - 1) // line != 1))
        def _():
            for slot in (first - 2, first - 1):
                fold(slot)

        return carry

    gather.start()
    share = 2 * line // 4
    for at in range(4):
        lax.fori_loop(at * share, (at + 1) * share, ahead, 0)
        steps = range(1, line + 1)[at * line // 4 : (at + 1) * line // 4]
        for k in steps:
            if k < line:
                gather.along(k, row_twin.start)
            gather.across(k - 1, row_twin.start)
    lax.fori_loop(0, 2 * line, step, 0)
    for slot in (count - 2, count - 1):
        fold(slot)

    def fold_late(slot, carry):
        fold(slot)
        return carry

    lax.fori_loop(line, 2 * line, fold_late, 0)

    def weight_grad(number, i):
        left, right = ((cots, active), (rows, d_gate), (rows, d_up))[number]
        left = left.reshape(count * length, width)
        span = pl.ds(512 * i, 512)
        grads[number, span, :] = contract_rows(left[:, span], right[...])

    def store(number):
        out_ref = (grad_down_ref, grad_gate_ref, grad_up_ref)[number]
        stores.append(pltpu.make_async_copy(grads.at[number], out_ref, store_sems.at[number]))
        stores[-1].start()

    def mix_tile(tile, carry):
        pair, two, flat, gate = tile_of(tile)
        mix = contract_cols(active[flat, :], down_ref[...])
        mix_stage[two] = (gate * mix).astype(BF16).reshape(2, length, width)
        for slot in pair:
            mix_twin.start(slot)
        return carry

    stores = []
    pieces = width // 512
    order = ends_first(line)
    for at, z in enumerate(order):
        lax.fori_loop(2 * line * at // line, 2 * line * (at + 1) // line, mix_tile, 0)
        reduce.fold_b(z)
    for at, z in enumerate(order):
        if at < pieces:
            weight_grad(0, at)
        reduce.fold_b(line + z)
        reduce.send_a(z)
    for i in range(line, pieces):
        weight_grad(0, i)
    store(0)
    reduce.finish_line()
    for i in range(pieces):
        weight_grad(1, i)
    store(1)
    reduce.result(total)
    d_rows_ref[:, mine] = total[...]
    last = remote(total, d_rows_ref.at[:, mine], last_sems.at[0], last_sems.at[1], place.twin())
    last.start()
    for i in range(pieces):
        weight_grad(2, i)
    store(2)

    def mix_fold(slot, carry):
        mix_twin.take(slot)
        mix_parts[slot] = (mix_parts[slot].astype(F32) + mix_stage[slot, :, mine].astype(F32)).astype(BF16)
        return carry

    lax.fori_loop(0, count, mix_fold, 0)
    stores.append(pltpu.make_async_copy(mix_parts, mix_ref, store_sems.at[3]))
    stores[-1].start()
    reduce.settle()
    gather.settle()

    def settle(slot, carry):
        pl.when(slot != place.z)(lambda: row_twin.wait_send(slot))
        grad_twin.wait_send(slot)
        mix_twin.wait_send(slot)
        return carry

    lax.fori_loop(0, count, settle, 0)
    for c in stores:
        c.wait()
    last.wait()


def run_experts(line, rows, cots, notes, gate, up, down):
    count = 4 * line
    length, width = rows.shape
    half, hidden = width // 2, gate.shape[1]
    grad = jax.ShapeDtypeStruct((width, hidden), F32)
    return pl.pallas_call(
        functools.partial(experts_kernel, line),
        out_shape=[
            jax.ShapeDtypeStruct((length, width), F32),
            jax.ShapeDtypeStruct((count, length, half), BF16),
            grad,
            grad,
            grad,
        ],
        in_specs=[IN_VMEM, ANY, IN_VMEM, IN_VMEM, IN_VMEM, IN_VMEM],
        out_specs=[IN_VMEM, ANY, ANY, ANY, ANY],
        scratch_shapes=[
            pltpu.VMEM((count, length, width), BF16),
            pltpu.VMEM((count, length, width), BF16),
            pltpu.VMEM((count * length, hidden), BF16),
            pltpu.VMEM((count * length, hidden), BF16),
            pltpu.VMEM((count * length, hidden), BF16),
            pltpu.VMEM((count * length, hidden), F32),
            pltpu.VMEM((count, length, width), BF16),
            pltpu.VMEM((count, length, width), BF16),
            pltpu.VMEM((count, length, half), BF16),
            pltpu.VMEM((count, length, half), BF16),
            pltpu.VMEM((3, width, hidden), F32),
            pltpu.VMEM((length, half), F32),
        ]
        + reduce_scratch(line, (length, half))
        + [
            pltpu.SemaphoreType.DMA((5 * line,)),
            pltpu.SemaphoreType.DMA((count,)),
            pltpu.SemaphoreType.DMA((6, count)),
            pltpu.SemaphoreType.DMA((count,)),
            pltpu.SemaphoreType.DMA((2,)),
            pltpu.SemaphoreType.DMA((4,)),
        ],
        compiler_params=params(2),
        name="run_experts",
    )(rows, cots, notes, gate, up, down)


def backward_kernel(
    line,
    group_size,
    tokens_ref,
    hidden_ref,
    d_rows_ref,
    cot_ref,
    normed_ref,
    head_out_ref,
    queries_ref,
    keys_ref,
    values_ref,
    probs_ref,
    gains_ref,
    peak_ref,
    tables_ref,
    query_keep,
    key_keep,
    value_keep,
    out_keep,
    mix_ref,
    input_grad_ref,
    output_ref,
    query_sum,
    key_sum,
    value_sum,
    out_sum,
    notes,
    *scratch,
):
    place = Place(line)
    count = 4 * line
    length, width = tokens_ref.shape
    q_cols, kv_cols = queries_ref.shape[1], keys_ref.shape[1]
    shard = width // count
    chunks = q_cols // 128
    (query_all, key_all, value_all, out_all), work = scratch[:4], scratch[4:9]
    rest = scratch[9:34]
    (
        total,
        d_heads,
        d_query,
        d_key,
        d_value,
        part_mine,
        part_other,
        d_hidden_keep,
        mix_total,
        note,
        weight_sems,
        load_sems,
        last_sems,
        part_sems,
        note_sends,
        note_recvs,
    ) = scratch[34:]
    by_part = lambda slot: part_of(place, slot)
    reduces = [
        Reduce(place, work[i], *rest[5 * i : 5 * i + 5], *(() if i == 4 else (by_part,))) for i in range(5)
    ]

    def load(slot):
        return pltpu.make_async_copy(mix_ref.at[slot], work[4].at[slot], load_sems.at[slot])

    def begin(slot, carry):
        load(slot).start()
        return carry

    def loaded(slot, carry):
        load(slot).wait()
        return carry

    lax.fori_loop(0, count, begin, 0)
    weights = [
        pltpu.make_async_copy(src, dst, weight_sems.at[i])
        for i, (src, dst) in enumerate(
            ((out_keep, out_all), (query_keep, query_all), (key_keep, key_all), (value_keep, value_all))
        )
    ]
    for c in weights:
        c.start()
    enter(place)
    lax.fori_loop(0, count, loaded, 0)
    mine, theirs = halves(place, width)
    outs = (query_sum, key_sum, value_sum, out_sum, total)
    order = (4, 3, 0, 1, 2)
    last = remote(total, mix_total.at[:, mine], last_sems.at[0], last_sems.at[1], place.twin())

    def finish(at):
        i = order[at]
        reduces[i].result(outs[i])
        if i == 4:
            mix_total[:, mine] = total[...]
            last.start()

    run = Reductions([reduces[i] for i in order], finish)
    run.start()
    hidden = hidden_ref[...]
    inv_moe = lax.rsqrt(jnp.mean(hidden * hidden, axis=1, keepdims=True) + EPSILON)
    unit_moe = hidden * inv_moe
    d_rows = d_rows_ref[...]
    scaled = d_rows * gains_ref[2:3, :]
    d_hidden = cot_ref[...].astype(F32) + inv_moe * (
        scaled - unit_moe * jnp.mean(scaled * unit_moe, axis=1, keepdims=True)
    )
    d_hidden_keep[...] = d_hidden
    moe_gain = jnp.sum(d_rows * unit_moe, axis=0, keepdims=True)
    d_attn = (RESIDUAL * d_hidden).astype(BF16)
    run.run(2)
    work[3][...] = contract_rows(d_attn, head_out_ref[...]).astype(BF16).reshape(count, shard, q_cols)
    run.run(2)
    weights[0].wait()
    d_heads[...] = jnp.dot(
        d_attn, out_all[...].reshape(width, q_cols), preferred_element_type=F32
    ).astype(BF16)
    run.run(1)
    lane = lax.broadcasted_iota(jnp.int32, (length, 128), 1)
    d_key[...] = jnp.zeros_like(d_key)
    d_value[...] = jnp.zeros_like(d_value)
    tables = [tables_ref[i] for i in range(3)]
    for j in range(chunks):
        d_out = chunk_of(d_heads, j)
        keys = pair_of(keys_ref, j, group_size, lane)
        d_prob = contract_cols(d_out, pair_of(values_ref, j, group_size, lane))
        low, d_scores = [], []
        for half in (0, 1):
            side = slice(length * half, length * (half + 1))
            prob = probs_ref[j, :, side]
            grad = d_prob[:, side]
            inner = jnp.sum(prob * grad, axis=1, keepdims=True)
            d_scores.append((prob * (grad - inner)).astype(BF16))
            low.append(prob.astype(BF16))
        d_scores = jnp.concatenate(d_scores, axis=1)
        d_values = contract_rows(jnp.concatenate(low, axis=1), d_out)
        d_keys = contract_rows(d_scores, chunk_of(queries_ref, j)) * SCORE_SCALE
        turned = rope_chunk(
            jnp.dot(d_scores, keys, preferred_element_type=F32) * SCORE_SCALE, tables, -1.0
        )
        d_query[:, 128 * j : 128 * (j + 1)] = turned.astype(BF16)
        for half in (0, 1):
            group = (2 * j + half) // group_size
            side = slice(length * half, length * (half + 1))
            cols = slice(128 * (group // 2), 128 * (group // 2 + 1))
            d_key[:, cols] += place_half(d_keys[side], half, group % 2, lane)
            d_value[:, cols] += place_half(d_values[side], half, group % 2, lane)
        run.run(1)
    normed = normed_ref[...]
    work[0][...] = contract_rows(normed, d_query[...]).astype(BF16).reshape(count, shard, q_cols)
    d_key_lin = jnp.concatenate(
        [rope_chunk(chunk_of(d_key, j), tables, -1.0) for j in range(kv_cols // 128)], axis=1
    ).astype(BF16)
    d_value_lin = d_value[...].astype(BF16)
    run.run(2)
    work[1][...] = contract_rows(normed, d_key_lin).astype(BF16).reshape(count, shard, kv_cols)
    work[2][...] = contract_rows(normed, d_value_lin).astype(BF16).reshape(count, shard, kv_cols)
    run.run(2)
    for c in weights[1:]:
        c.wait()
    part_mine[...] = (
        contract_cols(d_query[...], query_all[...].reshape(width, q_cols))
        + contract_cols(d_key_lin, key_all[...].reshape(width, kv_cols))
        + contract_cols(d_value_lin, value_all[...].reshape(width, kv_cols))
    )
    swap = remote(part_mine, part_other, part_sems.at[0], part_sems.at[1], place.twin())
    swap.start()
    run.run(2)
    swap.wait()
    d_normed = part_mine[...] + part_other[...]
    inputs = tokens_ref[...].astype(F32)
    inv_attn = lax.rsqrt(jnp.mean(inputs * inputs, axis=1, keepdims=True) + EPSILON)
    unit_attn = inputs * inv_attn
    scaled = d_normed * gains_ref[1:2, :]
    input_grad_ref[...] = d_hidden_keep[...] + inv_attn * (
        scaled - unit_attn * jnp.mean(scaled * unit_attn, axis=1, keepdims=True)
    )
    attn_gain = jnp.sum(d_normed * unit_attn, axis=0, keepdims=True)
    rows = jnp.concatenate([attn_gain, moe_gain, jnp.zeros((6, width), F32)], axis=0)
    row = lax.broadcasted_iota(jnp.int32, (8, 128), 0)
    peaks = jnp.broadcast_to(peak_ref[0:1, :], (8, 128))
    for p in range(count):
        turned = pltpu.roll(rows, width - shard * p, 1) if p else rows
        note[p] = jnp.where(row == 2, peaks, turned[:, :128])
    exchange = Notes(place, note, notes, note_sends, note_recvs, False)
    exchange.start()
    run.complete()
    for r in reduces:
        r.settle()
    last.wait()
    output_ref[...] = (hidden_ref[...] + RESIDUAL * mix_total[...]).astype(BF16)
    exchange.finish()


def run_backward(line, group_size, kept, keeps, mix):
    count = 4 * line
    tokens, queries, keys = kept[0], kept[6], kept[7]
    length, width = tokens.shape
    q_cols, kv_cols = queries.shape[1], keys.shape[1]
    blocks = [x.shape[1:] for x in keeps] + [mix.shape[1:]]
    half = width // 2
    shape = jax.ShapeDtypeStruct
    outs = (
        [shape((length, width), F32), shape((length, width), BF16)]
        + [shape(s, F32) for s in blocks[:4]]
        + [shape((count, 8, 128), F32)]
    )
    return pl.pallas_call(
        functools.partial(backward_kernel, line, group_size),
        out_shape=outs,
        in_specs=[IN_VMEM] * len(kept) + [ANY] * 5,
        out_specs=[IN_VMEM] * len(outs),
        scratch_shapes=[pltpu.VMEM(x.shape, BF16) for x in keeps]
        + [pltpu.VMEM((count, *s), BF16) for s in blocks]
        + [x for s in blocks for x in reduce_scratch(line, s)]
        + [
            pltpu.VMEM((length, half), F32),
            pltpu.VMEM((length, q_cols), BF16),
            pltpu.VMEM((length, q_cols), BF16),
            pltpu.VMEM((length, kv_cols), F32),
            pltpu.VMEM((length, kv_cols), F32),
            pltpu.VMEM((length, width), F32),
            pltpu.VMEM((length, width), F32),
            pltpu.VMEM((length, width), F32),
            pltpu.VMEM((length, width), F32),
            pltpu.VMEM((count, 8, 128), F32),
            pltpu.SemaphoreType.DMA((4,)),
            pltpu.SemaphoreType.DMA((count,)),
            pltpu.SemaphoreType.DMA((2,)),
            pltpu.SemaphoreType.DMA((2,)),
            pltpu.SemaphoreType.DMA((count,)),
            pltpu.SemaphoreType.DMA((count,)),
        ],
        compiler_params=params(3),
        name="run_backward",
    )(*kept, *keeps, mix)


def finish_kernel(
    group_size,
    output_in,
    input_grad_in,
    query_in,
    key_in,
    value_in,
    out_in,
    notes,
    query_ref,
    key_ref,
    gate_in,
    up_in,
    down_in,
    output,
    input_grad,
    grad_query,
    grad_key,
    grad_value,
    grad_out,
    gains,
    clipped_query,
    clipped_key,
    grad_gate,
    grad_up,
    grad_down,
    stage,
    sems,
):
    pairs = ((gate_in, grad_gate), (up_in, grad_up), (down_in, grad_down))
    takes = [pltpu.make_async_copy(src, stage.at[i], sems.at[0, i]) for i, (src, _) in enumerate(pairs)]
    copies = [pltpu.make_async_copy(stage.at[i], dst.at[0], sems.at[1, i]) for i, (_, dst) in enumerate(pairs)]
    for c in takes:
        c.start()
    output[...] = output_in[...]
    input_grad[...] = input_grad_in[...]
    grad_query[...] = query_in[...]
    grad_key[...] = key_in[...]
    grad_value[...] = value_in[...]
    grad_out[...] = out_in[...]
    for take, c in zip(takes, copies):
        take.wait()
        c.start()
    total, peaks = notes[0], notes[0]
    for p in range(1, notes.shape[0]):
        total = total + notes[p]
        peaks = jnp.maximum(peaks, notes[p])
    gains[...] = total
    factor = CLIP_LIMIT / jnp.maximum(peaks, CLIP_LIMIT)
    root = jnp.sqrt(factor)
    lane = lax.broadcasted_iota(jnp.int32, (8, 128), 1)

    def scale(h):
        return jnp.max(jnp.where(lane == h, root, 0.0), axis=1, keepdims=True)[2:3, :]

    heads = query_ref.shape[1] // HEAD_SIZE
    wide = lax.broadcasted_iota(jnp.int32, (1, 128), 1)
    scales = [scale(h) for h in range(heads)]
    for j in range(heads // 2):
        row = jnp.where(wide < HEAD_SIZE, scales[2 * j], scales[2 * j + 1])
        cols = slice(128 * j, 128 * (j + 1))
        clipped_query[:, cols] = query_ref[:, cols].astype(F32) * row
    least = [
        functools.reduce(jnp.minimum, scales[group_size * g : group_size * (g + 1)])
        for g in range(heads // group_size)
    ]
    for j in range(len(least) // 2):
        row = jnp.where(wide < HEAD_SIZE, least[2 * j], least[2 * j + 1])
        cols = slice(128 * j, 128 * (j + 1))
        clipped_key[:, cols] = key_ref[:, cols].astype(F32) * row
    for c in copies:
        c.wait()


def finish(group_size, found, notes, query, key, expert_grads):
    shape = jax.ShapeDtypeStruct
    outs = [shape(x.shape, x.dtype) for x in found] + [
        shape((8, 128), F32),
        shape(query.shape, F32),
        shape(key.shape, F32),
    ]
    return pl.pallas_call(
        functools.partial(finish_kernel, group_size),
        out_shape=outs + [shape((1, *g.shape), F32) for g in expert_grads],
        in_specs=[IN_VMEM] * 9 + [ANY] * 3,
        out_specs=[IN_VMEM] * 9 + [ANY] * 3,
        scratch_shapes=[
            pltpu.VMEM((3, *expert_grads[0].shape), F32),
            pltpu.SemaphoreType.DMA((2, 3)),
        ],
        compiler_params=pltpu.CompilerParams(vmem_limit_bytes=56 * 2**20),
        name="finish",
    )(*found, notes, query, key, *expert_grads)


def on_device_dense(
    tokens,
    attn_norm_gain,
    w_query,
    key_projection,
    value_projection,
    w_out,
    moe_norm_gain,
    w_gate,
    w_up,
    w_down,
    router_logits,
    expert_ids,
    segment_ids,
    parents,
    cotangent,
):
    length, model_width = tokens.shape
    q_cols, kv_cols = w_query.shape[1], key_projection.shape[1]
    q_heads, kv_heads = q_cols // HEAD_SIZE, kv_cols // HEAD_SIZE
    group_size = q_heads // kv_heads
    count = lax.axis_size("dp")
    line = count // 4
    shard = attn_norm_gain.shape[0]
    (moe_in, hidden, normed, head_out, queries, keys, values, probs, peak, tables, gains, notes, *keeps, cots) = run_forward(
        line,
        group_size,
        tokens,
        w_query,
        key_projection,
        value_projection,
        w_out,
        cotangent,
        attn_norm_gain[None],
        moe_norm_gain[None],
        router_logits,
        expert_ids,
        segment_ids,
        parents,
    )
    d_moe_in, mix_parts, *expert_grads = run_experts(
        line, moe_in, cots, notes, w_gate[0], w_up[0], w_down[0]
    )
    kept = (tokens, hidden, d_moe_in, cotangent, normed, head_out, queries, keys, values, probs, gains, peak, tables)
    input_grad, output, *grads, sums = run_backward(line, group_size, kept, keeps, mix_parts)
    output, input_grad, gq, gk, gv, go, gains, clipped_query, clipped_key, gg, gu, gd = finish(
        group_size, (output, input_grad, *grads), sums, w_query, key_projection, expert_grads
    )
    return (
        output,
        input_grad,
        gains[0, :shard],
        gq,
        gk,
        gv,
        go,
        gains[1, :shard],
        gg,
        gu,
        gd,
        clipped_query,
        clipped_key,
    )


DENSE_BYTES = 8 * 2**20


def on_device(*args):
    tokens, w_gate = args[0], args[7]
    count, ranks = lax.axis_size("dp"), lax.axis_size("tensor")
    rows_bytes = count * tokens.shape[0] * tokens.shape[1] * 2
    whole_experts = w_gate.shape[2] * ranks == FFE
    dense = whole_experts and ranks == 2 and count % 8 == 0 and rows_bytes <= DENSE_BYTES
    return on_device_dense(*args) if dense else on_device_general(*args)


def solution(mesh):
    in_specs = (
        P("dp", None),
        P("dp"),
        P("dp", "tensor"),
        P("dp", "tensor"),
        P("dp", "tensor"),
        P("dp", "tensor"),
        P("dp"),
        P("dp", None, "tensor"),
        P("dp", None, "tensor"),
        P("dp", None, "tensor"),
        P("dp", None),
        P("dp", None),
        P("dp", None),
        P("dp", None),
        P("dp", None),
    )
    out_specs = (
        P("dp", None),
        P("dp", None),
        P("dp"),
        P("dp", "tensor"),
        P("dp", "tensor"),
        P("dp", "tensor"),
        P("dp", "tensor"),
        P("dp"),
        P("dp", None, "tensor"),
        P("dp", None, "tensor"),
        P("dp", None, "tensor"),
        P("dp", "tensor"),
        P("dp", "tensor"),
    )
    return jax.shard_map(
        on_device, mesh=mesh, in_specs=in_specs, out_specs=out_specs, check_vma=False
    )
```

```python
import functools

import jax
import jax.numpy as jnp
from jax import lax
from jax.experimental import pallas as pl
from jax.experimental.pallas import tpu as pltpu
from jax.sharding import PartitionSpec as P

HEAD_SIZE = 64
FFE = 512
TOP = 8


EPSILON = 1e-06
SCORE_SCALE = 1.0 / 64.0
RESIDUAL = 0.22
THETA = 10000.0
CLIP_LIMIT = 2.0
NEGATIVE = -1e30


def tree_layout(seg_row, par_row):
    tree_length = seg_row.shape[0]
    seg_count = par_row.shape[0]
    seg_index = jnp.arange(seg_count, dtype=jnp.int32)
    member = (seg_row[:, None] == seg_index[None, :]).astype(jnp.int32)
    seg_len = jnp.sum(member, axis=0)
    seg_start = jnp.sum(jnp.where(seg_index[:, None] > seg_index[None, :], seg_len[None, :], 0), axis=1)
    parent_hot = (par_row[:, None] == seg_index[None, :]).astype(jnp.int32)
    grand_parent = jnp.sum(parent_hot * par_row[None, :], axis=1)
    grand_hot = (grand_parent[:, None] == seg_index[None, :]).astype(jnp.int32)
    parent_len = jnp.sum(parent_hot * seg_len[None, :], axis=1)
    grand_len = jnp.sum(grand_hot * seg_len[None, :], axis=1)
    offset = jnp.where(seg_index != 0, parent_len, 0) + jnp.where(par_row != 0, grand_len, 0)
    tok_start = jnp.sum(member * seg_start[None, :], axis=1)
    tok_offset = jnp.sum(member * offset[None, :], axis=1)
    places = jnp.arange(tree_length, dtype=jnp.int32)
    position = (places - tok_start + tok_offset).astype(jnp.float32)
    identity = (seg_index[:, None] == seg_index[None, :]).astype(jnp.int32)
    ancestor = jnp.minimum(identity + parent_hot + grand_hot, 1)
    reached = jnp.dot(member, ancestor)
    linked = jnp.dot(reached, member.T) > 0
    allowed = linked & (places[None, :] <= places[:, None])
    return (position, allowed)


def rope_tables(position, head_dim):
    half_dim = head_dim // 2
    frequency = THETA ** (-2.0 * jnp.arange(half_dim, dtype=jnp.float32) / head_dim)
    angles = position[:, None] * frequency[None, :]
    return (jnp.cos(angles)[:, None, :], jnp.sin(angles)[:, None, :])


def apply_rotary(values_in, cosine_table, sine_values):
    half_dim = values_in.shape[-1] // 2
    first_half = values_in[..., :half_dim]
    second_half = values_in[..., half_dim:]
    return jnp.concatenate(
        [
            first_half * cosine_table - second_half * sine_values,
            second_half * cosine_table + first_half * sine_values,
        ],
        axis=-1,
    )


def rotate_back(grads_in, cosine_table, sine_values):
    half_dim = grads_in.shape[-1] // 2
    first_half = grads_in[..., :half_dim]
    second_half = grads_in[..., half_dim:]
    return jnp.concatenate(
        [
            first_half * cosine_table + second_half * sine_values,
            second_half * cosine_table - first_half * sine_values,
        ],
        axis=-1,
    )


def slot_tables(routes, experts, capacity):
    flat_ids = routes.reshape(-1)
    row_count = flat_ids.shape[0]
    member = (flat_ids[:, None] == jnp.arange(experts, dtype=jnp.int32)[None, :]).astype(jnp.int32)
    row_total = flat_ids.shape[0]
    before = jnp.dot((jnp.arange(row_total)[:, None] > jnp.arange(row_total)[None, :]).astype(jnp.float32), member.astype(jnp.float32), precision=lax.Precision.HIGHEST).astype(jnp.int32)
    slot_index = jnp.sum(before * member, axis=1)
    target = flat_ids * capacity + slot_index
    source = (
        jnp.full((experts * capacity,), -1, jnp.int32)
        .at[target]
        .set(jnp.arange(row_count, dtype=jnp.int32))
    )
    return (flat_ids, slot_index, source)


def contract_rows(left, right):
    return lax.dot_general(
        left, right, (((0,), (0,)), ((), ())), preferred_element_type=jnp.float32
    )


def contract_cols(left, right):
    return lax.dot_general(
        left, right, (((1,), (1,)), ((), ())), preferred_element_type=jnp.float32
    )


def expert_forward(inputs, gate_w, up_w, down_w):
    gate_pre = jnp.dot(inputs, gate_w, preferred_element_type=jnp.float32)
    up_pre = jnp.dot(inputs, up_w, preferred_element_type=jnp.float32)
    active = (gate_pre / (1.0 + jnp.exp(-gate_pre)) * up_pre).astype(jnp.bfloat16)
    return (contract_cols(active, down_w), (gate_pre, up_pre, active))


def expert_backward(inputs, grads_out, gate_w, up_w, down_w, kept_acts):
    gate_pre, up_pre, active = kept_acts
    d_active = jnp.dot(grads_out, down_w, preferred_element_type=jnp.float32)
    grad_down = contract_rows(grads_out, active)
    sigmoid_val = 1.0 / (1.0 + jnp.exp(-gate_pre))
    d_gate = (d_active * up_pre * sigmoid_val * (1.0 + gate_pre * (1.0 - sigmoid_val))).astype(
        jnp.bfloat16
    )
    d_up = (d_active * gate_pre * sigmoid_val).astype(jnp.bfloat16)
    grad_gate = contract_rows(inputs, d_gate)
    grad_up = contract_rows(inputs, d_up)
    d_inputs = contract_cols(d_gate, gate_w) + contract_cols(d_up, up_w)
    return (d_inputs, grad_gate, grad_up, grad_down)


def send_rows(rows_in):
    return lax.all_to_all(rows_in, "dp", split_axis=0, concat_axis=0, tiled=True)


def return_rows(rows_in):
    return lax.all_to_all(
        rows_in.astype(jnp.bfloat16), "dp", split_axis=0, concat_axis=0, tiled=True
    ).astype(rows_in.dtype)


def send_grads(rows_in):
    return lax.all_to_all(rows_in, "dp", split_axis=0, concat_axis=0, tiled=True)


def return_grads(rows_in):
    return lax.all_to_all(
        rows_in.astype(jnp.bfloat16), "dp", split_axis=0, concat_axis=0, tiled=True
    ).astype(rows_in.dtype)


def share_slots(partial_rows):
    return lax.psum_scatter(partial_rows, "tensor", scatter_dimension=1, tiled=True)


def on_device_general(
    tokens,
    attn_norm_gain,
    w_query,
    key_projection,
    value_projection,
    w_out,
    moe_norm_gain,
    w_gate,
    w_up,
    w_down,
    router_logits,
    expert_ids,
    segment_ids,
    parents,
    cotangent,
):
    length = tokens.shape[0]
    model_width = tokens.shape[1]
    q_cols = w_query.shape[1]
    kv_cols = key_projection.shape[1]
    q_heads = q_cols // HEAD_SIZE
    kv_heads = kv_cols // HEAD_SIZE
    group_size = q_heads // kv_heads
    dp_size = lax.axis_size("dp")
    tensor_ranks = lax.axis_size("tensor")
    replicas = FFE // (w_gate.shape[2] * tensor_ranks)
    experts = dp_size // replicas
    capacity = 4 * (9 * length * TOP // (32 * experts))
    share_rows = capacity // tensor_ranks
    first_slot = lax.axis_index("tensor") * share_rows
    block_rows = min(length, 512)
    attn_gain, moe_gain, query_w, key_weight, value_weight, out_w = (
        lax.all_gather(attn_norm_gain, "dp", axis=0, tiled=True),
        lax.all_gather(moe_norm_gain, "dp", axis=0, tiled=True),
        lax.all_gather(w_query, "dp", axis=0, tiled=True),
        lax.all_gather(key_projection, "dp", axis=0, tiled=True),
        lax.all_gather(value_projection, "dp", axis=0, tiled=True),
        lax.all_gather(w_out, "dp", axis=0, tiled=True),
    )
    attn_gain_f = attn_gain.astype(jnp.float32)
    moe_gain_f = moe_gain.astype(jnp.float32)
    inputs = tokens.astype(jnp.float32)
    inv_attn = lax.rsqrt(jnp.mean(inputs * inputs, axis=1, keepdims=True) + EPSILON)
    unit_attn = inputs * inv_attn
    normalized_rows = (unit_attn * attn_gain_f).astype(jnp.bfloat16)
    position, allowed = tree_layout(segment_ids[0], parents[0])
    cosine_table, sine_values = rope_tables(position, HEAD_SIZE)
    query_linear = jnp.dot(normalized_rows, query_w, preferred_element_type=jnp.float32).reshape(
        length, q_heads, HEAD_SIZE
    )
    key_linear = jnp.dot(normalized_rows, key_weight, preferred_element_type=jnp.float32).reshape(
        length, kv_heads, HEAD_SIZE
    )
    query_heads = (
        apply_rotary(query_linear, cosine_table, sine_values)
        .astype(jnp.bfloat16)
        .reshape(length, kv_heads, group_size, HEAD_SIZE)
    )
    key_heads = apply_rotary(key_linear, cosine_table, sine_values).astype(jnp.bfloat16)
    value_heads = (
        jnp.dot(normalized_rows, value_weight, preferred_element_type=jnp.float32)
        .astype(jnp.bfloat16)
        .reshape(length, kv_heads, HEAD_SIZE)
    )
    q_block = query_heads
    mask_rows = allowed[None, None]
    scores = (
        jnp.einsum("qhgd,khd->hgqk", q_block, key_heads, preferred_element_type=jnp.float32)
        * SCORE_SCALE
    )
    scores = jnp.where(mask_rows, scores, NEGATIVE)
    peak_parts = [jnp.max(scores, axis=(2, 3))]
    row_max = jnp.max(scores, axis=3, keepdims=True)
    expo = jnp.exp(scores - row_max)
    row_total = jnp.sum(expo, axis=3, keepdims=True)
    lse_parts = [row_max + jnp.log(row_total)]
    prob_low = (expo / row_total).astype(jnp.bfloat16)
    block_outs = jnp.einsum(
        "hgqk,khd->qhgd", prob_low, value_heads, preferred_element_type=jnp.float32
    )
    head_out = block_outs.reshape(length, q_cols).astype(jnp.bfloat16)
    attn_mix = lax.psum(contract_cols(head_out, out_w), "tensor")
    hidden = inputs + RESIDUAL * attn_mix
    head_peak = lax.pmax(jnp.max(jnp.stack(peak_parts), axis=0).reshape(q_heads), "dp")
    inv_moe = lax.rsqrt(jnp.mean(hidden * hidden, axis=1, keepdims=True) + EPSILON)
    unit_moe = hidden * inv_moe
    moe_in = (unit_moe * moe_gain_f).astype(jnp.bfloat16)
    logit_max = jnp.max(router_logits, axis=1, keepdims=True)
    logit_exp = jnp.exp(router_logits - logit_max)
    gate_probs = logit_exp / jnp.sum(logit_exp, axis=1, keepdims=True)
    flat_ids, slot_index, source = slot_tables(expert_ids, experts, capacity)
    filled = source >= 0
    source_row = jnp.maximum(source, 0)
    source_token = source_row // TOP
    dispatch_rows = jnp.where(
        filled[:, None], moe_in[source_token], jnp.zeros((), jnp.bfloat16)
    ).reshape(experts, capacity, model_width)
    arrived = send_rows(jnp.repeat(dispatch_rows, replicas, axis=0))
    gate_w, up_w, down_w = (w_gate[0], w_up[0], w_down[0])
    expert_in = arrived.reshape(dp_size * capacity, model_width)
    expert_out, kept_acts = expert_forward(expert_in, gate_w, up_w, down_w)
    partial_out = share_slots(expert_out.reshape(dp_size, capacity, model_width))
    back_parts = return_rows(partial_out).reshape(experts, replicas, share_rows, model_width)
    back_rows = (
        jnp.sum(back_parts, axis=1).astype(jnp.bfloat16).reshape(experts * share_rows, model_width)
    )
    own_slot = ((slot_index >= first_slot) & (slot_index < first_slot + share_rows)).reshape(
        length, TOP
    )
    local_index = (
        flat_ids * share_rows + jnp.clip(slot_index - first_slot, 0, share_rows - 1)
    ).reshape(length, TOP)
    mix_part = jnp.zeros((length, model_width), jnp.float32)
    for column in range(TOP):
        gate_weight = jnp.where(own_slot[:, column], gate_probs[:, column], 0.0)
        mix_part = mix_part + gate_weight[:, None] * back_rows[local_index[:, column]].astype(
            jnp.float32
        )
    expert_mix = lax.psum(mix_part.astype(jnp.bfloat16), "tensor").astype(jnp.float32)
    output = (hidden + RESIDUAL * expert_mix).astype(jnp.bfloat16)
    grad_output = cotangent.astype(jnp.float32)
    mix_grad = RESIDUAL * grad_output
    row_gate = gate_probs.reshape(-1)[source_row]
    grad_rows = (
        jnp.where(filled[:, None], row_gate[:, None] * mix_grad[source_token], 0.0)
        .astype(jnp.bfloat16)
        .reshape(experts, capacity, model_width)
    )
    grad_arrived = send_grads(jnp.repeat(grad_rows, replicas, axis=0)).reshape(
        dp_size * capacity, model_width
    )
    d_inputs, grad_gate, grad_up, grad_down = expert_backward(
        expert_in, grad_arrived, gate_w, up_w, down_w, kept_acts
    )
    d_back = share_slots(d_inputs.reshape(dp_size, capacity, model_width))
    grad_gate, grad_up, grad_down = (grad_gate[None], grad_up[None], grad_down[None])
    d_parts = return_grads(d_back).reshape(experts, replicas, share_rows, model_width)
    d_returned = (
        jnp.sum(d_parts, axis=1).astype(jnp.bfloat16).reshape(experts * share_rows, model_width)
    )
    d_mix_part = jnp.zeros((length, model_width), jnp.float32)
    for column in range(TOP):
        d_mix_part = d_mix_part + jnp.where(
            own_slot[:, column][:, None],
            d_returned[local_index[:, column]].astype(jnp.float32),
            0.0,
        )
    d_moe_in = lax.psum(d_mix_part, "tensor")
    scaled_moe = d_moe_in * moe_gain_f
    grad_moe_gain = jnp.sum(d_moe_in * unit_moe, axis=0)
    d_hidden = grad_output + inv_moe * (
        scaled_moe - unit_moe * jnp.mean(scaled_moe * unit_moe, axis=1, keepdims=True)
    )
    d_attn = (RESIDUAL * d_hidden).astype(jnp.bfloat16)
    grad_out_w = contract_rows(d_attn, head_out)
    d_heads = (
        jnp.dot(d_attn, out_w, preferred_element_type=jnp.float32)
        .astype(jnp.bfloat16)
        .reshape(length, kv_heads, group_size, HEAD_SIZE)
    )
    d_query_parts = []
    d_key = jnp.zeros((length, kv_heads, HEAD_SIZE), jnp.float32)
    d_value = jnp.zeros((length, kv_heads, HEAD_SIZE), jnp.float32)
    for block_number, row_begin in enumerate(range(0, length, block_rows)):
        q_block = query_heads
        mask_rows = allowed[None, None]
        scores = (
            jnp.einsum("qhgd,khd->hgqk", q_block, key_heads, preferred_element_type=jnp.float32)
            * SCORE_SCALE
        )
        scores = jnp.where(mask_rows, scores, NEGATIVE)
        prob_full = jnp.exp(scores - lse_parts[block_number])
        prob_low = prob_full.astype(jnp.bfloat16)
        d_value = jnp.einsum(
            "hgqk,qhgd->khd", prob_low, d_heads, preferred_element_type=jnp.float32
        )
        d_prob = jnp.einsum(
            "qhgd,khd->hgqk", d_heads, value_heads, preferred_element_type=jnp.float32
        )
        inner = jnp.sum(prob_full * d_prob, axis=3, keepdims=True)
        d_scores = (prob_full * (d_prob - inner)).astype(jnp.bfloat16)
        d_query_parts.append(
            jnp.einsum("hgqk,khd->qhgd", d_scores, key_heads, preferred_element_type=jnp.float32)
            * SCORE_SCALE
        )
        d_key = (
            jnp.einsum("hgqk,qhgd->khd", d_scores, q_block, preferred_element_type=jnp.float32)
            * SCORE_SCALE
        )
    d_query_all = d_query_parts[0].reshape(length, q_heads, HEAD_SIZE)
    d_query_lin = (
        rotate_back(d_query_all, cosine_table, sine_values)
        .astype(jnp.bfloat16)
        .reshape(length, q_cols)
    )
    d_key_lin = (
        rotate_back(d_key, cosine_table, sine_values).astype(jnp.bfloat16).reshape(length, kv_cols)
    )
    d_value_lin = d_value.astype(jnp.bfloat16).reshape(length, kv_cols)
    grad_query_w = contract_rows(normalized_rows, d_query_lin)
    grad_key_w = contract_rows(normalized_rows, d_key_lin)
    grad_value_w = contract_rows(normalized_rows, d_value_lin)
    d_normed_part = (
        contract_cols(d_query_lin, query_w)
        + contract_cols(d_key_lin, key_weight)
        + contract_cols(d_value_lin, value_weight)
    )
    d_normed = lax.psum(d_normed_part.astype(jnp.bfloat16), "tensor").astype(jnp.float32)
    scaled_attn = d_normed * attn_gain_f
    grad_attn_gain = jnp.sum(d_normed * unit_attn, axis=0)
    input_grad = d_hidden + inv_attn * (
        scaled_attn - unit_attn * jnp.mean(scaled_attn * unit_attn, axis=1, keepdims=True)
    )
    reduced = (
        lax.psum_scatter(grad_attn_gain, "dp", scatter_dimension=0, tiled=True),
        lax.psum_scatter(grad_moe_gain, "dp", scatter_dimension=0, tiled=True),
        lax.psum_scatter(grad_query_w, "dp", scatter_dimension=0, tiled=True),
        lax.psum_scatter(grad_key_w, "dp", scatter_dimension=0, tiled=True),
        lax.psum_scatter(grad_value_w, "dp", scatter_dimension=0, tiled=True),
        lax.psum_scatter(grad_out_w, "dp", scatter_dimension=0, tiled=True),
    )
    scale_factor = CLIP_LIMIT / jnp.maximum(head_peak, CLIP_LIMIT)
    query_scale = jnp.repeat(jnp.sqrt(scale_factor), HEAD_SIZE)
    key_clip_scale = jnp.repeat(
        jnp.sqrt(jnp.min(scale_factor.reshape(kv_heads, group_size), axis=1)), HEAD_SIZE
    )
    clipped_query = w_query.astype(jnp.float32) * query_scale[None, :]
    clipped_key = key_projection.astype(jnp.float32) * key_clip_scale[None, :]
    return (
        output,
        input_grad,
        reduced[0],
        reduced[2],
        reduced[3],
        reduced[4],
        reduced[5],
        reduced[1],
        grad_gate,
        grad_up,
        grad_down,
        clipped_query,
        clipped_key,
    )


MESH_IDS = pl.DeviceIdType.MESH
F32 = jnp.float32
BF16 = jnp.bfloat16


class Place:
    def __init__(self, line):
        self.line = line
        self.count = 4 * line
        me = lax.axis_index("dp")
        self.core = lax.axis_index("tensor")
        self.me = me
        self.z = me // 4
        y, x = (me // 2) % 2, me % 2
        self.step_a, self.step_b = 2 - self.core, 1 + self.core
        self.a = y * (1 - self.core) + x * self.core
        self.b = x * (1 - self.core) + y * self.core

    def part(self, z, a, b):
        return z * 4 + a * self.step_a + b * self.step_b

    def up(self):
        return (self.me + 4, self.core)

    def down(self):
        return (self.me - 4, self.core)

    def beside_a(self):
        return (self.me + self.step_a * (1 - 2 * self.a), self.core)

    def beside_b(self):
        return (self.me + self.step_b * (1 - 2 * self.b), self.core)

    def twin(self):
        return (self.me, 1 - self.core)

    def peer(self, offset):
        return lax.rem(self.me + offset, self.count)


def enter(place):
    barrier = pltpu.get_barrier_semaphore()

    def greet(offset, carry):
        pl.semaphore_signal(
            barrier, inc=1, device_id=(place.peer(offset), place.core), device_id_type=MESH_IDS
        )
        return carry

    lax.fori_loop(1, place.count, greet, 0)
    pl.semaphore_signal(barrier, inc=1, device_id=place.twin(), device_id_type=MESH_IDS)
    pl.semaphore_wait(barrier, place.count)


def remote(src, dst, send_sem, recv_sem, device):
    return pltpu.make_async_remote_copy(
        src_ref=src,
        dst_ref=dst,
        send_sem=send_sem,
        recv_sem=recv_sem,
        device_id=device,
        device_id_type=MESH_IDS,
    )


class Notes:
    def __init__(self, place, src, dst, send_sem, recv_sem, alike):
        self.place, self.src, self.dst = place, src, dst
        self.send_sem, self.recv_sem, self.alike = send_sem, recv_sem, alike

    def _copy(self, offset, source):
        place = self.place
        to = place.peer(offset)
        return remote(
            self.src if self.alike else self.src.at[to],
            self.dst.at[source],
            self.send_sem.at[offset],
            self.recv_sem.at[source],
            (to, place.core),
        )

    def start(self):
        def send(offset, carry):
            self._copy(offset, self.place.me).start()
            return carry

        lax.fori_loop(1, self.place.count, send, 0)
        me = self.place.me
        self.dst[me] = self.src[...] if self.alike else self.src[me]

    def finish(self):
        def settle(offset, carry):
            self._copy(offset, self.place.peer(offset)).wait_recv()
            self._copy(offset, self.place.me).wait_send()
            return carry

        lax.fori_loop(1, self.place.count, settle, 0)


class Gather:
    def __init__(self, place, view, send_sem, recv_sem, fixed=False):
        self.place, self.view, self.fixed = place, view, fixed
        self.send_sem, self.recv_sem = send_sem, recv_sem

    def _copy(self, source, target, sem, device):
        there = self.view(source if self.fixed else target)
        return remote(self.view(source), there, self.send_sem.at[sem], self.recv_sem.at[target], device)

    def _to_z(self, step):
        place = self.place
        own = place.z
        return self._copy(own, own, step + place.line - 1, (place.me + 4 * step, place.core))

    def _to_a(self, z):
        line = self.place.line
        return self._copy(z, line + z, 2 * line - 1 + z, self.place.beside_a())

    def _to_b(self, slot):
        line = self.place.line
        return self._copy(slot, 2 * line + slot, 3 * line - 1 + slot, self.place.beside_b())

    def take(self, slot):
        self._copy(slot, slot, 0, self.place.beside_b()).wait_recv()

    def near(self, step, action):
        place = self.place
        if step == 0:
            action(place.z)
        else:
            pl.when(place.z >= step)(lambda: action(place.z - step))
            pl.when(place.z + step < place.line)(lambda: action(place.z + step))

    def start(self):
        place = self.place

        def reach(step):
            pl.when(place.z >= step)(lambda: self._to_z(-step).start())
            pl.when(place.z + step < place.line)(lambda: self._to_z(step).start())

        reach(1)
        self._to_a(place.z).start()
        self._to_b(place.z).start()
        for step in range(2, place.line):
            reach(step)

    def along(self, step, then=None):
        def pass_on(z):
            self.take(z)
            self._to_a(z).start()
            self._to_b(z).start()
            if then is not None:
                then(z)

        self.near(step, pass_on)

    def across(self, step, then=None):
        line = self.place.line

        def pass_on(z):
            self.take(line + z)
            self._to_b(line + z).start()
            if then is not None:
                then(line + z)

        self.near(step, pass_on)

    def settle(self):
        place = self.place
        line = place.line

        def wait(z, carry):
            self._to_a(z).wait_send()
            self._to_b(z).wait_send()
            self._to_b(line + z).wait_send()
            pl.when(z != place.z)(lambda: self._to_z(z - place.z).wait_send())
            return carry

        lax.fori_loop(0, line, wait, 0)

    def take_rest(self):
        line = self.place.line

        def wait(k, carry):
            self.take(2 * line + k)
            return carry

        lax.fori_loop(0, 2 * line, wait, 0)


def gather_all(gathers, thens=None):
    line = gathers[0].place.line
    thens = thens or [None] * len(gathers)
    gathers[0].start()
    for i, (g, then) in enumerate(zip(gathers, thens)):
        for step in range(1, line + 1):
            if step < line:
                g.along(step, then)
            if step == line - 1 and i + 1 < len(gathers):
                gathers[i + 1].start()
            g.across(step - 1, then)


class Twin:
    def __init__(self, place, source, target, send_sem, recv_sem):
        self.place, self.source, self.target = place, source, target
        self.send_sem, self.recv_sem = send_sem, recv_sem

    def copy(self, slot):
        line = self.place.line
        group = slot // line
        there = slot + line * ((group % 2) - (group // 2))
        return remote(
            self.source(slot),
            self.target(there),
            self.send_sem.at[slot],
            self.recv_sem.at[there],
            self.place.twin(),
        )

    def start(self, slot):
        self.copy(slot).start()

    def take(self, slot):
        remote(
            self.source(slot),
            self.target(slot),
            self.send_sem.at[slot],
            self.recv_sem.at[slot],
            self.place.twin(),
        ).wait_recv()

    def wait_send(self, slot):
        self.copy(slot).wait_send()


class Reduce:
    def __init__(self, place, parts, from_b, from_a, from_z, send_sem, recv_sem, index=lambda slot: slot):
        self.place, self.parts, self.index = place, parts, index
        self.from_b, self.from_a, self.from_z = from_b, from_a, from_z
        self.send_sem, self.recv_sem = send_sem, recv_sem

    def _copy(self, source, target, sem, device):
        return remote(source, target, self.send_sem.at[sem], self.recv_sem.at[sem], device)

    def _to_b(self, k):
        line = self.place.line
        return self._copy(self.parts.at[self.index(2 * line + k)], self.from_b.at[k], k, self.place.beside_b())

    def _to_a(self, z):
        line = self.place.line
        block = self.parts.at[self.index(line + z)]
        return self._copy(block, self.from_a.at[z], 2 * line + z, self.place.beside_a())

    def _to_z(self, target):
        place, line = self.place, self.place.line
        return remote(
            self.parts.at[self.index(target)],
            self.from_z.at[place.z],
            self.send_sem.at[3 * line + target],
            self.recv_sem.at[3 * line + place.z],
            (place.me + 4 * (target - place.z), place.core),
        )

    def _add(self, slot, block):
        at = self.index(slot)
        self.parts[at] = (self.parts[at].astype(F32) + block.astype(F32)).astype(BF16)

    def send_b(self, k):
        self._to_b(k).start()

    def fold_b(self, k):
        self._to_b(k).wait_recv()
        self._add(k, self.from_b[k])

    def send_a(self, z):
        self._to_a(z).start()

    def fold_a(self, z):
        self._to_a(z).wait_recv()
        self._add(z, self.from_a[z])

    def send_line(self):
        place = self.place
        for z in ends_first(place.line):
            pl.when(place.z != z)(lambda z=z: self._to_z(z).start())

    def fold_line_a(self):
        line = self.place.line
        for z in ends_first(line):
            self.fold_b(line + z)
            self.send_a(z)

    def fold_line_own(self):
        for z in ends_first(self.place.line):
            self.fold_b(z)

    def finish_line(self):
        for z in ends_first(self.place.line):
            self.fold_a(z)
        self.send_line()

    def result(self, out):
        place, line = self.place, self.place.line
        out[...] = self.parts[self.index(place.z)].astype(F32)

        def add(z, carry):
            @pl.when(z != place.z)
            def _():
                remote(
                    self.from_z.at[z], self.from_z.at[z], self.send_sem.at[0], self.recv_sem.at[3 * line + z], place.up()
                ).wait_recv()
                out[...] += self.from_z[z].astype(F32)

            return carry

        lax.fori_loop(0, line, add, 0)

    def settle_b(self):
        def wait(k, carry):
            self._to_b(k).wait_send()
            return carry

        lax.fori_loop(0, 2 * self.place.line, wait, 0)

    def settle_a(self):
        place = self.place

        def wait(z, carry):
            self._to_a(z).wait_send()
            pl.when(place.z != z)(lambda: self._to_z(z).wait_send())
            return carry

        lax.fori_loop(0, place.line, wait, 0)

    def settle(self):
        self.settle_b()
        self.settle_a()


class PackedGather(Gather):
    def __init__(self, place, dense, packed, compact, picks, mine, send_sem, recv_sem, twin_sems):
        self.place, self.dense, self.packed, self.compact = place, dense, packed, compact
        self.own_pick, self.other_pick = picks
        self.mine, self.fixed = mine, False
        self.send_sem, self.recv_sem = send_sem, recv_sem
        view = lambda slot: compact.at[slot, :, mine]
        self.twin = Twin(place, view, view, twin_sems.at[0], twin_sems.at[1])

    def view(self, slot):
        return self.dense.at[slot]

    def _to_b(self, slot):
        line = self.place.line
        return remote(
            self.packed.at[slot],
            self.compact.at[2 * line + slot, :, self.mine],
            self.send_sem.at[3 * line - 1 + slot],
            self.recv_sem.at[2 * line + slot],
            self.place.beside_b(),
        )

    def take_compact(self, slot):
        line = self.place.line
        self._to_b(slot - 2 * line).wait_recv()
        self.twin.start(slot)

    def take(self, slot):
        self._copy(slot, slot, 0, self.place.beside_b()).wait_recv()

    def pack(self, slot):
        block = self.dense[slot]
        self.packed[slot] = jnp.dot(self.other_pick[slot], block, preferred_element_type=F32).astype(BF16)
        self._to_b(slot).start()
        self.compact[slot, :, self.mine] = jnp.dot(
            self.own_pick[slot], block, preferred_element_type=F32
        ).astype(BF16)
        self.twin.start(slot)

    def start(self):
        place = self.place

        def reach(step):
            pl.when(place.z >= step)(lambda: self._to_z(-step).start())
            pl.when(place.z + step < place.line)(lambda: self._to_z(step).start())

        reach(1)
        self._to_a(place.z).start()
        for step in range(2, place.line):
            reach(step)
        self.pack(place.z)

    def along(self, step):
        def pass_on(z):
            self.take(z)
            self._to_a(z).start()
            self.pack(z)

        self.near(step, pass_on)

    def across(self, step):
        line = self.place.line

        def pass_on(z):
            self.take(line + z)
            self.pack(line + z)

        self.near(step, pass_on)


class PackedReduce(Reduce):
    def __init__(self, place, compact, picks, *rest):
        super().__init__(place, *rest)
        self.compact = compact
        self.own_pick, self.other_pick = picks

    def _to_b(self, k):
        line = self.place.line
        return self._copy(self.compact.at[2 * line + k], self.from_b.at[k], k, self.place.beside_b())

    def fold_b(self, k):
        self._to_b(k).wait_recv()
        own = contract_rows(self.own_pick[k], self.compact[k])
        self.parts[k] = (own + contract_rows(self.other_pick[k], self.from_b[k])).astype(BF16)


def selections(place, notes, own_pick, other_pick, gates=None):
    line = place.line
    cap, length = own_pick.shape[1:]
    rows = [notes[part_of(place, slot)][0:1, :] for slot in range(4 * line)]
    for slot in range(2 * line):
        note = notes[part_of(place, slot)]
        rows.append(jnp.where(place.core == 0, note[3:4, :], note[4:5, :]))
    before = lax.broadcasted_iota(jnp.int32, (length, length), 0) < lax.broadcasted_iota(
        jnp.int32, (length, length), 1
    )
    weights = jnp.concatenate(rows, axis=0)
    rank = jnp.dot(
        jnp.where(weights > 0.0, 1.0, 0.0).astype(BF16),
        jnp.where(before, 1.0, 0.0).astype(BF16),
        preferred_element_type=F32,
    )
    rank = jnp.where(weights > 0.0, rank, -1.0)
    number = lax.broadcasted_iota(jnp.int32, (cap, length), 0).astype(F32)
    for i in range(len(rows)):
        pick = jnp.where(rank[i : i + 1, :] == number, 1.0, 0.0)
        if i >= 4 * line:
            other_pick[i - 4 * line] = pick.astype(BF16)
            continue
        own_pick[i] = pick.astype(BF16)
        if gates is not None:
            gates[cap * i : cap * (i + 1), :] = jnp.sum(pick * rows[i], axis=1, keepdims=True)


AHEAD = 8


class Reductions:
    def __init__(self, reduces, finish):
        self.reduces, self.finish = reduces, finish
        self.at = self.sent = self.limit = 0
        line = self.line = reduces[0].place.line
        self.ks = [line + z for z in ends_first(line)] + ends_first(line)
        self.steps = [(i, k) for i in range(len(reduces)) for k in self.ks]

    def ready(self, number):
        self.limit = 2 * self.line * number
        self._send()

    def _send(self):
        while self.sent < min(self.at + AHEAD, self.limit):
            i, k = self.steps[self.sent]
            self.reduces[i].send_b(k)
            self.sent += 1

    def run(self, number):
        for _ in range(number):
            self._step()

    def _step(self):
        i, k = self.steps[self.at]
        self.at += 1
        self._send()
        self.reduces[i].fold_b(k)
        if k >= self.line:
            self.reduces[i].send_a(k - self.line)
        if k == self.ks[self.line - 1] and i > 0:
            self.reduces[i - 1].finish_line()
        if k == self.ks[-1] and i > 0:
            self.finish(i - 1)

    def complete(self):
        self.run(len(self.steps) - self.at)
        self.reduces[-1].finish_line()
        self.finish(len(self.reduces) - 1)


def reduce_scratch(line, block):
    return [
        pltpu.VMEM((2 * line, *block), BF16),
        pltpu.VMEM((line, *block), BF16),
        pltpu.VMEM((line, *block), BF16),
        pltpu.SemaphoreType.DMA((4 * line,)),
        pltpu.SemaphoreType.DMA((4 * line,)),
    ]


def ends_first(line):
    order = []
    for i in range((line + 1) // 2):
        order += [i] if i == line - 1 - i else [i, line - 1 - i]
    return order


def part_of(place, slot):
    line = place.line
    group, z = slot // line, slot % line
    flip_a, flip_b = group % 2, group // 2
    a = place.a + flip_a * (1 - 2 * place.a)
    b = place.b + flip_b * (1 - 2 * place.b)
    return place.part(z, a, b)


def halves(place, width):
    half = width // 2
    mine = pl.ds(pl.multiple_of(place.core * half, 128), half)
    theirs = pl.ds(pl.multiple_of((1 - place.core) * half, 128), half)
    return mine, theirs


def place_half(chunk, have, want, lane):
    chunk = chunk if have == want else pltpu.roll(chunk, HEAD_SIZE, 1)
    return jnp.where(lane // HEAD_SIZE == want, chunk, 0.0)


def rope_chunk(chunk, tables, sign):
    ahead = pltpu.roll(chunk, 128 - HEAD_SIZE // 2, 1)
    behind = pltpu.roll(chunk, HEAD_SIZE // 2, 1)
    return chunk * tables[0] + sign * (ahead * tables[1] + behind * tables[2])


def chunk_of(ref, j):
    return ref[:, 128 * j : 128 * (j + 1)]


def pair_of(ref, j, group_size, lane):
    both = []
    for half in (0, 1):
        group = (2 * j + half) // group_size
        both.append(place_half(chunk_of(ref, group // 2).astype(F32), group % 2, half, lane))
    return jnp.concatenate(both, axis=0).astype(BF16)


def spread_gains(notes, shard, width):
    total = jnp.zeros((8, width), F32)
    for p in range(notes.shape[0]):
        row = jnp.concatenate([notes[p], jnp.zeros((8, width - 128), F32)], axis=1)
        total += pltpu.roll(row, shard * p, 1) if p else row
    return total


def gate_table(logits, ids, experts):
    expo = jnp.exp(logits - jnp.max(logits, axis=0, keepdims=True))
    probs = expo / jnp.sum(expo, axis=0, keepdims=True)
    top, length = logits.shape
    expert = lax.broadcasted_iota(jnp.int32, (experts, length), 0)
    table = jnp.zeros((experts, length), F32)
    for c in range(top):
        table += jnp.where(ids[c : c + 1, :] == expert, probs[c : c + 1, :], 0.0)
    return table


def write_notes(note_ref, gates, gains):
    shard = gains[0].shape[1]
    row = lax.broadcasted_iota(jnp.int32, (8, 128), 0)
    pad = jnp.zeros((1, 128 - shard), F32)
    shared = jnp.zeros((8, 128), F32)
    for i, gain in enumerate(gains):
        shared = jnp.where(row == i + 1, jnp.concatenate([gain, pad], axis=1), shared)
    for p in range(note_ref.shape[0]):
        tile = shared
        for at, e in ((0, p), (3, p + 1 - 2 * (p % 2)), (4, p + 2 - 4 * (p // 2 % 2))):
            tile = jnp.where(row == at, gates[e : e + 1, :], tile)
        note_ref[p] = tile


def tree_tables(segments, parents, length):
    row = lax.broadcasted_iota(jnp.int32, (length, length), 0)
    lane = lax.broadcasted_iota(jnp.int32, (length, length), 1)

    def total(x):
        return jnp.sum(x.astype(F32), axis=1, keepdims=True)

    own_row = segments.astype(F32)
    own = total(jnp.where(row == lane, own_row, 0.0))
    kinds = parents.shape[1]
    kind = lax.broadcasted_iota(jnp.int32, (length, kinds), 1).astype(F32)
    above = parents.astype(F32)
    parent = total(jnp.where(kind == own, above, 0.0))
    grand = total(jnp.where(kind == parent, above, 0.0))
    in_parent, in_grand = own_row == parent, own_row == grand
    start = total(jnp.where(own_row < own, 1.0, 0.0))
    offset = jnp.where(own != 0.0, total(jnp.where(in_parent, 1.0, 0.0)), 0.0)
    offset += jnp.where(parent != 0.0, total(jnp.where(in_grand, 1.0, 0.0)), 0.0)
    place = lax.broadcasted_iota(jnp.int32, (length, 1), 0).astype(F32)
    linked = jnp.logical_or(own_row == own, jnp.logical_or(in_parent, in_grand))
    return place - start + offset, jnp.logical_and(linked, lane <= row)


def write_tables(tables_ref, position):
    lane = lax.broadcasted_iota(jnp.int32, (1, 128), 1)
    half = HEAD_SIZE // 2
    frequency = THETA ** ((lane % half).astype(F32) * (-2.0 / HEAD_SIZE))
    angles = position * frequency
    sine = jnp.sin(angles)
    first = lane % HEAD_SIZE < half
    tables_ref[0] = jnp.cos(angles)
    tables_ref[1] = jnp.where(first, -sine, 0.0)
    tables_ref[2] = jnp.where(first, 0.0, sine)


def forward_kernel(
    line,
    group_size,
    tokens_ref,
    query_ref,
    key_ref,
    value_ref,
    out_ref,
    cot_ref,
    gain_a_ref,
    gain_m_ref,
    logits_ref,
    ids_ref,
    segments_ref,
    parents_ref,
    moe_in_ref,
    hidden_ref,
    normed_ref,
    head_out_ref,
    queries_ref,
    keys_ref,
    values_ref,
    probs_ref,
    peak_ref,
    tables_ref,
    gains_ref,
    notes,
    query_keep,
    key_keep,
    value_keep,
    out_keep,
    cot_keep,
    query_all,
    key_all,
    value_all,
    out_all,
    cot_dense,
    cot_packed,
    cot_all,
    own_pick,
    other_pick,
    mix_mine,
    mix_other,
    note_ref,
    sends,
    recvs,
    note_send,
    note_recv,
    twin_sems,
    local_sems,
    keep_sems,
    mix_sems,
):
    place = Place(line)
    count = 4 * line
    length, width = tokens_ref.shape
    shard, q_cols = query_ref.shape
    chunks = q_cols // 128
    span, _ = halves(place, width)
    own = []
    blocks = ((query_ref, query_all), (key_ref, key_all), (value_ref, value_all), (out_ref, out_all))
    for i, (src, dst) in enumerate(blocks):
        own.append(pltpu.make_async_copy(src, dst.at[place.me], local_sems.at[i]))
    own.append(pltpu.make_async_copy(cot_ref.at[:, span], cot_dense.at[place.z], local_sems.at[4]))
    for c in own:
        c.start()
    enter(place)
    note = Notes(place, note_ref, notes, note_send, note_recv, False)
    for c in own:
        c.wait()
    gathers = [
        Gather(place, lambda s, ref=ref: ref.at[part_of(place, s)], sends.at[i], recvs.at[i], True)
        for i, ref in enumerate((query_all, key_all, value_all, out_all))
    ]
    picks = (own_pick, other_pick)
    cot = PackedGather(place, cot_dense, cot_packed, cot_all, picks, span, sends.at[4], recvs.at[4], twin_sems)
    twin = cot.twin
    out = gathers[3]
    for g in gathers[:3]:
        g.start()
    gains = [g[...].astype(F32) for g in (gain_a_ref, gain_m_ref)]
    write_notes(note_ref, gate_table(logits_ref[...], ids_ref[...], count), gains)
    note.start()
    inputs = tokens_ref[...].astype(F32)
    inv_attn = lax.rsqrt(jnp.mean(inputs * inputs, axis=1, keepdims=True) + EPSILON)
    for g in gathers[:3]:
        g.along(1)
    note.finish()
    gains_ref[...] = spread_gains(notes, shard, width)
    normed_ref[...] = (inputs * inv_attn * gains_ref[1:2, :]).astype(BF16)
    for g in gathers[:3]:
        g.across(0)
    position, allowed = tree_tables(segments_ref[...], parents_ref[...], length)
    write_tables(tables_ref, position)
    selections(place, notes, own_pick, other_pick)
    for step in range(2, line + 1):
        for g in gathers[:3]:
            if step < line:
                g.along(step)
            g.across(step - 1)
        if step == line - 1:
            out.start()
            cot.start()
    for g in gathers[:3]:
        g.take_rest()
    normed = normed_ref[...]
    tables = [tables_ref[i] for i in range(3)]
    query_lin = jnp.dot(normed, query_all[...].reshape(width, q_cols), preferred_element_type=F32)
    for j in range(chunks):
        queries_ref[:, 128 * j : 128 * (j + 1)] = rope_chunk(
            query_lin[:, 128 * j : 128 * (j + 1)], tables, 1.0
        ).astype(BF16)
    kv_cols = key_ref.shape[1]
    key_lin = jnp.dot(normed, key_all[...].reshape(width, kv_cols), preferred_element_type=F32)
    for j in range(kv_cols // 128):
        keys_ref[:, 128 * j : 128 * (j + 1)] = rope_chunk(
            key_lin[:, 128 * j : 128 * (j + 1)], tables, 1.0
        ).astype(BF16)
    values_ref[...] = jnp.dot(
        normed, value_all[...].reshape(width, kv_cols), preferred_element_type=F32
    ).astype(BF16)
    lane = lax.broadcasted_iota(jnp.int32, (length, 128), 1)
    small_lane = lax.broadcasted_iota(jnp.int32, (8, 128), 1)
    peaks = jnp.zeros((8, 128), F32)
    for step in range(1, line + 1):
        if step < line:
            out.along(step)
            cot.along(step)
        out.across(step - 1)
        cot.across(step - 1)
    for j in range(chunks):
        both = contract_cols(chunk_of(queries_ref, j), pair_of(keys_ref, j, group_size, lane)) * SCORE_SCALE
        low = []
        for half in (0, 1):
            scores = jnp.where(allowed, both[:, length * half : length * (half + 1)], NEGATIVE)
            row_max = jnp.max(scores, axis=1, keepdims=True)
            peak = jnp.max(row_max, axis=0, keepdims=True)
            peaks = jnp.where(small_lane == 2 * j + half, peak, peaks)
            expo = jnp.exp(scores - row_max)
            prob = expo / jnp.sum(expo, axis=1, keepdims=True)
            probs_ref[j, :, length * half : length * (half + 1)] = prob
            low.append(prob.astype(BF16))
        mixed = jnp.dot(
            jnp.concatenate(low, axis=1),
            pair_of(values_ref, j, group_size, lane),
            preferred_element_type=F32,
        )
        head_out_ref[:, 128 * j : 128 * (j + 1)] = mixed.astype(BF16)
    peak_ref[...] = peaks
    keeps = [
        pltpu.make_async_copy(src, dst, keep_sems.at[i])
        for i, (src, dst) in enumerate(
            (
                (query_all, query_keep),
                (key_all, key_keep),
                (value_all, value_keep),
                (out_all, out_keep),
                (cot_all, cot_keep),
            )
        )
    ]
    for c in keeps[:3]:
        c.start()
    out.take_rest()
    keeps[3].start()
    mix_mine[...] = contract_cols(head_out_ref[...], out_all[...].reshape(width, q_cols))
    swap = remote(mix_mine, mix_other, mix_sems.at[0], mix_sems.at[1], place.twin())
    swap.start()
    swap.wait()
    hidden = tokens_ref[...].astype(F32) + RESIDUAL * (mix_mine[...] + mix_other[...])
    hidden_ref[...] = hidden
    inv_moe = lax.rsqrt(jnp.mean(hidden * hidden, axis=1, keepdims=True) + EPSILON)
    moe_in_ref[...] = (hidden * inv_moe * gains_ref[2:3, :]).astype(BF16)

    def rest(slot, carry):
        cot.take_compact(slot)
        return carry

    lax.fori_loop(2 * line, count, rest, 0)
    for g in gathers + [cot]:
        g.settle()

    def other(slot, carry):
        twin.wait_send(slot)
        twin.take(slot)
        return carry

    lax.fori_loop(0, count, other, 0)
    keeps[4].start()
    for c in keeps:
        c.wait()


ANY = pl.BlockSpec(memory_space=pl.ANY)
IN_VMEM = pl.BlockSpec(memory_space=pltpu.VMEM)


def params(number):
    return pltpu.CompilerParams(
        collective_id=number, has_side_effects=True, vmem_limit_bytes=56 * 2**20
    )


def capacity_of(length, experts):
    most = 4 * (9 * length * TOP // (32 * experts))
    return min(-(-most // 16) * 16, length)


def run_forward(line, group_size, tokens, query, key, value, out, cotangent, *small):
    count = 4 * line
    length, width = tokens.shape
    q_cols, kv_cols = query.shape[1], key.shape[1]
    half, cap = width // 2, capacity_of(length, count)
    blocks = [x.shape for x in (query, key, value, out)] + [(cap, width)]
    shape = jax.ShapeDtypeStruct
    outs = [
        shape((length, width), BF16),
        shape((length, width), F32),
        shape((length, width), BF16),
        shape((length, q_cols), BF16),
        shape((length, q_cols), BF16),
        shape((length, kv_cols), BF16),
        shape((length, kv_cols), BF16),
        shape((q_cols // 128, length, 2 * length), F32),
        shape((8, 128), F32),
        shape((3, length, 128), F32),
        shape((8, width), F32),
        shape((count, 8, 128), F32),
    ]
    return pl.pallas_call(
        functools.partial(forward_kernel, line, group_size),
        out_shape=outs + [shape((count, *s), BF16) for s in blocks],
        in_specs=[IN_VMEM] + [ANY] * 5 + [IN_VMEM] * len(small),
        out_specs=[IN_VMEM] * len(outs) + [ANY] * 5,
        scratch_shapes=[pltpu.VMEM((count, *s), BF16) for s in blocks[:4]]
        + [
            pltpu.VMEM((2 * line, length, half), BF16),
            pltpu.VMEM((2 * line, cap, half), BF16),
            pltpu.VMEM((count, cap, width), BF16),
            pltpu.VMEM((count, cap, length), BF16),
            pltpu.VMEM((2 * line, cap, length), BF16),
            pltpu.VMEM((length, width), F32),
            pltpu.VMEM((length, width), F32),
            pltpu.VMEM((count, 8, 128), F32),
            pltpu.SemaphoreType.DMA((5, 5 * line)),
            pltpu.SemaphoreType.DMA((5, count)),
            pltpu.SemaphoreType.DMA((count,)),
            pltpu.SemaphoreType.DMA((count,)),
            pltpu.SemaphoreType.DMA((2, count)),
            pltpu.SemaphoreType.DMA((5,)),
            pltpu.SemaphoreType.DMA((5,)),
            pltpu.SemaphoreType.DMA((2,)),
        ],
        compiler_params=params(0),
        name="run_forward",
    )(tokens, query, key, value, out, cotangent, *small)


def experts_kernel(
    line,
    rows_ref,
    cot_ref,
    notes_ref,
    gate_ref,
    up_ref,
    down_ref,
    d_rows_ref,
    mix_ref,
    grad_gate_ref,
    grad_up_ref,
    grad_down_ref,
    dense,
    packed,
    rows,
    cots,
    own_pick,
    other_pick,
    gates,
    active,
    d_gate,
    d_up,
    d_active,
    grad_stage,
    mix_stage,
    grad_compact,
    mix_compact,
    grad_dense,
    mix_dense,
    grads,
    total,
    grad_from_b,
    mix_from_b,
    from_a,
    from_z,
    reduce_sems,
    gather_send,
    gather_recv,
    twin_sems,
    load_sems,
    last_sems,
    store_sems,
):
    place = Place(line)
    count = 4 * line
    cap, width = rows.shape[1:]
    tile_rows = line * cap
    mine, theirs = halves(place, width)
    load = pltpu.make_async_copy(cot_ref, cots, load_sems)
    load.start()
    dense[place.z] = rows_ref[:, mine]
    picks = (own_pick, other_pick)
    selections(place, notes_ref, own_pick, other_pick, gates)
    enter(place)
    gather = PackedGather(place, dense, packed, rows, picks, mine, gather_send, gather_recv, twin_sems)
    grad_twin = Twin(
        place,
        lambda s: grad_stage.at[s, :, theirs],
        lambda s: grad_compact.at[s],
        twin_sems.at[2],
        twin_sems.at[3],
    )
    mix_twin = Twin(
        place, lambda s: mix_stage.at[s, :, theirs], lambda s: mix_compact.at[s], twin_sems.at[4], twin_sems.at[5]
    )
    reduce = PackedReduce(
        place, grad_compact, picks, grad_dense, grad_from_b, from_a, from_z, reduce_sems.at[0], reduce_sems.at[1]
    )
    mix_reduce = PackedReduce(
        place, mix_compact, picks, mix_dense, mix_from_b, None, None, reduce_sems.at[2], reduce_sems.at[3]
    )

    def group_of(group):
        return pl.ds(line * group, line), pl.ds(tile_rows * group, tile_rows)

    def slots_of(group):
        return [line * group + z for z in range(line)]

    def ahead(group):
        some, flat = group_of(group)
        cot = cots[some].reshape(tile_rows, width).astype(F32)
        d_out = (gates[flat, :] * (RESIDUAL * cot)).astype(BF16)
        cots[some] = d_out.reshape(line, cap, width)
        d_active[flat, :] = jnp.dot(d_out, down_ref[...], preferred_element_type=F32)

    def work(group):
        some, flat = group_of(group)
        for slot in slots_of(group):
            gather.twin.take(slot)
        x = rows[some].reshape(tile_rows, width)
        gate_pre = jnp.dot(x, gate_ref[...], preferred_element_type=F32)
        up_pre = jnp.dot(x, up_ref[...], preferred_element_type=F32)
        sigmoid = 1.0 / (1.0 + jnp.exp(-gate_pre))
        silu = gate_pre * sigmoid
        active[flat, :] = (silu * up_pre).astype(BF16)
        d_act = d_active[flat, :]
        d_g = (d_act * up_pre * sigmoid * (1.0 + gate_pre * (1.0 - sigmoid))).astype(BF16)
        d_u = (d_act * silu).astype(BF16)
        d_gate[flat, :] = d_g
        d_up[flat, :] = d_u
        d_in = contract_cols(d_g, gate_ref[...]) + contract_cols(d_u, up_ref[...])
        grad_stage[some] = d_in.astype(BF16).reshape(line, cap, width)
        for slot in slots_of(group):
            grad_twin.start(slot)

    def mix_work(group):
        some, flat = group_of(group)
        mix = gates[flat, :] * contract_cols(active[flat, :], down_ref[...])
        mix_stage[some] = mix.astype(BF16).reshape(line, cap, width)
        for slot in slots_of(group):
            mix_twin.start(slot)

    def fold(twin, stage, compact, group, send=None):
        def one(slot, carry):
            twin.take(slot)
            compact[slot] = (compact[slot].astype(F32) + stage[slot, :, mine].astype(F32)).astype(BF16)
            if send is not None:
                send(slot - 2 * line)
            return carry

        lax.fori_loop(line * group, line * (group + 1), one, 0)

    def take_group(group):
        for slot in slots_of(group):
            gather.take_compact(slot)

    def weight_grad(number, i):
        left, right = ((cots, active), (rows, d_gate), (rows, d_up))[number]
        left = left.reshape(count * cap, width)
        span = pl.ds(512 * i, 512)
        grads[number, span, :] = contract_rows(left[:, span], right[...])

    stores = []

    def store(number):
        out_ref = (grad_down_ref, grad_gate_ref, grad_up_ref)[number]
        stores.append(pltpu.make_async_copy(grads.at[number], out_ref, store_sems.at[number]))
        stores[-1].start()

    grad_fold = functools.partial(fold, grad_twin, grad_stage, grad_compact)
    mix_fold = functools.partial(fold, mix_twin, mix_stage, mix_compact)
    gather.start()
    load.wait()
    for at in range(max(line, 4)):
        if at < 4:
            ahead(at)
        if at < line:
            if at + 1 < line:
                gather.along(at + 1)
            gather.across(at)
    work(0)
    take_group(2)
    work(2)
    work(1)
    take_group(3)
    grad_fold(2, reduce.send_b)
    work(3)
    grad_fold(3, reduce.send_b)
    mix_work(1)
    grad_fold(0)
    mix_work(2)
    grad_fold(1)
    mix_work(3)
    mix_fold(2, mix_reduce.send_b)
    mix_work(0)
    pieces = width // 512
    order = ends_first(line)
    for z in order:
        reduce.fold_b(z)
    weight_grad(0, 0)
    for at, z in enumerate(order):
        reduce.fold_b(line + z)
        reduce.send_a(z)
    mix_fold(3, mix_reduce.send_b)
    for i in range(1, pieces):
        weight_grad(0, i)
    store(0)
    reduce.finish_line()
    for i in range(pieces):
        weight_grad(1, i)
    store(1)
    mix_fold(0)
    mix_fold(1)
    reduce.result(total)
    d_rows_ref[:, mine] = total[...]
    last = remote(total, d_rows_ref.at[:, mine], last_sems.at[0], last_sems.at[1], place.twin())
    last.start()
    for i in range(pieces):
        weight_grad(2, i)
    store(2)
    for k in range(2 * line):
        mix_reduce.fold_b(k)
    stores.append(pltpu.make_async_copy(mix_dense, mix_ref, store_sems.at[3]))
    stores[-1].start()
    reduce.settle()
    mix_reduce.settle_b()
    gather.settle()

    def settle(slot, carry):
        gather.twin.wait_send(slot)
        grad_twin.wait_send(slot)
        mix_twin.wait_send(slot)
        return carry

    lax.fori_loop(0, count, settle, 0)
    for c in stores:
        c.wait()
    last.wait()


def run_experts(line, rows, cots, notes, gate, up, down):
    count = 4 * line
    length, width = rows.shape
    cap = cots.shape[1]
    half, hidden = width // 2, gate.shape[1]
    grad = jax.ShapeDtypeStruct((width, hidden), F32)
    return pl.pallas_call(
        functools.partial(experts_kernel, line),
        out_shape=[
            jax.ShapeDtypeStruct((length, width), F32),
            jax.ShapeDtypeStruct((2 * line, length, half), BF16),
            grad,
            grad,
            grad,
        ],
        in_specs=[IN_VMEM, ANY, IN_VMEM, IN_VMEM, IN_VMEM, IN_VMEM],
        out_specs=[IN_VMEM, ANY, ANY, ANY, ANY],
        scratch_shapes=[
            pltpu.VMEM((2 * line, length, half), BF16),
            pltpu.VMEM((2 * line, cap, half), BF16),
            pltpu.VMEM((count, cap, width), BF16),
            pltpu.VMEM((count, cap, width), BF16),
            pltpu.VMEM((count, cap, length), BF16),
            pltpu.VMEM((2 * line, cap, length), BF16),
            pltpu.VMEM((count * cap, 1), F32),
            pltpu.VMEM((count * cap, hidden), BF16),
            pltpu.VMEM((count * cap, hidden), BF16),
            pltpu.VMEM((count * cap, hidden), BF16),
            pltpu.VMEM((count * cap, hidden), F32),
            pltpu.VMEM((count, cap, width), BF16),
            pltpu.VMEM((count, cap, width), BF16),
            pltpu.VMEM((count, cap, half), BF16),
            pltpu.VMEM((count, cap, half), BF16),
            pltpu.VMEM((2 * line, length, half), BF16),
            pltpu.VMEM((2 * line, length, half), BF16),
            pltpu.VMEM((3, width, hidden), F32),
            pltpu.VMEM((length, half), F32),
            pltpu.VMEM((2 * line, cap, half), BF16),
            pltpu.VMEM((2 * line, cap, half), BF16),
            pltpu.VMEM((line, length, half), BF16),
            pltpu.VMEM((line, length, half), BF16),
            pltpu.SemaphoreType.DMA((4, 4 * line)),
            pltpu.SemaphoreType.DMA((5 * line,)),
            pltpu.SemaphoreType.DMA((count,)),
            pltpu.SemaphoreType.DMA((6, count)),
            pltpu.SemaphoreType.DMA,
            pltpu.SemaphoreType.DMA((2,)),
            pltpu.SemaphoreType.DMA((4,)),
        ],
        compiler_params=params(2),
        name="run_experts",
    )(rows, cots, notes, gate, up, down)


def backward_kernel(
    line,
    group_size,
    tokens_ref,
    hidden_ref,
    d_rows_ref,
    cot_ref,
    normed_ref,
    head_out_ref,
    queries_ref,
    keys_ref,
    values_ref,
    probs_ref,
    gains_ref,
    peak_ref,
    tables_ref,
    query_keep,
    key_keep,
    value_keep,
    out_keep,
    mix_ref,
    input_grad_ref,
    output_ref,
    query_sum,
    key_sum,
    value_sum,
    out_sum,
    notes,
    *scratch,
):
    place = Place(line)
    count = 4 * line
    length, width = tokens_ref.shape
    q_cols, kv_cols = queries_ref.shape[1], keys_ref.shape[1]
    shard = width // count
    chunks = q_cols // 128
    (query_all, key_all, value_all, out_all), work = scratch[:4], scratch[4:9]
    rest = scratch[9:34]
    (
        total,
        d_heads,
        d_query,
        d_key,
        d_value,
        part_mine,
        part_other,
        d_hidden_keep,
        mix_total,
        note,
        weight_sems,
        load_sems,
        last_sems,
        part_sems,
        note_sends,
        note_recvs,
    ) = scratch[34:]
    by_part = lambda slot: part_of(place, slot)
    reduces = [
        Reduce(place, work[i], *rest[5 * i : 5 * i + 5], *(() if i == 4 else (by_part,))) for i in range(5)
    ]

    def load(slot):
        return pltpu.make_async_copy(mix_ref.at[slot], work[4].at[slot], load_sems.at[slot])

    def begin(slot, carry):
        load(slot).start()
        return carry

    def loaded(slot, carry):
        load(slot).wait()
        return carry

    lax.fori_loop(0, 2 * line, begin, 0)
    weights = [
        pltpu.make_async_copy(src, dst, weight_sems.at[i])
        for i, (src, dst) in enumerate(
            ((out_keep, out_all), (query_keep, query_all), (key_keep, key_all), (value_keep, value_all))
        )
    ]
    for c in weights:
        c.start()
    enter(place)
    lax.fori_loop(0, 2 * line, loaded, 0)
    mine, theirs = halves(place, width)
    outs = (query_sum, key_sum, value_sum, out_sum, total)
    order = (3, 0, 1, 2)
    mix = reduces[4]
    for z in ends_first(line):
        mix.send_a(z)
    last = remote(total, mix_total.at[:, mine], last_sems.at[0], last_sems.at[1], place.twin())

    def finish(at):
        i = order[at]
        reduces[i].result(outs[i])

    run = Reductions([reduces[i] for i in order], finish)
    hidden = hidden_ref[...]
    inv_moe = lax.rsqrt(jnp.mean(hidden * hidden, axis=1, keepdims=True) + EPSILON)
    unit_moe = hidden * inv_moe
    d_rows = d_rows_ref[...]
    scaled = d_rows * gains_ref[2:3, :]
    d_hidden = cot_ref[...].astype(F32) + inv_moe * (
        scaled - unit_moe * jnp.mean(scaled * unit_moe, axis=1, keepdims=True)
    )
    d_hidden_keep[...] = d_hidden
    moe_gain = jnp.sum(d_rows * unit_moe, axis=0, keepdims=True)
    d_attn = (RESIDUAL * d_hidden).astype(BF16)
    work[3][...] = contract_rows(d_attn, head_out_ref[...]).astype(BF16).reshape(count, shard, q_cols)
    run.ready(1)
    weights[0].wait()
    d_heads[...] = jnp.dot(
        d_attn, out_all[...].reshape(width, q_cols), preferred_element_type=F32
    ).astype(BF16)
    lane = lax.broadcasted_iota(jnp.int32, (length, 128), 1)
    d_key[...] = jnp.zeros_like(d_key)
    d_value[...] = jnp.zeros_like(d_value)
    tables = [tables_ref[i] for i in range(3)]
    mix.finish_line()
    for j in range(chunks):
        d_out = chunk_of(d_heads, j)
        keys = pair_of(keys_ref, j, group_size, lane)
        d_prob = contract_cols(d_out, pair_of(values_ref, j, group_size, lane))
        low, d_scores = [], []
        for half in (0, 1):
            side = slice(length * half, length * (half + 1))
            prob = probs_ref[j, :, side]
            grad = d_prob[:, side]
            inner = jnp.sum(prob * grad, axis=1, keepdims=True)
            d_scores.append((prob * (grad - inner)).astype(BF16))
            low.append(prob.astype(BF16))
        d_scores = jnp.concatenate(d_scores, axis=1)
        d_values = contract_rows(jnp.concatenate(low, axis=1), d_out)
        d_keys = contract_rows(d_scores, chunk_of(queries_ref, j)) * SCORE_SCALE
        turned = rope_chunk(
            jnp.dot(d_scores, keys, preferred_element_type=F32) * SCORE_SCALE, tables, -1.0
        )
        d_query[:, 128 * j : 128 * (j + 1)] = turned.astype(BF16)
        for half in (0, 1):
            group = (2 * j + half) // group_size
            side = slice(length * half, length * (half + 1))
            cols = slice(128 * (group // 2), 128 * (group // 2 + 1))
            d_key[:, cols] += place_half(d_keys[side], half, group % 2, lane)
            d_value[:, cols] += place_half(d_values[side], half, group % 2, lane)
        run.run(1)
    normed = normed_ref[...]
    work[0][...] = contract_rows(normed, d_query[...]).astype(BF16).reshape(count, shard, q_cols)
    run.ready(2)
    d_key_lin = jnp.concatenate(
        [rope_chunk(chunk_of(d_key, j), tables, -1.0) for j in range(kv_cols // 128)], axis=1
    ).astype(BF16)
    d_value_lin = d_value[...].astype(BF16)
    run.run(2)
    work[1][...] = contract_rows(normed, d_key_lin).astype(BF16).reshape(count, shard, kv_cols)
    work[2][...] = contract_rows(normed, d_value_lin).astype(BF16).reshape(count, shard, kv_cols)
    run.ready(4)
    run.run(2)
    mix.result(total)
    mix_total[:, mine] = total[...]
    last.start()
    for c in weights[1:]:
        c.wait()
    part_mine[...] = (
        contract_cols(d_query[...], query_all[...].reshape(width, q_cols))
        + contract_cols(d_key_lin, key_all[...].reshape(width, kv_cols))
        + contract_cols(d_value_lin, value_all[...].reshape(width, kv_cols))
    )
    swap = remote(part_mine, part_other, part_sems.at[0], part_sems.at[1], place.twin())
    swap.start()
    run.run(4)
    swap.wait()
    d_normed = part_mine[...] + part_other[...]
    inputs = tokens_ref[...].astype(F32)
    inv_attn = lax.rsqrt(jnp.mean(inputs * inputs, axis=1, keepdims=True) + EPSILON)
    unit_attn = inputs * inv_attn
    scaled = d_normed * gains_ref[1:2, :]
    input_grad_ref[...] = d_hidden_keep[...] + inv_attn * (
        scaled - unit_attn * jnp.mean(scaled * unit_attn, axis=1, keepdims=True)
    )
    attn_gain = jnp.sum(d_normed * unit_attn, axis=0, keepdims=True)
    rows = jnp.concatenate([attn_gain, moe_gain, jnp.zeros((6, width), F32)], axis=0)
    row = lax.broadcasted_iota(jnp.int32, (8, 128), 0)
    peaks = jnp.broadcast_to(peak_ref[0:1, :], (8, 128))
    for p in range(count):
        turned = pltpu.roll(rows, width - shard * p, 1) if p else rows
        note[p] = jnp.where(row == 2, peaks, turned[:, :128])
    exchange = Notes(place, note, notes, note_sends, note_recvs, False)
    exchange.start()
    run.complete()
    for r in reduces[:4]:
        r.settle()
    mix.settle_a()
    last.wait()
    output_ref[...] = (hidden_ref[...] + RESIDUAL * mix_total[...]).astype(BF16)
    exchange.finish()


def run_backward(line, group_size, kept, keeps, mix):
    count = 4 * line
    tokens, queries, keys = kept[0], kept[6], kept[7]
    length, width = tokens.shape
    q_cols, kv_cols = queries.shape[1], keys.shape[1]
    blocks = [x.shape[1:] for x in keeps] + [mix.shape[1:]]
    half = width // 2
    shape = jax.ShapeDtypeStruct
    outs = (
        [shape((length, width), F32), shape((length, width), BF16)]
        + [shape(s, F32) for s in blocks[:4]]
        + [shape((count, 8, 128), F32)]
    )
    return pl.pallas_call(
        functools.partial(backward_kernel, line, group_size),
        out_shape=outs,
        in_specs=[IN_VMEM] * len(kept) + [ANY] * 5,
        out_specs=[IN_VMEM] * len(outs),
        scratch_shapes=[pltpu.VMEM(x.shape, BF16) for x in keeps]
        + [pltpu.VMEM((count, *s), BF16) for s in blocks[:4]]
        + [pltpu.VMEM(mix.shape, BF16)]
        + [x for s in blocks for x in reduce_scratch(line, s)]
        + [
            pltpu.VMEM((length, half), F32),
            pltpu.VMEM((length, q_cols), BF16),
            pltpu.VMEM((length, q_cols), BF16),
            pltpu.VMEM((length, kv_cols), F32),
            pltpu.VMEM((length, kv_cols), F32),
            pltpu.VMEM((length, width), F32),
            pltpu.VMEM((length, width), F32),
            pltpu.VMEM((length, width), F32),
            pltpu.VMEM((length, width), F32),
            pltpu.VMEM((count, 8, 128), F32),
            pltpu.SemaphoreType.DMA((4,)),
            pltpu.SemaphoreType.DMA((count,)),
            pltpu.SemaphoreType.DMA((2,)),
            pltpu.SemaphoreType.DMA((2,)),
            pltpu.SemaphoreType.DMA((count,)),
            pltpu.SemaphoreType.DMA((count,)),
        ],
        compiler_params=params(3),
        name="run_backward",
    )(*kept, *keeps, mix)


def finish_kernel(
    group_size,
    output_in,
    input_grad_in,
    query_in,
    key_in,
    value_in,
    out_in,
    notes,
    query_ref,
    key_ref,
    gate_in,
    up_in,
    down_in,
    output,
    input_grad,
    grad_query,
    grad_key,
    grad_value,
    grad_out,
    gain_a,
    gain_m,
    clipped_query,
    clipped_key,
    grad_gate,
    grad_up,
    grad_down,
    stage,
    sems,
):
    pairs = ((gate_in, grad_gate), (up_in, grad_up), (down_in, grad_down))
    takes = [pltpu.make_async_copy(src, stage.at[i], sems.at[0, i]) for i, (src, _) in enumerate(pairs)]
    copies = [pltpu.make_async_copy(stage.at[i], dst.at[0], sems.at[1, i]) for i, (_, dst) in enumerate(pairs)]
    for c in takes:
        c.start()
    output[...] = output_in[...]
    input_grad[...] = input_grad_in[...]
    grad_query[...] = query_in[...]
    grad_key[...] = key_in[...]
    grad_value[...] = value_in[...]
    grad_out[...] = out_in[...]
    for take, c in zip(takes, copies):
        take.wait()
        c.start()
    total, peaks = notes[0], notes[0]
    for p in range(1, notes.shape[0]):
        total = total + notes[p]
        peaks = jnp.maximum(peaks, notes[p])
    shard = gain_a.shape[1]
    gain_a[...] = total[0:1, :shard]
    gain_m[...] = total[1:2, :shard]
    factor = CLIP_LIMIT / jnp.maximum(peaks, CLIP_LIMIT)
    root = jnp.sqrt(factor)
    lane = lax.broadcasted_iota(jnp.int32, (8, 128), 1)

    def scale(h):
        return jnp.max(jnp.where(lane == h, root, 0.0), axis=1, keepdims=True)[2:3, :]

    heads = query_ref.shape[1] // HEAD_SIZE
    wide = lax.broadcasted_iota(jnp.int32, (1, 128), 1)
    scales = [scale(h) for h in range(heads)]
    for j in range(heads // 2):
        row = jnp.where(wide < HEAD_SIZE, scales[2 * j], scales[2 * j + 1])
        cols = slice(128 * j, 128 * (j + 1))
        clipped_query[:, cols] = query_ref[:, cols].astype(F32) * row
    least = [
        functools.reduce(jnp.minimum, scales[group_size * g : group_size * (g + 1)])
        for g in range(heads // group_size)
    ]
    for j in range(len(least) // 2):
        row = jnp.where(wide < HEAD_SIZE, least[2 * j], least[2 * j + 1])
        cols = slice(128 * j, 128 * (j + 1))
        clipped_key[:, cols] = key_ref[:, cols].astype(F32) * row
    for c in copies:
        c.wait()


def finish(group_size, found, notes, query, key, expert_grads):
    shape = jax.ShapeDtypeStruct
    shard = query.shape[0]
    outs = [shape(x.shape, x.dtype) for x in found] + [
        shape((1, shard), F32),
        shape((1, shard), F32),
        shape(query.shape, F32),
        shape(key.shape, F32),
    ]
    return pl.pallas_call(
        functools.partial(finish_kernel, group_size),
        out_shape=outs + [shape((1, *g.shape), F32) for g in expert_grads],
        in_specs=[IN_VMEM] * 9 + [ANY] * 3,
        out_specs=[IN_VMEM] * 10 + [ANY] * 3,
        scratch_shapes=[
            pltpu.VMEM((3, *expert_grads[0].shape), F32),
            pltpu.SemaphoreType.DMA((2, 3)),
        ],
        compiler_params=pltpu.CompilerParams(vmem_limit_bytes=56 * 2**20),
        name="finish",
    )(*found, notes, query, key, *expert_grads)


def on_device_dense(
    tokens,
    attn_norm_gain,
    w_query,
    key_projection,
    value_projection,
    w_out,
    moe_norm_gain,
    w_gate,
    w_up,
    w_down,
    router_logits,
    expert_ids,
    segment_ids,
    parents,
    cotangent,
):
    length, model_width = tokens.shape
    q_cols, kv_cols = w_query.shape[1], key_projection.shape[1]
    q_heads, kv_heads = q_cols // HEAD_SIZE, kv_cols // HEAD_SIZE
    group_size = q_heads // kv_heads
    count = lax.axis_size("dp")
    line = count // 4
    shard = attn_norm_gain.shape[0]
    (moe_in, hidden, normed, head_out, queries, keys, values, probs, peak, tables, gains, notes, *keeps, cots) = run_forward(
        line,
        group_size,
        tokens,
        w_query,
        key_projection,
        value_projection,
        w_out,
        cotangent,
        attn_norm_gain[None],
        moe_norm_gain[None],
        router_logits.T,
        expert_ids.T,
        segment_ids,
        parents,
    )
    d_moe_in, mix_parts, *expert_grads = run_experts(
        line, moe_in, cots, notes, w_gate[0], w_up[0], w_down[0]
    )
    kept = (tokens, hidden, d_moe_in, cotangent, normed, head_out, queries, keys, values, probs, gains, peak, tables)
    input_grad, output, *grads, sums = run_backward(line, group_size, kept, keeps, mix_parts)
    output, input_grad, gq, gk, gv, go, gain_a, gain_m, clipped_query, clipped_key, gg, gu, gd = finish(
        group_size, (output, input_grad, *grads), sums, w_query, key_projection, expert_grads
    )
    return (
        output,
        input_grad,
        gain_a[0],
        gq,
        gk,
        gv,
        go,
        gain_m[0],
        gg,
        gu,
        gd,
        clipped_query,
        clipped_key,
    )


DENSE_BYTES = 8 * 2**20


def on_device(*args):
    tokens, w_gate = args[0], args[7]
    count, ranks = lax.axis_size("dp"), lax.axis_size("tensor")
    rows_bytes = count * tokens.shape[0] * tokens.shape[1] * 2
    whole_experts = w_gate.shape[2] * ranks == FFE
    dense = whole_experts and ranks == 2 and count % 8 == 0 and rows_bytes <= DENSE_BYTES
    return on_device_dense(*args) if dense else on_device_general(*args)


def solution(mesh):
    in_specs = (
        P("dp", None),
        P("dp"),
        P("dp", "tensor"),
        P("dp", "tensor"),
        P("dp", "tensor"),
        P("dp", "tensor"),
        P("dp"),
        P("dp", None, "tensor"),
        P("dp", None, "tensor"),
        P("dp", None, "tensor"),
        P("dp", None),
        P("dp", None),
        P("dp", None),
        P("dp", None),
        P("dp", None),
    )
    out_specs = (
        P("dp", None),
        P("dp", None),
        P("dp"),
        P("dp", "tensor"),
        P("dp", "tensor"),
        P("dp", "tensor"),
        P("dp", "tensor"),
        P("dp"),
        P("dp", None, "tensor"),
        P("dp", None, "tensor"),
        P("dp", None, "tensor"),
        P("dp", "tensor"),
        P("dp", "tensor"),
    )
    return jax.shard_map(
        on_device, mesh=mesh, in_specs=in_specs, out_specs=out_specs, check_vma=False
    )
```

```python
import functools

import jax
import jax.numpy as jnp
from jax import lax
from jax.experimental import pallas as pl
from jax.experimental.pallas import tpu as pltpu
from jax.sharding import PartitionSpec as P

HEAD_SIZE = 64
FFE = 512
TOP = 8


EPSILON = 1e-06
SCORE_SCALE = 1.0 / 64.0
RESIDUAL = 0.22
THETA = 10000.0
CLIP_LIMIT = 2.0
NEGATIVE = -1e30


def tree_layout(seg_row, par_row):
    tree_length = seg_row.shape[0]
    seg_count = par_row.shape[0]
    seg_index = jnp.arange(seg_count, dtype=jnp.int32)
    member = (seg_row[:, None] == seg_index[None, :]).astype(jnp.int32)
    seg_len = jnp.sum(member, axis=0)
    seg_start = jnp.sum(jnp.where(seg_index[:, None] > seg_index[None, :], seg_len[None, :], 0), axis=1)
    parent_hot = (par_row[:, None] == seg_index[None, :]).astype(jnp.int32)
    grand_parent = jnp.sum(parent_hot * par_row[None, :], axis=1)
    grand_hot = (grand_parent[:, None] == seg_index[None, :]).astype(jnp.int32)
    parent_len = jnp.sum(parent_hot * seg_len[None, :], axis=1)
    grand_len = jnp.sum(grand_hot * seg_len[None, :], axis=1)
    offset = jnp.where(seg_index != 0, parent_len, 0) + jnp.where(par_row != 0, grand_len, 0)
    tok_start = jnp.sum(member * seg_start[None, :], axis=1)
    tok_offset = jnp.sum(member * offset[None, :], axis=1)
    places = jnp.arange(tree_length, dtype=jnp.int32)
    position = (places - tok_start + tok_offset).astype(jnp.float32)
    identity = (seg_index[:, None] == seg_index[None, :]).astype(jnp.int32)
    ancestor = jnp.minimum(identity + parent_hot + grand_hot, 1)
    reached = jnp.dot(member, ancestor)
    linked = jnp.dot(reached, member.T) > 0
    allowed = linked & (places[None, :] <= places[:, None])
    return (position, allowed)


def rope_tables(position, head_dim):
    half_dim = head_dim // 2
    frequency = THETA ** (-2.0 * jnp.arange(half_dim, dtype=jnp.float32) / head_dim)
    angles = position[:, None] * frequency[None, :]
    return (jnp.cos(angles)[:, None, :], jnp.sin(angles)[:, None, :])


def apply_rotary(values_in, cosine_table, sine_values):
    half_dim = values_in.shape[-1] // 2
    first_half = values_in[..., :half_dim]
    second_half = values_in[..., half_dim:]
    return jnp.concatenate(
        [
            first_half * cosine_table - second_half * sine_values,
            second_half * cosine_table + first_half * sine_values,
        ],
        axis=-1,
    )


def rotate_back(grads_in, cosine_table, sine_values):
    half_dim = grads_in.shape[-1] // 2
    first_half = grads_in[..., :half_dim]
    second_half = grads_in[..., half_dim:]
    return jnp.concatenate(
        [
            first_half * cosine_table + second_half * sine_values,
            second_half * cosine_table - first_half * sine_values,
        ],
        axis=-1,
    )


def slot_tables(routes, experts, capacity):
    flat_ids = routes.reshape(-1)
    row_count = flat_ids.shape[0]
    member = (flat_ids[:, None] == jnp.arange(experts, dtype=jnp.int32)[None, :]).astype(jnp.int32)
    row_total = flat_ids.shape[0]
    before = jnp.dot((jnp.arange(row_total)[:, None] > jnp.arange(row_total)[None, :]).astype(jnp.float32), member.astype(jnp.float32), precision=lax.Precision.HIGHEST).astype(jnp.int32)
    slot_index = jnp.sum(before * member, axis=1)
    target = flat_ids * capacity + slot_index
    source = (
        jnp.full((experts * capacity,), -1, jnp.int32)
        .at[target]
        .set(jnp.arange(row_count, dtype=jnp.int32))
    )
    return (flat_ids, slot_index, source)


def contract_rows(left, right):
    return lax.dot_general(
        left, right, (((0,), (0,)), ((), ())), preferred_element_type=jnp.float32
    )


def contract_cols(left, right):
    return lax.dot_general(
        left, right, (((1,), (1,)), ((), ())), preferred_element_type=jnp.float32
    )


def expert_forward(inputs, gate_w, up_w, down_w):
    gate_pre = jnp.dot(inputs, gate_w, preferred_element_type=jnp.float32)
    up_pre = jnp.dot(inputs, up_w, preferred_element_type=jnp.float32)
    active = (gate_pre / (1.0 + jnp.exp(-gate_pre)) * up_pre).astype(jnp.bfloat16)
    return (contract_cols(active, down_w), (gate_pre, up_pre, active))


def expert_backward(inputs, grads_out, gate_w, up_w, down_w, kept_acts):
    gate_pre, up_pre, active = kept_acts
    d_active = jnp.dot(grads_out, down_w, preferred_element_type=jnp.float32)
    grad_down = contract_rows(grads_out, active)
    sigmoid_val = 1.0 / (1.0 + jnp.exp(-gate_pre))
    d_gate = (d_active * up_pre * sigmoid_val * (1.0 + gate_pre * (1.0 - sigmoid_val))).astype(
        jnp.bfloat16
    )
    d_up = (d_active * gate_pre * sigmoid_val).astype(jnp.bfloat16)
    grad_gate = contract_rows(inputs, d_gate)
    grad_up = contract_rows(inputs, d_up)
    d_inputs = contract_cols(d_gate, gate_w) + contract_cols(d_up, up_w)
    return (d_inputs, grad_gate, grad_up, grad_down)


def send_rows(rows_in):
    return lax.all_to_all(rows_in, "dp", split_axis=0, concat_axis=0, tiled=True)


def return_rows(rows_in):
    return lax.all_to_all(
        rows_in.astype(jnp.bfloat16), "dp", split_axis=0, concat_axis=0, tiled=True
    ).astype(rows_in.dtype)


def send_grads(rows_in):
    return lax.all_to_all(rows_in, "dp", split_axis=0, concat_axis=0, tiled=True)


def return_grads(rows_in):
    return lax.all_to_all(
        rows_in.astype(jnp.bfloat16), "dp", split_axis=0, concat_axis=0, tiled=True
    ).astype(rows_in.dtype)


def share_slots(partial_rows):
    return lax.psum_scatter(partial_rows, "tensor", scatter_dimension=1, tiled=True)


def on_device_general(
    tokens,
    attn_norm_gain,
    w_query,
    key_projection,
    value_projection,
    w_out,
    moe_norm_gain,
    w_gate,
    w_up,
    w_down,
    router_logits,
    expert_ids,
    segment_ids,
    parents,
    cotangent,
):
    length = tokens.shape[0]
    model_width = tokens.shape[1]
    q_cols = w_query.shape[1]
    kv_cols = key_projection.shape[1]
    q_heads = q_cols // HEAD_SIZE
    kv_heads = kv_cols // HEAD_SIZE
    group_size = q_heads // kv_heads
    dp_size = lax.axis_size("dp")
    tensor_ranks = lax.axis_size("tensor")
    replicas = FFE // (w_gate.shape[2] * tensor_ranks)
    experts = dp_size // replicas
    capacity = 4 * (9 * length * TOP // (32 * experts))
    share_rows = capacity // tensor_ranks
    first_slot = lax.axis_index("tensor") * share_rows
    block_rows = min(length, 512)
    attn_gain, moe_gain, query_w, key_weight, value_weight, out_w = (
        lax.all_gather(attn_norm_gain, "dp", axis=0, tiled=True),
        lax.all_gather(moe_norm_gain, "dp", axis=0, tiled=True),
        lax.all_gather(w_query, "dp", axis=0, tiled=True),
        lax.all_gather(key_projection, "dp", axis=0, tiled=True),
        lax.all_gather(value_projection, "dp", axis=0, tiled=True),
        lax.all_gather(w_out, "dp", axis=0, tiled=True),
    )
    attn_gain_f = attn_gain.astype(jnp.float32)
    moe_gain_f = moe_gain.astype(jnp.float32)
    inputs = tokens.astype(jnp.float32)
    inv_attn = lax.rsqrt(jnp.mean(inputs * inputs, axis=1, keepdims=True) + EPSILON)
    unit_attn = inputs * inv_attn
    normalized_rows = (unit_attn * attn_gain_f).astype(jnp.bfloat16)
    position, allowed = tree_layout(segment_ids[0], parents[0])
    cosine_table, sine_values = rope_tables(position, HEAD_SIZE)
    query_linear = jnp.dot(normalized_rows, query_w, preferred_element_type=jnp.float32).reshape(
        length, q_heads, HEAD_SIZE
    )
    key_linear = jnp.dot(normalized_rows, key_weight, preferred_element_type=jnp.float32).reshape(
        length, kv_heads, HEAD_SIZE
    )
    query_heads = (
        apply_rotary(query_linear, cosine_table, sine_values)
        .astype(jnp.bfloat16)
        .reshape(length, kv_heads, group_size, HEAD_SIZE)
    )
    key_heads = apply_rotary(key_linear, cosine_table, sine_values).astype(jnp.bfloat16)
    value_heads = (
        jnp.dot(normalized_rows, value_weight, preferred_element_type=jnp.float32)
        .astype(jnp.bfloat16)
        .reshape(length, kv_heads, HEAD_SIZE)
    )
    q_block = query_heads
    mask_rows = allowed[None, None]
    scores = (
        jnp.einsum("qhgd,khd->hgqk", q_block, key_heads, preferred_element_type=jnp.float32)
        * SCORE_SCALE
    )
    scores = jnp.where(mask_rows, scores, NEGATIVE)
    peak_parts = [jnp.max(scores, axis=(2, 3))]
    row_max = jnp.max(scores, axis=3, keepdims=True)
    expo = jnp.exp(scores - row_max)
    row_total = jnp.sum(expo, axis=3, keepdims=True)
    lse_parts = [row_max + jnp.log(row_total)]
    prob_low = (expo / row_total).astype(jnp.bfloat16)
    block_outs = jnp.einsum(
        "hgqk,khd->qhgd", prob_low, value_heads, preferred_element_type=jnp.float32
    )
    head_out = block_outs.reshape(length, q_cols).astype(jnp.bfloat16)
    attn_mix = lax.psum(contract_cols(head_out, out_w), "tensor")
    hidden = inputs + RESIDUAL * attn_mix
    head_peak = lax.pmax(jnp.max(jnp.stack(peak_parts), axis=0).reshape(q_heads), "dp")
    inv_moe = lax.rsqrt(jnp.mean(hidden * hidden, axis=1, keepdims=True) + EPSILON)
    unit_moe = hidden * inv_moe
    moe_in = (unit_moe * moe_gain_f).astype(jnp.bfloat16)
    logit_max = jnp.max(router_logits, axis=1, keepdims=True)
    logit_exp = jnp.exp(router_logits - logit_max)
    gate_probs = logit_exp / jnp.sum(logit_exp, axis=1, keepdims=True)
    flat_ids, slot_index, source = slot_tables(expert_ids, experts, capacity)
    filled = source >= 0
    source_row = jnp.maximum(source, 0)
    source_token = source_row // TOP
    dispatch_rows = jnp.where(
        filled[:, None], moe_in[source_token], jnp.zeros((), jnp.bfloat16)
    ).reshape(experts, capacity, model_width)
    arrived = send_rows(jnp.repeat(dispatch_rows, replicas, axis=0))
    gate_w, up_w, down_w = (w_gate[0], w_up[0], w_down[0])
    expert_in = arrived.reshape(dp_size * capacity, model_width)
    expert_out, kept_acts = expert_forward(expert_in, gate_w, up_w, down_w)
    partial_out = share_slots(expert_out.reshape(dp_size, capacity, model_width))
    back_parts = return_rows(partial_out).reshape(experts, replicas, share_rows, model_width)
    back_rows = (
        jnp.sum(back_parts, axis=1).astype(jnp.bfloat16).reshape(experts * share_rows, model_width)
    )
    own_slot = ((slot_index >= first_slot) & (slot_index < first_slot + share_rows)).reshape(
        length, TOP
    )
    local_index = (
        flat_ids * share_rows + jnp.clip(slot_index - first_slot, 0, share_rows - 1)
    ).reshape(length, TOP)
    mix_part = jnp.zeros((length, model_width), jnp.float32)
    for column in range(TOP):
        gate_weight = jnp.where(own_slot[:, column], gate_probs[:, column], 0.0)
        mix_part = mix_part + gate_weight[:, None] * back_rows[local_index[:, column]].astype(
            jnp.float32
        )
    expert_mix = lax.psum(mix_part.astype(jnp.bfloat16), "tensor").astype(jnp.float32)
    output = (hidden + RESIDUAL * expert_mix).astype(jnp.bfloat16)
    grad_output = cotangent.astype(jnp.float32)
    mix_grad = RESIDUAL * grad_output
    row_gate = gate_probs.reshape(-1)[source_row]
    grad_rows = (
        jnp.where(filled[:, None], row_gate[:, None] * mix_grad[source_token], 0.0)
        .astype(jnp.bfloat16)
        .reshape(experts, capacity, model_width)
    )
    grad_arrived = send_grads(jnp.repeat(grad_rows, replicas, axis=0)).reshape(
        dp_size * capacity, model_width
    )
    d_inputs, grad_gate, grad_up, grad_down = expert_backward(
        expert_in, grad_arrived, gate_w, up_w, down_w, kept_acts
    )
    d_back = share_slots(d_inputs.reshape(dp_size, capacity, model_width))
    grad_gate, grad_up, grad_down = (grad_gate[None], grad_up[None], grad_down[None])
    d_parts = return_grads(d_back).reshape(experts, replicas, share_rows, model_width)
    d_returned = (
        jnp.sum(d_parts, axis=1).astype(jnp.bfloat16).reshape(experts * share_rows, model_width)
    )
    d_mix_part = jnp.zeros((length, model_width), jnp.float32)
    for column in range(TOP):
        d_mix_part = d_mix_part + jnp.where(
            own_slot[:, column][:, None],
            d_returned[local_index[:, column]].astype(jnp.float32),
            0.0,
        )
    d_moe_in = lax.psum(d_mix_part, "tensor")
    scaled_moe = d_moe_in * moe_gain_f
    grad_moe_gain = jnp.sum(d_moe_in * unit_moe, axis=0)
    d_hidden = grad_output + inv_moe * (
        scaled_moe - unit_moe * jnp.mean(scaled_moe * unit_moe, axis=1, keepdims=True)
    )
    d_attn = (RESIDUAL * d_hidden).astype(jnp.bfloat16)
    grad_out_w = contract_rows(d_attn, head_out)
    d_heads = (
        jnp.dot(d_attn, out_w, preferred_element_type=jnp.float32)
        .astype(jnp.bfloat16)
        .reshape(length, kv_heads, group_size, HEAD_SIZE)
    )
    d_query_parts = []
    d_key = jnp.zeros((length, kv_heads, HEAD_SIZE), jnp.float32)
    d_value = jnp.zeros((length, kv_heads, HEAD_SIZE), jnp.float32)
    for block_number, row_begin in enumerate(range(0, length, block_rows)):
        q_block = query_heads
        mask_rows = allowed[None, None]
        scores = (
            jnp.einsum("qhgd,khd->hgqk", q_block, key_heads, preferred_element_type=jnp.float32)
            * SCORE_SCALE
        )
        scores = jnp.where(mask_rows, scores, NEGATIVE)
        prob_full = jnp.exp(scores - lse_parts[block_number])
        prob_low = prob_full.astype(jnp.bfloat16)
        d_value = jnp.einsum(
            "hgqk,qhgd->khd", prob_low, d_heads, preferred_element_type=jnp.float32
        )
        d_prob = jnp.einsum(
            "qhgd,khd->hgqk", d_heads, value_heads, preferred_element_type=jnp.float32
        )
        inner = jnp.sum(prob_full * d_prob, axis=3, keepdims=True)
        d_scores = (prob_full * (d_prob - inner)).astype(jnp.bfloat16)
        d_query_parts.append(
            jnp.einsum("hgqk,khd->qhgd", d_scores, key_heads, preferred_element_type=jnp.float32)
            * SCORE_SCALE
        )
        d_key = (
            jnp.einsum("hgqk,qhgd->khd", d_scores, q_block, preferred_element_type=jnp.float32)
            * SCORE_SCALE
        )
    d_query_all = d_query_parts[0].reshape(length, q_heads, HEAD_SIZE)
    d_query_lin = (
        rotate_back(d_query_all, cosine_table, sine_values)
        .astype(jnp.bfloat16)
        .reshape(length, q_cols)
    )
    d_key_lin = (
        rotate_back(d_key, cosine_table, sine_values).astype(jnp.bfloat16).reshape(length, kv_cols)
    )
    d_value_lin = d_value.astype(jnp.bfloat16).reshape(length, kv_cols)
    grad_query_w = contract_rows(normalized_rows, d_query_lin)
    grad_key_w = contract_rows(normalized_rows, d_key_lin)
    grad_value_w = contract_rows(normalized_rows, d_value_lin)
    d_normed_part = (
        contract_cols(d_query_lin, query_w)
        + contract_cols(d_key_lin, key_weight)
        + contract_cols(d_value_lin, value_weight)
    )
    d_normed = lax.psum(d_normed_part.astype(jnp.bfloat16), "tensor").astype(jnp.float32)
    scaled_attn = d_normed * attn_gain_f
    grad_attn_gain = jnp.sum(d_normed * unit_attn, axis=0)
    input_grad = d_hidden + inv_attn * (
        scaled_attn - unit_attn * jnp.mean(scaled_attn * unit_attn, axis=1, keepdims=True)
    )
    reduced = (
        lax.psum_scatter(grad_attn_gain, "dp", scatter_dimension=0, tiled=True),
        lax.psum_scatter(grad_moe_gain, "dp", scatter_dimension=0, tiled=True),
        lax.psum_scatter(grad_query_w, "dp", scatter_dimension=0, tiled=True),
        lax.psum_scatter(grad_key_w, "dp", scatter_dimension=0, tiled=True),
        lax.psum_scatter(grad_value_w, "dp", scatter_dimension=0, tiled=True),
        lax.psum_scatter(grad_out_w, "dp", scatter_dimension=0, tiled=True),
    )
    scale_factor = CLIP_LIMIT / jnp.maximum(head_peak, CLIP_LIMIT)
    query_scale = jnp.repeat(jnp.sqrt(scale_factor), HEAD_SIZE)
    key_clip_scale = jnp.repeat(
        jnp.sqrt(jnp.min(scale_factor.reshape(kv_heads, group_size), axis=1)), HEAD_SIZE
    )
    clipped_query = w_query.astype(jnp.float32) * query_scale[None, :]
    clipped_key = key_projection.astype(jnp.float32) * key_clip_scale[None, :]
    return (
        output,
        input_grad,
        reduced[0],
        reduced[2],
        reduced[3],
        reduced[4],
        reduced[5],
        reduced[1],
        grad_gate,
        grad_up,
        grad_down,
        clipped_query,
        clipped_key,
    )


MESH_IDS = pl.DeviceIdType.MESH
F32 = jnp.float32
BF16 = jnp.bfloat16


class Place:
    def __init__(self, line):
        self.line = line
        self.count = 4 * line
        me = lax.axis_index("dp")
        self.core = lax.axis_index("tensor")
        self.me = me
        self.z = me // 4
        y, x = (me // 2) % 2, me % 2
        self.step_a, self.step_b = 2 - self.core, 1 + self.core
        self.a = y * (1 - self.core) + x * self.core
        self.b = x * (1 - self.core) + y * self.core

    def part(self, z, a, b):
        return z * 4 + a * self.step_a + b * self.step_b

    def up(self):
        return (self.me + 4, self.core)

    def down(self):
        return (self.me - 4, self.core)

    def beside_a(self):
        return (self.me + self.step_a * (1 - 2 * self.a), self.core)

    def beside_b(self):
        return (self.me + self.step_b * (1 - 2 * self.b), self.core)

    def twin(self):
        return (self.me, 1 - self.core)

    def peer(self, offset):
        return lax.rem(self.me + offset, self.count)


def enter(place):
    barrier = pltpu.get_barrier_semaphore()

    def greet(offset, carry):
        pl.semaphore_signal(
            barrier, inc=1, device_id=(place.peer(offset), place.core), device_id_type=MESH_IDS
        )
        return carry

    lax.fori_loop(1, place.count, greet, 0)
    pl.semaphore_signal(barrier, inc=1, device_id=place.twin(), device_id_type=MESH_IDS)
    pl.semaphore_wait(barrier, place.count)


def remote(src, dst, send_sem, recv_sem, device):
    return pltpu.make_async_remote_copy(
        src_ref=src,
        dst_ref=dst,
        send_sem=send_sem,
        recv_sem=recv_sem,
        device_id=device,
        device_id_type=MESH_IDS,
    )


class Notes:
    def __init__(self, place, src, dst, send_sem, recv_sem, alike):
        self.place, self.src, self.dst = place, src, dst
        self.send_sem, self.recv_sem, self.alike = send_sem, recv_sem, alike

    def _copy(self, offset, source):
        place = self.place
        to = place.peer(offset)
        return remote(
            self.src if self.alike else self.src.at[to],
            self.dst.at[source],
            self.send_sem.at[offset],
            self.recv_sem.at[source],
            (to, place.core),
        )

    def start(self):
        def send(offset, carry):
            self._copy(offset, self.place.me).start()
            return carry

        lax.fori_loop(1, self.place.count, send, 0)
        me = self.place.me
        self.dst[me] = self.src[...] if self.alike else self.src[me]

    def finish(self):
        def settle(offset, carry):
            self._copy(offset, self.place.peer(offset)).wait_recv()
            self._copy(offset, self.place.me).wait_send()
            return carry

        lax.fori_loop(1, self.place.count, settle, 0)


class Gather:
    def __init__(self, place, view, send_sem, recv_sem, fixed=False):
        self.place, self.view, self.fixed = place, view, fixed
        self.send_sem, self.recv_sem = send_sem, recv_sem

    def _copy(self, source, target, sem, device):
        there = self.view(source if self.fixed else target)
        return remote(self.view(source), there, self.send_sem.at[sem], self.recv_sem.at[target], device)

    def _to_z(self, z, way):
        place = self.place
        device = place.up() if way == 0 else place.down()
        return self._copy(z, z, way * place.line + z, device)

    def _to_a(self, z):
        line = self.place.line
        return self._copy(z, line + z, 2 * line + z, self.place.beside_a())

    def _to_b(self, slot):
        line = self.place.line
        return self._copy(slot, 2 * line + slot, 3 * line + slot, self.place.beside_b())

    def take(self, slot):
        self._copy(slot, slot, 0, self.place.beside_b()).wait_recv()

    def near(self, step, action):
        place = self.place
        if step == 0:
            action(place.z)
        else:
            pl.when(place.z >= step)(lambda: action(place.z - step))
            pl.when(place.z + step < place.line)(lambda: action(place.z + step))

    def hand_on(self, slot):
        self._to_b(slot).start()

    def start(self):
        place = self.place
        pl.when(place.z < place.line - 1)(lambda: self._to_z(place.z, 0).start())
        pl.when(place.z > 0)(lambda: self._to_z(place.z, 1).start())
        self._to_a(self.place.z).start()
        self.hand_on(self.place.z)

    def along(self, step):
        place = self.place

        def pass_on(z):
            self.take(z)
            pl.when(jnp.logical_and(z < place.z, place.z < place.line - 1))(lambda: self._to_z(z, 0).start())
            pl.when(jnp.logical_and(z > place.z, place.z > 0))(lambda: self._to_z(z, 1).start())
            self._to_a(z).start()
            self.hand_on(z)

        self.near(step, pass_on)

    def across(self, step):
        line = self.place.line

        def pass_on(z):
            self.take(line + z)
            self.hand_on(line + z)

        self.near(step, pass_on)

    def step(self, number):
        if number == 0:
            self.start()
            return
        if number < self.place.line:
            self.along(number)
        self.across(number - 1)

    def settle(self):
        place = self.place
        line = place.line

        def wait(z, carry):
            self._to_a(z).wait_send()
            self._to_b(z).wait_send()
            self._to_b(line + z).wait_send()
            pl.when(jnp.logical_and(z <= place.z, place.z < line - 1))(lambda: self._to_z(z, 0).wait_send())
            pl.when(jnp.logical_and(z >= place.z, place.z > 0))(lambda: self._to_z(z, 1).wait_send())
            return carry

        lax.fori_loop(0, line, wait, 0)

    def take_rest(self):
        line = self.place.line

        def wait(k, carry):
            self.take(2 * line + k)
            return carry

        lax.fori_loop(0, 2 * line, wait, 0)


class Pipeline:
    def __init__(self, gathers, lag):
        self.gathers, self.lag, self.at = gathers, lag, 0
        self.steps = gathers[0].place.line + 1

    def run(self, number):
        for _ in range(number):
            for i, g in enumerate(self.gathers):
                step = self.at - self.lag * i
                if 0 <= step < self.steps:
                    g.step(step)
            self.at += 1

    def until(self, index):
        self.run(max(0, self.lag * index + self.steps - self.at))


class Twin:
    def __init__(self, place, source, target, send_sem, recv_sem):
        self.place, self.source, self.target = place, source, target
        self.send_sem, self.recv_sem = send_sem, recv_sem

    def copy(self, slot):
        line = self.place.line
        group = slot // line
        there = slot + line * ((group % 2) - (group // 2))
        return remote(
            self.source(slot),
            self.target(there),
            self.send_sem.at[slot],
            self.recv_sem.at[there],
            self.place.twin(),
        )

    def start(self, slot):
        self.copy(slot).start()

    def take(self, slot):
        remote(
            self.source(slot),
            self.target(slot),
            self.send_sem.at[slot],
            self.recv_sem.at[slot],
            self.place.twin(),
        ).wait_recv()

    def wait_send(self, slot):
        self.copy(slot).wait_send()


class Reduce:
    def __init__(self, place, parts, from_b, from_a, from_z, send_sem, recv_sem, index=lambda slot: slot):
        self.place, self.parts, self.index = place, parts, index
        self.from_b, self.from_a, self.from_z = from_b, from_a, from_z
        self.send_sem, self.recv_sem = send_sem, recv_sem

    def _copy(self, source, target, sem, device):
        return remote(source, target, self.send_sem.at[sem], self.recv_sem.at[sem], device)

    def _to_b(self, k):
        line = self.place.line
        return self._copy(self.parts.at[self.index(2 * line + k)], self.from_b.at[k], k, self.place.beside_b())

    def _to_a(self, z):
        line = self.place.line
        block = self.parts.at[self.index(line + z)]
        return self._copy(block, self.from_a.at[z], 2 * line + z, self.place.beside_a())

    def _to_z(self, target):
        place, line = self.place, self.place.line
        return remote(
            self.parts.at[self.index(target)],
            self.from_z.at[place.z],
            self.send_sem.at[3 * line + target],
            self.recv_sem.at[3 * line + place.z],
            (place.me + 4 * (target - place.z), place.core),
        )

    def _add(self, slot, block):
        at = self.index(slot)
        self.parts[at] = (self.parts[at].astype(F32) + block.astype(F32)).astype(BF16)

    def send_b(self, k):
        self._to_b(k).start()

    def fold_b(self, k):
        self._to_b(k).wait_recv()
        self._add(k, self.from_b[k])

    def send_a(self, z):
        self._to_a(z).start()

    def fold_a(self, z):
        self._to_a(z).wait_recv()
        self._add(z, self.from_a[z])

    def fold_line_a(self):
        line = self.place.line
        for z in ends_first(line):
            self.fold_b(line + z)
            self.send_a(z)

    def fold_line_own(self):
        for z in ends_first(self.place.line):
            self.fold_b(z)

    def finish_line(self):
        for z in ends_first(self.place.line):
            self.fold_a(z)
            pl.when(self.place.z != z)(lambda z=z: self._to_z(z).start())

    def result(self, out):
        place, line = self.place, self.place.line
        out[...] = self.parts[self.index(place.z)].astype(F32)

        def add(z, carry):
            @pl.when(z != place.z)
            def _():
                remote(
                    self.from_z.at[z], self.from_z.at[z], self.send_sem.at[0], self.recv_sem.at[3 * line + z], place.up()
                ).wait_recv()
                out[...] += self.from_z[z].astype(F32)

            return carry

        lax.fori_loop(0, line, add, 0)

    def settle_b(self):
        def wait(k, carry):
            self._to_b(k).wait_send()
            return carry

        lax.fori_loop(0, 2 * self.place.line, wait, 0)

    def settle_a(self):
        place = self.place

        def wait(z, carry):
            self._to_a(z).wait_send()
            pl.when(place.z != z)(lambda: self._to_z(z).wait_send())
            return carry

        lax.fori_loop(0, place.line, wait, 0)

    def settle(self):
        self.settle_b()
        self.settle_a()


class PackedGather(Gather):
    def __init__(self, place, dense, packed, compact, picks, mine, send_sem, recv_sem, twin_sems):
        self.place, self.dense, self.packed, self.compact = place, dense, packed, compact
        self.own_pick, self.other_pick = picks
        self.mine, self.fixed = mine, False
        self.send_sem, self.recv_sem = send_sem, recv_sem
        view = lambda slot: compact.at[slot, :, mine]
        self.twin = Twin(place, view, view, twin_sems.at[0], twin_sems.at[1])

    def view(self, slot):
        return self.dense.at[slot]

    def _to_b(self, slot):
        line = self.place.line
        return remote(
            self.packed.at[slot],
            self.compact.at[2 * line + slot, :, self.mine],
            self.send_sem.at[3 * line + slot],
            self.recv_sem.at[2 * line + slot],
            self.place.beside_b(),
        )

    def take_compact(self, slot):
        line = self.place.line
        self._to_b(slot - 2 * line).wait_recv()
        self.twin.start(slot)

    def take(self, slot):
        self._copy(slot, slot, 0, self.place.beside_b()).wait_recv()

    def hand_on(self, slot):
        block = self.dense[slot]
        self.packed[slot] = jnp.dot(self.other_pick[slot], block, preferred_element_type=F32).astype(BF16)
        self._to_b(slot).start()
        self.compact[slot, :, self.mine] = jnp.dot(
            self.own_pick[slot], block, preferred_element_type=F32
        ).astype(BF16)
        self.twin.start(slot)


class PackedReduce(Reduce):
    def __init__(self, place, compact, picks, *rest):
        super().__init__(place, *rest)
        self.compact = compact
        self.own_pick, self.other_pick = picks

    def _to_b(self, k):
        line = self.place.line
        return self._copy(self.compact.at[2 * line + k], self.from_b.at[k], k, self.place.beside_b())

    def fold_b(self, k):
        self._to_b(k).wait_recv()
        own = contract_rows(self.own_pick[k], self.compact[k])
        self.parts[k] = (own + contract_rows(self.other_pick[k], self.from_b[k])).astype(BF16)


def selections(place, notes, own_pick, other_pick, gates=None):
    line = place.line
    cap, length = own_pick.shape[1:]
    rows = [notes[part_of(place, slot)][0:1, :] for slot in range(4 * line)]
    for slot in range(2 * line):
        note = notes[part_of(place, slot)]
        rows.append(jnp.where(place.core == 0, note[3:4, :], note[4:5, :]))
    before = lax.broadcasted_iota(jnp.int32, (length, length), 0) < lax.broadcasted_iota(
        jnp.int32, (length, length), 1
    )
    weights = jnp.concatenate(rows, axis=0)
    rank = jnp.dot(
        jnp.where(weights > 0.0, 1.0, 0.0).astype(BF16),
        jnp.where(before, 1.0, 0.0).astype(BF16),
        preferred_element_type=F32,
    )
    rank = jnp.where(weights > 0.0, rank, -1.0)
    number = lax.broadcasted_iota(jnp.int32, (cap, length), 0).astype(F32)
    for i in range(len(rows)):
        pick = jnp.where(rank[i : i + 1, :] == number, 1.0, 0.0)
        if i >= 4 * line:
            other_pick[i - 4 * line] = pick.astype(BF16)
            continue
        own_pick[i] = pick.astype(BF16)
        if gates is not None:
            gates[cap * i : cap * (i + 1), :] = jnp.sum(pick * rows[i], axis=1, keepdims=True)


AHEAD = 8


class Reductions:
    def __init__(self, reduces, finish):
        self.reduces, self.finish = reduces, finish
        self.at = self.sent = self.limit = 0
        line = self.line = reduces[0].place.line
        self.ks = [line + z for z in ends_first(line)] + ends_first(line)
        self.steps = [(i, k) for i in range(len(reduces)) for k in self.ks]

    def ready(self, number):
        self.limit = 2 * self.line * number
        self._send()

    def _send(self):
        while self.sent < min(self.at + AHEAD, self.limit):
            i, k = self.steps[self.sent]
            self.reduces[i].send_b(k)
            self.sent += 1

    def run(self, number):
        for _ in range(number):
            self._step()

    def _step(self):
        i, k = self.steps[self.at]
        self.at += 1
        self._send()
        self.reduces[i].fold_b(k)
        if k >= self.line:
            self.reduces[i].send_a(k - self.line)
        if k == self.ks[self.line - 1] and i > 0:
            self.reduces[i - 1].finish_line()
        if k == self.ks[-1] and i > 0:
            self.finish(i - 1)

    def complete(self):
        self.run(len(self.steps) - self.at)
        self.reduces[-1].finish_line()
        self.finish(len(self.reduces) - 1)


def reduce_scratch(line, block):
    return [
        pltpu.VMEM((2 * line, *block), BF16),
        pltpu.VMEM((line, *block), BF16),
        pltpu.VMEM((line, *block), BF16),
        pltpu.SemaphoreType.DMA((4 * line,)),
        pltpu.SemaphoreType.DMA((4 * line,)),
    ]


def ends_first(line):
    order = []
    for i in range((line + 1) // 2):
        order += [i] if i == line - 1 - i else [i, line - 1 - i]
    return order


def part_of(place, slot):
    line = place.line
    group, z = slot // line, slot % line
    flip_a, flip_b = group % 2, group // 2
    a = place.a + flip_a * (1 - 2 * place.a)
    b = place.b + flip_b * (1 - 2 * place.b)
    return place.part(z, a, b)


PIECES = 2


def pieces_of(place, width):
    piece = width // 2 // PIECES

    def spans(core):
        starts = [pl.multiple_of((core * PIECES + i) * piece, 128) for i in range(PIECES)]
        return [pl.ds(start, piece) for start in starts]

    return spans(place.core), spans(1 - place.core), piece


def halves(place, width):
    half = width // 2
    mine = pl.ds(pl.multiple_of(place.core * half, 128), half)
    theirs = pl.ds(pl.multiple_of((1 - place.core) * half, 128), half)
    return mine, theirs


def place_half(chunk, have, want, lane):
    chunk = chunk if have == want else pltpu.roll(chunk, HEAD_SIZE, 1)
    return jnp.where(lane // HEAD_SIZE == want, chunk, 0.0)


def rope_chunk(chunk, tables, sign):
    ahead = pltpu.roll(chunk, 128 - HEAD_SIZE // 2, 1)
    behind = pltpu.roll(chunk, HEAD_SIZE // 2, 1)
    return chunk * tables[0] + sign * (ahead * tables[1] + behind * tables[2])


def chunk_of(ref, j):
    return ref[:, 128 * j : 128 * (j + 1)]


def pair_of(ref, j, group_size, lane):
    both = []
    for half in (0, 1):
        group = (2 * j + half) // group_size
        both.append(place_half(chunk_of(ref, group // 2).astype(F32), group % 2, half, lane))
    return jnp.concatenate(both, axis=0).astype(BF16)


def spread_gains(notes, shard, width):
    total = jnp.zeros((8, width), F32)
    for p in range(notes.shape[0]):
        row = jnp.concatenate([notes[p], jnp.zeros((8, width - 128), F32)], axis=1)
        total += pltpu.roll(row, shard * p, 1) if p else row
    return total


def gate_table(logits, ids, experts):
    expo = jnp.exp(logits - jnp.max(logits, axis=0, keepdims=True))
    probs = expo / jnp.sum(expo, axis=0, keepdims=True)
    top, length = logits.shape
    expert = lax.broadcasted_iota(jnp.int32, (experts, length), 0)
    table = jnp.zeros((experts, length), F32)
    for c in range(top):
        table += jnp.where(ids[c : c + 1, :] == expert, probs[c : c + 1, :], 0.0)
    return table


def write_notes(note_ref, gates, gains):
    shard = gains[0].shape[1]
    row = lax.broadcasted_iota(jnp.int32, (8, 128), 0)
    pad = jnp.zeros((1, 128 - shard), F32)
    shared = jnp.zeros((8, 128), F32)
    for i, gain in enumerate(gains):
        shared = jnp.where(row == i + 1, jnp.concatenate([gain, pad], axis=1), shared)
    for p in range(note_ref.shape[0]):
        tile = shared
        for at, e in ((0, p), (3, p + 1 - 2 * (p % 2)), (4, p + 2 - 4 * (p // 2 % 2))):
            tile = jnp.where(row == at, gates[e : e + 1, :], tile)
        note_ref[p] = tile


def tree_tables(segments, parents, length):
    row = lax.broadcasted_iota(jnp.int32, (length, length), 0)
    lane = lax.broadcasted_iota(jnp.int32, (length, length), 1)

    def total(x):
        return jnp.sum(x.astype(F32), axis=1, keepdims=True)

    own_row = segments.astype(F32)
    own = total(jnp.where(row == lane, own_row, 0.0))
    kinds = parents.shape[1]
    kind = lax.broadcasted_iota(jnp.int32, (length, kinds), 1).astype(F32)
    above = parents.astype(F32)
    parent = total(jnp.where(kind == own, above, 0.0))
    grand = total(jnp.where(kind == parent, above, 0.0))
    in_parent, in_grand = own_row == parent, own_row == grand
    start = total(jnp.where(own_row < own, 1.0, 0.0))
    offset = jnp.where(own != 0.0, total(jnp.where(in_parent, 1.0, 0.0)), 0.0)
    offset += jnp.where(parent != 0.0, total(jnp.where(in_grand, 1.0, 0.0)), 0.0)
    place = lax.broadcasted_iota(jnp.int32, (length, 1), 0).astype(F32)
    linked = jnp.logical_or(own_row == own, jnp.logical_or(in_parent, in_grand))
    return place - start + offset, jnp.logical_and(linked, lane <= row)


def write_tables(tables_ref, position):
    lane = lax.broadcasted_iota(jnp.int32, (1, 128), 1)
    half = HEAD_SIZE // 2
    frequency = THETA ** ((lane % half).astype(F32) * (-2.0 / HEAD_SIZE))
    angles = position * frequency
    sine = jnp.sin(angles)
    first = lane % HEAD_SIZE < half
    tables_ref[0] = jnp.cos(angles)
    tables_ref[1] = jnp.where(first, -sine, 0.0)
    tables_ref[2] = jnp.where(first, 0.0, sine)


def forward_kernel(
    line,
    group_size,
    tokens_ref,
    query_ref,
    key_ref,
    value_ref,
    out_ref,
    cot_ref,
    gain_a_ref,
    gain_m_ref,
    logits_ref,
    ids_ref,
    segments_ref,
    parents_ref,
    moe_in_ref,
    hidden_ref,
    normed_ref,
    head_out_ref,
    queries_ref,
    keys_ref,
    values_ref,
    probs_ref,
    peak_ref,
    tables_ref,
    gains_ref,
    notes,
    query_keep,
    key_keep,
    value_keep,
    out_keep,
    cot_keep,
    query_all,
    key_all,
    value_all,
    out_all,
    cot_dense,
    cot_packed,
    cot_all,
    own_pick,
    other_pick,
    mix_mine,
    mix_other,
    note_ref,
    sends,
    recvs,
    note_send,
    note_recv,
    twin_sems,
    local_sems,
    keep_sems,
    mix_sems,
):
    place = Place(line)
    count = 4 * line
    length, width = tokens_ref.shape
    shard, q_cols = query_ref.shape
    chunks = q_cols // 128
    spans, _, piece = pieces_of(place, width)
    own = []
    blocks = ((query_ref, query_all), (key_ref, key_all), (value_ref, value_all), (out_ref, out_all))
    for i, (src, dst) in enumerate(blocks):
        own.append(pltpu.make_async_copy(src, dst.at[place.me], local_sems.at[i]))
    for i in range(PIECES):
        own.append(pltpu.make_async_copy(cot_ref.at[:, spans[i]], cot_dense.at[i, place.z], local_sems.at[4 + i]))
    for c in own:
        c.start()
    enter(place)
    note = Notes(place, note_ref, notes, note_send, note_recv, False)
    for c in own:
        c.wait()
    gathers = [
        Gather(place, lambda s, ref=ref: ref.at[part_of(place, s)], sends.at[i], recvs.at[i], True)
        for i, ref in enumerate((query_all, key_all, value_all, out_all))
    ]
    picks = (own_pick, other_pick)
    cots = [
        PackedGather(
            place,
            cot_dense.at[i],
            cot_packed.at[i],
            cot_all,
            picks,
            spans[i],
            sends.at[4 + i],
            recvs.at[4 + i],
            twin_sems.at[i],
        )
        for i in range(PIECES)
    ]
    out = gathers[3]
    pipeline = Pipeline([gathers[i] for i in (1, 2, 0, 3)] + cots, 1)
    pipeline.run(1)
    gains = [g[...].astype(F32) for g in (gain_a_ref, gain_m_ref)]
    write_notes(note_ref, gate_table(logits_ref[...], ids_ref[...], count), gains)
    note.start()
    inputs = tokens_ref[...].astype(F32)
    inv_attn = lax.rsqrt(jnp.mean(inputs * inputs, axis=1, keepdims=True) + EPSILON)
    pipeline.run(1)
    note.finish()
    gains_ref[...] = spread_gains(notes, shard, width)
    normed_ref[...] = (inputs * inv_attn * gains_ref[1:2, :]).astype(BF16)
    pipeline.run(1)
    position, allowed = tree_tables(segments_ref[...], parents_ref[...], length)
    write_tables(tables_ref, position)
    pipeline.run(1)
    selections(place, notes, own_pick, other_pick)
    pipeline.until(2)
    for g in gathers[:3]:
        g.take_rest()
    normed = normed_ref[...]
    tables = [tables_ref[i] for i in range(3)]
    query_lin = jnp.dot(normed, query_all[...].reshape(width, q_cols), preferred_element_type=F32)
    for j in range(chunks):
        queries_ref[:, 128 * j : 128 * (j + 1)] = rope_chunk(
            query_lin[:, 128 * j : 128 * (j + 1)], tables, 1.0
        ).astype(BF16)
    kv_cols = key_ref.shape[1]
    key_lin = jnp.dot(normed, key_all[...].reshape(width, kv_cols), preferred_element_type=F32)
    for j in range(kv_cols // 128):
        keys_ref[:, 128 * j : 128 * (j + 1)] = rope_chunk(
            key_lin[:, 128 * j : 128 * (j + 1)], tables, 1.0
        ).astype(BF16)
    values_ref[...] = jnp.dot(
        normed, value_all[...].reshape(width, kv_cols), preferred_element_type=F32
    ).astype(BF16)
    lane = lax.broadcasted_iota(jnp.int32, (length, 128), 1)
    small_lane = lax.broadcasted_iota(jnp.int32, (8, 128), 1)
    peaks = jnp.zeros((8, 128), F32)
    pipeline.run(1)
    for j in range(chunks):
        both = contract_cols(chunk_of(queries_ref, j), pair_of(keys_ref, j, group_size, lane)) * SCORE_SCALE
        low = []
        for half in (0, 1):
            scores = jnp.where(allowed, both[:, length * half : length * (half + 1)], NEGATIVE)
            row_max = jnp.max(scores, axis=1, keepdims=True)
            peak = jnp.max(row_max, axis=0, keepdims=True)
            peaks = jnp.where(small_lane == 2 * j + half, peak, peaks)
            expo = jnp.exp(scores - row_max)
            prob = expo / jnp.sum(expo, axis=1, keepdims=True)
            probs_ref[j, :, length * half : length * (half + 1)] = prob
            low.append(prob.astype(BF16))
        mixed = jnp.dot(
            jnp.concatenate(low, axis=1),
            pair_of(values_ref, j, group_size, lane),
            preferred_element_type=F32,
        )
        head_out_ref[:, 128 * j : 128 * (j + 1)] = mixed.astype(BF16)
        pipeline.run(1)
    peak_ref[...] = peaks
    keeps = [
        pltpu.make_async_copy(src, dst, keep_sems.at[i])
        for i, (src, dst) in enumerate(
            (
                (query_all, query_keep),
                (key_all, key_keep),
                (value_all, value_keep),
                (out_all, out_keep),
                (cot_all, cot_keep),
            )
        )
    ]
    for c in keeps[:3]:
        c.start()
    out.take_rest()
    keeps[3].start()
    mix_mine[...] = contract_cols(head_out_ref[...], out_all[...].reshape(width, q_cols))
    swap = remote(mix_mine, mix_other, mix_sems.at[0], mix_sems.at[1], place.twin())
    swap.start()
    swap.wait()
    hidden = tokens_ref[...].astype(F32) + RESIDUAL * (mix_mine[...] + mix_other[...])
    hidden_ref[...] = hidden
    inv_moe = lax.rsqrt(jnp.mean(hidden * hidden, axis=1, keepdims=True) + EPSILON)
    moe_in_ref[...] = (hidden * inv_moe * gains_ref[2:3, :]).astype(BF16)

    pipeline.until(len(pipeline.gathers) - 1)

    def rest(slot, carry):
        for cot in cots:
            cot.take_compact(slot)
        return carry

    lax.fori_loop(2 * line, count, rest, 0)
    for g in gathers + cots:
        g.settle()

    def other(slot, carry):
        for cot in cots:
            cot.twin.wait_send(slot)
            cot.twin.take(slot)
        return carry

    lax.fori_loop(0, count, other, 0)
    keeps[4].start()
    for c in keeps:
        c.wait()


ANY = pl.BlockSpec(memory_space=pl.ANY)
IN_VMEM = pl.BlockSpec(memory_space=pltpu.VMEM)


def params(number):
    return pltpu.CompilerParams(
        collective_id=number, has_side_effects=True, vmem_limit_bytes=56 * 2**20
    )


def capacity_of(length, experts):
    most = 4 * (9 * length * TOP // (32 * experts))
    return min(-(-most // 16) * 16, length)


def run_forward(line, group_size, tokens, query, key, value, out, cotangent, *small):
    count = 4 * line
    length, width = tokens.shape
    q_cols, kv_cols = query.shape[1], key.shape[1]
    half, cap = width // 2, capacity_of(length, count)
    blocks = [x.shape for x in (query, key, value, out)] + [(cap, width)]
    shape = jax.ShapeDtypeStruct
    outs = [
        shape((length, width), BF16),
        shape((length, width), F32),
        shape((length, width), BF16),
        shape((length, q_cols), BF16),
        shape((length, q_cols), BF16),
        shape((length, kv_cols), BF16),
        shape((length, kv_cols), BF16),
        shape((q_cols // 128, length, 2 * length), F32),
        shape((8, 128), F32),
        shape((3, length, 128), F32),
        shape((8, width), F32),
        shape((count, 8, 128), F32),
    ]
    return pl.pallas_call(
        functools.partial(forward_kernel, line, group_size),
        out_shape=outs + [shape((count, *s), BF16) for s in blocks],
        in_specs=[IN_VMEM] + [ANY] * 5 + [IN_VMEM] * len(small),
        out_specs=[IN_VMEM] * len(outs) + [ANY] * 5,
        scratch_shapes=[pltpu.VMEM((count, *s), BF16) for s in blocks[:4]]
        + [
            pltpu.VMEM((PIECES, 2 * line, length, half // PIECES), BF16),
            pltpu.VMEM((PIECES, 2 * line, cap, half // PIECES), BF16),
            pltpu.VMEM((count, cap, width), BF16),
            pltpu.VMEM((count, cap, length), BF16),
            pltpu.VMEM((2 * line, cap, length), BF16),
            pltpu.VMEM((length, width), F32),
            pltpu.VMEM((length, width), F32),
            pltpu.VMEM((count, 8, 128), F32),
            pltpu.SemaphoreType.DMA((4 + PIECES, 5 * line)),
            pltpu.SemaphoreType.DMA((4 + PIECES, count)),
            pltpu.SemaphoreType.DMA((count,)),
            pltpu.SemaphoreType.DMA((count,)),
            pltpu.SemaphoreType.DMA((PIECES, 2, count)),
            pltpu.SemaphoreType.DMA((4 + PIECES,)),
            pltpu.SemaphoreType.DMA((5,)),
            pltpu.SemaphoreType.DMA((2,)),
        ],
        compiler_params=params(0),
        name="run_forward",
    )(tokens, query, key, value, out, cotangent, *small)


def experts_kernel(
    line,
    rows_ref,
    cot_ref,
    notes_ref,
    gate_ref,
    up_ref,
    down_ref,
    d_rows_ref,
    mix_ref,
    grad_gate_ref,
    grad_up_ref,
    grad_down_ref,
    dense,
    packed,
    rows,
    cots,
    own_pick,
    other_pick,
    gates,
    active,
    d_gate,
    d_up,
    d_active,
    grad_stage,
    mix_stage,
    grad_compact,
    mix_compact,
    grad_dense,
    mix_dense,
    grads,
    total,
    grad_from_b,
    mix_from_b,
    from_a,
    from_z,
    reduce_sems,
    gather_send,
    gather_recv,
    twin_sems,
    load_sems,
    last_sems,
    store_sems,
):
    place = Place(line)
    count = 4 * line
    cap, width = rows.shape[1:]
    tile_rows = line * cap
    mine, _ = halves(place, width)
    spans, their_spans, piece = pieces_of(place, width)
    load = pltpu.make_async_copy(cot_ref, cots, load_sems)
    load.start()
    for i in range(PIECES):
        dense[i, place.z] = rows_ref[:, spans[i]]
    picks = (own_pick, other_pick)
    selections(place, notes_ref, own_pick, other_pick, gates)
    enter(place)
    gathers = [
        PackedGather(
            place,
            dense.at[i],
            packed.at[i],
            rows,
            picks,
            spans[i],
            gather_send.at[i],
            gather_recv.at[i],
            twin_sems.at[i],
        )
        for i in range(PIECES)
    ]
    grad_twins = [
        Twin(
            place,
            lambda s, i=i: grad_stage.at[s, :, their_spans[i]],
            lambda s, i=i: grad_compact.at[i, s],
            twin_sems.at[PIECES + i, 0],
            twin_sems.at[PIECES + i, 1],
        )
        for i in range(PIECES)
    ]
    mix_twin = Twin(
        place,
        lambda s: mix_stage.at[s, :, halves(place, width)[1]],
        lambda s: mix_compact.at[s],
        twin_sems.at[2 * PIECES, 0],
        twin_sems.at[2 * PIECES, 1],
    )
    reduces = [
        PackedReduce(
            place,
            grad_compact.at[i],
            picks,
            grad_dense.at[i],
            grad_from_b.at[i],
            from_a.at[i],
            from_z.at[i],
            reduce_sems.at[i, 0],
            reduce_sems.at[i, 1],
        )
        for i in range(PIECES)
    ]
    mix_reduce = PackedReduce(
        place,
        mix_compact,
        picks,
        mix_dense,
        mix_from_b,
        None,
        None,
        reduce_sems.at[PIECES, 0],
        reduce_sems.at[PIECES, 1],
    )

    def group_of(group):
        return pl.ds(line * group, line), pl.ds(tile_rows * group, tile_rows)

    def slots_of(group):
        return [line * group + z for z in range(line)]

    def ahead(group):
        some, flat = group_of(group)
        cot = cots[some].reshape(tile_rows, width).astype(F32)
        d_out = (gates[flat, :] * (RESIDUAL * cot)).astype(BF16)
        cots[some] = d_out.reshape(line, cap, width)
        d_active[flat, :] = jnp.dot(d_out, down_ref[...], preferred_element_type=F32)

    def work(group):
        some, flat = group_of(group)
        for slot in slots_of(group):
            for g in gathers:
                g.twin.take(slot)
        x = rows[some].reshape(tile_rows, width)
        gate_pre = jnp.dot(x, gate_ref[...], preferred_element_type=F32)
        up_pre = jnp.dot(x, up_ref[...], preferred_element_type=F32)
        sigmoid = 1.0 / (1.0 + jnp.exp(-gate_pre))
        silu = gate_pre * sigmoid
        active[flat, :] = (silu * up_pre).astype(BF16)
        d_act = d_active[flat, :]
        d_g = (d_act * up_pre * sigmoid * (1.0 + gate_pre * (1.0 - sigmoid))).astype(BF16)
        d_u = (d_act * silu).astype(BF16)
        d_gate[flat, :] = d_g
        d_up[flat, :] = d_u
        d_in = contract_cols(d_g, gate_ref[...]) + contract_cols(d_u, up_ref[...])
        grad_stage[some] = d_in.astype(BF16).reshape(line, cap, width)
        for twin in grad_twins:
            for slot in slots_of(group):
                twin.start(slot)

    def mix_work(group):
        some, flat = group_of(group)
        mix = gates[flat, :] * contract_cols(active[flat, :], down_ref[...])
        mix_stage[some] = mix.astype(BF16).reshape(line, cap, width)
        for slot in slots_of(group):
            mix_twin.start(slot)

    def fold(twin, stage, span, compact, group, send=None):
        def one(slot, carry):
            twin.take(slot)
            compact[slot] = (compact[slot].astype(F32) + stage[slot, :, span].astype(F32)).astype(BF16)
            if send is not None:
                send(slot - 2 * line)
            return carry

        lax.fori_loop(line * group, line * (group + 1), one, 0)

    def grad_fold(group, send=False):
        for i in range(PIECES):
            to_b = reduces[i].send_b if send else None
            fold(grad_twins[i], grad_stage, spans[i], grad_compact.at[i], group, to_b)

    def take_group(group):
        for slot in slots_of(group):
            for g in gathers:
                g.take_compact(slot)

    def weight_grad(number, i):
        left, right = ((cots, active), (rows, d_gate), (rows, d_up))[number]
        left = left.reshape(count * cap, width)
        span = pl.ds(512 * i, 512)
        grads[number, span, :] = contract_rows(left[:, span], right[...])

    stores = []

    def store(number):
        out_ref = (grad_down_ref, grad_gate_ref, grad_up_ref)[number]
        stores.append(pltpu.make_async_copy(grads.at[number], out_ref, store_sems.at[number]))
        stores[-1].start()

    mix_fold = functools.partial(fold, mix_twin, mix_stage, mine, mix_compact)
    pipeline = Pipeline(gathers, 0)
    pipeline.run(1)
    load.wait()
    for group in range(4):
        ahead(group)
        pipeline.run(1)
    pipeline.until(PIECES - 1)
    work(0)
    take_group(2)
    work(2)
    work(1)
    take_group(3)
    grad_fold(2, True)
    work(3)
    grad_fold(3, True)
    mix_work(1)
    grad_fold(0)
    mix_work(2)
    grad_fold(1)
    mix_work(3)
    mix_fold(2, mix_reduce.send_b)
    mix_work(0)
    columns = width // 512
    order = ends_first(line)
    for r in reduces:
        for z in order:
            r.fold_b(z)
    weight_grad(0, 0)
    for at, r in enumerate(reduces):
        for z in order:
            r.fold_b(line + z)
            r.send_a(z)
        if at == 0:
            mix_fold(3, mix_reduce.send_b)
    for i in range(1, columns):
        weight_grad(0, i)
    store(0)
    for r in reduces:
        r.finish_line()
        weight_grad(1, reduces.index(r))
    for i in range(PIECES, columns):
        weight_grad(1, i)
    store(1)
    mix_fold(0)
    mix_fold(1)
    lasts = []
    for i, r in enumerate(reduces):
        r.result(total.at[i])
        d_rows_ref[:, spans[i]] = total[i]
        there = d_rows_ref.at[:, spans[i]]
        lasts.append(remote(total.at[i], there, last_sems.at[0, i], last_sems.at[1, i], place.twin()))
        lasts[-1].start()
    for i in range(columns):
        weight_grad(2, i)
    store(2)
    for k in range(2 * line):
        mix_reduce.fold_b(k)
    stores.append(pltpu.make_async_copy(mix_dense, mix_ref, store_sems.at[3]))
    stores[-1].start()
    for r in reduces:
        r.settle()
    mix_reduce.settle_b()
    for g in gathers:
        g.settle()

    twins = [g.twin for g in gathers] + grad_twins + [mix_twin]

    def settle(slot, carry):
        for twin in twins:
            twin.wait_send(slot)
        return carry

    lax.fori_loop(0, count, settle, 0)
    for c in stores + lasts:
        c.wait()


def run_experts(line, rows, cots, notes, gate, up, down):
    count = 4 * line
    length, width = rows.shape
    cap = cots.shape[1]
    half, hidden = width // 2, gate.shape[1]
    piece = half // PIECES
    grad = jax.ShapeDtypeStruct((width, hidden), F32)
    return pl.pallas_call(
        functools.partial(experts_kernel, line),
        out_shape=[
            jax.ShapeDtypeStruct((length, width), F32),
            jax.ShapeDtypeStruct((2 * line, length, half), BF16),
            grad,
            grad,
            grad,
        ],
        in_specs=[IN_VMEM, ANY, IN_VMEM, IN_VMEM, IN_VMEM, IN_VMEM],
        out_specs=[IN_VMEM, ANY, ANY, ANY, ANY],
        scratch_shapes=[
            pltpu.VMEM((PIECES, 2 * line, length, piece), BF16),
            pltpu.VMEM((PIECES, 2 * line, cap, piece), BF16),
            pltpu.VMEM((count, cap, width), BF16),
            pltpu.VMEM((count, cap, width), BF16),
            pltpu.VMEM((count, cap, length), BF16),
            pltpu.VMEM((2 * line, cap, length), BF16),
            pltpu.VMEM((count * cap, 1), F32),
            pltpu.VMEM((count * cap, hidden), BF16),
            pltpu.VMEM((count * cap, hidden), BF16),
            pltpu.VMEM((count * cap, hidden), BF16),
            pltpu.VMEM((count * cap, hidden), F32),
            pltpu.VMEM((count, cap, width), BF16),
            pltpu.VMEM((count, cap, width), BF16),
            pltpu.VMEM((PIECES, count, cap, piece), BF16),
            pltpu.VMEM((count, cap, half), BF16),
            pltpu.VMEM((PIECES, 2 * line, length, piece), BF16),
            pltpu.VMEM((2 * line, length, half), BF16),
            pltpu.VMEM((3, width, hidden), F32),
            pltpu.VMEM((PIECES, length, piece), F32),
            pltpu.VMEM((PIECES, 2 * line, cap, piece), BF16),
            pltpu.VMEM((2 * line, cap, half), BF16),
            pltpu.VMEM((PIECES, line, length, piece), BF16),
            pltpu.VMEM((PIECES, line, length, piece), BF16),
            pltpu.SemaphoreType.DMA((PIECES + 1, 2, 4 * line)),
            pltpu.SemaphoreType.DMA((PIECES, 5 * line)),
            pltpu.SemaphoreType.DMA((PIECES, count)),
            pltpu.SemaphoreType.DMA((2 * PIECES + 1, 2, count)),
            pltpu.SemaphoreType.DMA,
            pltpu.SemaphoreType.DMA((2, PIECES)),
            pltpu.SemaphoreType.DMA((4,)),
        ],
        compiler_params=params(2),
        name="run_experts",
    )(rows, cots, notes, gate, up, down)


def backward_kernel(
    line,
    group_size,
    tokens_ref,
    hidden_ref,
    d_rows_ref,
    cot_ref,
    normed_ref,
    head_out_ref,
    queries_ref,
    keys_ref,
    values_ref,
    probs_ref,
    gains_ref,
    peak_ref,
    tables_ref,
    query_keep,
    key_keep,
    value_keep,
    out_keep,
    mix_ref,
    input_grad_ref,
    output_ref,
    query_sum,
    key_sum,
    value_sum,
    out_sum,
    notes,
    *scratch,
):
    place = Place(line)
    count = 4 * line
    length, width = tokens_ref.shape
    q_cols, kv_cols = queries_ref.shape[1], keys_ref.shape[1]
    shard = width // count
    chunks = q_cols // 128
    (query_all, key_all, value_all, out_all), work = scratch[:4], scratch[4:9]
    rest = scratch[9:34]
    (
        total,
        d_heads,
        d_query,
        d_key,
        d_value,
        part_mine,
        part_other,
        d_hidden_keep,
        mix_total,
        note,
        weight_sems,
        load_sems,
        last_sems,
        part_sems,
        note_sends,
        note_recvs,
    ) = scratch[34:]
    by_part = lambda slot: part_of(place, slot)
    reduces = [
        Reduce(place, work[i], *rest[5 * i : 5 * i + 5], *(() if i == 4 else (by_part,))) for i in range(5)
    ]

    def load(slot):
        return pltpu.make_async_copy(mix_ref.at[slot], work[4].at[slot], load_sems.at[slot])

    def begin(slot, carry):
        load(slot).start()
        return carry

    def loaded(slot, carry):
        load(slot).wait()
        return carry

    lax.fori_loop(0, 2 * line, begin, 0)
    weights = [
        pltpu.make_async_copy(src, dst, weight_sems.at[i])
        for i, (src, dst) in enumerate(
            ((out_keep, out_all), (query_keep, query_all), (key_keep, key_all), (value_keep, value_all))
        )
    ]
    for c in weights:
        c.start()
    enter(place)
    lax.fori_loop(0, 2 * line, loaded, 0)
    mine, theirs = halves(place, width)
    outs = (query_sum, key_sum, value_sum, out_sum, total)
    order = (3, 0, 1, 2)
    mix = reduces[4]
    for z in ends_first(line):
        mix.send_a(z)
    last = remote(total, mix_total.at[:, mine], last_sems.at[0], last_sems.at[1], place.twin())

    def finish(at):
        i = order[at]
        reduces[i].result(outs[i])

    run = Reductions([reduces[i] for i in order], finish)
    hidden = hidden_ref[...]
    inv_moe = lax.rsqrt(jnp.mean(hidden * hidden, axis=1, keepdims=True) + EPSILON)
    unit_moe = hidden * inv_moe
    d_rows = d_rows_ref[...]
    scaled = d_rows * gains_ref[2:3, :]
    d_hidden = cot_ref[...].astype(F32) + inv_moe * (
        scaled - unit_moe * jnp.mean(scaled * unit_moe, axis=1, keepdims=True)
    )
    d_hidden_keep[...] = d_hidden
    moe_gain = jnp.sum(d_rows * unit_moe, axis=0, keepdims=True)
    d_attn = (RESIDUAL * d_hidden).astype(BF16)
    work[3][...] = contract_rows(d_attn, head_out_ref[...]).astype(BF16).reshape(count, shard, q_cols)
    run.ready(1)
    weights[0].wait()
    d_heads[...] = jnp.dot(
        d_attn, out_all[...].reshape(width, q_cols), preferred_element_type=F32
    ).astype(BF16)
    lane = lax.broadcasted_iota(jnp.int32, (length, 128), 1)
    d_key[...] = jnp.zeros_like(d_key)
    d_value[...] = jnp.zeros_like(d_value)
    tables = [tables_ref[i] for i in range(3)]
    mix.finish_line()
    for j in range(chunks):
        d_out = chunk_of(d_heads, j)
        keys = pair_of(keys_ref, j, group_size, lane)
        d_prob = contract_cols(d_out, pair_of(values_ref, j, group_size, lane))
        low, d_scores = [], []
        for half in (0, 1):
            side = slice(length * half, length * (half + 1))
            prob = probs_ref[j, :, side]
            grad = d_prob[:, side]
            inner = jnp.sum(prob * grad, axis=1, keepdims=True)
            d_scores.append((prob * (grad - inner)).astype(BF16))
            low.append(prob.astype(BF16))
        d_scores = jnp.concatenate(d_scores, axis=1)
        d_values = contract_rows(jnp.concatenate(low, axis=1), d_out)
        d_keys = contract_rows(d_scores, chunk_of(queries_ref, j)) * SCORE_SCALE
        turned = rope_chunk(
            jnp.dot(d_scores, keys, preferred_element_type=F32) * SCORE_SCALE, tables, -1.0
        )
        d_query[:, 128 * j : 128 * (j + 1)] = turned.astype(BF16)
        for half in (0, 1):
            group = (2 * j + half) // group_size
            side = slice(length * half, length * (half + 1))
            cols = slice(128 * (group // 2), 128 * (group // 2 + 1))
            d_key[:, cols] += place_half(d_keys[side], half, group % 2, lane)
            d_value[:, cols] += place_half(d_values[side], half, group % 2, lane)
        run.run(1)
    normed = normed_ref[...]
    work[0][...] = contract_rows(normed, d_query[...]).astype(BF16).reshape(count, shard, q_cols)
    run.ready(2)
    d_key_lin = jnp.concatenate(
        [rope_chunk(chunk_of(d_key, j), tables, -1.0) for j in range(kv_cols // 128)], axis=1
    ).astype(BF16)
    d_value_lin = d_value[...].astype(BF16)
    run.run(2)
    work[1][...] = contract_rows(normed, d_key_lin).astype(BF16).reshape(count, shard, kv_cols)
    work[2][...] = contract_rows(normed, d_value_lin).astype(BF16).reshape(count, shard, kv_cols)
    run.ready(4)
    run.run(2)
    mix.result(total)
    mix_total[:, mine] = total[...]
    last.start()
    for c in weights[1:]:
        c.wait()
    part_mine[...] = (
        contract_cols(d_query[...], query_all[...].reshape(width, q_cols))
        + contract_cols(d_key_lin, key_all[...].reshape(width, kv_cols))
        + contract_cols(d_value_lin, value_all[...].reshape(width, kv_cols))
    )
    swap = remote(part_mine, part_other, part_sems.at[0], part_sems.at[1], place.twin())
    swap.start()
    run.run(4)
    swap.wait()
    d_normed = part_mine[...] + part_other[...]
    inputs = tokens_ref[...].astype(F32)
    inv_attn = lax.rsqrt(jnp.mean(inputs * inputs, axis=1, keepdims=True) + EPSILON)
    unit_attn = inputs * inv_attn
    scaled = d_normed * gains_ref[1:2, :]
    input_grad_ref[...] = d_hidden_keep[...] + inv_attn * (
        scaled - unit_attn * jnp.mean(scaled * unit_attn, axis=1, keepdims=True)
    )
    attn_gain = jnp.sum(d_normed * unit_attn, axis=0, keepdims=True)
    rows = jnp.concatenate([attn_gain, moe_gain, jnp.zeros((6, width), F32)], axis=0)
    row = lax.broadcasted_iota(jnp.int32, (8, 128), 0)
    peaks = jnp.broadcast_to(peak_ref[0:1, :], (8, 128))
    for p in range(count):
        turned = pltpu.roll(rows, width - shard * p, 1) if p else rows
        note[p] = jnp.where(row == 2, peaks, turned[:, :128])
    exchange = Notes(place, note, notes, note_sends, note_recvs, False)
    exchange.start()
    run.complete()
    for r in reduces[:4]:
        r.settle()
    mix.settle_a()
    last.wait()
    output_ref[...] = (hidden_ref[...] + RESIDUAL * mix_total[...]).astype(BF16)
    exchange.finish()


def run_backward(line, group_size, kept, keeps, mix):
    count = 4 * line
    tokens, queries, keys = kept[0], kept[6], kept[7]
    length, width = tokens.shape
    q_cols, kv_cols = queries.shape[1], keys.shape[1]
    blocks = [x.shape[1:] for x in keeps] + [mix.shape[1:]]
    half = width // 2
    shape = jax.ShapeDtypeStruct
    outs = (
        [shape((length, width), F32), shape((length, width), BF16)]
        + [shape(s, F32) for s in blocks[:4]]
        + [shape((count, 8, 128), F32)]
    )
    return pl.pallas_call(
        functools.partial(backward_kernel, line, group_size),
        out_shape=outs,
        in_specs=[IN_VMEM] * len(kept) + [ANY] * 5,
        out_specs=[IN_VMEM] * len(outs),
        scratch_shapes=[pltpu.VMEM(x.shape, BF16) for x in keeps]
        + [pltpu.VMEM((count, *s), BF16) for s in blocks[:4]]
        + [pltpu.VMEM(mix.shape, BF16)]
        + [x for s in blocks for x in reduce_scratch(line, s)]
        + [
            pltpu.VMEM((length, half), F32),
            pltpu.VMEM((length, q_cols), BF16),
            pltpu.VMEM((length, q_cols), BF16),
            pltpu.VMEM((length, kv_cols), F32),
            pltpu.VMEM((length, kv_cols), F32),
            pltpu.VMEM((length, width), F32),
            pltpu.VMEM((length, width), F32),
            pltpu.VMEM((length, width), F32),
            pltpu.VMEM((length, width), F32),
            pltpu.VMEM((count, 8, 128), F32),
            pltpu.SemaphoreType.DMA((4,)),
            pltpu.SemaphoreType.DMA((count,)),
            pltpu.SemaphoreType.DMA((2,)),
            pltpu.SemaphoreType.DMA((2,)),
            pltpu.SemaphoreType.DMA((count,)),
            pltpu.SemaphoreType.DMA((count,)),
        ],
        compiler_params=params(3),
        name="run_backward",
    )(*kept, *keeps, mix)


def finish_kernel(
    group_size,
    output_in,
    input_grad_in,
    query_in,
    key_in,
    value_in,
    out_in,
    notes,
    query_ref,
    key_ref,
    gate_in,
    up_in,
    down_in,
    output,
    input_grad,
    grad_query,
    grad_key,
    grad_value,
    grad_out,
    gain_a,
    gain_m,
    clipped_query,
    clipped_key,
    grad_gate,
    grad_up,
    grad_down,
    stage,
    sems,
):
    pairs = ((gate_in, grad_gate), (up_in, grad_up), (down_in, grad_down))
    takes = [pltpu.make_async_copy(src, stage.at[i], sems.at[0, i]) for i, (src, _) in enumerate(pairs)]
    copies = [pltpu.make_async_copy(stage.at[i], dst.at[0], sems.at[1, i]) for i, (_, dst) in enumerate(pairs)]
    for c in takes:
        c.start()
    output[...] = output_in[...]
    input_grad[...] = input_grad_in[...]
    grad_query[...] = query_in[...]
    grad_key[...] = key_in[...]
    grad_value[...] = value_in[...]
    grad_out[...] = out_in[...]
    for take, c in zip(takes, copies):
        take.wait()
        c.start()
    total, peaks = notes[0], notes[0]
    for p in range(1, notes.shape[0]):
        total = total + notes[p]
        peaks = jnp.maximum(peaks, notes[p])
    shard = gain_a.shape[1]
    gain_a[...] = total[0:1, :shard]
    gain_m[...] = total[1:2, :shard]
    factor = CLIP_LIMIT / jnp.maximum(peaks, CLIP_LIMIT)
    root = jnp.sqrt(factor)
    lane = lax.broadcasted_iota(jnp.int32, (8, 128), 1)

    def scale(h):
        return jnp.max(jnp.where(lane == h, root, 0.0), axis=1, keepdims=True)[2:3, :]

    heads = query_ref.shape[1] // HEAD_SIZE
    wide = lax.broadcasted_iota(jnp.int32, (1, 128), 1)
    scales = [scale(h) for h in range(heads)]
    for j in range(heads // 2):
        row = jnp.where(wide < HEAD_SIZE, scales[2 * j], scales[2 * j + 1])
        cols = slice(128 * j, 128 * (j + 1))
        clipped_query[:, cols] = query_ref[:, cols].astype(F32) * row
    least = [
        functools.reduce(jnp.minimum, scales[group_size * g : group_size * (g + 1)])
        for g in range(heads // group_size)
    ]
    for j in range(len(least) // 2):
        row = jnp.where(wide < HEAD_SIZE, least[2 * j], least[2 * j + 1])
        cols = slice(128 * j, 128 * (j + 1))
        clipped_key[:, cols] = key_ref[:, cols].astype(F32) * row
    for c in copies:
        c.wait()


def finish(group_size, found, notes, query, key, expert_grads):
    shape = jax.ShapeDtypeStruct
    shard = query.shape[0]
    outs = [shape(x.shape, x.dtype) for x in found] + [
        shape((1, shard), F32),
        shape((1, shard), F32),
        shape(query.shape, F32),
        shape(key.shape, F32),
    ]
    return pl.pallas_call(
        functools.partial(finish_kernel, group_size),
        out_shape=outs + [shape((1, *g.shape), F32) for g in expert_grads],
        in_specs=[IN_VMEM] * 9 + [ANY] * 3,
        out_specs=[IN_VMEM] * 10 + [ANY] * 3,
        scratch_shapes=[
            pltpu.VMEM((3, *expert_grads[0].shape), F32),
            pltpu.SemaphoreType.DMA((2, 3)),
        ],
        compiler_params=pltpu.CompilerParams(vmem_limit_bytes=56 * 2**20),
        name="finish",
    )(*found, notes, query, key, *expert_grads)


def on_device_dense(
    tokens,
    attn_norm_gain,
    w_query,
    key_projection,
    value_projection,
    w_out,
    moe_norm_gain,
    w_gate,
    w_up,
    w_down,
    router_logits,
    expert_ids,
    segment_ids,
    parents,
    cotangent,
):
    length, model_width = tokens.shape
    q_cols, kv_cols = w_query.shape[1], key_projection.shape[1]
    q_heads, kv_heads = q_cols // HEAD_SIZE, kv_cols // HEAD_SIZE
    group_size = q_heads // kv_heads
    count = lax.axis_size("dp")
    line = count // 4
    shard = attn_norm_gain.shape[0]
    (moe_in, hidden, normed, head_out, queries, keys, values, probs, peak, tables, gains, notes, *keeps, cots) = run_forward(
        line,
        group_size,
        tokens,
        w_query,
        key_projection,
        value_projection,
        w_out,
        cotangent,
        attn_norm_gain[None],
        moe_norm_gain[None],
        router_logits.T,
        expert_ids.T,
        segment_ids,
        parents,
    )
    d_moe_in, mix_parts, *expert_grads = run_experts(
        line, moe_in, cots, notes, w_gate[0], w_up[0], w_down[0]
    )
    kept = (tokens, hidden, d_moe_in, cotangent, normed, head_out, queries, keys, values, probs, gains, peak, tables)
    input_grad, output, *grads, sums = run_backward(line, group_size, kept, keeps, mix_parts)
    output, input_grad, gq, gk, gv, go, gain_a, gain_m, clipped_query, clipped_key, gg, gu, gd = finish(
        group_size, (output, input_grad, *grads), sums, w_query, key_projection, expert_grads
    )
    return (
        output,
        input_grad,
        gain_a[0],
        gq,
        gk,
        gv,
        go,
        gain_m[0],
        gg,
        gu,
        gd,
        clipped_query,
        clipped_key,
    )


DENSE_BYTES = 8 * 2**20


def on_device(*args):
    tokens, w_gate = args[0], args[7]
    count, ranks = lax.axis_size("dp"), lax.axis_size("tensor")
    rows_bytes = count * tokens.shape[0] * tokens.shape[1] * 2
    whole_experts = w_gate.shape[2] * ranks == FFE
    dense = whole_experts and ranks == 2 and count % 8 == 0 and rows_bytes <= DENSE_BYTES
    return on_device_dense(*args) if dense else on_device_general(*args)


def solution(mesh):
    in_specs = (
        P("dp", None),
        P("dp"),
        P("dp", "tensor"),
        P("dp", "tensor"),
        P("dp", "tensor"),
        P("dp", "tensor"),
        P("dp"),
        P("dp", None, "tensor"),
        P("dp", None, "tensor"),
        P("dp", None, "tensor"),
        P("dp", None),
        P("dp", None),
        P("dp", None),
        P("dp", None),
        P("dp", None),
    )
    out_specs = (
        P("dp", None),
        P("dp", None),
        P("dp"),
        P("dp", "tensor"),
        P("dp", "tensor"),
        P("dp", "tensor"),
        P("dp", "tensor"),
        P("dp"),
        P("dp", None, "tensor"),
        P("dp", None, "tensor"),
        P("dp", None, "tensor"),
        P("dp", "tensor"),
        P("dp", "tensor"),
    )
    return jax.shard_map(
        on_device, mesh=mesh, in_specs=in_specs, out_specs=out_specs, check_vma=False
    )
```

```python
import functools
import types

import jax
import jax.numpy as jnp
from jax import lax
from jax.experimental import pallas as pl
from jax.experimental.pallas import tpu as pltpu
from jax.sharding import PartitionSpec as P

HEAD_SIZE = 64
FFE = 512
TOP = 8


EPSILON = 1e-06
SCORE_SCALE = 1.0 / 64.0
RESIDUAL = 0.22
THETA = 10000.0
CLIP_LIMIT = 2.0
NEGATIVE = -1e30


def tree_layout(seg_row, par_row):
    tree_length = seg_row.shape[0]
    seg_count = par_row.shape[0]
    seg_index = jnp.arange(seg_count, dtype=jnp.int32)
    member = (seg_row[:, None] == seg_index[None, :]).astype(jnp.int32)
    seg_len = jnp.sum(member, axis=0)
    seg_start = jnp.sum(jnp.where(seg_index[:, None] > seg_index[None, :], seg_len[None, :], 0), axis=1)
    parent_hot = (par_row[:, None] == seg_index[None, :]).astype(jnp.int32)
    grand_parent = jnp.sum(parent_hot * par_row[None, :], axis=1)
    grand_hot = (grand_parent[:, None] == seg_index[None, :]).astype(jnp.int32)
    parent_len = jnp.sum(parent_hot * seg_len[None, :], axis=1)
    grand_len = jnp.sum(grand_hot * seg_len[None, :], axis=1)
    offset = jnp.where(seg_index != 0, parent_len, 0) + jnp.where(par_row != 0, grand_len, 0)
    tok_start = jnp.sum(member * seg_start[None, :], axis=1)
    tok_offset = jnp.sum(member * offset[None, :], axis=1)
    places = jnp.arange(tree_length, dtype=jnp.int32)
    position = (places - tok_start + tok_offset).astype(jnp.float32)
    identity = (seg_index[:, None] == seg_index[None, :]).astype(jnp.int32)
    ancestor = jnp.minimum(identity + parent_hot + grand_hot, 1)
    reached = jnp.dot(member, ancestor)
    linked = jnp.dot(reached, member.T) > 0
    allowed = linked & (places[None, :] <= places[:, None])
    return (position, allowed)


def rope_tables(position, head_dim):
    half_dim = head_dim // 2
    frequency = THETA ** (-2.0 * jnp.arange(half_dim, dtype=jnp.float32) / head_dim)
    angles = position[:, None] * frequency[None, :]
    return (jnp.cos(angles)[:, None, :], jnp.sin(angles)[:, None, :])


def apply_rotary(values_in, cosine_table, sine_values):
    half_dim = values_in.shape[-1] // 2
    first_half = values_in[..., :half_dim]
    second_half = values_in[..., half_dim:]
    return jnp.concatenate(
        [
            first_half * cosine_table - second_half * sine_values,
            second_half * cosine_table + first_half * sine_values,
        ],
        axis=-1,
    )


def rotate_back(grads_in, cosine_table, sine_values):
    half_dim = grads_in.shape[-1] // 2
    first_half = grads_in[..., :half_dim]
    second_half = grads_in[..., half_dim:]
    return jnp.concatenate(
        [
            first_half * cosine_table + second_half * sine_values,
            second_half * cosine_table - first_half * sine_values,
        ],
        axis=-1,
    )


def slot_tables(routes, experts, capacity):
    flat_ids = routes.reshape(-1)
    row_count = flat_ids.shape[0]
    member = (flat_ids[:, None] == jnp.arange(experts, dtype=jnp.int32)[None, :]).astype(jnp.int32)
    row_total = flat_ids.shape[0]
    before = jnp.dot((jnp.arange(row_total)[:, None] > jnp.arange(row_total)[None, :]).astype(jnp.float32), member.astype(jnp.float32), precision=lax.Precision.HIGHEST).astype(jnp.int32)
    slot_index = jnp.sum(before * member, axis=1)
    target = flat_ids * capacity + slot_index
    source = (
        jnp.full((experts * capacity,), -1, jnp.int32)
        .at[target]
        .set(jnp.arange(row_count, dtype=jnp.int32))
    )
    return (flat_ids, slot_index, source)


def contract_rows(left, right):
    return lax.dot_general(
        left, right, (((0,), (0,)), ((), ())), preferred_element_type=jnp.float32
    )


def contract_cols(left, right):
    return lax.dot_general(
        left, right, (((1,), (1,)), ((), ())), preferred_element_type=jnp.float32
    )


def expert_forward(inputs, gate_w, up_w, down_w):
    gate_pre = jnp.dot(inputs, gate_w, preferred_element_type=jnp.float32)
    up_pre = jnp.dot(inputs, up_w, preferred_element_type=jnp.float32)
    active = (gate_pre / (1.0 + jnp.exp(-gate_pre)) * up_pre).astype(jnp.bfloat16)
    return (contract_cols(active, down_w), (gate_pre, up_pre, active))


def expert_backward(inputs, grads_out, gate_w, up_w, down_w, kept_acts):
    gate_pre, up_pre, active = kept_acts
    d_active = jnp.dot(grads_out, down_w, preferred_element_type=jnp.float32)
    grad_down = contract_rows(grads_out, active)
    sigmoid_val = 1.0 / (1.0 + jnp.exp(-gate_pre))
    d_gate = (d_active * up_pre * sigmoid_val * (1.0 + gate_pre * (1.0 - sigmoid_val))).astype(
        jnp.bfloat16
    )
    d_up = (d_active * gate_pre * sigmoid_val).astype(jnp.bfloat16)
    grad_gate = contract_rows(inputs, d_gate)
    grad_up = contract_rows(inputs, d_up)
    d_inputs = contract_cols(d_gate, gate_w) + contract_cols(d_up, up_w)
    return (d_inputs, grad_gate, grad_up, grad_down)


def send_rows(rows_in):
    return lax.all_to_all(rows_in, "dp", split_axis=0, concat_axis=0, tiled=True)


def return_rows(rows_in):
    return lax.all_to_all(
        rows_in.astype(jnp.bfloat16), "dp", split_axis=0, concat_axis=0, tiled=True
    ).astype(rows_in.dtype)


def send_grads(rows_in):
    return lax.all_to_all(rows_in, "dp", split_axis=0, concat_axis=0, tiled=True)


def return_grads(rows_in):
    return lax.all_to_all(
        rows_in.astype(jnp.bfloat16), "dp", split_axis=0, concat_axis=0, tiled=True
    ).astype(rows_in.dtype)


def share_slots(partial_rows):
    return lax.psum_scatter(partial_rows, "tensor", scatter_dimension=1, tiled=True)


def on_device_general(
    tokens,
    attn_norm_gain,
    w_query,
    key_projection,
    value_projection,
    w_out,
    moe_norm_gain,
    w_gate,
    w_up,
    w_down,
    router_logits,
    expert_ids,
    segment_ids,
    parents,
    cotangent,
):
    length = tokens.shape[0]
    model_width = tokens.shape[1]
    q_cols = w_query.shape[1]
    kv_cols = key_projection.shape[1]
    q_heads = q_cols // HEAD_SIZE
    kv_heads = kv_cols // HEAD_SIZE
    group_size = q_heads // kv_heads
    dp_size = lax.axis_size("dp")
    tensor_ranks = lax.axis_size("tensor")
    replicas = FFE // (w_gate.shape[2] * tensor_ranks)
    experts = dp_size // replicas
    capacity = 4 * (9 * length * TOP // (32 * experts))
    share_rows = capacity // tensor_ranks
    first_slot = lax.axis_index("tensor") * share_rows
    block_rows = min(length, 512)
    attn_gain, moe_gain, query_w, key_weight, value_weight, out_w = (
        lax.all_gather(attn_norm_gain, "dp", axis=0, tiled=True),
        lax.all_gather(moe_norm_gain, "dp", axis=0, tiled=True),
        lax.all_gather(w_query, "dp", axis=0, tiled=True),
        lax.all_gather(key_projection, "dp", axis=0, tiled=True),
        lax.all_gather(value_projection, "dp", axis=0, tiled=True),
        lax.all_gather(w_out, "dp", axis=0, tiled=True),
    )
    attn_gain_f = attn_gain.astype(jnp.float32)
    moe_gain_f = moe_gain.astype(jnp.float32)
    inputs = tokens.astype(jnp.float32)
    inv_attn = lax.rsqrt(jnp.mean(inputs * inputs, axis=1, keepdims=True) + EPSILON)
    unit_attn = inputs * inv_attn
    normalized_rows = (unit_attn * attn_gain_f).astype(jnp.bfloat16)
    position, allowed = tree_layout(segment_ids[0], parents[0])
    cosine_table, sine_values = rope_tables(position, HEAD_SIZE)
    query_linear = jnp.dot(normalized_rows, query_w, preferred_element_type=jnp.float32).reshape(
        length, q_heads, HEAD_SIZE
    )
    key_linear = jnp.dot(normalized_rows, key_weight, preferred_element_type=jnp.float32).reshape(
        length, kv_heads, HEAD_SIZE
    )
    query_heads = (
        apply_rotary(query_linear, cosine_table, sine_values)
        .astype(jnp.bfloat16)
        .reshape(length, kv_heads, group_size, HEAD_SIZE)
    )
    key_heads = apply_rotary(key_linear, cosine_table, sine_values).astype(jnp.bfloat16)
    value_heads = (
        jnp.dot(normalized_rows, value_weight, preferred_element_type=jnp.float32)
        .astype(jnp.bfloat16)
        .reshape(length, kv_heads, HEAD_SIZE)
    )
    q_block = query_heads
    mask_rows = allowed[None, None]
    scores = (
        jnp.einsum("qhgd,khd->hgqk", q_block, key_heads, preferred_element_type=jnp.float32)
        * SCORE_SCALE
    )
    scores = jnp.where(mask_rows, scores, NEGATIVE)
    peak_parts = [jnp.max(scores, axis=(2, 3))]
    row_max = jnp.max(scores, axis=3, keepdims=True)
    expo = jnp.exp(scores - row_max)
    row_total = jnp.sum(expo, axis=3, keepdims=True)
    lse_parts = [row_max + jnp.log(row_total)]
    prob_low = (expo / row_total).astype(jnp.bfloat16)
    block_outs = jnp.einsum(
        "hgqk,khd->qhgd", prob_low, value_heads, preferred_element_type=jnp.float32
    )
    head_out = block_outs.reshape(length, q_cols).astype(jnp.bfloat16)
    attn_mix = lax.psum(contract_cols(head_out, out_w), "tensor")
    hidden = inputs + RESIDUAL * attn_mix
    head_peak = lax.pmax(jnp.max(jnp.stack(peak_parts), axis=0).reshape(q_heads), "dp")
    inv_moe = lax.rsqrt(jnp.mean(hidden * hidden, axis=1, keepdims=True) + EPSILON)
    unit_moe = hidden * inv_moe
    moe_in = (unit_moe * moe_gain_f).astype(jnp.bfloat16)
    logit_max = jnp.max(router_logits, axis=1, keepdims=True)
    logit_exp = jnp.exp(router_logits - logit_max)
    gate_probs = logit_exp / jnp.sum(logit_exp, axis=1, keepdims=True)
    flat_ids, slot_index, source = slot_tables(expert_ids, experts, capacity)
    filled = source >= 0
    source_row = jnp.maximum(source, 0)
    source_token = source_row // TOP
    dispatch_rows = jnp.where(
        filled[:, None], moe_in[source_token], jnp.zeros((), jnp.bfloat16)
    ).reshape(experts, capacity, model_width)
    arrived = send_rows(jnp.repeat(dispatch_rows, replicas, axis=0))
    gate_w, up_w, down_w = (w_gate[0], w_up[0], w_down[0])
    expert_in = arrived.reshape(dp_size * capacity, model_width)
    expert_out, kept_acts = expert_forward(expert_in, gate_w, up_w, down_w)
    partial_out = share_slots(expert_out.reshape(dp_size, capacity, model_width))
    back_parts = return_rows(partial_out).reshape(experts, replicas, share_rows, model_width)
    back_rows = (
        jnp.sum(back_parts, axis=1).astype(jnp.bfloat16).reshape(experts * share_rows, model_width)
    )
    own_slot = ((slot_index >= first_slot) & (slot_index < first_slot + share_rows)).reshape(
        length, TOP
    )
    local_index = (
        flat_ids * share_rows + jnp.clip(slot_index - first_slot, 0, share_rows - 1)
    ).reshape(length, TOP)
    mix_part = jnp.zeros((length, model_width), jnp.float32)
    for column in range(TOP):
        gate_weight = jnp.where(own_slot[:, column], gate_probs[:, column], 0.0)
        mix_part = mix_part + gate_weight[:, None] * back_rows[local_index[:, column]].astype(
            jnp.float32
        )
    expert_mix = lax.psum(mix_part.astype(jnp.bfloat16), "tensor").astype(jnp.float32)
    output = (hidden + RESIDUAL * expert_mix).astype(jnp.bfloat16)
    grad_output = cotangent.astype(jnp.float32)
    mix_grad = RESIDUAL * grad_output
    row_gate = gate_probs.reshape(-1)[source_row]
    grad_rows = (
        jnp.where(filled[:, None], row_gate[:, None] * mix_grad[source_token], 0.0)
        .astype(jnp.bfloat16)
        .reshape(experts, capacity, model_width)
    )
    grad_arrived = send_grads(jnp.repeat(grad_rows, replicas, axis=0)).reshape(
        dp_size * capacity, model_width
    )
    d_inputs, grad_gate, grad_up, grad_down = expert_backward(
        expert_in, grad_arrived, gate_w, up_w, down_w, kept_acts
    )
    d_back = share_slots(d_inputs.reshape(dp_size, capacity, model_width))
    grad_gate, grad_up, grad_down = (grad_gate[None], grad_up[None], grad_down[None])
    d_parts = return_grads(d_back).reshape(experts, replicas, share_rows, model_width)
    d_returned = (
        jnp.sum(d_parts, axis=1).astype(jnp.bfloat16).reshape(experts * share_rows, model_width)
    )
    d_mix_part = jnp.zeros((length, model_width), jnp.float32)
    for column in range(TOP):
        d_mix_part = d_mix_part + jnp.where(
            own_slot[:, column][:, None],
            d_returned[local_index[:, column]].astype(jnp.float32),
            0.0,
        )
    d_moe_in = lax.psum(d_mix_part, "tensor")
    scaled_moe = d_moe_in * moe_gain_f
    grad_moe_gain = jnp.sum(d_moe_in * unit_moe, axis=0)
    d_hidden = grad_output + inv_moe * (
        scaled_moe - unit_moe * jnp.mean(scaled_moe * unit_moe, axis=1, keepdims=True)
    )
    d_attn = (RESIDUAL * d_hidden).astype(jnp.bfloat16)
    grad_out_w = contract_rows(d_attn, head_out)
    d_heads = (
        jnp.dot(d_attn, out_w, preferred_element_type=jnp.float32)
        .astype(jnp.bfloat16)
        .reshape(length, kv_heads, group_size, HEAD_SIZE)
    )
    d_query_parts = []
    d_key = jnp.zeros((length, kv_heads, HEAD_SIZE), jnp.float32)
    d_value = jnp.zeros((length, kv_heads, HEAD_SIZE), jnp.float32)
    for block_number, row_begin in enumerate(range(0, length, block_rows)):
        q_block = query_heads
        mask_rows = allowed[None, None]
        scores = (
            jnp.einsum("qhgd,khd->hgqk", q_block, key_heads, preferred_element_type=jnp.float32)
            * SCORE_SCALE
        )
        scores = jnp.where(mask_rows, scores, NEGATIVE)
        prob_full = jnp.exp(scores - lse_parts[block_number])
        prob_low = prob_full.astype(jnp.bfloat16)
        d_value = jnp.einsum(
            "hgqk,qhgd->khd", prob_low, d_heads, preferred_element_type=jnp.float32
        )
        d_prob = jnp.einsum(
            "qhgd,khd->hgqk", d_heads, value_heads, preferred_element_type=jnp.float32
        )
        inner = jnp.sum(prob_full * d_prob, axis=3, keepdims=True)
        d_scores = (prob_full * (d_prob - inner)).astype(jnp.bfloat16)
        d_query_parts.append(
            jnp.einsum("hgqk,khd->qhgd", d_scores, key_heads, preferred_element_type=jnp.float32)
            * SCORE_SCALE
        )
        d_key = (
            jnp.einsum("hgqk,qhgd->khd", d_scores, q_block, preferred_element_type=jnp.float32)
            * SCORE_SCALE
        )
    d_query_all = d_query_parts[0].reshape(length, q_heads, HEAD_SIZE)
    d_query_lin = (
        rotate_back(d_query_all, cosine_table, sine_values)
        .astype(jnp.bfloat16)
        .reshape(length, q_cols)
    )
    d_key_lin = (
        rotate_back(d_key, cosine_table, sine_values).astype(jnp.bfloat16).reshape(length, kv_cols)
    )
    d_value_lin = d_value.astype(jnp.bfloat16).reshape(length, kv_cols)
    grad_query_w = contract_rows(normalized_rows, d_query_lin)
    grad_key_w = contract_rows(normalized_rows, d_key_lin)
    grad_value_w = contract_rows(normalized_rows, d_value_lin)
    d_normed_part = (
        contract_cols(d_query_lin, query_w)
        + contract_cols(d_key_lin, key_weight)
        + contract_cols(d_value_lin, value_weight)
    )
    d_normed = lax.psum(d_normed_part.astype(jnp.bfloat16), "tensor").astype(jnp.float32)
    scaled_attn = d_normed * attn_gain_f
    grad_attn_gain = jnp.sum(d_normed * unit_attn, axis=0)
    input_grad = d_hidden + inv_attn * (
        scaled_attn - unit_attn * jnp.mean(scaled_attn * unit_attn, axis=1, keepdims=True)
    )
    reduced = (
        lax.psum_scatter(grad_attn_gain, "dp", scatter_dimension=0, tiled=True),
        lax.psum_scatter(grad_moe_gain, "dp", scatter_dimension=0, tiled=True),
        lax.psum_scatter(grad_query_w, "dp", scatter_dimension=0, tiled=True),
        lax.psum_scatter(grad_key_w, "dp", scatter_dimension=0, tiled=True),
        lax.psum_scatter(grad_value_w, "dp", scatter_dimension=0, tiled=True),
        lax.psum_scatter(grad_out_w, "dp", scatter_dimension=0, tiled=True),
    )
    scale_factor = CLIP_LIMIT / jnp.maximum(head_peak, CLIP_LIMIT)
    query_scale = jnp.repeat(jnp.sqrt(scale_factor), HEAD_SIZE)
    key_clip_scale = jnp.repeat(
        jnp.sqrt(jnp.min(scale_factor.reshape(kv_heads, group_size), axis=1)), HEAD_SIZE
    )
    clipped_query = w_query.astype(jnp.float32) * query_scale[None, :]
    clipped_key = key_projection.astype(jnp.float32) * key_clip_scale[None, :]
    return (
        output,
        input_grad,
        reduced[0],
        reduced[2],
        reduced[3],
        reduced[4],
        reduced[5],
        reduced[1],
        grad_gate,
        grad_up,
        grad_down,
        clipped_query,
        clipped_key,
    )


MESH_IDS = pl.DeviceIdType.MESH
F32 = jnp.float32
BF16 = jnp.bfloat16


class Place:
    def __init__(self, line):
        self.line = line
        self.count = 4 * line
        me = lax.axis_index("dp")
        self.core = lax.axis_index("tensor")
        self.me = me
        self.z = me // 4
        y, x = (me // 2) % 2, me % 2
        self.step_a, self.step_b = 2 - self.core, 1 + self.core
        self.a = y * (1 - self.core) + x * self.core
        self.b = x * (1 - self.core) + y * self.core

    def part(self, z, a, b):
        return z * 4 + a * self.step_a + b * self.step_b

    def up(self):
        return (self.me + 4, self.core)

    def down(self):
        return (self.me - 4, self.core)

    def beside_a(self):
        return (self.me + self.step_a * (1 - 2 * self.a), self.core)

    def beside_b(self):
        return (self.me + self.step_b * (1 - 2 * self.b), self.core)

    def twin(self):
        return (self.me, 1 - self.core)

    def peer(self, offset):
        return lax.rem(self.me + offset, self.count)


def enter(place):
    barrier = pltpu.get_barrier_semaphore()

    def greet(offset, carry):
        pl.semaphore_signal(
            barrier, inc=1, device_id=(place.peer(offset), place.core), device_id_type=MESH_IDS
        )
        return carry

    lax.fori_loop(1, place.count, greet, 0)
    pl.semaphore_signal(barrier, inc=1, device_id=place.twin(), device_id_type=MESH_IDS)
    pl.semaphore_wait(barrier, place.count)


def remote(src, dst, send_sem, recv_sem, device):
    return pltpu.make_async_remote_copy(
        src_ref=src,
        dst_ref=dst,
        send_sem=send_sem,
        recv_sem=recv_sem,
        device_id=device,
        device_id_type=MESH_IDS,
    )


class Notes:
    def __init__(self, place, src, dst, send_sem, recv_sem, alike):
        self.place, self.src, self.dst = place, src, dst
        self.send_sem, self.recv_sem, self.alike = send_sem, recv_sem, alike

    def _copy(self, offset, source):
        place = self.place
        to = place.peer(offset)
        return remote(
            self.src if self.alike else self.src.at[to],
            self.dst.at[source],
            self.send_sem.at[offset],
            self.recv_sem.at[source],
            (to, place.core),
        )

    def start(self):
        def send(offset, carry):
            self._copy(offset, self.place.me).start()
            return carry

        lax.fori_loop(1, self.place.count, send, 0)
        me = self.place.me
        self.dst[me] = self.src[...] if self.alike else self.src[me]

    def finish(self):
        def settle(offset, carry):
            self._copy(offset, self.place.peer(offset)).wait_recv()
            self._copy(offset, self.place.me).wait_send()
            return carry

        lax.fori_loop(1, self.place.count, settle, 0)


class Gather:
    def __init__(self, place, view, send_sem, recv_sem, fixed=False):
        self.place, self.view, self.fixed = place, view, fixed
        self.send_sem, self.recv_sem = send_sem, recv_sem

    def _copy(self, source, target, sem, device):
        there = self.view(source if self.fixed else target)
        return remote(self.view(source), there, self.send_sem.at[sem], self.recv_sem.at[target], device)

    def _to_z(self, z, way):
        place = self.place
        device = place.up() if way == 0 else place.down()
        return self._copy(z, z, way * place.line + z, device)

    def _to_a(self, z):
        line = self.place.line
        return self._copy(z, line + z, 2 * line + z, self.place.beside_a())

    def _to_b(self, slot):
        line = self.place.line
        return self._copy(slot, 2 * line + slot, 3 * line + slot, self.place.beside_b())

    def take(self, slot):
        self._copy(slot, slot, 0, self.place.beside_b()).wait_recv()

    def near(self, step, action):
        place = self.place
        if step == 0:
            action(place.z)
        else:
            pl.when(place.z >= step)(lambda: action(place.z - step))
            pl.when(place.z + step < place.line)(lambda: action(place.z + step))

    def hand_on(self, slot):
        self._to_b(slot).start()

    def start(self):
        place = self.place
        pl.when(place.z < place.line - 1)(lambda: self._to_z(place.z, 0).start())
        pl.when(place.z > 0)(lambda: self._to_z(place.z, 1).start())
        self._to_a(self.place.z).start()
        self.hand_on(self.place.z)

    def along(self, step):
        place = self.place

        def pass_on(z):
            self.take(z)
            pl.when(jnp.logical_and(z < place.z, place.z < place.line - 1))(lambda: self._to_z(z, 0).start())
            pl.when(jnp.logical_and(z > place.z, place.z > 0))(lambda: self._to_z(z, 1).start())
            self._to_a(z).start()
            self.hand_on(z)

        self.near(step, pass_on)

    def across(self, step):
        line = self.place.line

        def pass_on(z):
            self.take(line + z)
            self.hand_on(line + z)

        self.near(step, pass_on)

    def step(self, number):
        if number == 0:
            self.start()
            return
        if number < self.place.line:
            self.along(number)
        self.across(number - 1)

    def settle(self):
        place = self.place
        line = place.line

        def wait(z, carry):
            self._to_a(z).wait_send()
            self._to_b(z).wait_send()
            self._to_b(line + z).wait_send()
            pl.when(jnp.logical_and(z <= place.z, place.z < line - 1))(lambda: self._to_z(z, 0).wait_send())
            pl.when(jnp.logical_and(z >= place.z, place.z > 0))(lambda: self._to_z(z, 1).wait_send())
            return carry

        lax.fori_loop(0, line, wait, 0)

    def take_rest(self):
        line = self.place.line

        def wait(k, carry):
            self.take(2 * line + k)
            return carry

        lax.fori_loop(0, 2 * line, wait, 0)


class Pipeline:
    def __init__(self, gathers, starts):
        self.gathers, self.starts, self.at = gathers, starts, 0
        self.steps = gathers[0].place.line + 1

    def run(self, number):
        for _ in range(number):
            for g, start in zip(self.gathers, self.starts):
                if 0 <= self.at - start < self.steps:
                    g.step(self.at - start)
            self.at += 1

    def until(self, index):
        self.run(max(0, self.starts[index] + self.steps - self.at))


class Twin:
    def __init__(self, place, source, target, send_sem, recv_sem):
        self.place, self.source, self.target = place, source, target
        self.send_sem, self.recv_sem = send_sem, recv_sem

    def copy(self, slot):
        line = self.place.line
        group = slot // line
        there = slot + line * ((group % 2) - (group // 2))
        return remote(
            self.source(slot),
            self.target(there),
            self.send_sem.at[slot],
            self.recv_sem.at[there],
            self.place.twin(),
        )

    def start(self, slot):
        self.copy(slot).start()

    def take(self, slot):
        remote(
            self.source(slot),
            self.target(slot),
            self.send_sem.at[slot],
            self.recv_sem.at[slot],
            self.place.twin(),
        ).wait_recv()

    def wait_send(self, slot):
        self.copy(slot).wait_send()


class Reduce:
    def __init__(self, place, parts, from_b, from_a, from_z, send_sem, recv_sem, index=lambda slot: slot):
        self.place, self.parts, self.index = place, parts, index
        self.from_b, self.from_a, self.from_z = from_b, from_a, from_z
        self.send_sem, self.recv_sem = send_sem, recv_sem

    def _copy(self, source, target, sem, device):
        return remote(source, target, self.send_sem.at[sem], self.recv_sem.at[sem], device)

    def _to_b(self, k):
        line = self.place.line
        return self._copy(self.parts.at[self.index(2 * line + k)], self.from_b.at[k], k, self.place.beside_b())

    def _to_a(self, z):
        line = self.place.line
        block = self.parts.at[self.index(line + z)]
        return self._copy(block, self.from_a.at[z], 2 * line + z, self.place.beside_a())

    def _to_z(self, target):
        place, line = self.place, self.place.line
        return remote(
            self.parts.at[self.index(target)],
            self.from_z.at[place.z],
            self.send_sem.at[3 * line + target],
            self.recv_sem.at[3 * line + place.z],
            (place.me + 4 * (target - place.z), place.core),
        )

    def _add(self, slot, block):
        at = self.index(slot)
        self.parts[at] = (self.parts[at].astype(F32) + block.astype(F32)).astype(BF16)

    def send_b(self, k):
        self._to_b(k).start()

    def fold_b(self, k):
        self._to_b(k).wait_recv()
        self._add(k, self.from_b[k])

    def send_a(self, z):
        self._to_a(z).start()

    def fold_a(self, z):
        self._to_a(z).wait_recv()
        self._add(z, self.from_a[z])

    def fold_line_a(self):
        line = self.place.line
        for z in ends_first(line):
            self.fold_b(line + z)
            self.send_a(z)

    def fold_line_own(self):
        for z in ends_first(self.place.line):
            self.fold_b(z)

    def send_z(self, z):
        pl.when(self.place.z != z)(lambda: self._to_z(z).start())

    def finish_line(self):
        for z in ends_first(self.place.line):
            self.fold_a(z)
            self.send_z(z)

    def result(self, out):
        place, line = self.place, self.place.line
        out[...] = self.parts[self.index(place.z)].astype(F32)

        def add(z, carry):
            @pl.when(z != place.z)
            def _():
                remote(
                    self.from_z.at[z], self.from_z.at[z], self.send_sem.at[0], self.recv_sem.at[3 * line + z], place.up()
                ).wait_recv()
                out[...] += self.from_z[z].astype(F32)

            return carry

        lax.fori_loop(0, line, add, 0)

    def settle_b(self):
        def wait(k, carry):
            self._to_b(k).wait_send()
            return carry

        lax.fori_loop(0, 2 * self.place.line, wait, 0)

    def settle_hop_a(self):
        def wait(z, carry):
            self._to_a(z).wait_send()
            return carry

        lax.fori_loop(0, self.place.line, wait, 0)

    def settle_z(self):
        place = self.place

        def wait(z, carry):
            pl.when(place.z != z)(lambda: self._to_z(z).wait_send())
            return carry

        lax.fori_loop(0, place.line, wait, 0)

    def settle(self):
        self.settle_b()
        self.settle_hop_a()
        self.settle_z()


class PackedGather(Gather):
    def __init__(self, place, dense, packed, compact, picks, mine, send_sem, recv_sem, twin_sems):
        self.place, self.dense, self.packed, self.compact = place, dense, packed, compact
        self.own_pick, self.other_pick = picks
        self.mine, self.fixed = mine, False
        self.send_sem, self.recv_sem = send_sem, recv_sem
        view = lambda slot: compact.at[slot, :, mine]
        self.twin = Twin(place, view, view, twin_sems.at[0], twin_sems.at[1])

    def view(self, slot):
        return self.dense.at[slot]

    def _to_b(self, slot):
        line = self.place.line
        return remote(
            self.packed.at[slot],
            self.compact.at[2 * line + slot, :, self.mine],
            self.send_sem.at[3 * line + slot],
            self.recv_sem.at[2 * line + slot],
            self.place.beside_b(),
        )

    def take_compact(self, slot):
        line = self.place.line
        self._to_b(slot - 2 * line).wait_recv()
        self.twin.start(slot)

    def take(self, slot):
        self._copy(slot, slot, 0, self.place.beside_b()).wait_recv()

    def hand_on(self, slot):
        block = self.dense[slot]
        self.packed[slot] = jnp.dot(self.other_pick[slot], block, preferred_element_type=F32).astype(BF16)
        self._to_b(slot).start()
        self.compact[slot, :, self.mine] = jnp.dot(
            self.own_pick[slot], block, preferred_element_type=F32
        ).astype(BF16)
        self.twin.start(slot)


class PackedReduce(Reduce):
    def __init__(self, place, compact, picks, *rest):
        super().__init__(place, *rest)
        self.compact = compact
        self.own_pick, self.other_pick = picks

    def _to_b(self, k):
        line = self.place.line
        return self._copy(self.compact.at[2 * line + k], self.from_b.at[k], k, self.place.beside_b())

    def fold_b(self, k):
        self._to_b(k).wait_recv()
        own = contract_rows(self.own_pick[k], self.compact[k])
        self.parts[k] = (own + contract_rows(self.other_pick[k], self.from_b[k])).astype(BF16)


def selections(place, notes, own_pick, other_pick, gates=None):
    line = place.line
    cap, length = own_pick.shape[1:]
    rows = [notes[part_of(place, slot)][0:1, :] for slot in range(4 * line)]
    for slot in range(2 * line):
        note = notes[part_of(place, slot)]
        rows.append(jnp.where(place.core == 0, note[3:4, :], note[4:5, :]))
    before = lax.broadcasted_iota(jnp.int32, (length, length), 0) < lax.broadcasted_iota(
        jnp.int32, (length, length), 1
    )
    weights = jnp.concatenate(rows, axis=0)
    rank = jnp.dot(
        jnp.where(weights > 0.0, 1.0, 0.0).astype(BF16),
        jnp.where(before, 1.0, 0.0).astype(BF16),
        preferred_element_type=F32,
    )
    rank = jnp.where(weights > 0.0, rank, -1.0)
    number = lax.broadcasted_iota(jnp.int32, (cap, length), 0).astype(F32)
    for i in range(len(rows)):
        pick = jnp.where(rank[i : i + 1, :] == number, 1.0, 0.0)
        if i >= 4 * line:
            other_pick[i - 4 * line] = pick.astype(BF16)
            continue
        own_pick[i] = pick.astype(BF16)
        if gates is not None:
            gates[cap * i : cap * (i + 1), :] = jnp.sum(pick * rows[i], axis=1, keepdims=True)


AHEAD = 8


class Reductions:
    def __init__(self, reduces, finish):
        self.reduces, self.finish = reduces, finish
        self.at = self.sent = self.limit = 0
        line = self.line = reduces[0].place.line
        self.ks = [line + z for z in ends_first(line)] + ends_first(line)
        self.steps = [(i, k) for i in range(len(reduces)) for k in self.ks]

    def ready(self, number):
        self.limit = 2 * self.line * number
        self._send()

    def _send(self):
        while self.sent < min(self.at + AHEAD, self.limit):
            i, k = self.steps[self.sent]
            self.reduces[i].send_b(k)
            self.sent += 1

    def run(self, number):
        for _ in range(number):
            self._step()

    def _step(self):
        i, k = self.steps[self.at]
        self.at += 1
        self._send()
        self.reduces[i].fold_b(k)
        if k >= self.line:
            self.reduces[i].send_a(k - self.line)
        if k == self.ks[self.line - 1] and i > 0:
            self.reduces[i - 1].finish_line()
        if k == self.ks[-1] and i > 0:
            self.finish(i - 1)

    def complete(self):
        self.run(len(self.steps) - self.at)
        self.reduces[-1].finish_line()
        self.finish(len(self.reduces) - 1)


def reduce_scratch(line, block):
    return [
        pltpu.VMEM((2 * line, *block), BF16),
        pltpu.VMEM((line, *block), BF16),
        pltpu.VMEM((line, *block), BF16),
        pltpu.SemaphoreType.DMA((4 * line,)),
        pltpu.SemaphoreType.DMA((4 * line,)),
    ]


def ends_first(line):
    order = []
    for i in range((line + 1) // 2):
        order += [i] if i == line - 1 - i else [i, line - 1 - i]
    return order


def part_of(place, slot):
    line = place.line
    group, z = slot // line, slot % line
    flip_a, flip_b = group % 2, group // 2
    a = place.a + flip_a * (1 - 2 * place.a)
    b = place.b + flip_b * (1 - 2 * place.b)
    return place.part(z, a, b)


PIECES = 2


def pieces_of(place, width):
    piece = width // 2 // PIECES

    def spans(core):
        starts = [pl.multiple_of((core * PIECES + i) * piece, 128) for i in range(PIECES)]
        return [pl.ds(start, piece) for start in starts]

    return spans(place.core), spans(1 - place.core), piece


def halves(place, width):
    half = width // 2
    mine = pl.ds(pl.multiple_of(place.core * half, 128), half)
    theirs = pl.ds(pl.multiple_of((1 - place.core) * half, 128), half)
    return mine, theirs


def place_half(chunk, have, want, lane):
    chunk = chunk if have == want else pltpu.roll(chunk, HEAD_SIZE, 1)
    return jnp.where(lane // HEAD_SIZE == want, chunk, 0.0)


def rope_chunk(chunk, tables, sign):
    ahead = pltpu.roll(chunk, 128 - HEAD_SIZE // 2, 1)
    behind = pltpu.roll(chunk, HEAD_SIZE // 2, 1)
    return chunk * tables[0] + sign * (ahead * tables[1] + behind * tables[2])


def chunk_of(ref, j):
    return ref[:, 128 * j : 128 * (j + 1)]


def pair_of(ref, j, group_size, lane):
    both = []
    for half in (0, 1):
        group = (2 * j + half) // group_size
        both.append(place_half(chunk_of(ref, group // 2).astype(F32), group % 2, half, lane))
    return jnp.concatenate(both, axis=0).astype(BF16)


def spread_gains(notes, shard, width):
    total = jnp.zeros((8, width), F32)
    for p in range(notes.shape[0]):
        row = jnp.concatenate([notes[p], jnp.zeros((8, width - 128), F32)], axis=1)
        total += pltpu.roll(row, shard * p, 1) if p else row
    return total


def gate_table(logits, ids, experts):
    expo = jnp.exp(logits - jnp.max(logits, axis=0, keepdims=True))
    probs = expo / jnp.sum(expo, axis=0, keepdims=True)
    top, length = logits.shape
    expert = lax.broadcasted_iota(jnp.int32, (experts, length), 0)
    table = jnp.zeros((experts, length), F32)
    for c in range(top):
        table += jnp.where(ids[c : c + 1, :] == expert, probs[c : c + 1, :], 0.0)
    return table


def write_notes(note_ref, gates, gains):
    shard = gains[0].shape[1]
    row = lax.broadcasted_iota(jnp.int32, (8, 128), 0)
    pad = jnp.zeros((1, 128 - shard), F32)
    shared = jnp.zeros((8, 128), F32)
    for i, gain in enumerate(gains):
        shared = jnp.where(row == i + 1, jnp.concatenate([gain, pad], axis=1), shared)
    for p in range(note_ref.shape[0]):
        tile = shared
        for at, e in ((0, p), (3, p + 1 - 2 * (p % 2)), (4, p + 2 - 4 * (p // 2 % 2))):
            tile = jnp.where(row == at, gates[e : e + 1, :], tile)
        note_ref[p] = tile


def tree_tables(segments, parents, length):
    row = lax.broadcasted_iota(jnp.int32, (length, length), 0)
    lane = lax.broadcasted_iota(jnp.int32, (length, length), 1)

    def total(x):
        return jnp.sum(x.astype(F32), axis=1, keepdims=True)

    own_row = segments.astype(F32)
    own = total(jnp.where(row == lane, own_row, 0.0))
    kinds = parents.shape[1]
    kind = lax.broadcasted_iota(jnp.int32, (length, kinds), 1).astype(F32)
    above = parents.astype(F32)
    parent = total(jnp.where(kind == own, above, 0.0))
    grand = total(jnp.where(kind == parent, above, 0.0))
    in_parent, in_grand = own_row == parent, own_row == grand
    start = total(jnp.where(own_row < own, 1.0, 0.0))
    offset = jnp.where(own != 0.0, total(jnp.where(in_parent, 1.0, 0.0)), 0.0)
    offset += jnp.where(parent != 0.0, total(jnp.where(in_grand, 1.0, 0.0)), 0.0)
    place = lax.broadcasted_iota(jnp.int32, (length, 1), 0).astype(F32)
    linked = jnp.logical_or(own_row == own, jnp.logical_or(in_parent, in_grand))
    return place - start + offset, jnp.logical_and(linked, lane <= row)


def write_tables(tables_ref, position):
    lane = lax.broadcasted_iota(jnp.int32, (1, 128), 1)
    half = HEAD_SIZE // 2
    frequency = THETA ** ((lane % half).astype(F32) * (-2.0 / HEAD_SIZE))
    angles = position * frequency
    sine = jnp.sin(angles)
    first = lane % HEAD_SIZE < half
    tables_ref[0] = jnp.cos(angles)
    tables_ref[1] = jnp.where(first, -sine, 0.0)
    tables_ref[2] = jnp.where(first, 0.0, sine)


def forward_part(
    place,
    group_size,
    tokens_ref,
    query_ref,
    key_ref,
    value_ref,
    out_ref,
    cot_ref,
    gain_a_ref,
    gain_m_ref,
    logits_ref,
    ids_ref,
    segments_ref,
    parents_ref,
    moe_in_ref,
    hidden_ref,
    normed_ref,
    head_out_ref,
    queries_ref,
    keys_ref,
    values_ref,
    probs_ref,
    peak_ref,
    tables_ref,
    gains_ref,
    notes,
    query_keep,
    key_keep,
    value_keep,
    out_keep,
    query_all,
    key_all,
    value_all,
    out_all,
    cot_dense,
    cot_packed,
    cot_all,
    own_pick,
    other_pick,
    gates,
    mix_mine,
    mix_other,
    note_ref,
    sends,
    recvs,
    note_send,
    note_recv,
    cot_twins,
    local_sems,
    keep_sems,
    mix_sems,
    kept,
):
    line = place.line
    count = 4 * line
    length, width = tokens_ref.shape
    shard, q_cols = query_ref.shape
    chunks = q_cols // 128
    spans, _, piece = pieces_of(place, width)
    own = []
    blocks = ((query_ref, query_all), (key_ref, key_all), (value_ref, value_all), (out_ref, out_all))
    for i, (src, dst) in enumerate(blocks):
        own.append(pltpu.make_async_copy(src, dst.at[place.me], local_sems.at[i]))
    for i in range(PIECES):
        own.append(pltpu.make_async_copy(cot_ref.at[:, spans[i]], cot_dense.at[i, place.z], local_sems.at[4 + i]))
    for c in own:
        c.start()
    enter(place)
    note = Notes(place, note_ref, notes, note_send, note_recv, False)
    for c in own:
        c.wait()
    gathers = [
        Gather(place, lambda s, ref=ref: ref.at[part_of(place, s)], sends.at[i], recvs.at[i], True)
        for i, ref in enumerate((query_all, key_all, value_all, out_all))
    ]
    picks = (own_pick, other_pick)
    cots = [
        PackedGather(
            place,
            cot_dense.at[i],
            cot_packed.at[i],
            cot_all,
            picks,
            spans[i],
            sends.at[4 + i],
            recvs.at[4 + i],
            cot_twins.at[i],
        )
        for i in range(PIECES)
    ]
    out = gathers[3]
    pipeline = Pipeline([gathers[i] for i in (1, 2, 0, 3)] + cots, STARTS)
    pipeline.run(1)
    gains = [g[...].astype(F32) for g in (gain_a_ref, gain_m_ref)]
    write_notes(note_ref, gate_table(logits_ref[...], ids_ref[...], count), gains)
    note.start()
    inputs = tokens_ref[...].astype(F32)
    inv_attn = lax.rsqrt(jnp.mean(inputs * inputs, axis=1, keepdims=True) + EPSILON)
    pipeline.run(1)
    note.finish()
    gains_ref[...] = spread_gains(notes, shard, width)
    normed_ref[...] = (inputs * inv_attn * gains_ref[1:2, :]).astype(BF16)
    pipeline.run(1)
    position, allowed = tree_tables(segments_ref[...], parents_ref[...], length)
    write_tables(tables_ref, position)
    pipeline.run(1)
    selections(place, notes, own_pick, other_pick, gates)
    pipeline.until(2)
    for g in gathers[:3]:
        g.take_rest()
    normed = normed_ref[...]
    tables = [tables_ref[i] for i in range(3)]
    query_lin = jnp.dot(normed, query_all[...].reshape(width, q_cols), preferred_element_type=F32)
    for j in range(chunks):
        queries_ref[:, 128 * j : 128 * (j + 1)] = rope_chunk(
            query_lin[:, 128 * j : 128 * (j + 1)], tables, 1.0
        ).astype(BF16)
    kv_cols = key_ref.shape[1]
    key_lin = jnp.dot(normed, key_all[...].reshape(width, kv_cols), preferred_element_type=F32)
    for j in range(kv_cols // 128):
        keys_ref[:, 128 * j : 128 * (j + 1)] = rope_chunk(
            key_lin[:, 128 * j : 128 * (j + 1)], tables, 1.0
        ).astype(BF16)
    values_ref[...] = jnp.dot(
        normed, value_all[...].reshape(width, kv_cols), preferred_element_type=F32
    ).astype(BF16)
    lane = lax.broadcasted_iota(jnp.int32, (length, 128), 1)
    small_lane = lax.broadcasted_iota(jnp.int32, (8, 128), 1)
    peaks = jnp.zeros((8, 128), F32)
    pipeline.run(1)
    for j in range(chunks):
        both = contract_cols(chunk_of(queries_ref, j), pair_of(keys_ref, j, group_size, lane)) * SCORE_SCALE
        low = []
        for half in (0, 1):
            scores = jnp.where(allowed, both[:, length * half : length * (half + 1)], NEGATIVE)
            row_max = jnp.max(scores, axis=1, keepdims=True)
            peak = jnp.max(row_max, axis=0, keepdims=True)
            peaks = jnp.where(small_lane == 2 * j + half, peak, peaks)
            expo = jnp.exp(scores - row_max)
            prob = expo / jnp.sum(expo, axis=1, keepdims=True)
            probs_ref[j, :, length * half : length * (half + 1)] = prob
            low.append(prob.astype(BF16))
        mixed = jnp.dot(
            jnp.concatenate(low, axis=1),
            pair_of(values_ref, j, group_size, lane),
            preferred_element_type=F32,
        )
        head_out_ref[:, 128 * j : 128 * (j + 1)] = mixed.astype(BF16)
        pipeline.run(1)
    peak_ref[...] = peaks
    pairs = [(query_all, query_keep), (key_all, key_keep), (value_all, value_keep), *kept[:-1]]
    pairs += [(out_all, out_keep), kept[-1]]
    keeps = [pltpu.make_async_copy(src, dst, keep_sems.at[i]) for i, (src, dst) in enumerate(pairs)]
    for c in keeps[:-2]:
        c.start()
    out.take_rest()
    keeps[-2].start()
    mix_mine[...] = contract_cols(head_out_ref[...], out_all[...].reshape(width, q_cols))
    swap = remote(mix_mine, mix_other, mix_sems.at[0], mix_sems.at[1], place.twin())
    swap.start()
    swap.wait()
    hidden = tokens_ref[...].astype(F32) + RESIDUAL * (mix_mine[...] + mix_other[...])
    hidden_ref[...] = hidden
    keeps[-1].start()
    inv_moe = lax.rsqrt(jnp.mean(hidden * hidden, axis=1, keepdims=True) + EPSILON)
    moe_in_ref[...] = (hidden * inv_moe * gains_ref[2:3, :]).astype(BF16)

    pipeline.until(len(pipeline.gathers) - 1)

    def take_cots():
        def rest(slot, carry):
            for cot in cots:
                cot.take_compact(slot)
            return carry

        lax.fori_loop(2 * line, count, rest, 0)

    def take_twins(group):
        for slot in range(line * group, line * (group + 1)):
            for cot in cots:
                cot.twin.take(slot)
                cot.twin.wait_send(slot)

    def settle():
        for g in gathers + cots:
            g.settle()
        for c in keeps:
            c.wait()

    return take_cots, take_twins, settle


ANY = pl.BlockSpec(memory_space=pl.ANY)
IN_VMEM = pl.BlockSpec(memory_space=pltpu.VMEM)


def params(number):
    return pltpu.CompilerParams(
        collective_id=number, has_side_effects=True, vmem_limit_bytes=60 * 2**20
    )


def capacity_of(length, experts):
    most = 4 * (9 * length * TOP // (32 * experts))
    return min(-(-most // 16) * 16, length)


def experts_part(
    place,
    rows_ref,
    gate_ref,
    up_ref,
    down_ref,
    d_rows_ref,
    mix_ref,
    dense,
    packed,
    rows,
    cots,
    own_pick,
    other_pick,
    gates,
    active,
    d_gate,
    d_up,
    d_active,
    grad_stage,
    mix_stage,
    grad_compact,
    mix_compact,
    grad_dense,
    mix_dense,
    total,
    grad_from_b,
    mix_from_b,
    mix_from_a,
    from_a,
    from_z,
    reduce_sems,
    gather_send,
    gather_recv,
    row_twins,
    last_sems,
    store_sems,
    stored,
    take_cots,
    take_twins,
    settle_before,
):
    line = place.line
    count = 4 * line
    cap, width = rows.shape[1:]
    tile_rows = line * cap
    mine, _ = halves(place, width)
    spans, their_spans, piece = pieces_of(place, width)
    for i in range(PIECES):
        dense[i, place.z] = rows_ref[:, spans[i]]
    picks = (own_pick, other_pick)
    gathers = [
        PackedGather(
            place,
            dense.at[i],
            packed.at[i],
            rows,
            picks,
            spans[i],
            gather_send.at[i],
            gather_recv.at[i],
            row_twins.at[i],
        )
        for i in range(PIECES)
    ]
    grad_twins = [
        Twin(
            place,
            lambda s, i=i: grad_stage.at[s, :, their_spans[i]],
            lambda s, i=i: grad_compact.at[i, s],
            row_twins.at[PIECES + i, 0],
            row_twins.at[PIECES + i, 1],
        )
        for i in range(PIECES)
    ]
    mix_twin = Twin(
        place,
        lambda s: mix_stage.at[s, :, halves(place, width)[1]],
        lambda s: mix_compact.at[s],
        row_twins.at[2 * PIECES, 0],
        row_twins.at[2 * PIECES, 1],
    )
    reduces = [
        PackedReduce(
            place,
            grad_compact.at[i],
            picks,
            grad_dense.at[i],
            grad_from_b.at[i],
            from_a.at[i],
            from_z.at[i],
            reduce_sems.at[i, 0],
            reduce_sems.at[i, 1],
        )
        for i in range(PIECES)
    ]
    mix_reduce = PackedReduce(
        place,
        mix_compact,
        picks,
        mix_dense,
        mix_from_b,
        mix_from_a,
        None,
        reduce_sems.at[PIECES, 0],
        reduce_sems.at[PIECES, 1],
    )

    def group_of(group):
        return pl.ds(line * group, line), pl.ds(tile_rows * group, tile_rows)

    def slots_of(group):
        return [line * group + z for z in range(line)]

    def ahead(group):
        some, flat = group_of(group)
        cot = cots[some].reshape(tile_rows, width).astype(F32)
        d_out = (gates[flat, :] * (RESIDUAL * cot)).astype(BF16)
        cots[some] = d_out.reshape(line, cap, width)
        d_active[flat, :] = jnp.dot(d_out, down_ref[...], preferred_element_type=F32)

    def work(group):
        some, flat = group_of(group)
        for slot in slots_of(group):
            for g in gathers:
                g.twin.take(slot)
        x = rows[some].reshape(tile_rows, width)
        gate_pre = jnp.dot(x, gate_ref[...], preferred_element_type=F32)
        up_pre = jnp.dot(x, up_ref[...], preferred_element_type=F32)
        sigmoid = 1.0 / (1.0 + jnp.exp(-gate_pre))
        silu = gate_pre * sigmoid
        active[flat, :] = (silu * up_pre).astype(BF16)
        d_act = d_active[flat, :]
        d_g = (d_act * up_pre * sigmoid * (1.0 + gate_pre * (1.0 - sigmoid))).astype(BF16)
        d_u = (d_act * silu).astype(BF16)
        d_gate[flat, :] = d_g
        d_up[flat, :] = d_u
        d_in = contract_cols(d_g, gate_ref[...]) + contract_cols(d_u, up_ref[...])
        grad_stage[some] = d_in.astype(BF16).reshape(line, cap, width)
        for twin in grad_twins:
            for slot in slots_of(group):
                twin.start(slot)

    def mix_work(group):
        some, flat = group_of(group)
        mix = gates[flat, :] * contract_cols(active[flat, :], down_ref[...])
        mix_stage[some] = mix.astype(BF16).reshape(line, cap, width)
        for slot in slots_of(group):
            mix_twin.start(slot)

    def fold(twin, stage, span, compact, group, send=None):
        def one(slot, carry):
            twin.take(slot)
            compact[slot] = (compact[slot].astype(F32) + stage[slot, :, span].astype(F32)).astype(BF16)
            if send is not None:
                send(slot - 2 * line)
            return carry

        lax.fori_loop(line * group, line * (group + 1), one, 0)

    def grad_fold(i, group, send=False):
        to_b = reduces[i].send_b if send else None
        fold(grad_twins[i], grad_stage, spans[i], grad_compact.at[i], group, to_b)

    def take_group(group):
        for slot in slots_of(group):
            for g in gathers:
                g.take_compact(slot)

    stores = []
    mix_fold = functools.partial(fold, mix_twin, mix_stage, mine, mix_compact)
    pipeline = Pipeline(gathers, [0] * PIECES)
    pipeline.run(1)
    take_cots()
    for group in range(4):
        pipeline.run(1)
        take_twins(group)
        ahead(group)
    pipeline.until(PIECES - 1)
    work(0)
    take_group(2)
    work(2)
    work(1)
    take_group(3)
    order = ends_first(line)
    grad_fold(0, 2, True)
    for i in range(1, PIECES):
        grad_fold(i, 2)
    work(3)
    for i, (source, target) in enumerate(stored):
        stores.append(pltpu.make_async_copy(source, target, store_sems.at[i]))
        stores[-1].start()
    grad_fold(0, 3, True)
    for i in range(1, PIECES):
        for z in range(line):
            reduces[i].send_b(z)
        grad_fold(i, 3, True)
    mix_work(1)
    for i in range(PIECES):
        grad_fold(i, 1)
    mix_work(2)
    mix_fold(2, mix_reduce.send_b)
    for i in range(PIECES):
        grad_fold(i, 0)
    fillers = [
        lambda: mix_work(3),
        lambda: mix_fold(3, mix_reduce.send_b),
        lambda: mix_work(0),
        lambda: mix_fold(1),
        lambda: mix_fold(0),
    ]
    for i, r in enumerate(reduces):
        for z in order:
            r.fold_b(line + z)
            r.send_a(z)
        if fillers:
            fillers.pop(0)()
        for z in order:
            r.fold_b(z)
        if i > 0:
            reduces[i - 1].finish_line()
        if fillers:
            fillers.pop(0)()
    reduces[-1].finish_line()
    for filler in fillers:
        filler()
    for z in order:
        mix_reduce.fold_b(line + z)
        mix_reduce.send_a(z)
    for z in order:
        mix_reduce.fold_b(z)
    lasts = []
    for i, r in enumerate(reduces):
        r.result(total.at[i])
        d_rows_ref[:, spans[i]] = total[i]
        there = d_rows_ref.at[:, spans[i]]
        lasts.append(remote(total.at[i], there, last_sems.at[0, i], last_sems.at[1, i], place.twin()))
        lasts[-1].start()
    for z in order:
        mix_reduce.fold_a(z)
    stores.append(pltpu.make_async_copy(mix_dense.at[pl.ds(0, line)], mix_ref, store_sems.at[len(stored)]))
    stores[-1].start()
    for r in reduces:
        r.settle()
    mix_reduce.settle_b()
    mix_reduce.settle_hop_a()
    for g in gathers:
        g.settle()

    twins = [g.twin for g in gathers] + grad_twins + [mix_twin]

    def settle(slot, carry):
        for twin in twins:
            twin.wait_send(slot)
        return carry

    lax.fori_loop(0, count, settle, 0)
    for c in stores + lasts:
        c.wait()
    settle_before()


STARTS = (0, 1, 2, 3, 4, 5)
STARTS = (0, 1, 2, 3, 4, 5)


def taken(function, found):
    code = function.__code__
    return {name: found[name] for name in code.co_varnames[: code.co_argcount] if name in found}


def front_kernel(line, group_size, names, *refs):
    found = dict(zip(names, refs))
    r = types.SimpleNamespace(**found)
    place = Place(line)
    sources = (r.gate_hbm, r.up_hbm, r.down_hbm)
    loads = [
        pltpu.make_async_copy(source.at[0], target, r.load_sems.at[i])
        for i, (source, target) in enumerate(zip(sources, (r.gate_ref, r.up_ref, r.down_ref)))
    ]
    for c in loads:
        c.start()
    kept = (
        (r.normed_ref, r.normed_out),
        (r.head_out_ref, r.head_out_out),
        (r.queries_ref, r.queries_out),
        (r.keys_ref, r.keys_out),
        (r.values_ref, r.values_out),
        (r.probs_ref, r.probs_out),
        (r.hidden_ref, r.hidden_out),
    )
    rest = forward_part(place, group_size, kept=kept, **taken(forward_part, found))
    for c in loads:
        c.wait()
    stored = (
        (r.rows, r.rows_out),
        (r.cot_all, r.cots_out),
        (r.active, r.active_out),
        (r.d_gate, r.d_gate_out),
        (r.d_up, r.d_up_out),
    )
    experts_part(
        place,
        r.moe_in_ref,
        cots=r.cot_all,
        stored=stored,
        take_cots=rest[0],
        take_twins=rest[1],
        settle_before=rest[2],
        **taken(experts_part, found),
    )


def run_front(line, group_size, big, small, expert_weights):
    count = 4 * line
    tokens, query, key, value, out, cotangent = big
    length, width = tokens.shape
    q_cols, kv_cols = query.shape[1], key.shape[1]
    hidden = expert_weights[0].shape[2]
    half, cap = width // 2, capacity_of(length, count)
    piece, lines = half // PIECES, 2 * line
    inputs = dict(
        tokens_ref=(tokens, IN_VMEM),
        query_ref=(query, ANY),
        key_ref=(key, ANY),
        value_ref=(value, ANY),
        out_ref=(out, ANY),
        cot_ref=(cotangent, ANY),
        gain_a_ref=(small[0], IN_VMEM),
        gain_m_ref=(small[1], IN_VMEM),
        logits_ref=(small[2], IN_VMEM),
        ids_ref=(small[3], IN_VMEM),
        segments_ref=(small[4], IN_VMEM),
        parents_ref=(small[5], IN_VMEM),
        gate_hbm=(expert_weights[0], ANY),
        up_hbm=(expert_weights[1], ANY),
        down_hbm=(expert_weights[2], ANY),
    )
    rows, inner = (length, width), (count * cap, hidden)
    probs = (q_cols // 128, length, 2 * length)
    outputs = dict(
        hidden_out=(rows, F32, ANY),
        normed_out=(rows, BF16, ANY),
        head_out_out=((length, q_cols), BF16, ANY),
        queries_out=((length, q_cols), BF16, ANY),
        keys_out=((length, kv_cols), BF16, ANY),
        values_out=((length, kv_cols), BF16, ANY),
        probs_out=(probs, F32, ANY),
        peak_ref=((8, 128), F32, IN_VMEM),
        tables_ref=((3, length, 128), F32, IN_VMEM),
        gains_ref=((8, width), F32, IN_VMEM),
        query_keep=((count, *query.shape), BF16, ANY),
        key_keep=((count, *key.shape), BF16, ANY),
        value_keep=((count, *value.shape), BF16, ANY),
        out_keep=((count, *out.shape), BF16, ANY),
        d_rows_ref=(rows, F32, IN_VMEM),
        mix_ref=((line, length, half), BF16, ANY),
        rows_out=((count, cap, width), BF16, ANY),
        cots_out=((count, cap, width), BF16, ANY),
        active_out=(inner, BF16, ANY),
        d_gate_out=(inner, BF16, ANY),
        d_up_out=(inner, BF16, ANY),
    )
    vmem, dma = pltpu.VMEM, pltpu.SemaphoreType.DMA
    dense = vmem((PIECES, lines, length, piece), BF16)
    packed = vmem((PIECES, lines, cap, piece), BF16)
    one_line = vmem((PIECES, line, length, piece), BF16)
    compact = vmem((count, cap, width), BF16)
    scratch = dict(
        hidden_ref=vmem(rows, F32),
        normed_ref=vmem(rows, BF16),
        head_out_ref=vmem((length, q_cols), BF16),
        queries_ref=vmem((length, q_cols), BF16),
        keys_ref=vmem((length, kv_cols), BF16),
        values_ref=vmem((length, kv_cols), BF16),
        probs_ref=vmem(probs, F32),
        query_all=vmem((count, *query.shape), BF16),
        key_all=vmem((count, *key.shape), BF16),
        value_all=vmem((count, *value.shape), BF16),
        out_all=vmem((count, *out.shape), BF16),
        moe_in_ref=vmem(rows, BF16),
        notes=vmem((count, 8, 128), F32),
        note_ref=vmem((count, 8, 128), F32),
        cot_dense=dense,
        cot_packed=packed,
        cot_all=compact,
        own_pick=vmem((count, cap, length), BF16),
        other_pick=vmem((lines, cap, length), BF16),
        gates=vmem((count * cap, 1), F32),
        mix_mine=vmem(rows, F32),
        mix_other=vmem(rows, F32),
        dense=dense,
        packed=packed,
        rows=compact,
        active=vmem(inner, BF16),
        d_gate=vmem(inner, BF16),
        d_up=vmem(inner, BF16),
        d_active=vmem(inner, F32),
        grad_stage=compact,
        mix_stage=compact,
        grad_compact=vmem((PIECES, count, cap, piece), BF16),
        mix_compact=vmem((count, cap, half), BF16),
        grad_dense=dense,
        mix_dense=vmem((lines, length, half), BF16),
        total=vmem((PIECES, length, piece), F32),
        grad_from_b=packed,
        mix_from_b=vmem((lines, cap, half), BF16),
        mix_from_a=vmem((line, length, half), BF16),
        from_a=one_line,
        from_z=one_line,
        gate_ref=vmem((width, hidden), BF16),
        up_ref=vmem((width, hidden), BF16),
        down_ref=vmem((width, hidden), BF16),
        sends=dma((4 + PIECES, 5 * line)),
        recvs=dma((4 + PIECES, count)),
        note_send=dma((count,)),
        note_recv=dma((count,)),
        cot_twins=dma((PIECES, 2, count)),
        local_sems=dma((4 + PIECES,)),
        keep_sems=dma((11,)),
        mix_sems=dma((2,)),
        load_sems=dma((3,)),
        reduce_sems=dma((PIECES + 1, 2, 4 * line)),
        gather_send=dma((PIECES, 5 * line)),
        gather_recv=dma((PIECES, count)),
        row_twins=dma((2 * PIECES + 1, 2, count)),
        last_sems=dma((2, PIECES)),
        store_sems=dma((6,)),
    )
    names = [*inputs, *outputs, *scratch]
    results = pl.pallas_call(
        functools.partial(front_kernel, line, group_size, names),
        out_shape=[jax.ShapeDtypeStruct(shape, kind) for shape, kind, _ in outputs.values()],
        in_specs=[spec for _, spec in inputs.values()],
        out_specs=[spec for _, _, spec in outputs.values()],
        scratch_shapes=list(scratch.values()),
        compiler_params=params(0),
        name="run_front",
    )(*(x for x, _ in inputs.values()))
    return types.SimpleNamespace(**dict(zip(outputs, results)))


def backward_kernel(
    line,
    group_size,
    tokens_ref,
    hidden_ref,
    d_rows_ref,
    cot_ref,
    normed_ref,
    head_out_ref,
    queries_ref,
    keys_ref,
    values_ref,
    probs_ref,
    gains_ref,
    peak_ref,
    tables_ref,
    query_keep,
    key_keep,
    value_keep,
    out_keep,
    mix_ref,
    rows_hbm,
    cots_hbm,
    active_hbm,
    d_gate_hbm,
    d_up_hbm,
    input_grad_ref,
    output_ref,
    query_sum,
    key_sum,
    value_sum,
    out_sum,
    notes,
    grad_gate_ref,
    grad_up_ref,
    grad_down_ref,
    *scratch,
):
    place = Place(line)
    count = 4 * line
    length, width = tokens_ref.shape
    q_cols, kv_cols = queries_ref.shape[1], keys_ref.shape[1]
    shard = width // count
    chunks = q_cols // 128
    (query_all, key_all, value_all, out_all), work = scratch[:4], scratch[4:9]
    rest = scratch[9:34]
    (
        total,
        d_heads,
        d_query,
        d_key,
        d_value,
        part_mine,
        part_other,
        d_hidden_keep,
        mix_total,
        note,
        weight_sems,
        load_sems,
        last_sems,
        part_sems,
        note_sends,
        note_recvs,
        expert_rows,
        cots,
        active,
        d_gate,
        d_up,
        grads,
        expert_sems,
        store_sems,
    ) = scratch[34:]
    by_part = lambda slot: part_of(place, slot)
    reduces = [
        Reduce(place, work[i], *rest[5 * i : 5 * i + 5], *(() if i == 4 else (by_part,))) for i in range(5)
    ]

    def load(slot):
        return pltpu.make_async_copy(mix_ref.at[slot], work[4].at[slot], load_sems.at[slot])

    def begin(slot, carry):
        load(slot).start()
        return carry

    def loaded(slot, carry):
        load(slot).wait()
        return carry

    lax.fori_loop(0, line, begin, 0)
    weights = [
        pltpu.make_async_copy(src, dst, weight_sems.at[i])
        for i, (src, dst) in enumerate(
            ((out_keep, out_all), (query_keep, query_all), (key_keep, key_all), (value_keep, value_all))
        )
    ]
    for c in weights:
        c.start()
    experts = [
        pltpu.make_async_copy(src, dst, expert_sems.at[i])
        for i, (src, dst) in enumerate(
            ((rows_hbm, expert_rows), (cots_hbm, cots), (active_hbm, active), (d_gate_hbm, d_gate), (d_up_hbm, d_up))
        )
    ]
    for c in experts:
        c.start()
    stores = [
        pltpu.make_async_copy(grads.at[i], dst, store_sems.at[i])
        for i, dst in enumerate((grad_gate_ref, grad_up_ref, grad_down_ref))
    ]
    columns = width // 512

    def weight_grad(at):
        number, i = at // columns, at % columns
        left, right = ((expert_rows, d_gate), (expert_rows, d_up), (cots, active))[number]
        left = left.reshape(left.shape[0] * left.shape[1], width)
        span = pl.ds(512 * i, 512)
        grads[number, span, :] = contract_rows(left[:, span], right[...])
        if i == columns - 1:
            stores[number].start()

    enter(place)
    lax.fori_loop(0, line, loaded, 0)
    mine, theirs = halves(place, width)
    outs = (query_sum, key_sum, value_sum, out_sum, total)
    order = (3, 0, 1, 2)
    mix = reduces[4]
    for z in ends_first(line):
        mix.send_z(z)
    last = remote(total, mix_total.at[:, mine], last_sems.at[0], last_sems.at[1], place.twin())

    def finish(at):
        i = order[at]
        reduces[i].result(outs[i])

    run = Reductions([reduces[i] for i in order], finish)
    hidden = hidden_ref[...]
    inv_moe = lax.rsqrt(jnp.mean(hidden * hidden, axis=1, keepdims=True) + EPSILON)
    unit_moe = hidden * inv_moe
    d_rows = d_rows_ref[...]
    scaled = d_rows * gains_ref[2:3, :]
    d_hidden = cot_ref[...].astype(F32) + inv_moe * (
        scaled - unit_moe * jnp.mean(scaled * unit_moe, axis=1, keepdims=True)
    )
    d_hidden_keep[...] = d_hidden
    moe_gain = jnp.sum(d_rows * unit_moe, axis=0, keepdims=True)
    d_attn = (RESIDUAL * d_hidden).astype(BF16)
    work[3][...] = contract_rows(d_attn, head_out_ref[...]).astype(BF16).reshape(count, shard, q_cols)
    run.ready(1)
    weights[0].wait()
    d_heads[...] = jnp.dot(
        d_attn, out_all[...].reshape(width, q_cols), preferred_element_type=F32
    ).astype(BF16)
    lane = lax.broadcasted_iota(jnp.int32, (length, 128), 1)
    d_key[...] = jnp.zeros_like(d_key)
    d_value[...] = jnp.zeros_like(d_value)
    tables = [tables_ref[i] for i in range(3)]
    for j in range(chunks):
        d_out = chunk_of(d_heads, j)
        keys = pair_of(keys_ref, j, group_size, lane)
        d_prob = contract_cols(d_out, pair_of(values_ref, j, group_size, lane))
        low, d_scores = [], []
        for half in (0, 1):
            side = slice(length * half, length * (half + 1))
            prob = probs_ref[j, :, side]
            grad = d_prob[:, side]
            inner = jnp.sum(prob * grad, axis=1, keepdims=True)
            d_scores.append((prob * (grad - inner)).astype(BF16))
            low.append(prob.astype(BF16))
        d_scores = jnp.concatenate(d_scores, axis=1)
        d_values = contract_rows(jnp.concatenate(low, axis=1), d_out)
        d_keys = contract_rows(d_scores, chunk_of(queries_ref, j)) * SCORE_SCALE
        turned = rope_chunk(
            jnp.dot(d_scores, keys, preferred_element_type=F32) * SCORE_SCALE, tables, -1.0
        )
        d_query[:, 128 * j : 128 * (j + 1)] = turned.astype(BF16)
        for half in (0, 1):
            group = (2 * j + half) // group_size
            side = slice(length * half, length * (half + 1))
            cols = slice(128 * (group // 2), 128 * (group // 2 + 1))
            d_key[:, cols] += place_half(d_keys[side], half, group % 2, lane)
            d_value[:, cols] += place_half(d_values[side], half, group % 2, lane)
        run.run(1)
    normed = normed_ref[...]
    work[0][...] = contract_rows(normed, d_query[...]).astype(BF16).reshape(count, shard, q_cols)
    run.ready(2)
    d_key_lin = jnp.concatenate(
        [rope_chunk(chunk_of(d_key, j), tables, -1.0) for j in range(kv_cols // 128)], axis=1
    ).astype(BF16)
    d_value_lin = d_value[...].astype(BF16)
    run.run(2)
    work[1][...] = contract_rows(normed, d_key_lin).astype(BF16).reshape(count, shard, kv_cols)
    work[2][...] = contract_rows(normed, d_value_lin).astype(BF16).reshape(count, shard, kv_cols)
    run.ready(4)
    run.run(2)
    mix.result(total)
    mix_total[:, mine] = total[...]
    last.start()
    for c in weights[1:]:
        c.wait()
    part_mine[...] = (
        contract_cols(d_query[...], query_all[...].reshape(width, q_cols))
        + contract_cols(d_key_lin, key_all[...].reshape(width, kv_cols))
        + contract_cols(d_value_lin, value_all[...].reshape(width, kv_cols))
    )
    swap = remote(part_mine, part_other, part_sems.at[0], part_sems.at[1], place.twin())
    swap.start()
    run.run(4)
    swap.wait()
    d_normed = part_mine[...] + part_other[...]
    inputs = tokens_ref[...].astype(F32)
    inv_attn = lax.rsqrt(jnp.mean(inputs * inputs, axis=1, keepdims=True) + EPSILON)
    unit_attn = inputs * inv_attn
    scaled = d_normed * gains_ref[1:2, :]
    input_grad_ref[...] = d_hidden_keep[...] + inv_attn * (
        scaled - unit_attn * jnp.mean(scaled * unit_attn, axis=1, keepdims=True)
    )
    attn_gain = jnp.sum(d_normed * unit_attn, axis=0, keepdims=True)
    rows = jnp.concatenate([attn_gain, moe_gain, jnp.zeros((6, width), F32)], axis=0)
    row = lax.broadcasted_iota(jnp.int32, (8, 128), 0)
    peaks = jnp.broadcast_to(peak_ref[0:1, :], (8, 128))
    for p in range(count):
        turned = pltpu.roll(rows, width - shard * p, 1) if p else rows
        note[p] = jnp.where(row == 2, peaks, turned[:, :128])
    exchange = Notes(place, note, notes, note_sends, note_recvs, False)
    exchange.start()
    for c in experts:
        c.wait()
    for at in range(3 * columns):
        weight_grad(at)
        run.run(2)
    run.complete()
    for r in reduces[:4]:
        r.settle()
    mix.settle_z()
    last.wait()
    output_ref[...] = (hidden_ref[...] + RESIDUAL * mix_total[...]).astype(BF16)
    exchange.finish()
    for c in stores:
        c.wait()


def run_backward(line, group_size, kept, keeps, mix, experts):
    count = 4 * line
    tokens, queries, keys = kept[0], kept[6], kept[7]
    length, width = tokens.shape
    q_cols, kv_cols = queries.shape[1], keys.shape[1]
    blocks = [x.shape[1:] for x in keeps] + [mix.shape[1:]]
    half = width // 2
    shape = jax.ShapeDtypeStruct
    outs = (
        [shape((length, width), F32), shape((length, width), BF16)]
        + [shape(s, F32) for s in blocks[:4]]
        + [shape((count, 8, 128), F32)]
    )
    kinds = [IN_VMEM] * len(outs) + [ANY] * 3
    hidden = experts[2].shape[1]
    outs += [shape((width, hidden), F32)] * 3
    return pl.pallas_call(
        functools.partial(backward_kernel, line, group_size),
        out_shape=outs,
        in_specs=[IN_VMEM] * len(kept) + [ANY] * 10,
        out_specs=kinds,
        scratch_shapes=[pltpu.VMEM(x.shape, BF16) for x in keeps]
        + [pltpu.VMEM((count, *s), BF16) for s in blocks[:4]]
        + [pltpu.VMEM(mix.shape, BF16)]
        + [x for s in blocks for x in reduce_scratch(line, s)]
        + [
            pltpu.VMEM((length, half), F32),
            pltpu.VMEM((length, q_cols), BF16),
            pltpu.VMEM((length, q_cols), BF16),
            pltpu.VMEM((length, kv_cols), F32),
            pltpu.VMEM((length, kv_cols), F32),
            pltpu.VMEM((length, width), F32),
            pltpu.VMEM((length, width), F32),
            pltpu.VMEM((length, width), F32),
            pltpu.VMEM((length, width), F32),
            pltpu.VMEM((count, 8, 128), F32),
            pltpu.SemaphoreType.DMA((4,)),
            pltpu.SemaphoreType.DMA((count,)),
            pltpu.SemaphoreType.DMA((2,)),
            pltpu.SemaphoreType.DMA((2,)),
            pltpu.SemaphoreType.DMA((count,)),
            pltpu.SemaphoreType.DMA((count,)),
        ]
        + [pltpu.VMEM(x.shape, BF16) for x in experts]
        + [
            pltpu.VMEM((3, width, hidden), F32),
            pltpu.SemaphoreType.DMA((5,)),
            pltpu.SemaphoreType.DMA((3,)),
        ],
        compiler_params=params(3),
        name="run_backward",
    )(*kept, *keeps, mix, *experts)


def finish_kernel(
    group_size,
    output_in,
    input_grad_in,
    query_in,
    key_in,
    value_in,
    out_in,
    notes,
    query_ref,
    key_ref,
    gate_in,
    up_in,
    down_in,
    output,
    input_grad,
    grad_query,
    grad_key,
    grad_value,
    grad_out,
    gain_a,
    gain_m,
    clipped_query,
    clipped_key,
    grad_gate,
    grad_up,
    grad_down,
    stage,
    sems,
):
    pairs = ((gate_in, grad_gate), (up_in, grad_up), (down_in, grad_down))
    takes = [pltpu.make_async_copy(src, stage.at[i], sems.at[0, i]) for i, (src, _) in enumerate(pairs)]
    copies = [pltpu.make_async_copy(stage.at[i], dst.at[0], sems.at[1, i]) for i, (_, dst) in enumerate(pairs)]
    for c in takes:
        c.start()
    output[...] = output_in[...]
    input_grad[...] = input_grad_in[...]
    grad_query[...] = query_in[...]
    grad_key[...] = key_in[...]
    grad_value[...] = value_in[...]
    grad_out[...] = out_in[...]
    for take, c in zip(takes, copies):
        take.wait()
        c.start()
    total, peaks = notes[0], notes[0]
    for p in range(1, notes.shape[0]):
        total = total + notes[p]
        peaks = jnp.maximum(peaks, notes[p])
    shard = gain_a.shape[1]
    gain_a[...] = total[0:1, :shard]
    gain_m[...] = total[1:2, :shard]
    factor = CLIP_LIMIT / jnp.maximum(peaks, CLIP_LIMIT)
    root = jnp.sqrt(factor)
    lane = lax.broadcasted_iota(jnp.int32, (8, 128), 1)

    def scale(h):
        return jnp.max(jnp.where(lane == h, root, 0.0), axis=1, keepdims=True)[2:3, :]

    heads = query_ref.shape[1] // HEAD_SIZE
    wide = lax.broadcasted_iota(jnp.int32, (1, 128), 1)
    scales = [scale(h) for h in range(heads)]
    for j in range(heads // 2):
        row = jnp.where(wide < HEAD_SIZE, scales[2 * j], scales[2 * j + 1])
        cols = slice(128 * j, 128 * (j + 1))
        clipped_query[:, cols] = query_ref[:, cols].astype(F32) * row
    least = [
        functools.reduce(jnp.minimum, scales[group_size * g : group_size * (g + 1)])
        for g in range(heads // group_size)
    ]
    for j in range(len(least) // 2):
        row = jnp.where(wide < HEAD_SIZE, least[2 * j], least[2 * j + 1])
        cols = slice(128 * j, 128 * (j + 1))
        clipped_key[:, cols] = key_ref[:, cols].astype(F32) * row
    for c in copies:
        c.wait()


def finish(group_size, found, notes, query, key, expert_grads):
    shape = jax.ShapeDtypeStruct
    shard = query.shape[0]
    outs = [shape(x.shape, x.dtype) for x in found] + [
        shape((1, shard), F32),
        shape((1, shard), F32),
        shape(query.shape, F32),
        shape(key.shape, F32),
    ]
    return pl.pallas_call(
        functools.partial(finish_kernel, group_size),
        out_shape=outs + [shape((1, *g.shape), F32) for g in expert_grads],
        in_specs=[IN_VMEM] * 9 + [ANY] * 3,
        out_specs=[IN_VMEM] * 10 + [ANY] * 3,
        scratch_shapes=[
            pltpu.VMEM((3, *expert_grads[0].shape), F32),
            pltpu.SemaphoreType.DMA((2, 3)),
        ],
        compiler_params=pltpu.CompilerParams(vmem_limit_bytes=56 * 2**20),
        name="finish",
    )(*found, notes, query, key, *expert_grads)


def on_device_dense(
    tokens,
    attn_norm_gain,
    w_query,
    key_projection,
    value_projection,
    w_out,
    moe_norm_gain,
    w_gate,
    w_up,
    w_down,
    router_logits,
    expert_ids,
    segment_ids,
    parents,
    cotangent,
):
    length, model_width = tokens.shape
    q_cols, kv_cols = w_query.shape[1], key_projection.shape[1]
    q_heads, kv_heads = q_cols // HEAD_SIZE, kv_cols // HEAD_SIZE
    group_size = q_heads // kv_heads
    count = lax.axis_size("dp")
    line = count // 4
    shard = attn_norm_gain.shape[0]
    small = (
        attn_norm_gain[None],
        moe_norm_gain[None],
        router_logits.T,
        expert_ids.T,
        segment_ids,
        parents,
    )
    big = (tokens, w_query, key_projection, value_projection, w_out, cotangent)
    front = run_front(line, group_size, big, small, (w_gate, w_up, w_down))
    keeps = (front.query_keep, front.key_keep, front.value_keep, front.out_keep)
    experts = (front.rows_out, front.cots_out, front.active_out, front.d_gate_out, front.d_up_out)
    kept = (
        tokens,
        front.hidden_out,
        front.d_rows_ref,
        cotangent,
        front.normed_out,
        front.head_out_out,
        front.queries_out,
        front.keys_out,
        front.values_out,
        front.probs_out,
        front.gains_ref,
        front.peak_ref,
        front.tables_ref,
    )
    input_grad, output, *grads = run_backward(line, group_size, kept, keeps, front.mix_ref, experts)
    grads, sums, expert_grads = grads[:4], grads[4], grads[5:]
    output, input_grad, gq, gk, gv, go, gain_a, gain_m, clipped_query, clipped_key, gg, gu, gd = finish(
        group_size, (output, input_grad, *grads), sums, w_query, key_projection, expert_grads
    )
    return (
        output,
        input_grad,
        gain_a[0],
        gq,
        gk,
        gv,
        go,
        gain_m[0],
        gg,
        gu,
        gd,
        clipped_query,
        clipped_key,
    )


DENSE_BYTES = 8 * 2**20


def on_device(*args):
    tokens, w_gate = args[0], args[7]
    count, ranks = lax.axis_size("dp"), lax.axis_size("tensor")
    rows_bytes = count * tokens.shape[0] * tokens.shape[1] * 2
    whole_experts = w_gate.shape[2] * ranks == FFE
    dense = whole_experts and ranks == 2 and count % 8 == 0 and rows_bytes <= DENSE_BYTES
    return on_device_dense(*args) if dense else on_device_general(*args)


def solution(mesh):
    in_specs = (
        P("dp", None),
        P("dp"),
        P("dp", "tensor"),
        P("dp", "tensor"),
        P("dp", "tensor"),
        P("dp", "tensor"),
        P("dp"),
        P("dp", None, "tensor"),
        P("dp", None, "tensor"),
        P("dp", None, "tensor"),
        P("dp", None),
        P("dp", None),
        P("dp", None),
        P("dp", None),
        P("dp", None),
    )
    out_specs = (
        P("dp", None),
        P("dp", None),
        P("dp"),
        P("dp", "tensor"),
        P("dp", "tensor"),
        P("dp", "tensor"),
        P("dp", "tensor"),
        P("dp"),
        P("dp", None, "tensor"),
        P("dp", None, "tensor"),
        P("dp", None, "tensor"),
        P("dp", "tensor"),
        P("dp", "tensor"),
    )
    return jax.shard_map(
        on_device, mesh=mesh, in_specs=in_specs, out_specs=out_specs, check_vma=False
    )
```

```python
import functools
import types

import jax
import jax.numpy as jnp
from jax import lax
from jax.experimental import pallas as pl
from jax.experimental.pallas import tpu as pltpu
from jax.sharding import PartitionSpec as P

HEAD_SIZE = 64
FFE = 512
TOP = 8


EPSILON = 1e-06
SCORE_SCALE = 1.0 / 64.0
RESIDUAL = 0.22
THETA = 10000.0
CLIP_LIMIT = 2.0
NEGATIVE = -1e30


def tree_layout(seg_row, par_row):
    tree_length = seg_row.shape[0]
    seg_count = par_row.shape[0]
    seg_index = jnp.arange(seg_count, dtype=jnp.int32)
    member = (seg_row[:, None] == seg_index[None, :]).astype(jnp.int32)
    seg_len = jnp.sum(member, axis=0)
    seg_start = jnp.sum(jnp.where(seg_index[:, None] > seg_index[None, :], seg_len[None, :], 0), axis=1)
    parent_hot = (par_row[:, None] == seg_index[None, :]).astype(jnp.int32)
    grand_parent = jnp.sum(parent_hot * par_row[None, :], axis=1)
    grand_hot = (grand_parent[:, None] == seg_index[None, :]).astype(jnp.int32)
    parent_len = jnp.sum(parent_hot * seg_len[None, :], axis=1)
    grand_len = jnp.sum(grand_hot * seg_len[None, :], axis=1)
    offset = jnp.where(seg_index != 0, parent_len, 0) + jnp.where(par_row != 0, grand_len, 0)
    tok_start = jnp.sum(member * seg_start[None, :], axis=1)
    tok_offset = jnp.sum(member * offset[None, :], axis=1)
    places = jnp.arange(tree_length, dtype=jnp.int32)
    position = (places - tok_start + tok_offset).astype(jnp.float32)
    identity = (seg_index[:, None] == seg_index[None, :]).astype(jnp.int32)
    ancestor = jnp.minimum(identity + parent_hot + grand_hot, 1)
    reached = jnp.dot(member, ancestor)
    linked = jnp.dot(reached, member.T) > 0
    allowed = linked & (places[None, :] <= places[:, None])
    return (position, allowed)


def rope_tables(position, head_dim):
    half_dim = head_dim // 2
    frequency = THETA ** (-2.0 * jnp.arange(half_dim, dtype=jnp.float32) / head_dim)
    angles = position[:, None] * frequency[None, :]
    return (jnp.cos(angles)[:, None, :], jnp.sin(angles)[:, None, :])


def apply_rotary(values_in, cosine_table, sine_values):
    half_dim = values_in.shape[-1] // 2
    first_half = values_in[..., :half_dim]
    second_half = values_in[..., half_dim:]
    return jnp.concatenate(
        [
            first_half * cosine_table - second_half * sine_values,
            second_half * cosine_table + first_half * sine_values,
        ],
        axis=-1,
    )


def rotate_back(grads_in, cosine_table, sine_values):
    half_dim = grads_in.shape[-1] // 2
    first_half = grads_in[..., :half_dim]
    second_half = grads_in[..., half_dim:]
    return jnp.concatenate(
        [
            first_half * cosine_table + second_half * sine_values,
            second_half * cosine_table - first_half * sine_values,
        ],
        axis=-1,
    )


def slot_tables(routes, experts, capacity):
    flat_ids = routes.reshape(-1)
    row_count = flat_ids.shape[0]
    member = (flat_ids[:, None] == jnp.arange(experts, dtype=jnp.int32)[None, :]).astype(jnp.int32)
    row_total = flat_ids.shape[0]
    before = jnp.dot((jnp.arange(row_total)[:, None] > jnp.arange(row_total)[None, :]).astype(jnp.float32), member.astype(jnp.float32), precision=lax.Precision.HIGHEST).astype(jnp.int32)
    slot_index = jnp.sum(before * member, axis=1)
    target = flat_ids * capacity + slot_index
    source = (
        jnp.full((experts * capacity,), -1, jnp.int32)
        .at[target]
        .set(jnp.arange(row_count, dtype=jnp.int32))
    )
    return (flat_ids, slot_index, source)


def contract_rows(left, right):
    return lax.dot_general(
        left, right, (((0,), (0,)), ((), ())), preferred_element_type=jnp.float32
    )


def contract_cols(left, right):
    return lax.dot_general(
        left, right, (((1,), (1,)), ((), ())), preferred_element_type=jnp.float32
    )


def expert_forward(inputs, gate_w, up_w, down_w):
    gate_pre = jnp.dot(inputs, gate_w, preferred_element_type=jnp.float32)
    up_pre = jnp.dot(inputs, up_w, preferred_element_type=jnp.float32)
    active = (gate_pre / (1.0 + jnp.exp(-gate_pre)) * up_pre).astype(jnp.bfloat16)
    return (contract_cols(active, down_w), (gate_pre, up_pre, active))


def expert_backward(inputs, grads_out, gate_w, up_w, down_w, kept_acts):
    gate_pre, up_pre, active = kept_acts
    d_active = jnp.dot(grads_out, down_w, preferred_element_type=jnp.float32)
    grad_down = contract_rows(grads_out, active)
    sigmoid_val = 1.0 / (1.0 + jnp.exp(-gate_pre))
    d_gate = (d_active * up_pre * sigmoid_val * (1.0 + gate_pre * (1.0 - sigmoid_val))).astype(
        jnp.bfloat16
    )
    d_up = (d_active * gate_pre * sigmoid_val).astype(jnp.bfloat16)
    grad_gate = contract_rows(inputs, d_gate)
    grad_up = contract_rows(inputs, d_up)
    d_inputs = contract_cols(d_gate, gate_w) + contract_cols(d_up, up_w)
    return (d_inputs, grad_gate, grad_up, grad_down)


def send_rows(rows_in):
    return lax.all_to_all(rows_in, "dp", split_axis=0, concat_axis=0, tiled=True)


def return_rows(rows_in):
    return lax.all_to_all(
        rows_in.astype(jnp.bfloat16), "dp", split_axis=0, concat_axis=0, tiled=True
    ).astype(rows_in.dtype)


def send_grads(rows_in):
    return lax.all_to_all(rows_in, "dp", split_axis=0, concat_axis=0, tiled=True)


def return_grads(rows_in):
    return lax.all_to_all(
        rows_in.astype(jnp.bfloat16), "dp", split_axis=0, concat_axis=0, tiled=True
    ).astype(rows_in.dtype)


def share_slots(partial_rows):
    return lax.psum_scatter(partial_rows, "tensor", scatter_dimension=1, tiled=True)


def on_device_general(
    tokens,
    attn_norm_gain,
    w_query,
    key_projection,
    value_projection,
    w_out,
    moe_norm_gain,
    w_gate,
    w_up,
    w_down,
    router_logits,
    expert_ids,
    segment_ids,
    parents,
    cotangent,
):
    length = tokens.shape[0]
    model_width = tokens.shape[1]
    q_cols = w_query.shape[1]
    kv_cols = key_projection.shape[1]
    q_heads = q_cols // HEAD_SIZE
    kv_heads = kv_cols // HEAD_SIZE
    group_size = q_heads // kv_heads
    dp_size = lax.axis_size("dp")
    tensor_ranks = lax.axis_size("tensor")
    replicas = FFE // (w_gate.shape[2] * tensor_ranks)
    experts = dp_size // replicas
    capacity = 4 * (9 * length * TOP // (32 * experts))
    share_rows = capacity // tensor_ranks
    first_slot = lax.axis_index("tensor") * share_rows
    block_rows = min(length, 512)
    attn_gain, moe_gain, query_w, key_weight, value_weight, out_w = (
        lax.all_gather(attn_norm_gain, "dp", axis=0, tiled=True),
        lax.all_gather(moe_norm_gain, "dp", axis=0, tiled=True),
        lax.all_gather(w_query, "dp", axis=0, tiled=True),
        lax.all_gather(key_projection, "dp", axis=0, tiled=True),
        lax.all_gather(value_projection, "dp", axis=0, tiled=True),
        lax.all_gather(w_out, "dp", axis=0, tiled=True),
    )
    attn_gain_f = attn_gain.astype(jnp.float32)
    moe_gain_f = moe_gain.astype(jnp.float32)
    inputs = tokens.astype(jnp.float32)
    inv_attn = lax.rsqrt(jnp.mean(inputs * inputs, axis=1, keepdims=True) + EPSILON)
    unit_attn = inputs * inv_attn
    normalized_rows = (unit_attn * attn_gain_f).astype(jnp.bfloat16)
    position, allowed = tree_layout(segment_ids[0], parents[0])
    cosine_table, sine_values = rope_tables(position, HEAD_SIZE)
    query_linear = jnp.dot(normalized_rows, query_w, preferred_element_type=jnp.float32).reshape(
        length, q_heads, HEAD_SIZE
    )
    key_linear = jnp.dot(normalized_rows, key_weight, preferred_element_type=jnp.float32).reshape(
        length, kv_heads, HEAD_SIZE
    )
    query_heads = (
        apply_rotary(query_linear, cosine_table, sine_values)
        .astype(jnp.bfloat16)
        .reshape(length, kv_heads, group_size, HEAD_SIZE)
    )
    key_heads = apply_rotary(key_linear, cosine_table, sine_values).astype(jnp.bfloat16)
    value_heads = (
        jnp.dot(normalized_rows, value_weight, preferred_element_type=jnp.float32)
        .astype(jnp.bfloat16)
        .reshape(length, kv_heads, HEAD_SIZE)
    )
    q_block = query_heads
    mask_rows = allowed[None, None]
    scores = (
        jnp.einsum("qhgd,khd->hgqk", q_block, key_heads, preferred_element_type=jnp.float32)
        * SCORE_SCALE
    )
    scores = jnp.where(mask_rows, scores, NEGATIVE)
    peak_parts = [jnp.max(scores, axis=(2, 3))]
    row_max = jnp.max(scores, axis=3, keepdims=True)
    expo = jnp.exp(scores - row_max)
    row_total = jnp.sum(expo, axis=3, keepdims=True)
    lse_parts = [row_max + jnp.log(row_total)]
    prob_low = (expo / row_total).astype(jnp.bfloat16)
    block_outs = jnp.einsum(
        "hgqk,khd->qhgd", prob_low, value_heads, preferred_element_type=jnp.float32
    )
    head_out = block_outs.reshape(length, q_cols).astype(jnp.bfloat16)
    attn_mix = lax.psum(contract_cols(head_out, out_w), "tensor")
    hidden = inputs + RESIDUAL * attn_mix
    head_peak = lax.pmax(jnp.max(jnp.stack(peak_parts), axis=0).reshape(q_heads), "dp")
    inv_moe = lax.rsqrt(jnp.mean(hidden * hidden, axis=1, keepdims=True) + EPSILON)
    unit_moe = hidden * inv_moe
    moe_in = (unit_moe * moe_gain_f).astype(jnp.bfloat16)
    logit_max = jnp.max(router_logits, axis=1, keepdims=True)
    logit_exp = jnp.exp(router_logits - logit_max)
    gate_probs = logit_exp / jnp.sum(logit_exp, axis=1, keepdims=True)
    flat_ids, slot_index, source = slot_tables(expert_ids, experts, capacity)
    filled = source >= 0
    source_row = jnp.maximum(source, 0)
    source_token = source_row // TOP
    dispatch_rows = jnp.where(
        filled[:, None], moe_in[source_token], jnp.zeros((), jnp.bfloat16)
    ).reshape(experts, capacity, model_width)
    arrived = send_rows(jnp.repeat(dispatch_rows, replicas, axis=0))
    gate_w, up_w, down_w = (w_gate[0], w_up[0], w_down[0])
    expert_in = arrived.reshape(dp_size * capacity, model_width)
    expert_out, kept_acts = expert_forward(expert_in, gate_w, up_w, down_w)
    partial_out = share_slots(expert_out.reshape(dp_size, capacity, model_width))
    back_parts = return_rows(partial_out).reshape(experts, replicas, share_rows, model_width)
    back_rows = (
        jnp.sum(back_parts, axis=1).astype(jnp.bfloat16).reshape(experts * share_rows, model_width)
    )
    own_slot = ((slot_index >= first_slot) & (slot_index < first_slot + share_rows)).reshape(
        length, TOP
    )
    local_index = (
        flat_ids * share_rows + jnp.clip(slot_index - first_slot, 0, share_rows - 1)
    ).reshape(length, TOP)
    mix_part = jnp.zeros((length, model_width), jnp.float32)
    for column in range(TOP):
        gate_weight = jnp.where(own_slot[:, column], gate_probs[:, column], 0.0)
        mix_part = mix_part + gate_weight[:, None] * back_rows[local_index[:, column]].astype(
            jnp.float32
        )
    expert_mix = lax.psum(mix_part.astype(jnp.bfloat16), "tensor").astype(jnp.float32)
    output = (hidden + RESIDUAL * expert_mix).astype(jnp.bfloat16)
    grad_output = cotangent.astype(jnp.float32)
    mix_grad = RESIDUAL * grad_output
    row_gate = gate_probs.reshape(-1)[source_row]
    grad_rows = (
        jnp.where(filled[:, None], row_gate[:, None] * mix_grad[source_token], 0.0)
        .astype(jnp.bfloat16)
        .reshape(experts, capacity, model_width)
    )
    grad_arrived = send_grads(jnp.repeat(grad_rows, replicas, axis=0)).reshape(
        dp_size * capacity, model_width
    )
    d_inputs, grad_gate, grad_up, grad_down = expert_backward(
        expert_in, grad_arrived, gate_w, up_w, down_w, kept_acts
    )
    d_back = share_slots(d_inputs.reshape(dp_size, capacity, model_width))
    grad_gate, grad_up, grad_down = (grad_gate[None], grad_up[None], grad_down[None])
    d_parts = return_grads(d_back).reshape(experts, replicas, share_rows, model_width)
    d_returned = (
        jnp.sum(d_parts, axis=1).astype(jnp.bfloat16).reshape(experts * share_rows, model_width)
    )
    d_mix_part = jnp.zeros((length, model_width), jnp.float32)
    for column in range(TOP):
        d_mix_part = d_mix_part + jnp.where(
            own_slot[:, column][:, None],
            d_returned[local_index[:, column]].astype(jnp.float32),
            0.0,
        )
    d_moe_in = lax.psum(d_mix_part, "tensor")
    scaled_moe = d_moe_in * moe_gain_f
    grad_moe_gain = jnp.sum(d_moe_in * unit_moe, axis=0)
    d_hidden = grad_output + inv_moe * (
        scaled_moe - unit_moe * jnp.mean(scaled_moe * unit_moe, axis=1, keepdims=True)
    )
    d_attn = (RESIDUAL * d_hidden).astype(jnp.bfloat16)
    grad_out_w = contract_rows(d_attn, head_out)
    d_heads = (
        jnp.dot(d_attn, out_w, preferred_element_type=jnp.float32)
        .astype(jnp.bfloat16)
        .reshape(length, kv_heads, group_size, HEAD_SIZE)
    )
    d_query_parts = []
    d_key = jnp.zeros((length, kv_heads, HEAD_SIZE), jnp.float32)
    d_value = jnp.zeros((length, kv_heads, HEAD_SIZE), jnp.float32)
    for block_number, row_begin in enumerate(range(0, length, block_rows)):
        q_block = query_heads
        mask_rows = allowed[None, None]
        scores = (
            jnp.einsum("qhgd,khd->hgqk", q_block, key_heads, preferred_element_type=jnp.float32)
            * SCORE_SCALE
        )
        scores = jnp.where(mask_rows, scores, NEGATIVE)
        prob_full = jnp.exp(scores - lse_parts[block_number])
        prob_low = prob_full.astype(jnp.bfloat16)
        d_value = jnp.einsum(
            "hgqk,qhgd->khd", prob_low, d_heads, preferred_element_type=jnp.float32
        )
        d_prob = jnp.einsum(
            "qhgd,khd->hgqk", d_heads, value_heads, preferred_element_type=jnp.float32
        )
        inner = jnp.sum(prob_full * d_prob, axis=3, keepdims=True)
        d_scores = (prob_full * (d_prob - inner)).astype(jnp.bfloat16)
        d_query_parts.append(
            jnp.einsum("hgqk,khd->qhgd", d_scores, key_heads, preferred_element_type=jnp.float32)
            * SCORE_SCALE
        )
        d_key = (
            jnp.einsum("hgqk,qhgd->khd", d_scores, q_block, preferred_element_type=jnp.float32)
            * SCORE_SCALE
        )
    d_query_all = d_query_parts[0].reshape(length, q_heads, HEAD_SIZE)
    d_query_lin = (
        rotate_back(d_query_all, cosine_table, sine_values)
        .astype(jnp.bfloat16)
        .reshape(length, q_cols)
    )
    d_key_lin = (
        rotate_back(d_key, cosine_table, sine_values).astype(jnp.bfloat16).reshape(length, kv_cols)
    )
    d_value_lin = d_value.astype(jnp.bfloat16).reshape(length, kv_cols)
    grad_query_w = contract_rows(normalized_rows, d_query_lin)
    grad_key_w = contract_rows(normalized_rows, d_key_lin)
    grad_value_w = contract_rows(normalized_rows, d_value_lin)
    d_normed_part = (
        contract_cols(d_query_lin, query_w)
        + contract_cols(d_key_lin, key_weight)
        + contract_cols(d_value_lin, value_weight)
    )
    d_normed = lax.psum(d_normed_part.astype(jnp.bfloat16), "tensor").astype(jnp.float32)
    scaled_attn = d_normed * attn_gain_f
    grad_attn_gain = jnp.sum(d_normed * unit_attn, axis=0)
    input_grad = d_hidden + inv_attn * (
        scaled_attn - unit_attn * jnp.mean(scaled_attn * unit_attn, axis=1, keepdims=True)
    )
    reduced = (
        lax.psum_scatter(grad_attn_gain, "dp", scatter_dimension=0, tiled=True),
        lax.psum_scatter(grad_moe_gain, "dp", scatter_dimension=0, tiled=True),
        lax.psum_scatter(grad_query_w, "dp", scatter_dimension=0, tiled=True),
        lax.psum_scatter(grad_key_w, "dp", scatter_dimension=0, tiled=True),
        lax.psum_scatter(grad_value_w, "dp", scatter_dimension=0, tiled=True),
        lax.psum_scatter(grad_out_w, "dp", scatter_dimension=0, tiled=True),
    )
    scale_factor = CLIP_LIMIT / jnp.maximum(head_peak, CLIP_LIMIT)
    query_scale = jnp.repeat(jnp.sqrt(scale_factor), HEAD_SIZE)
    key_clip_scale = jnp.repeat(
        jnp.sqrt(jnp.min(scale_factor.reshape(kv_heads, group_size), axis=1)), HEAD_SIZE
    )
    clipped_query = w_query.astype(jnp.float32) * query_scale[None, :]
    clipped_key = key_projection.astype(jnp.float32) * key_clip_scale[None, :]
    return (
        output,
        input_grad,
        reduced[0],
        reduced[2],
        reduced[3],
        reduced[4],
        reduced[5],
        reduced[1],
        grad_gate,
        grad_up,
        grad_down,
        clipped_query,
        clipped_key,
    )


MESH_IDS = pl.DeviceIdType.MESH
F32 = jnp.float32
BF16 = jnp.bfloat16


class Place:
    def __init__(self, line):
        self.line = line
        self.count = 4 * line
        me = lax.axis_index("dp")
        self.core = lax.axis_index("tensor")
        self.me = me
        self.z = me // 4
        y, x = (me // 2) % 2, me % 2
        self.step_a, self.step_b = 2 - self.core, 1 + self.core
        self.a = y * (1 - self.core) + x * self.core
        self.b = x * (1 - self.core) + y * self.core

    def part(self, z, a, b):
        return z * 4 + a * self.step_a + b * self.step_b

    def up(self):
        return (self.me + 4, self.core)

    def down(self):
        return (self.me - 4, self.core)

    def beside_a(self):
        return (self.me + self.step_a * (1 - 2 * self.a), self.core)

    def beside_b(self):
        return (self.me + self.step_b * (1 - 2 * self.b), self.core)

    def twin(self):
        return (self.me, 1 - self.core)

    def peer(self, offset):
        return lax.rem(self.me + offset, self.count)


def enter(place):
    barrier = pltpu.get_barrier_semaphore()

    def greet(offset, carry):
        pl.semaphore_signal(
            barrier, inc=1, device_id=(place.peer(offset), place.core), device_id_type=MESH_IDS
        )
        return carry

    lax.fori_loop(1, place.count, greet, 0)
    pl.semaphore_signal(barrier, inc=1, device_id=place.twin(), device_id_type=MESH_IDS)
    pl.semaphore_wait(barrier, place.count)


def remote(src, dst, send_sem, recv_sem, device):
    return pltpu.make_async_remote_copy(
        src_ref=src,
        dst_ref=dst,
        send_sem=send_sem,
        recv_sem=recv_sem,
        device_id=device,
        device_id_type=MESH_IDS,
    )


class Notes:
    def __init__(self, place, src, dst, send_sem, recv_sem, alike):
        self.place, self.src, self.dst = place, src, dst
        self.send_sem, self.recv_sem, self.alike = send_sem, recv_sem, alike

    def _copy(self, offset, source):
        place = self.place
        to = place.peer(offset)
        return remote(
            self.src if self.alike else self.src.at[to],
            self.dst.at[source],
            self.send_sem.at[offset],
            self.recv_sem.at[source],
            (to, place.core),
        )

    def start(self):
        def send(offset, carry):
            self._copy(offset, self.place.me).start()
            return carry

        lax.fori_loop(1, self.place.count, send, 0)
        me = self.place.me
        self.dst[me] = self.src[...] if self.alike else self.src[me]

    def finish(self):
        def settle(offset, carry):
            self._copy(offset, self.place.peer(offset)).wait_recv()
            self._copy(offset, self.place.me).wait_send()
            return carry

        lax.fori_loop(1, self.place.count, settle, 0)


class Gather:
    def __init__(self, place, view, send_sem, recv_sem, fixed=False):
        self.place, self.view, self.fixed = place, view, fixed
        self.send_sem, self.recv_sem = send_sem, recv_sem

    def _copy(self, source, target, sem, device):
        there = self.view(source if self.fixed else target)
        return remote(self.view(source), there, self.send_sem.at[sem], self.recv_sem.at[target], device)

    def _to_z(self, z, way):
        place = self.place
        device = place.up() if way == 0 else place.down()
        return self._copy(z, z, way * place.line + z, device)

    def _to_a(self, z):
        line = self.place.line
        return self._copy(z, line + z, 2 * line + z, self.place.beside_a())

    def _to_b(self, slot):
        line = self.place.line
        return self._copy(slot, 2 * line + slot, 3 * line + slot, self.place.beside_b())

    def take(self, slot):
        self._copy(slot, slot, 0, self.place.beside_b()).wait_recv()

    def near(self, step, action):
        place = self.place
        if step == 0:
            action(place.z)
        else:
            pl.when(place.z >= step)(lambda: action(place.z - step))
            pl.when(place.z + step < place.line)(lambda: action(place.z + step))

    def hand_on(self, slot):
        self._to_b(slot).start()

    def start(self):
        place = self.place
        pl.when(place.z < place.line - 1)(lambda: self._to_z(place.z, 0).start())
        pl.when(place.z > 0)(lambda: self._to_z(place.z, 1).start())
        self._to_a(self.place.z).start()
        self.hand_on(self.place.z)

    def along(self, step):
        place = self.place

        def pass_on(z):
            self.take(z)
            pl.when(jnp.logical_and(z < place.z, place.z < place.line - 1))(lambda: self._to_z(z, 0).start())
            pl.when(jnp.logical_and(z > place.z, place.z > 0))(lambda: self._to_z(z, 1).start())
            self._to_a(z).start()
            self.hand_on(z)

        self.near(step, pass_on)

    def across(self, step):
        line = self.place.line

        def pass_on(z):
            self.take(line + z)
            self.hand_on(line + z)

        self.near(step, pass_on)

    def step(self, number):
        if number == 0:
            self.start()
            return
        if number < self.place.line:
            self.along(number)
        self.across(number - 1)

    def settle(self):
        place = self.place
        line = place.line

        def wait(z, carry):
            self._to_a(z).wait_send()
            self._to_b(z).wait_send()
            self._to_b(line + z).wait_send()
            pl.when(jnp.logical_and(z <= place.z, place.z < line - 1))(lambda: self._to_z(z, 0).wait_send())
            pl.when(jnp.logical_and(z >= place.z, place.z > 0))(lambda: self._to_z(z, 1).wait_send())
            return carry

        lax.fori_loop(0, line, wait, 0)

    def take_rest(self):
        line = self.place.line

        def wait(k, carry):
            self.take(2 * line + k)
            return carry

        lax.fori_loop(0, 2 * line, wait, 0)


class Pipeline:
    def __init__(self, gathers, starts):
        self.gathers, self.starts, self.at = gathers, starts, 0
        self.steps = gathers[0].place.line + 1

    def run(self, number):
        for _ in range(number):
            for g, start in zip(self.gathers, self.starts):
                if 0 <= self.at - start < self.steps:
                    g.step(self.at - start)
            self.at += 1

    def until(self, index):
        self.run(max(0, self.starts[index] + self.steps - self.at))


class Twin:
    def __init__(self, place, source, target, send_sem, recv_sem):
        self.place, self.source, self.target = place, source, target
        self.send_sem, self.recv_sem = send_sem, recv_sem

    def copy(self, slot):
        line = self.place.line
        group = slot // line
        there = slot + line * ((group % 2) - (group // 2))
        return remote(
            self.source(slot),
            self.target(there),
            self.send_sem.at[slot],
            self.recv_sem.at[there],
            self.place.twin(),
        )

    def start(self, slot):
        self.copy(slot).start()

    def take(self, slot):
        remote(
            self.source(slot),
            self.target(slot),
            self.send_sem.at[slot],
            self.recv_sem.at[slot],
            self.place.twin(),
        ).wait_recv()

    def wait_send(self, slot):
        self.copy(slot).wait_send()


class Reduce:
    def __init__(self, place, parts, from_b, from_a, from_z, send_sem, recv_sem, index=lambda slot: slot):
        self.place, self.parts, self.index = place, parts, index
        self.from_b, self.from_a, self.from_z = from_b, from_a, from_z
        self.send_sem, self.recv_sem = send_sem, recv_sem

    def _copy(self, source, target, sem, device):
        return remote(source, target, self.send_sem.at[sem], self.recv_sem.at[sem], device)

    def _to_b(self, k):
        line = self.place.line
        return self._copy(self.parts.at[self.index(2 * line + k)], self.from_b.at[k], k, self.place.beside_b())

    def _to_a(self, z):
        line = self.place.line
        block = self.parts.at[self.index(line + z)]
        return self._copy(block, self.from_a.at[z], 2 * line + z, self.place.beside_a())

    def _to_z(self, target):
        place, line = self.place, self.place.line
        return remote(
            self.parts.at[self.index(target)],
            self.from_z.at[place.z],
            self.send_sem.at[3 * line + target],
            self.recv_sem.at[3 * line + place.z],
            (place.me + 4 * (target - place.z), place.core),
        )

    def _add(self, slot, block):
        at = self.index(slot)
        self.parts[at] = (self.parts[at].astype(F32) + block.astype(F32)).astype(BF16)

    def send_b(self, k):
        self._to_b(k).start()

    def fold_b(self, k):
        self._to_b(k).wait_recv()
        self._add(k, self.from_b[k])

    def send_a(self, z):
        self._to_a(z).start()

    def fold_a(self, z):
        self._to_a(z).wait_recv()
        self._add(z, self.from_a[z])

    def fold_line_a(self):
        line = self.place.line
        for z in ends_first(line):
            self.fold_b(line + z)
            self.send_a(z)

    def fold_line_own(self):
        for z in ends_first(self.place.line):
            self.fold_b(z)

    def send_z(self, z):
        pl.when(self.place.z != z)(lambda: self._to_z(z).start())

    def finish_line(self):
        for z in ends_first(self.place.line):
            self.fold_a(z)
            self.send_z(z)

    def result(self, out):
        place, line = self.place, self.place.line
        out[...] = self.parts[self.index(place.z)].astype(F32)

        def add(z, carry):
            @pl.when(z != place.z)
            def _():
                remote(
                    self.from_z.at[z], self.from_z.at[z], self.send_sem.at[0], self.recv_sem.at[3 * line + z], place.up()
                ).wait_recv()
                out[...] += self.from_z[z].astype(F32)

            return carry

        lax.fori_loop(0, line, add, 0)

    def settle_b(self):
        def wait(k, carry):
            self._to_b(k).wait_send()
            return carry

        lax.fori_loop(0, 2 * self.place.line, wait, 0)

    def settle_hop_a(self):
        def wait(z, carry):
            self._to_a(z).wait_send()
            return carry

        lax.fori_loop(0, self.place.line, wait, 0)

    def settle_z(self):
        place = self.place

        def wait(z, carry):
            pl.when(place.z != z)(lambda: self._to_z(z).wait_send())
            return carry

        lax.fori_loop(0, place.line, wait, 0)

    def settle(self):
        self.settle_b()
        self.settle_hop_a()
        self.settle_z()


class PackedGather(Gather):
    def __init__(self, place, dense, packed, compact, picks, mine, send_sem, recv_sem, twin_sems):
        self.place, self.dense, self.packed, self.compact = place, dense, packed, compact
        self.own_pick, self.other_pick = picks
        self.mine, self.fixed = mine, False
        self.send_sem, self.recv_sem = send_sem, recv_sem
        view = lambda slot: compact.at[slot, :, mine]
        self.twin = Twin(place, view, view, twin_sems.at[0], twin_sems.at[1])

    def view(self, slot):
        return self.dense.at[slot]

    def _to_b(self, slot):
        line = self.place.line
        return remote(
            self.packed.at[slot],
            self.compact.at[2 * line + slot, :, self.mine],
            self.send_sem.at[3 * line + slot],
            self.recv_sem.at[2 * line + slot],
            self.place.beside_b(),
        )

    def take_compact(self, slot):
        line = self.place.line
        self._to_b(slot - 2 * line).wait_recv()
        self.twin.start(slot)

    def take(self, slot):
        self._copy(slot, slot, 0, self.place.beside_b()).wait_recv()

    def hand_on(self, slot):
        block = self.dense[slot]
        self.packed[slot] = jnp.dot(self.other_pick[slot], block, preferred_element_type=F32).astype(BF16)
        self._to_b(slot).start()
        self.compact[slot, :, self.mine] = jnp.dot(
            self.own_pick[slot], block, preferred_element_type=F32
        ).astype(BF16)
        self.twin.start(slot)


class PackedReduce(Reduce):
    def __init__(self, place, compact, picks, *rest):
        super().__init__(place, *rest)
        self.compact = compact
        self.own_pick, self.other_pick = picks

    def _to_b(self, k):
        line = self.place.line
        return self._copy(self.compact.at[2 * line + k], self.from_b.at[k], k, self.place.beside_b())

    def fold_b(self, k):
        self._to_b(k).wait_recv()
        own = contract_rows(self.own_pick[k], self.compact[k])
        self.parts[k] = (own + contract_rows(self.other_pick[k], self.from_b[k])).astype(BF16)


def selections(place, notes, own_pick, other_pick, gates=None):
    line = place.line
    cap, length = own_pick.shape[1:]
    rows = [notes[part_of(place, slot)][0:1, :] for slot in range(4 * line)]
    for slot in range(2 * line):
        note = notes[part_of(place, slot)]
        rows.append(jnp.where(place.core == 0, note[3:4, :], note[4:5, :]))
    before = lax.broadcasted_iota(jnp.int32, (length, length), 0) < lax.broadcasted_iota(
        jnp.int32, (length, length), 1
    )
    weights = jnp.concatenate(rows, axis=0)
    rank = jnp.dot(
        jnp.where(weights > 0.0, 1.0, 0.0).astype(BF16),
        jnp.where(before, 1.0, 0.0).astype(BF16),
        preferred_element_type=F32,
    )
    rank = jnp.where(weights > 0.0, rank, -1.0)
    number = lax.broadcasted_iota(jnp.int32, (cap, length), 0).astype(F32)
    for i in range(len(rows)):
        pick = jnp.where(rank[i : i + 1, :] == number, 1.0, 0.0)
        if i >= 4 * line:
            other_pick[i - 4 * line] = pick.astype(BF16)
            continue
        own_pick[i] = pick.astype(BF16)
        if gates is not None:
            gates[cap * i : cap * (i + 1), :] = jnp.sum(pick * rows[i], axis=1, keepdims=True)


AHEAD = 8


class Reductions:
    def __init__(self, reduces, finish):
        self.reduces, self.finish = reduces, finish
        self.at = self.sent = self.limit = 0
        line = self.line = reduces[0].place.line
        self.ks = [line + z for z in ends_first(line)] + ends_first(line)
        self.steps = [(i, k) for i in range(len(reduces)) for k in self.ks]

    def ready(self, number):
        self.limit = 2 * self.line * number
        self._send()

    def _send(self):
        while self.sent < min(self.at + AHEAD, self.limit):
            i, k = self.steps[self.sent]
            self.reduces[i].send_b(k)
            self.sent += 1

    def run(self, number):
        for _ in range(number):
            self._step()

    def _step(self):
        i, k = self.steps[self.at]
        self.at += 1
        self._send()
        self.reduces[i].fold_b(k)
        if k >= self.line:
            self.reduces[i].send_a(k - self.line)
        if k == self.ks[self.line - 1] and i > 0:
            self.reduces[i - 1].finish_line()
        if k == self.ks[-1] and i > 0:
            self.finish(i - 1)

    def complete(self):
        self.run(len(self.steps) - self.at)
        self.reduces[-1].finish_line()
        self.finish(len(self.reduces) - 1)


def reduce_scratch(line, block):
    return [
        pltpu.VMEM((2 * line, *block), BF16),
        pltpu.VMEM((line, *block), BF16),
        pltpu.VMEM((line, *block), BF16),
        pltpu.SemaphoreType.DMA((4 * line,)),
        pltpu.SemaphoreType.DMA((4 * line,)),
    ]


def ends_first(line):
    order = []
    for i in range((line + 1) // 2):
        order += [i] if i == line - 1 - i else [i, line - 1 - i]
    return order


def part_of(place, slot):
    line = place.line
    group, z = slot // line, slot % line
    flip_a, flip_b = group % 2, group // 2
    a = place.a + flip_a * (1 - 2 * place.a)
    b = place.b + flip_b * (1 - 2 * place.b)
    return place.part(z, a, b)


PIECES = 2


def pieces_of(place, width):
    piece = width // 2 // PIECES

    def spans(core):
        starts = [pl.multiple_of((core * PIECES + i) * piece, 128) for i in range(PIECES)]
        return [pl.ds(start, piece) for start in starts]

    return spans(place.core), spans(1 - place.core), piece


def halves(place, width):
    half = width // 2
    mine = pl.ds(pl.multiple_of(place.core * half, 128), half)
    theirs = pl.ds(pl.multiple_of((1 - place.core) * half, 128), half)
    return mine, theirs


def place_half(chunk, have, want, lane):
    chunk = chunk if have == want else pltpu.roll(chunk, HEAD_SIZE, 1)
    return jnp.where(lane // HEAD_SIZE == want, chunk, 0.0)


def rope_chunk(chunk, tables, sign):
    ahead = pltpu.roll(chunk, 128 - HEAD_SIZE // 2, 1)
    behind = pltpu.roll(chunk, HEAD_SIZE // 2, 1)
    return chunk * tables[0] + sign * (ahead * tables[1] + behind * tables[2])


def chunk_of(ref, j):
    return ref[:, 128 * j : 128 * (j + 1)]


def pair_of(ref, j, group_size, lane):
    both = []
    for half in (0, 1):
        group = (2 * j + half) // group_size
        both.append(place_half(chunk_of(ref, group // 2).astype(F32), group % 2, half, lane))
    return jnp.concatenate(both, axis=0).astype(BF16)


def spread_gains(notes, shard, width):
    total = jnp.zeros((8, width), F32)
    for p in range(notes.shape[0]):
        row = jnp.concatenate([notes[p], jnp.zeros((8, width - 128), F32)], axis=1)
        total += pltpu.roll(row, shard * p, 1) if p else row
    return total


def gate_table(logits, ids, experts):
    expo = jnp.exp(logits - jnp.max(logits, axis=0, keepdims=True))
    probs = expo / jnp.sum(expo, axis=0, keepdims=True)
    top, length = logits.shape
    expert = lax.broadcasted_iota(jnp.int32, (experts, length), 0)
    table = jnp.zeros((experts, length), F32)
    for c in range(top):
        table += jnp.where(ids[c : c + 1, :] == expert, probs[c : c + 1, :], 0.0)
    return table


def write_notes(note_ref, gates, gains):
    shard = gains[0].shape[1]
    row = lax.broadcasted_iota(jnp.int32, (8, 128), 0)
    pad = jnp.zeros((1, 128 - shard), F32)
    shared = jnp.zeros((8, 128), F32)
    for i, gain in enumerate(gains):
        shared = jnp.where(row == i + 1, jnp.concatenate([gain, pad], axis=1), shared)
    for p in range(note_ref.shape[0]):
        tile = shared
        for at, e in ((0, p), (3, p + 1 - 2 * (p % 2)), (4, p + 2 - 4 * (p // 2 % 2))):
            tile = jnp.where(row == at, gates[e : e + 1, :], tile)
        note_ref[p] = tile


def tree_tables(segments, parents, length):
    row = lax.broadcasted_iota(jnp.int32, (length, length), 0)
    lane = lax.broadcasted_iota(jnp.int32, (length, length), 1)

    def total(x):
        return jnp.sum(x.astype(F32), axis=1, keepdims=True)

    own_row = segments.astype(F32)
    own = total(jnp.where(row == lane, own_row, 0.0))
    kinds = parents.shape[1]
    kind = lax.broadcasted_iota(jnp.int32, (length, kinds), 1).astype(F32)
    above = parents.astype(F32)
    parent = total(jnp.where(kind == own, above, 0.0))
    grand = total(jnp.where(kind == parent, above, 0.0))
    in_parent, in_grand = own_row == parent, own_row == grand
    start = total(jnp.where(own_row < own, 1.0, 0.0))
    offset = jnp.where(own != 0.0, total(jnp.where(in_parent, 1.0, 0.0)), 0.0)
    offset += jnp.where(parent != 0.0, total(jnp.where(in_grand, 1.0, 0.0)), 0.0)
    place = lax.broadcasted_iota(jnp.int32, (length, 1), 0).astype(F32)
    linked = jnp.logical_or(own_row == own, jnp.logical_or(in_parent, in_grand))
    return place - start + offset, jnp.logical_and(linked, lane <= row)


def write_tables(tables_ref, position):
    lane = lax.broadcasted_iota(jnp.int32, (1, 128), 1)
    half = HEAD_SIZE // 2
    frequency = THETA ** ((lane % half).astype(F32) * (-2.0 / HEAD_SIZE))
    angles = position * frequency
    sine = jnp.sin(angles)
    first = lane % HEAD_SIZE < half
    tables_ref[0] = jnp.cos(angles)
    tables_ref[1] = jnp.where(first, -sine, 0.0)
    tables_ref[2] = jnp.where(first, 0.0, sine)


def forward_part(
    place,
    group_size,
    tokens_ref,
    query_ref,
    key_ref,
    value_ref,
    out_ref,
    cot_ref,
    gain_a_ref,
    gain_m_ref,
    logits_ref,
    ids_ref,
    segments_ref,
    parents_ref,
    moe_in_ref,
    hidden_ref,
    normed_ref,
    head_out_ref,
    queries_ref,
    keys_ref,
    values_ref,
    probs_ref,
    peak_ref,
    tables_ref,
    gains_ref,
    notes,
    query_keep,
    key_keep,
    value_keep,
    out_keep,
    query_all,
    key_all,
    value_all,
    out_all,
    cot_dense,
    cot_packed,
    cot_all,
    own_pick,
    other_pick,
    gates,
    mix_mine,
    mix_other,
    note_ref,
    sends,
    recvs,
    note_send,
    note_recv,
    cot_twins,
    local_sems,
    keep_sems,
    mix_sems,
    kept,
):
    line = place.line
    count = 4 * line
    length, width = tokens_ref.shape
    shard, q_cols = query_ref.shape
    chunks = q_cols // 128
    spans, _, piece = pieces_of(place, width)
    own = []
    blocks = ((query_ref, query_all), (key_ref, key_all), (value_ref, value_all), (out_ref, out_all))
    for i, (src, dst) in enumerate(blocks):
        own.append(pltpu.make_async_copy(src, dst.at[place.me], local_sems.at[i]))
    for i in range(PIECES):
        own.append(pltpu.make_async_copy(cot_ref.at[:, spans[i]], cot_dense.at[i, place.z], local_sems.at[4 + i]))
    for c in own:
        c.start()
    enter(place)
    note = Notes(place, note_ref, notes, note_send, note_recv, False)
    for c in own:
        c.wait()
    gathers = [
        Gather(place, lambda s, ref=ref: ref.at[part_of(place, s)], sends.at[i], recvs.at[i], True)
        for i, ref in enumerate((query_all, key_all, value_all, out_all))
    ]
    picks = (own_pick, other_pick)
    cots = [
        PackedGather(
            place,
            cot_dense.at[i],
            cot_packed.at[i],
            cot_all,
            picks,
            spans[i],
            sends.at[4 + i],
            recvs.at[4 + i],
            cot_twins.at[i],
        )
        for i in range(PIECES)
    ]
    out = gathers[3]
    pipeline = Pipeline([gathers[i] for i in (1, 2, 0, 3)] + cots, STARTS)
    pipeline.run(1)
    gains = [g[...].astype(F32) for g in (gain_a_ref, gain_m_ref)]
    write_notes(note_ref, gate_table(logits_ref[...], ids_ref[...], count), gains)
    note.start()
    inputs = tokens_ref[...].astype(F32)
    inv_attn = lax.rsqrt(jnp.mean(inputs * inputs, axis=1, keepdims=True) + EPSILON)
    pipeline.run(1)
    note.finish()
    gains_ref[...] = spread_gains(notes, shard, width)
    normed_ref[...] = (inputs * inv_attn * gains_ref[1:2, :]).astype(BF16)
    pipeline.run(1)
    position, allowed = tree_tables(segments_ref[...], parents_ref[...], length)
    write_tables(tables_ref, position)
    pipeline.run(1)
    selections(place, notes, own_pick, other_pick, gates)
    pipeline.until(2)
    for g in gathers[:3]:
        g.take_rest()
    normed = normed_ref[...]
    tables = [tables_ref[i] for i in range(3)]
    query_lin = jnp.dot(normed, query_all[...].reshape(width, q_cols), preferred_element_type=F32)
    for j in range(chunks):
        queries_ref[:, 128 * j : 128 * (j + 1)] = rope_chunk(
            query_lin[:, 128 * j : 128 * (j + 1)], tables, 1.0
        ).astype(BF16)
    kv_cols = key_ref.shape[1]
    key_lin = jnp.dot(normed, key_all[...].reshape(width, kv_cols), preferred_element_type=F32)
    for j in range(kv_cols // 128):
        keys_ref[:, 128 * j : 128 * (j + 1)] = rope_chunk(
            key_lin[:, 128 * j : 128 * (j + 1)], tables, 1.0
        ).astype(BF16)
    values_ref[...] = jnp.dot(
        normed, value_all[...].reshape(width, kv_cols), preferred_element_type=F32
    ).astype(BF16)
    lane = lax.broadcasted_iota(jnp.int32, (length, 128), 1)
    small_lane = lax.broadcasted_iota(jnp.int32, (8, 128), 1)
    peaks = jnp.zeros((8, 128), F32)
    pipeline.run(1)
    for j in range(chunks):
        both = contract_cols(chunk_of(queries_ref, j), pair_of(keys_ref, j, group_size, lane)) * SCORE_SCALE
        low = []
        for half in (0, 1):
            scores = jnp.where(allowed, both[:, length * half : length * (half + 1)], NEGATIVE)
            row_max = jnp.max(scores, axis=1, keepdims=True)
            peak = jnp.max(row_max, axis=0, keepdims=True)
            peaks = jnp.where(small_lane == 2 * j + half, peak, peaks)
            expo = jnp.exp(scores - row_max)
            prob = expo / jnp.sum(expo, axis=1, keepdims=True)
            probs_ref[j, :, length * half : length * (half + 1)] = prob
            low.append(prob.astype(BF16))
        mixed = jnp.dot(
            jnp.concatenate(low, axis=1),
            pair_of(values_ref, j, group_size, lane),
            preferred_element_type=F32,
        )
        head_out_ref[:, 128 * j : 128 * (j + 1)] = mixed.astype(BF16)
        pipeline.run(1)
    peak_ref[...] = peaks
    pairs = [(query_all, query_keep), (key_all, key_keep), (value_all, value_keep), *kept[:-1]]
    pairs += [(out_all, out_keep), kept[-1]]
    keeps = [pltpu.make_async_copy(src, dst, keep_sems.at[i]) for i, (src, dst) in enumerate(pairs)]
    for c in keeps[:-2]:
        c.start()
    out.take_rest()
    keeps[-2].start()
    mix_mine[...] = contract_cols(head_out_ref[...], out_all[...].reshape(width, q_cols))
    swap = remote(mix_mine, mix_other, mix_sems.at[0], mix_sems.at[1], place.twin())
    swap.start()
    swap.wait()
    hidden = tokens_ref[...].astype(F32) + RESIDUAL * (mix_mine[...] + mix_other[...])
    hidden_ref[...] = hidden
    keeps[-1].start()
    inv_moe = lax.rsqrt(jnp.mean(hidden * hidden, axis=1, keepdims=True) + EPSILON)
    moe_in_ref[...] = (hidden * inv_moe * gains_ref[2:3, :]).astype(BF16)

    pipeline.until(len(pipeline.gathers) - 1)

    def take_cots():
        def rest(slot, carry):
            for cot in cots:
                cot.take_compact(slot)
            return carry

        lax.fori_loop(2 * line, count, rest, 0)

    def take_twins(group):
        for slot in range(line * group, line * (group + 1)):
            for cot in cots:
                cot.twin.take(slot)
                cot.twin.wait_send(slot)

    def settle():
        for g in gathers + cots:
            g.settle()
        for c in keeps:
            c.wait()

    return take_cots, take_twins, settle


ANY = pl.BlockSpec(memory_space=pl.ANY)
IN_VMEM = pl.BlockSpec(memory_space=pltpu.VMEM)


def params(number):
    return pltpu.CompilerParams(
        collective_id=number, has_side_effects=True, vmem_limit_bytes=60 * 2**20
    )


def capacity_of(length, experts):
    most = 4 * (9 * length * TOP // (32 * experts))
    return min(-(-most // 16) * 16, length)


def experts_part(
    place,
    rows_ref,
    gate_ref,
    up_ref,
    down_ref,
    d_rows_ref,
    mix_ref,
    dense,
    packed,
    rows,
    cots,
    own_pick,
    other_pick,
    gates,
    active,
    d_gate,
    d_up,
    d_active,
    grad_stage,
    mix_stage,
    grad_compact,
    mix_compact,
    grad_dense,
    mix_dense,
    total,
    grad_from_b,
    mix_from_b,
    mix_from_a,
    from_a,
    from_z,
    reduce_sems,
    gather_send,
    gather_recv,
    row_twins,
    last_sems,
    store_sems,
    stored,
    take_cots,
    take_twins,
    settle_before,
):
    line = place.line
    count = 4 * line
    cap, width = rows.shape[1:]
    tile_rows = line * cap
    mine, _ = halves(place, width)
    spans, their_spans, piece = pieces_of(place, width)
    for i in range(PIECES):
        dense[i, place.z] = rows_ref[:, spans[i]]
    picks = (own_pick, other_pick)
    gathers = [
        PackedGather(
            place,
            dense.at[i],
            packed.at[i],
            rows,
            picks,
            spans[i],
            gather_send.at[i],
            gather_recv.at[i],
            row_twins.at[i],
        )
        for i in range(PIECES)
    ]
    grad_twins = [
        Twin(
            place,
            lambda s, i=i: grad_stage.at[s, :, their_spans[i]],
            lambda s, i=i: grad_compact.at[i, s],
            row_twins.at[PIECES + i, 0],
            row_twins.at[PIECES + i, 1],
        )
        for i in range(PIECES)
    ]
    mix_twin = Twin(
        place,
        lambda s: mix_stage.at[s, :, halves(place, width)[1]],
        lambda s: mix_compact.at[s],
        row_twins.at[2 * PIECES, 0],
        row_twins.at[2 * PIECES, 1],
    )
    reduces = [
        PackedReduce(
            place,
            grad_compact.at[i],
            picks,
            grad_dense.at[i],
            grad_from_b.at[i],
            from_a.at[i],
            from_z.at[i],
            reduce_sems.at[i, 0],
            reduce_sems.at[i, 1],
        )
        for i in range(PIECES)
    ]
    mix_reduce = PackedReduce(
        place,
        mix_compact,
        picks,
        mix_dense,
        mix_from_b,
        mix_from_a,
        None,
        reduce_sems.at[PIECES, 0],
        reduce_sems.at[PIECES, 1],
    )

    def group_of(group):
        first = pl.multiple_of(tile_rows * group, tile_rows)
        return pl.ds(line * group, line), pl.ds(first, tile_rows)

    def slots_of(group):
        return [line * group + z for z in range(line)]

    def ahead(group):
        some, flat = group_of(group)
        cot = cots[some].reshape(tile_rows, width).astype(F32)
        d_out = (gates[flat, :] * (RESIDUAL * cot)).astype(BF16)
        cots[some] = d_out.reshape(line, cap, width)
        d_active[flat, :] = jnp.dot(d_out, down_ref[...], preferred_element_type=F32)

    def work(group):
        some, flat = group_of(group)
        for slot in slots_of(group):
            for g in gathers:
                g.twin.take(slot)
        x = rows[some].reshape(tile_rows, width)
        gate_pre = jnp.dot(x, gate_ref[...], preferred_element_type=F32)
        up_pre = jnp.dot(x, up_ref[...], preferred_element_type=F32)
        sigmoid = 1.0 / (1.0 + jnp.exp(-gate_pre))
        silu = gate_pre * sigmoid
        active[flat, :] = (silu * up_pre).astype(BF16)
        d_act = d_active[flat, :]
        d_g = (d_act * up_pre * sigmoid * (1.0 + gate_pre * (1.0 - sigmoid))).astype(BF16)
        d_u = (d_act * silu).astype(BF16)
        d_gate[flat, :] = d_g
        d_up[flat, :] = d_u
        d_in = contract_cols(d_g, gate_ref[...]) + contract_cols(d_u, up_ref[...])
        grad_stage[some] = d_in.astype(BF16).reshape(line, cap, width)
        for twin in grad_twins:
            for slot in slots_of(group):
                twin.start(slot)

    def mix_work(group):
        some, flat = group_of(group)
        mix = gates[flat, :] * contract_cols(active[flat, :], down_ref[...])
        mix_stage[some] = mix.astype(BF16).reshape(line, cap, width)
        for slot in slots_of(group):
            mix_twin.start(slot)

    def fold(twin, stage, span, compact, group, send=None):
        def one(slot, carry):
            twin.take(slot)
            compact[slot] = (compact[slot].astype(F32) + stage[slot, :, span].astype(F32)).astype(BF16)
            if send is not None:
                send(slot - 2 * line)
            return carry

        lax.fori_loop(line * group, line * (group + 1), one, 0)

    def grad_fold(i, group, send=False):
        to_b = reduces[i].send_b if send else None
        fold(grad_twins[i], grad_stage, spans[i], grad_compact.at[i], group, to_b)

    def take_group(group):
        for slot in slots_of(group):
            for g in gathers:
                g.take_compact(slot)

    stores = []
    mix_fold = functools.partial(fold, mix_twin, mix_stage, mine, mix_compact)
    pipeline = Pipeline(gathers, [0] * PIECES)
    pipeline.run(1)
    take_cots()
    pipeline.run(2)
    for group in range(4):
        take_twins(group)

    def ahead_loop(group, carry):
        ahead(group)
        return carry

    lax.fori_loop(0, 4, ahead_loop, 0)
    pipeline.run(2)
    pipeline.until(PIECES - 1)
    work(0)
    take_group(2)
    work(2)
    work(1)
    take_group(3)
    order = ends_first(line)
    grad_fold(0, 2, True)
    for i in range(1, PIECES):
        grad_fold(i, 2)
    work(3)
    for i, (source, target) in enumerate(stored):
        stores.append(pltpu.make_async_copy(source, target, store_sems.at[i]))
        stores[-1].start()
    grad_fold(0, 3, True)
    for i in range(1, PIECES):
        for z in range(line):
            reduces[i].send_b(z)
        grad_fold(i, 3, True)
    mix_work(1)
    for i in range(PIECES):
        grad_fold(i, 1)
    mix_work(2)
    mix_fold(2, mix_reduce.send_b)
    for i in range(PIECES):
        grad_fold(i, 0)
    fillers = [
        lambda: mix_work(3),
        lambda: mix_fold(3, mix_reduce.send_b),
        lambda: mix_work(0),
        lambda: mix_fold(1),
        lambda: mix_fold(0),
    ]
    for i, r in enumerate(reduces):
        for z in order:
            r.fold_b(line + z)
            r.send_a(z)
        if fillers:
            fillers.pop(0)()
        for z in order:
            r.fold_b(z)
        if i > 0:
            reduces[i - 1].finish_line()
        if fillers:
            fillers.pop(0)()
    reduces[-1].finish_line()
    for filler in fillers:
        filler()
    for z in order:
        mix_reduce.fold_b(line + z)
        mix_reduce.send_a(z)
    for z in order:
        mix_reduce.fold_b(z)
    lasts = []
    for i, r in enumerate(reduces):
        r.result(total.at[i])
        d_rows_ref[:, spans[i]] = total[i]
        there = d_rows_ref.at[:, spans[i]]
        lasts.append(remote(total.at[i], there, last_sems.at[0, i], last_sems.at[1, i], place.twin()))
        lasts[-1].start()
    for z in order:
        mix_reduce.fold_a(z)
    stores.append(pltpu.make_async_copy(mix_dense.at[pl.ds(0, line)], mix_ref, store_sems.at[len(stored)]))
    stores[-1].start()
    for r in reduces:
        r.settle()
    mix_reduce.settle_b()
    mix_reduce.settle_hop_a()
    for g in gathers:
        g.settle()

    twins = [g.twin for g in gathers] + grad_twins + [mix_twin]

    def settle(slot, carry):
        for twin in twins:
            twin.wait_send(slot)
        return carry

    lax.fori_loop(0, count, settle, 0)
    for c in stores + lasts:
        c.wait()
    settle_before()


STARTS = (0, 1, 2, 3, 4, 5)
STARTS = (0, 1, 2, 3, 4, 5)


def taken(function, found):
    code = function.__code__
    return {name: found[name] for name in code.co_varnames[: code.co_argcount] if name in found}


def front_kernel(line, group_size, names, *refs):
    found = dict(zip(names, refs))
    r = types.SimpleNamespace(**found)
    place = Place(line)
    sources = (r.gate_hbm, r.up_hbm, r.down_hbm)
    loads = [
        pltpu.make_async_copy(source.at[0], target, r.load_sems.at[i])
        for i, (source, target) in enumerate(zip(sources, (r.gate_ref, r.up_ref, r.down_ref)))
    ]
    for c in loads:
        c.start()
    kept = (
        (r.normed_ref, r.normed_out),
        (r.head_out_ref, r.head_out_out),
        (r.queries_ref, r.queries_out),
        (r.keys_ref, r.keys_out),
        (r.values_ref, r.values_out),
        (r.probs_ref, r.probs_out),
        (r.hidden_ref, r.hidden_out),
    )
    rest = forward_part(place, group_size, kept=kept, **taken(forward_part, found))
    for c in loads:
        c.wait()
    stored = (
        (r.rows, r.rows_out),
        (r.cot_all, r.cots_out),
        (r.active, r.active_out),
        (r.d_gate, r.d_gate_out),
        (r.d_up, r.d_up_out),
    )
    experts_part(
        place,
        r.moe_in_ref,
        cots=r.cot_all,
        stored=stored,
        take_cots=rest[0],
        take_twins=rest[1],
        settle_before=rest[2],
        **taken(experts_part, found),
    )


def run_front(line, group_size, big, small, expert_weights):
    count = 4 * line
    tokens, query, key, value, out, cotangent = big
    length, width = tokens.shape
    q_cols, kv_cols = query.shape[1], key.shape[1]
    hidden = expert_weights[0].shape[2]
    half, cap = width // 2, capacity_of(length, count)
    piece, lines = half // PIECES, 2 * line
    inputs = dict(
        tokens_ref=(tokens, IN_VMEM),
        query_ref=(query, ANY),
        key_ref=(key, ANY),
        value_ref=(value, ANY),
        out_ref=(out, ANY),
        cot_ref=(cotangent, ANY),
        gain_a_ref=(small[0], IN_VMEM),
        gain_m_ref=(small[1], IN_VMEM),
        logits_ref=(small[2], IN_VMEM),
        ids_ref=(small[3], IN_VMEM),
        segments_ref=(small[4], IN_VMEM),
        parents_ref=(small[5], IN_VMEM),
        gate_hbm=(expert_weights[0], ANY),
        up_hbm=(expert_weights[1], ANY),
        down_hbm=(expert_weights[2], ANY),
    )
    rows, inner = (length, width), (count * cap, hidden)
    probs = (q_cols // 128, length, 2 * length)
    outputs = dict(
        hidden_out=(rows, F32, ANY),
        normed_out=(rows, BF16, ANY),
        head_out_out=((length, q_cols), BF16, ANY),
        queries_out=((length, q_cols), BF16, ANY),
        keys_out=((length, kv_cols), BF16, ANY),
        values_out=((length, kv_cols), BF16, ANY),
        probs_out=(probs, F32, ANY),
        peak_ref=((8, 128), F32, IN_VMEM),
        tables_ref=((3, length, 128), F32, IN_VMEM),
        gains_ref=((8, width), F32, IN_VMEM),
        query_keep=((count, *query.shape), BF16, ANY),
        key_keep=((count, *key.shape), BF16, ANY),
        value_keep=((count, *value.shape), BF16, ANY),
        out_keep=((count, *out.shape), BF16, ANY),
        d_rows_ref=(rows, F32, IN_VMEM),
        mix_ref=((line, length, half), BF16, ANY),
        rows_out=((count, cap, width), BF16, ANY),
        cots_out=((count, cap, width), BF16, ANY),
        active_out=(inner, BF16, ANY),
        d_gate_out=(inner, BF16, ANY),
        d_up_out=(inner, BF16, ANY),
    )
    vmem, dma = pltpu.VMEM, pltpu.SemaphoreType.DMA
    dense = vmem((PIECES, lines, length, piece), BF16)
    packed = vmem((PIECES, lines, cap, piece), BF16)
    one_line = vmem((PIECES, line, length, piece), BF16)
    compact = vmem((count, cap, width), BF16)
    scratch = dict(
        hidden_ref=vmem(rows, F32),
        normed_ref=vmem(rows, BF16),
        head_out_ref=vmem((length, q_cols), BF16),
        queries_ref=vmem((length, q_cols), BF16),
        keys_ref=vmem((length, kv_cols), BF16),
        values_ref=vmem((length, kv_cols), BF16),
        probs_ref=vmem(probs, F32),
        query_all=vmem((count, *query.shape), BF16),
        key_all=vmem((count, *key.shape), BF16),
        value_all=vmem((count, *value.shape), BF16),
        out_all=vmem((count, *out.shape), BF16),
        moe_in_ref=vmem(rows, BF16),
        notes=vmem((count, 8, 128), F32),
        note_ref=vmem((count, 8, 128), F32),
        cot_dense=dense,
        cot_packed=packed,
        cot_all=compact,
        own_pick=vmem((count, cap, length), BF16),
        other_pick=vmem((lines, cap, length), BF16),
        gates=vmem((count * cap, 1), F32),
        mix_mine=vmem(rows, F32),
        mix_other=vmem(rows, F32),
        dense=dense,
        packed=packed,
        rows=compact,
        active=vmem(inner, BF16),
        d_gate=vmem(inner, BF16),
        d_up=vmem(inner, BF16),
        d_active=vmem(inner, F32),
        grad_stage=compact,
        mix_stage=compact,
        grad_compact=vmem((PIECES, count, cap, piece), BF16),
        mix_compact=vmem((count, cap, half), BF16),
        grad_dense=dense,
        mix_dense=vmem((lines, length, half), BF16),
        total=vmem((PIECES, length, piece), F32),
        grad_from_b=packed,
        mix_from_b=vmem((lines, cap, half), BF16),
        mix_from_a=vmem((line, length, half), BF16),
        from_a=one_line,
        from_z=one_line,
        gate_ref=vmem((width, hidden), BF16),
        up_ref=vmem((width, hidden), BF16),
        down_ref=vmem((width, hidden), BF16),
        sends=dma((4 + PIECES, 5 * line)),
        recvs=dma((4 + PIECES, count)),
        note_send=dma((count,)),
        note_recv=dma((count,)),
        cot_twins=dma((PIECES, 2, count)),
        local_sems=dma((4 + PIECES,)),
        keep_sems=dma((11,)),
        mix_sems=dma((2,)),
        load_sems=dma((3,)),
        reduce_sems=dma((PIECES + 1, 2, 4 * line)),
        gather_send=dma((PIECES, 5 * line)),
        gather_recv=dma((PIECES, count)),
        row_twins=dma((2 * PIECES + 1, 2, count)),
        last_sems=dma((2, PIECES)),
        store_sems=dma((6,)),
    )
    names = [*inputs, *outputs, *scratch]
    results = pl.pallas_call(
        functools.partial(front_kernel, line, group_size, names),
        out_shape=[jax.ShapeDtypeStruct(shape, kind) for shape, kind, _ in outputs.values()],
        in_specs=[spec for _, spec in inputs.values()],
        out_specs=[spec for _, _, spec in outputs.values()],
        scratch_shapes=list(scratch.values()),
        compiler_params=params(0),
        name="run_front",
    )(*(x for x, _ in inputs.values()))
    return types.SimpleNamespace(**dict(zip(outputs, results)))


def backward_kernel(
    line,
    group_size,
    tokens_ref,
    hidden_ref,
    d_rows_ref,
    cot_ref,
    normed_ref,
    head_out_ref,
    queries_ref,
    keys_ref,
    values_ref,
    probs_ref,
    gains_ref,
    peak_ref,
    tables_ref,
    query_keep,
    key_keep,
    value_keep,
    out_keep,
    mix_ref,
    rows_hbm,
    cots_hbm,
    active_hbm,
    d_gate_hbm,
    d_up_hbm,
    input_grad_ref,
    output_ref,
    query_sum,
    key_sum,
    value_sum,
    out_sum,
    notes,
    grad_gate_ref,
    grad_up_ref,
    grad_down_ref,
    *scratch,
):
    place = Place(line)
    count = 4 * line
    length, width = tokens_ref.shape
    q_cols, kv_cols = queries_ref.shape[1], keys_ref.shape[1]
    shard = width // count
    chunks = q_cols // 128
    (query_all, key_all, value_all, out_all), work = scratch[:4], scratch[4:9]
    rest = scratch[9:34]
    (
        total,
        d_heads,
        d_query,
        d_key,
        d_value,
        part_mine,
        part_other,
        d_hidden_keep,
        mix_total,
        note,
        weight_sems,
        load_sems,
        last_sems,
        part_sems,
        note_sends,
        note_recvs,
        expert_rows,
        cots,
        active,
        d_gate,
        d_up,
        grads,
        expert_sems,
        store_sems,
    ) = scratch[34:]
    by_part = lambda slot: part_of(place, slot)
    reduces = [
        Reduce(place, work[i], *rest[5 * i : 5 * i + 5], *(() if i == 4 else (by_part,))) for i in range(5)
    ]

    def load(slot):
        return pltpu.make_async_copy(mix_ref.at[slot], work[4].at[slot], load_sems.at[slot])

    def begin(slot, carry):
        load(slot).start()
        return carry

    def loaded(slot, carry):
        load(slot).wait()
        return carry

    lax.fori_loop(0, line, begin, 0)
    weights = [
        pltpu.make_async_copy(src, dst, weight_sems.at[i])
        for i, (src, dst) in enumerate(
            ((out_keep, out_all), (query_keep, query_all), (key_keep, key_all), (value_keep, value_all))
        )
    ]
    for c in weights:
        c.start()
    experts = [
        pltpu.make_async_copy(src, dst, expert_sems.at[i])
        for i, (src, dst) in enumerate(
            ((rows_hbm, expert_rows), (cots_hbm, cots), (active_hbm, active), (d_gate_hbm, d_gate), (d_up_hbm, d_up))
        )
    ]
    for c in experts:
        c.start()
    stores = [
        pltpu.make_async_copy(grads.at[i], dst, store_sems.at[i])
        for i, dst in enumerate((grad_gate_ref, grad_up_ref, grad_down_ref))
    ]
    columns = width // 512

    def weight_grad(number):
        left, right = ((expert_rows, d_gate), (expert_rows, d_up), (cots, active))[number]
        left = left.reshape(left.shape[0] * left.shape[1], width)

        def some(i, carry):
            span = pl.ds(pl.multiple_of(512 * i, 512), 512)
            grads[number, span, :] = contract_rows(left[:, span], right[...])
            return carry

        lax.fori_loop(0, columns, some, 0)
        stores[number].start()

    enter(place)
    lax.fori_loop(0, line, loaded, 0)
    mine, theirs = halves(place, width)
    outs = (query_sum, key_sum, value_sum, out_sum, total)
    order = (3, 0, 1, 2)
    mix = reduces[4]
    for z in ends_first(line):
        mix.send_z(z)
    last = remote(total, mix_total.at[:, mine], last_sems.at[0], last_sems.at[1], place.twin())

    def finish(at):
        i = order[at]
        reduces[i].result(outs[i])

    run = Reductions([reduces[i] for i in order], finish)
    hidden = hidden_ref[...]
    inv_moe = lax.rsqrt(jnp.mean(hidden * hidden, axis=1, keepdims=True) + EPSILON)
    unit_moe = hidden * inv_moe
    d_rows = d_rows_ref[...]
    scaled = d_rows * gains_ref[2:3, :]
    d_hidden = cot_ref[...].astype(F32) + inv_moe * (
        scaled - unit_moe * jnp.mean(scaled * unit_moe, axis=1, keepdims=True)
    )
    d_hidden_keep[...] = d_hidden
    moe_gain = jnp.sum(d_rows * unit_moe, axis=0, keepdims=True)
    d_attn = (RESIDUAL * d_hidden).astype(BF16)
    work[3][...] = contract_rows(d_attn, head_out_ref[...]).astype(BF16).reshape(count, shard, q_cols)
    run.ready(1)
    weights[0].wait()
    d_heads[...] = jnp.dot(
        d_attn, out_all[...].reshape(width, q_cols), preferred_element_type=F32
    ).astype(BF16)
    lane = lax.broadcasted_iota(jnp.int32, (length, 128), 1)
    d_key[...] = jnp.zeros_like(d_key)
    d_value[...] = jnp.zeros_like(d_value)
    tables = [tables_ref[i] for i in range(3)]
    for j in range(chunks):
        d_out = chunk_of(d_heads, j)
        keys = pair_of(keys_ref, j, group_size, lane)
        d_prob = contract_cols(d_out, pair_of(values_ref, j, group_size, lane))
        low, d_scores = [], []
        for half in (0, 1):
            side = slice(length * half, length * (half + 1))
            prob = probs_ref[j, :, side]
            grad = d_prob[:, side]
            inner = jnp.sum(prob * grad, axis=1, keepdims=True)
            d_scores.append((prob * (grad - inner)).astype(BF16))
            low.append(prob.astype(BF16))
        d_scores = jnp.concatenate(d_scores, axis=1)
        d_values = contract_rows(jnp.concatenate(low, axis=1), d_out)
        d_keys = contract_rows(d_scores, chunk_of(queries_ref, j)) * SCORE_SCALE
        turned = rope_chunk(
            jnp.dot(d_scores, keys, preferred_element_type=F32) * SCORE_SCALE, tables, -1.0
        )
        d_query[:, 128 * j : 128 * (j + 1)] = turned.astype(BF16)
        for half in (0, 1):
            group = (2 * j + half) // group_size
            side = slice(length * half, length * (half + 1))
            cols = slice(128 * (group // 2), 128 * (group // 2 + 1))
            d_key[:, cols] += place_half(d_keys[side], half, group % 2, lane)
            d_value[:, cols] += place_half(d_values[side], half, group % 2, lane)
        run.run(1)
    normed = normed_ref[...]
    work[0][...] = contract_rows(normed, d_query[...]).astype(BF16).reshape(count, shard, q_cols)
    run.ready(2)
    d_key_lin = jnp.concatenate(
        [rope_chunk(chunk_of(d_key, j), tables, -1.0) for j in range(kv_cols // 128)], axis=1
    ).astype(BF16)
    d_value_lin = d_value[...].astype(BF16)
    run.run(2)
    work[1][...] = contract_rows(normed, d_key_lin).astype(BF16).reshape(count, shard, kv_cols)
    work[2][...] = contract_rows(normed, d_value_lin).astype(BF16).reshape(count, shard, kv_cols)
    run.ready(4)
    run.run(2)
    mix.result(total)
    mix_total[:, mine] = total[...]
    last.start()
    for c in weights[1:]:
        c.wait()
    part_mine[...] = (
        contract_cols(d_query[...], query_all[...].reshape(width, q_cols))
        + contract_cols(d_key_lin, key_all[...].reshape(width, kv_cols))
        + contract_cols(d_value_lin, value_all[...].reshape(width, kv_cols))
    )
    swap = remote(part_mine, part_other, part_sems.at[0], part_sems.at[1], place.twin())
    swap.start()
    run.run(4)
    swap.wait()
    d_normed = part_mine[...] + part_other[...]
    inputs = tokens_ref[...].astype(F32)
    inv_attn = lax.rsqrt(jnp.mean(inputs * inputs, axis=1, keepdims=True) + EPSILON)
    unit_attn = inputs * inv_attn
    scaled = d_normed * gains_ref[1:2, :]
    input_grad_ref[...] = d_hidden_keep[...] + inv_attn * (
        scaled - unit_attn * jnp.mean(scaled * unit_attn, axis=1, keepdims=True)
    )
    attn_gain = jnp.sum(d_normed * unit_attn, axis=0, keepdims=True)
    rows = jnp.concatenate([attn_gain, moe_gain, jnp.zeros((6, width), F32)], axis=0)
    row = lax.broadcasted_iota(jnp.int32, (8, 128), 0)
    peaks = jnp.broadcast_to(peak_ref[0:1, :], (8, 128))
    for p in range(count):
        turned = pltpu.roll(rows, width - shard * p, 1) if p else rows
        note[p] = jnp.where(row == 2, peaks, turned[:, :128])
    exchange = Notes(place, note, notes, note_sends, note_recvs, False)
    exchange.start()
    for c in experts:
        c.wait()
    for number in range(3):
        weight_grad(number)
        run.run(6)
    run.complete()
    for r in reduces[:4]:
        r.settle()
    mix.settle_z()
    last.wait()
    output_ref[...] = (hidden_ref[...] + RESIDUAL * mix_total[...]).astype(BF16)
    exchange.finish()
    for c in stores:
        c.wait()


def run_backward(line, group_size, kept, keeps, mix, experts):
    count = 4 * line
    tokens, queries, keys = kept[0], kept[6], kept[7]
    length, width = tokens.shape
    q_cols, kv_cols = queries.shape[1], keys.shape[1]
    blocks = [x.shape[1:] for x in keeps] + [mix.shape[1:]]
    half = width // 2
    shape = jax.ShapeDtypeStruct
    outs = (
        [shape((length, width), F32), shape((length, width), BF16)]
        + [shape(s, F32) for s in blocks[:4]]
        + [shape((count, 8, 128), F32)]
    )
    kinds = [IN_VMEM] * len(outs) + [ANY] * 3
    hidden = experts[2].shape[1]
    outs += [shape((width, hidden), F32)] * 3
    return pl.pallas_call(
        functools.partial(backward_kernel, line, group_size),
        out_shape=outs,
        in_specs=[IN_VMEM] * len(kept) + [ANY] * 10,
        out_specs=kinds,
        scratch_shapes=[pltpu.VMEM(x.shape, BF16) for x in keeps]
        + [pltpu.VMEM((count, *s), BF16) for s in blocks[:4]]
        + [pltpu.VMEM(mix.shape, BF16)]
        + [x for s in blocks for x in reduce_scratch(line, s)]
        + [
            pltpu.VMEM((length, half), F32),
            pltpu.VMEM((length, q_cols), BF16),
            pltpu.VMEM((length, q_cols), BF16),
            pltpu.VMEM((length, kv_cols), F32),
            pltpu.VMEM((length, kv_cols), F32),
            pltpu.VMEM((length, width), F32),
            pltpu.VMEM((length, width), F32),
            pltpu.VMEM((length, width), F32),
            pltpu.VMEM((length, width), F32),
            pltpu.VMEM((count, 8, 128), F32),
            pltpu.SemaphoreType.DMA((4,)),
            pltpu.SemaphoreType.DMA((count,)),
            pltpu.SemaphoreType.DMA((2,)),
            pltpu.SemaphoreType.DMA((2,)),
            pltpu.SemaphoreType.DMA((count,)),
            pltpu.SemaphoreType.DMA((count,)),
        ]
        + [pltpu.VMEM(x.shape, BF16) for x in experts]
        + [
            pltpu.VMEM((3, width, hidden), F32),
            pltpu.SemaphoreType.DMA((5,)),
            pltpu.SemaphoreType.DMA((3,)),
        ],
        compiler_params=params(3),
        name="run_backward",
    )(*kept, *keeps, mix, *experts)


def finish_kernel(
    group_size,
    output_in,
    input_grad_in,
    query_in,
    key_in,
    value_in,
    out_in,
    notes,
    query_ref,
    key_ref,
    gate_in,
    up_in,
    down_in,
    output,
    input_grad,
    grad_query,
    grad_key,
    grad_value,
    grad_out,
    gain_a,
    gain_m,
    clipped_query,
    clipped_key,
    grad_gate,
    grad_up,
    grad_down,
    stage,
    sems,
):
    pairs = ((gate_in, grad_gate), (up_in, grad_up), (down_in, grad_down))
    takes = [pltpu.make_async_copy(src, stage.at[i], sems.at[0, i]) for i, (src, _) in enumerate(pairs)]
    copies = [pltpu.make_async_copy(stage.at[i], dst.at[0], sems.at[1, i]) for i, (_, dst) in enumerate(pairs)]
    for c in takes:
        c.start()
    output[...] = output_in[...]
    input_grad[...] = input_grad_in[...]
    grad_query[...] = query_in[...]
    grad_key[...] = key_in[...]
    grad_value[...] = value_in[...]
    grad_out[...] = out_in[...]
    for take, c in zip(takes, copies):
        take.wait()
        c.start()
    total, peaks = notes[0], notes[0]
    for p in range(1, notes.shape[0]):
        total = total + notes[p]
        peaks = jnp.maximum(peaks, notes[p])
    shard = gain_a.shape[1]
    gain_a[...] = total[0:1, :shard]
    gain_m[...] = total[1:2, :shard]
    factor = CLIP_LIMIT / jnp.maximum(peaks, CLIP_LIMIT)
    root = jnp.sqrt(factor)
    lane = lax.broadcasted_iota(jnp.int32, (8, 128), 1)

    def scale(h):
        return jnp.max(jnp.where(lane == h, root, 0.0), axis=1, keepdims=True)[2:3, :]

    heads = query_ref.shape[1] // HEAD_SIZE
    wide = lax.broadcasted_iota(jnp.int32, (1, 128), 1)
    scales = [scale(h) for h in range(heads)]
    for j in range(heads // 2):
        row = jnp.where(wide < HEAD_SIZE, scales[2 * j], scales[2 * j + 1])
        cols = slice(128 * j, 128 * (j + 1))
        clipped_query[:, cols] = query_ref[:, cols].astype(F32) * row
    least = [
        functools.reduce(jnp.minimum, scales[group_size * g : group_size * (g + 1)])
        for g in range(heads // group_size)
    ]
    for j in range(len(least) // 2):
        row = jnp.where(wide < HEAD_SIZE, least[2 * j], least[2 * j + 1])
        cols = slice(128 * j, 128 * (j + 1))
        clipped_key[:, cols] = key_ref[:, cols].astype(F32) * row
    for c in copies:
        c.wait()


def finish(group_size, found, notes, query, key, expert_grads):
    shape = jax.ShapeDtypeStruct
    shard = query.shape[0]
    outs = [shape(x.shape, x.dtype) for x in found] + [
        shape((1, shard), F32),
        shape((1, shard), F32),
        shape(query.shape, F32),
        shape(key.shape, F32),
    ]
    return pl.pallas_call(
        functools.partial(finish_kernel, group_size),
        out_shape=outs + [shape((1, *g.shape), F32) for g in expert_grads],
        in_specs=[IN_VMEM] * 9 + [ANY] * 3,
        out_specs=[IN_VMEM] * 10 + [ANY] * 3,
        scratch_shapes=[
            pltpu.VMEM((3, *expert_grads[0].shape), F32),
            pltpu.SemaphoreType.DMA((2, 3)),
        ],
        compiler_params=pltpu.CompilerParams(vmem_limit_bytes=56 * 2**20),
        name="finish",
    )(*found, notes, query, key, *expert_grads)


def on_device_dense(
    tokens,
    attn_norm_gain,
    w_query,
    key_projection,
    value_projection,
    w_out,
    moe_norm_gain,
    w_gate,
    w_up,
    w_down,
    router_logits,
    expert_ids,
    segment_ids,
    parents,
    cotangent,
):
    length, model_width = tokens.shape
    q_cols, kv_cols = w_query.shape[1], key_projection.shape[1]
    q_heads, kv_heads = q_cols // HEAD_SIZE, kv_cols // HEAD_SIZE
    group_size = q_heads // kv_heads
    count = lax.axis_size("dp")
    line = count // 4
    shard = attn_norm_gain.shape[0]
    small = (
        attn_norm_gain[None],
        moe_norm_gain[None],
        router_logits.T,
        expert_ids.T,
        segment_ids,
        parents,
    )
    big = (tokens, w_query, key_projection, value_projection, w_out, cotangent)
    front = run_front(line, group_size, big, small, (w_gate, w_up, w_down))
    keeps = (front.query_keep, front.key_keep, front.value_keep, front.out_keep)
    experts = (front.rows_out, front.cots_out, front.active_out, front.d_gate_out, front.d_up_out)
    kept = (
        tokens,
        front.hidden_out,
        front.d_rows_ref,
        cotangent,
        front.normed_out,
        front.head_out_out,
        front.queries_out,
        front.keys_out,
        front.values_out,
        front.probs_out,
        front.gains_ref,
        front.peak_ref,
        front.tables_ref,
    )
    input_grad, output, *grads = run_backward(line, group_size, kept, keeps, front.mix_ref, experts)
    grads, sums, expert_grads = grads[:4], grads[4], grads[5:]
    output, input_grad, gq, gk, gv, go, gain_a, gain_m, clipped_query, clipped_key, gg, gu, gd = finish(
        group_size, (output, input_grad, *grads), sums, w_query, key_projection, expert_grads
    )
    return (
        output,
        input_grad,
        gain_a[0],
        gq,
        gk,
        gv,
        go,
        gain_m[0],
        gg,
        gu,
        gd,
        clipped_query,
        clipped_key,
    )


DENSE_BYTES = 8 * 2**20


def on_device(*args):
    tokens, w_gate = args[0], args[7]
    count, ranks = lax.axis_size("dp"), lax.axis_size("tensor")
    rows_bytes = count * tokens.shape[0] * tokens.shape[1] * 2
    whole_experts = w_gate.shape[2] * ranks == FFE
    dense = whole_experts and ranks == 2 and count % 8 == 0 and rows_bytes <= DENSE_BYTES
    return on_device_dense(*args) if dense else on_device_general(*args)


def solution(mesh):
    in_specs = (
        P("dp", None),
        P("dp"),
        P("dp", "tensor"),
        P("dp", "tensor"),
        P("dp", "tensor"),
        P("dp", "tensor"),
        P("dp"),
        P("dp", None, "tensor"),
        P("dp", None, "tensor"),
        P("dp", None, "tensor"),
        P("dp", None),
        P("dp", None),
        P("dp", None),
        P("dp", None),
        P("dp", None),
    )
    out_specs = (
        P("dp", None),
        P("dp", None),
        P("dp"),
        P("dp", "tensor"),
        P("dp", "tensor"),
        P("dp", "tensor"),
        P("dp", "tensor"),
        P("dp"),
        P("dp", None, "tensor"),
        P("dp", None, "tensor"),
        P("dp", None, "tensor"),
        P("dp", "tensor"),
        P("dp", "tensor"),
    )
    return jax.shard_map(
        on_device, mesh=mesh, in_specs=in_specs, out_specs=out_specs, check_vma=False
    )
```

```python
import functools
import types

import jax
import jax.numpy as jnp
from jax import lax
from jax.experimental import pallas as pl
from jax.experimental.pallas import tpu as pltpu
from jax.sharding import PartitionSpec as P

HEAD_SIZE = 64
FFE = 512
TOP = 8


EPSILON = 1e-06
SCORE_SCALE = 1.0 / 64.0
RESIDUAL = 0.22
THETA = 10000.0
CLIP_LIMIT = 2.0
NEGATIVE = -1e30


def tree_layout(seg_row, par_row):
    tree_length = seg_row.shape[0]
    seg_count = par_row.shape[0]
    seg_index = jnp.arange(seg_count, dtype=jnp.int32)
    member = (seg_row[:, None] == seg_index[None, :]).astype(jnp.int32)
    seg_len = jnp.sum(member, axis=0)
    seg_start = jnp.sum(jnp.where(seg_index[:, None] > seg_index[None, :], seg_len[None, :], 0), axis=1)
    parent_hot = (par_row[:, None] == seg_index[None, :]).astype(jnp.int32)
    grand_parent = jnp.sum(parent_hot * par_row[None, :], axis=1)
    grand_hot = (grand_parent[:, None] == seg_index[None, :]).astype(jnp.int32)
    parent_len = jnp.sum(parent_hot * seg_len[None, :], axis=1)
    grand_len = jnp.sum(grand_hot * seg_len[None, :], axis=1)
    offset = jnp.where(seg_index != 0, parent_len, 0) + jnp.where(par_row != 0, grand_len, 0)
    tok_start = jnp.sum(member * seg_start[None, :], axis=1)
    tok_offset = jnp.sum(member * offset[None, :], axis=1)
    places = jnp.arange(tree_length, dtype=jnp.int32)
    position = (places - tok_start + tok_offset).astype(jnp.float32)
    identity = (seg_index[:, None] == seg_index[None, :]).astype(jnp.int32)
    ancestor = jnp.minimum(identity + parent_hot + grand_hot, 1)
    reached = jnp.dot(member, ancestor)
    linked = jnp.dot(reached, member.T) > 0
    allowed = linked & (places[None, :] <= places[:, None])
    return (position, allowed)


def rope_tables(position, head_dim):
    half_dim = head_dim // 2
    frequency = THETA ** (-2.0 * jnp.arange(half_dim, dtype=jnp.float32) / head_dim)
    angles = position[:, None] * frequency[None, :]
    return (jnp.cos(angles)[:, None, :], jnp.sin(angles)[:, None, :])


def apply_rotary(values_in, cosine_table, sine_values):
    half_dim = values_in.shape[-1] // 2
    first_half = values_in[..., :half_dim]
    second_half = values_in[..., half_dim:]
    return jnp.concatenate(
        [
            first_half * cosine_table - second_half * sine_values,
            second_half * cosine_table + first_half * sine_values,
        ],
        axis=-1,
    )


def rotate_back(grads_in, cosine_table, sine_values):
    half_dim = grads_in.shape[-1] // 2
    first_half = grads_in[..., :half_dim]
    second_half = grads_in[..., half_dim:]
    return jnp.concatenate(
        [
            first_half * cosine_table + second_half * sine_values,
            second_half * cosine_table - first_half * sine_values,
        ],
        axis=-1,
    )


def slot_tables(routes, experts, capacity):
    flat_ids = routes.reshape(-1)
    row_count = flat_ids.shape[0]
    member = (flat_ids[:, None] == jnp.arange(experts, dtype=jnp.int32)[None, :]).astype(jnp.int32)
    row_total = flat_ids.shape[0]
    before = jnp.dot((jnp.arange(row_total)[:, None] > jnp.arange(row_total)[None, :]).astype(jnp.float32), member.astype(jnp.float32), precision=lax.Precision.HIGHEST).astype(jnp.int32)
    slot_index = jnp.sum(before * member, axis=1)
    target = flat_ids * capacity + slot_index
    source = (
        jnp.full((experts * capacity,), -1, jnp.int32)
        .at[target]
        .set(jnp.arange(row_count, dtype=jnp.int32))
    )
    return (flat_ids, slot_index, source)


def contract_rows(left, right):
    return lax.dot_general(
        left, right, (((0,), (0,)), ((), ())), preferred_element_type=jnp.float32
    )


def contract_cols(left, right):
    return lax.dot_general(
        left, right, (((1,), (1,)), ((), ())), preferred_element_type=jnp.float32
    )


def expert_forward(inputs, gate_w, up_w, down_w):
    gate_pre = jnp.dot(inputs, gate_w, preferred_element_type=jnp.float32)
    up_pre = jnp.dot(inputs, up_w, preferred_element_type=jnp.float32)
    active = (gate_pre / (1.0 + jnp.exp(-gate_pre)) * up_pre).astype(jnp.bfloat16)
    return (contract_cols(active, down_w), (gate_pre, up_pre, active))


def expert_backward(inputs, grads_out, gate_w, up_w, down_w, kept_acts):
    gate_pre, up_pre, active = kept_acts
    d_active = jnp.dot(grads_out, down_w, preferred_element_type=jnp.float32)
    grad_down = contract_rows(grads_out, active)
    sigmoid_val = 1.0 / (1.0 + jnp.exp(-gate_pre))
    d_gate = (d_active * up_pre * sigmoid_val * (1.0 + gate_pre * (1.0 - sigmoid_val))).astype(
        jnp.bfloat16
    )
    d_up = (d_active * gate_pre * sigmoid_val).astype(jnp.bfloat16)
    grad_gate = contract_rows(inputs, d_gate)
    grad_up = contract_rows(inputs, d_up)
    d_inputs = contract_cols(d_gate, gate_w) + contract_cols(d_up, up_w)
    return (d_inputs, grad_gate, grad_up, grad_down)


def send_rows(rows_in):
    return lax.all_to_all(rows_in, "dp", split_axis=0, concat_axis=0, tiled=True)


def return_rows(rows_in):
    return lax.all_to_all(
        rows_in.astype(jnp.bfloat16), "dp", split_axis=0, concat_axis=0, tiled=True
    ).astype(rows_in.dtype)


def send_grads(rows_in):
    return lax.all_to_all(rows_in, "dp", split_axis=0, concat_axis=0, tiled=True)


def return_grads(rows_in):
    return lax.all_to_all(
        rows_in.astype(jnp.bfloat16), "dp", split_axis=0, concat_axis=0, tiled=True
    ).astype(rows_in.dtype)


def share_slots(partial_rows):
    return lax.psum_scatter(partial_rows, "tensor", scatter_dimension=1, tiled=True)


def on_device_general(
    tokens,
    attn_norm_gain,
    w_query,
    key_projection,
    value_projection,
    w_out,
    moe_norm_gain,
    w_gate,
    w_up,
    w_down,
    router_logits,
    expert_ids,
    segment_ids,
    parents,
    cotangent,
):
    length = tokens.shape[0]
    model_width = tokens.shape[1]
    q_cols = w_query.shape[1]
    kv_cols = key_projection.shape[1]
    q_heads = q_cols // HEAD_SIZE
    kv_heads = kv_cols // HEAD_SIZE
    group_size = q_heads // kv_heads
    dp_size = lax.axis_size("dp")
    tensor_ranks = lax.axis_size("tensor")
    replicas = FFE // (w_gate.shape[2] * tensor_ranks)
    experts = dp_size // replicas
    capacity = 4 * (9 * length * TOP // (32 * experts))
    share_rows = capacity // tensor_ranks
    first_slot = lax.axis_index("tensor") * share_rows
    block_rows = min(length, 512)
    attn_gain, moe_gain, query_w, key_weight, value_weight, out_w = (
        lax.all_gather(attn_norm_gain, "dp", axis=0, tiled=True),
        lax.all_gather(moe_norm_gain, "dp", axis=0, tiled=True),
        lax.all_gather(w_query, "dp", axis=0, tiled=True),
        lax.all_gather(key_projection, "dp", axis=0, tiled=True),
        lax.all_gather(value_projection, "dp", axis=0, tiled=True),
        lax.all_gather(w_out, "dp", axis=0, tiled=True),
    )
    attn_gain_f = attn_gain.astype(jnp.float32)
    moe_gain_f = moe_gain.astype(jnp.float32)
    inputs = tokens.astype(jnp.float32)
    inv_attn = lax.rsqrt(jnp.mean(inputs * inputs, axis=1, keepdims=True) + EPSILON)
    unit_attn = inputs * inv_attn
    normalized_rows = (unit_attn * attn_gain_f).astype(jnp.bfloat16)
    position, allowed = tree_layout(segment_ids[0], parents[0])
    cosine_table, sine_values = rope_tables(position, HEAD_SIZE)
    query_linear = jnp.dot(normalized_rows, query_w, preferred_element_type=jnp.float32).reshape(
        length, q_heads, HEAD_SIZE
    )
    key_linear = jnp.dot(normalized_rows, key_weight, preferred_element_type=jnp.float32).reshape(
        length, kv_heads, HEAD_SIZE
    )
    query_heads = (
        apply_rotary(query_linear, cosine_table, sine_values)
        .astype(jnp.bfloat16)
        .reshape(length, kv_heads, group_size, HEAD_SIZE)
    )
    key_heads = apply_rotary(key_linear, cosine_table, sine_values).astype(jnp.bfloat16)
    value_heads = (
        jnp.dot(normalized_rows, value_weight, preferred_element_type=jnp.float32)
        .astype(jnp.bfloat16)
        .reshape(length, kv_heads, HEAD_SIZE)
    )
    q_block = query_heads
    mask_rows = allowed[None, None]
    scores = (
        jnp.einsum("qhgd,khd->hgqk", q_block, key_heads, preferred_element_type=jnp.float32)
        * SCORE_SCALE
    )
    scores = jnp.where(mask_rows, scores, NEGATIVE)
    peak_parts = [jnp.max(scores, axis=(2, 3))]
    row_max = jnp.max(scores, axis=3, keepdims=True)
    expo = jnp.exp(scores - row_max)
    row_total = jnp.sum(expo, axis=3, keepdims=True)
    lse_parts = [row_max + jnp.log(row_total)]
    prob_low = (expo / row_total).astype(jnp.bfloat16)
    block_outs = jnp.einsum(
        "hgqk,khd->qhgd", prob_low, value_heads, preferred_element_type=jnp.float32
    )
    head_out = block_outs.reshape(length, q_cols).astype(jnp.bfloat16)
    attn_mix = lax.psum(contract_cols(head_out, out_w), "tensor")
    hidden = inputs + RESIDUAL * attn_mix
    head_peak = lax.pmax(jnp.max(jnp.stack(peak_parts), axis=0).reshape(q_heads), "dp")
    inv_moe = lax.rsqrt(jnp.mean(hidden * hidden, axis=1, keepdims=True) + EPSILON)
    unit_moe = hidden * inv_moe
    moe_in = (unit_moe * moe_gain_f).astype(jnp.bfloat16)
    logit_max = jnp.max(router_logits, axis=1, keepdims=True)
    logit_exp = jnp.exp(router_logits - logit_max)
    gate_probs = logit_exp / jnp.sum(logit_exp, axis=1, keepdims=True)
    flat_ids, slot_index, source = slot_tables(expert_ids, experts, capacity)
    filled = source >= 0
    source_row = jnp.maximum(source, 0)
    source_token = source_row // TOP
    dispatch_rows = jnp.where(
        filled[:, None], moe_in[source_token], jnp.zeros((), jnp.bfloat16)
    ).reshape(experts, capacity, model_width)
    arrived = send_rows(jnp.repeat(dispatch_rows, replicas, axis=0))
    gate_w, up_w, down_w = (w_gate[0], w_up[0], w_down[0])
    expert_in = arrived.reshape(dp_size * capacity, model_width)
    expert_out, kept_acts = expert_forward(expert_in, gate_w, up_w, down_w)
    partial_out = share_slots(expert_out.reshape(dp_size, capacity, model_width))
    back_parts = return_rows(partial_out).reshape(experts, replicas, share_rows, model_width)
    back_rows = (
        jnp.sum(back_parts, axis=1).astype(jnp.bfloat16).reshape(experts * share_rows, model_width)
    )
    own_slot = ((slot_index >= first_slot) & (slot_index < first_slot + share_rows)).reshape(
        length, TOP
    )
    local_index = (
        flat_ids * share_rows + jnp.clip(slot_index - first_slot, 0, share_rows - 1)
    ).reshape(length, TOP)
    mix_part = jnp.zeros((length, model_width), jnp.float32)
    for column in range(TOP):
        gate_weight = jnp.where(own_slot[:, column], gate_probs[:, column], 0.0)
        mix_part = mix_part + gate_weight[:, None] * back_rows[local_index[:, column]].astype(
            jnp.float32
        )
    expert_mix = lax.psum(mix_part.astype(jnp.bfloat16), "tensor").astype(jnp.float32)
    output = (hidden + RESIDUAL * expert_mix).astype(jnp.bfloat16)
    grad_output = cotangent.astype(jnp.float32)
    mix_grad = RESIDUAL * grad_output
    row_gate = gate_probs.reshape(-1)[source_row]
    grad_rows = (
        jnp.where(filled[:, None], row_gate[:, None] * mix_grad[source_token], 0.0)
        .astype(jnp.bfloat16)
        .reshape(experts, capacity, model_width)
    )
    grad_arrived = send_grads(jnp.repeat(grad_rows, replicas, axis=0)).reshape(
        dp_size * capacity, model_width
    )
    d_inputs, grad_gate, grad_up, grad_down = expert_backward(
        expert_in, grad_arrived, gate_w, up_w, down_w, kept_acts
    )
    d_back = share_slots(d_inputs.reshape(dp_size, capacity, model_width))
    grad_gate, grad_up, grad_down = (grad_gate[None], grad_up[None], grad_down[None])
    d_parts = return_grads(d_back).reshape(experts, replicas, share_rows, model_width)
    d_returned = (
        jnp.sum(d_parts, axis=1).astype(jnp.bfloat16).reshape(experts * share_rows, model_width)
    )
    d_mix_part = jnp.zeros((length, model_width), jnp.float32)
    for column in range(TOP):
        d_mix_part = d_mix_part + jnp.where(
            own_slot[:, column][:, None],
            d_returned[local_index[:, column]].astype(jnp.float32),
            0.0,
        )
    d_moe_in = lax.psum(d_mix_part, "tensor")
    scaled_moe = d_moe_in * moe_gain_f
    grad_moe_gain = jnp.sum(d_moe_in * unit_moe, axis=0)
    d_hidden = grad_output + inv_moe * (
        scaled_moe - unit_moe * jnp.mean(scaled_moe * unit_moe, axis=1, keepdims=True)
    )
    d_attn = (RESIDUAL * d_hidden).astype(jnp.bfloat16)
    grad_out_w = contract_rows(d_attn, head_out)
    d_heads = (
        jnp.dot(d_attn, out_w, preferred_element_type=jnp.float32)
        .astype(jnp.bfloat16)
        .reshape(length, kv_heads, group_size, HEAD_SIZE)
    )
    d_query_parts = []
    d_key = jnp.zeros((length, kv_heads, HEAD_SIZE), jnp.float32)
    d_value = jnp.zeros((length, kv_heads, HEAD_SIZE), jnp.float32)
    for block_number, row_begin in enumerate(range(0, length, block_rows)):
        q_block = query_heads
        mask_rows = allowed[None, None]
        scores = (
            jnp.einsum("qhgd,khd->hgqk", q_block, key_heads, preferred_element_type=jnp.float32)
            * SCORE_SCALE
        )
        scores = jnp.where(mask_rows, scores, NEGATIVE)
        prob_full = jnp.exp(scores - lse_parts[block_number])
        prob_low = prob_full.astype(jnp.bfloat16)
        d_value = jnp.einsum(
            "hgqk,qhgd->khd", prob_low, d_heads, preferred_element_type=jnp.float32
        )
        d_prob = jnp.einsum(
            "qhgd,khd->hgqk", d_heads, value_heads, preferred_element_type=jnp.float32
        )
        inner = jnp.sum(prob_full * d_prob, axis=3, keepdims=True)
        d_scores = (prob_full * (d_prob - inner)).astype(jnp.bfloat16)
        d_query_parts.append(
            jnp.einsum("hgqk,khd->qhgd", d_scores, key_heads, preferred_element_type=jnp.float32)
            * SCORE_SCALE
        )
        d_key = (
            jnp.einsum("hgqk,qhgd->khd", d_scores, q_block, preferred_element_type=jnp.float32)
            * SCORE_SCALE
        )
    d_query_all = d_query_parts[0].reshape(length, q_heads, HEAD_SIZE)
    d_query_lin = (
        rotate_back(d_query_all, cosine_table, sine_values)
        .astype(jnp.bfloat16)
        .reshape(length, q_cols)
    )
    d_key_lin = (
        rotate_back(d_key, cosine_table, sine_values).astype(jnp.bfloat16).reshape(length, kv_cols)
    )
    d_value_lin = d_value.astype(jnp.bfloat16).reshape(length, kv_cols)
    grad_query_w = contract_rows(normalized_rows, d_query_lin)
    grad_key_w = contract_rows(normalized_rows, d_key_lin)
    grad_value_w = contract_rows(normalized_rows, d_value_lin)
    d_normed_part = (
        contract_cols(d_query_lin, query_w)
        + contract_cols(d_key_lin, key_weight)
        + contract_cols(d_value_lin, value_weight)
    )
    d_normed = lax.psum(d_normed_part.astype(jnp.bfloat16), "tensor").astype(jnp.float32)
    scaled_attn = d_normed * attn_gain_f
    grad_attn_gain = jnp.sum(d_normed * unit_attn, axis=0)
    input_grad = d_hidden + inv_attn * (
        scaled_attn - unit_attn * jnp.mean(scaled_attn * unit_attn, axis=1, keepdims=True)
    )
    reduced = (
        lax.psum_scatter(grad_attn_gain, "dp", scatter_dimension=0, tiled=True),
        lax.psum_scatter(grad_moe_gain, "dp", scatter_dimension=0, tiled=True),
        lax.psum_scatter(grad_query_w, "dp", scatter_dimension=0, tiled=True),
        lax.psum_scatter(grad_key_w, "dp", scatter_dimension=0, tiled=True),
        lax.psum_scatter(grad_value_w, "dp", scatter_dimension=0, tiled=True),
        lax.psum_scatter(grad_out_w, "dp", scatter_dimension=0, tiled=True),
    )
    scale_factor = CLIP_LIMIT / jnp.maximum(head_peak, CLIP_LIMIT)
    query_scale = jnp.repeat(jnp.sqrt(scale_factor), HEAD_SIZE)
    key_clip_scale = jnp.repeat(
        jnp.sqrt(jnp.min(scale_factor.reshape(kv_heads, group_size), axis=1)), HEAD_SIZE
    )
    clipped_query = w_query.astype(jnp.float32) * query_scale[None, :]
    clipped_key = key_projection.astype(jnp.float32) * key_clip_scale[None, :]
    return (
        output,
        input_grad,
        reduced[0],
        reduced[2],
        reduced[3],
        reduced[4],
        reduced[5],
        reduced[1],
        grad_gate,
        grad_up,
        grad_down,
        clipped_query,
        clipped_key,
    )


MESH_IDS = pl.DeviceIdType.MESH
F32 = jnp.float32
BF16 = jnp.bfloat16


class Place:
    def __init__(self, line):
        self.line = line
        self.count = 4 * line
        me = lax.axis_index("dp")
        self.core = lax.axis_index("tensor")
        self.me = me
        self.z = me // 4
        y, x = (me // 2) % 2, me % 2
        self.step_a, self.step_b = 2 - self.core, 1 + self.core
        self.a = y * (1 - self.core) + x * self.core
        self.b = x * (1 - self.core) + y * self.core

    def part(self, z, a, b):
        return z * 4 + a * self.step_a + b * self.step_b

    def up(self):
        return (self.me + 4, self.core)

    def down(self):
        return (self.me - 4, self.core)

    def beside_a(self):
        return (self.me + self.step_a * (1 - 2 * self.a), self.core)

    def beside_b(self):
        return (self.me + self.step_b * (1 - 2 * self.b), self.core)

    def twin(self):
        return (self.me, 1 - self.core)

    def peer(self, offset):
        return lax.rem(self.me + offset, self.count)


def enter(place):
    barrier = pltpu.get_barrier_semaphore()

    def greet(offset, carry):
        pl.semaphore_signal(
            barrier, inc=1, device_id=(place.peer(offset), place.core), device_id_type=MESH_IDS
        )
        return carry

    lax.fori_loop(1, place.count, greet, 0)
    pl.semaphore_signal(barrier, inc=1, device_id=place.twin(), device_id_type=MESH_IDS)
    pl.semaphore_wait(barrier, place.count)


def remote(src, dst, send_sem, recv_sem, device):
    return pltpu.make_async_remote_copy(
        src_ref=src,
        dst_ref=dst,
        send_sem=send_sem,
        recv_sem=recv_sem,
        device_id=device,
        device_id_type=MESH_IDS,
    )


class Notes:
    def __init__(self, place, src, dst, send_sem, recv_sem, alike):
        self.place, self.src, self.dst = place, src, dst
        self.send_sem, self.recv_sem, self.alike = send_sem, recv_sem, alike

    def _copy(self, offset, source):
        place = self.place
        to = place.peer(offset)
        return remote(
            self.src if self.alike else self.src.at[to],
            self.dst.at[source],
            self.send_sem.at[offset],
            self.recv_sem.at[source],
            (to, place.core),
        )

    def start(self):
        def send(offset, carry):
            self._copy(offset, self.place.me).start()
            return carry

        lax.fori_loop(1, self.place.count, send, 0)
        me = self.place.me
        self.dst[me] = self.src[...] if self.alike else self.src[me]

    def finish(self):
        def settle(offset, carry):
            self._copy(offset, self.place.peer(offset)).wait_recv()
            self._copy(offset, self.place.me).wait_send()
            return carry

        lax.fori_loop(1, self.place.count, settle, 0)


class Gather:
    def __init__(self, place, view, send_sem, recv_sem, fixed=False):
        self.place, self.view, self.fixed = place, view, fixed
        self.send_sem, self.recv_sem = send_sem, recv_sem

    def _copy(self, source, target, sem, device):
        there = self.view(source if self.fixed else target)
        return remote(self.view(source), there, self.send_sem.at[sem], self.recv_sem.at[target], device)

    def _to_z(self, z, way):
        place = self.place
        device = place.up() if way == 0 else place.down()
        return self._copy(z, z, way * place.line + z, device)

    def _to_a(self, z):
        line = self.place.line
        return self._copy(z, line + z, 2 * line + z, self.place.beside_a())

    def _to_b(self, slot):
        line = self.place.line
        return self._copy(slot, 2 * line + slot, 3 * line + slot, self.place.beside_b())

    def take(self, slot):
        self._copy(slot, slot, 0, self.place.beside_b()).wait_recv()

    def near(self, step, action):
        place = self.place
        if step == 0:
            action(place.z)
        else:
            pl.when(place.z >= step)(lambda: action(place.z - step))
            pl.when(place.z + step < place.line)(lambda: action(place.z + step))

    def hand_on(self, slot):
        self._to_b(slot).start()

    def start(self):
        place = self.place
        pl.when(place.z < place.line - 1)(lambda: self._to_z(place.z, 0).start())
        pl.when(place.z > 0)(lambda: self._to_z(place.z, 1).start())
        self._to_a(self.place.z).start()
        self.hand_on(self.place.z)

    def along(self, step):
        place = self.place

        def pass_on(z):
            self.take(z)
            pl.when(jnp.logical_and(z < place.z, place.z < place.line - 1))(lambda: self._to_z(z, 0).start())
            pl.when(jnp.logical_and(z > place.z, place.z > 0))(lambda: self._to_z(z, 1).start())
            self._to_a(z).start()
            self.hand_on(z)

        self.near(step, pass_on)

    def across(self, step):
        line = self.place.line

        def pass_on(z):
            self.take(line + z)
            self.hand_on(line + z)

        self.near(step, pass_on)

    def step(self, number):
        if number == 0:
            self.start()
            return
        if number < self.place.line:
            self.along(number)
        self.across(number - 1)

    def settle(self):
        place = self.place
        line = place.line

        def wait(z, carry):
            self._to_a(z).wait_send()
            self._to_b(z).wait_send()
            self._to_b(line + z).wait_send()
            pl.when(jnp.logical_and(z <= place.z, place.z < line - 1))(lambda: self._to_z(z, 0).wait_send())
            pl.when(jnp.logical_and(z >= place.z, place.z > 0))(lambda: self._to_z(z, 1).wait_send())
            return carry

        lax.fori_loop(0, line, wait, 0)

    def take_rest(self):
        line = self.place.line

        def wait(k, carry):
            self.take(2 * line + k)
            return carry

        lax.fori_loop(0, 2 * line, wait, 0)


class Pipeline:
    def __init__(self, gathers, starts):
        self.gathers, self.starts, self.at = gathers, starts, 0
        self.steps = gathers[0].place.line + 1

    def run(self, number):
        for _ in range(number):
            for g, start in zip(self.gathers, self.starts):
                if 0 <= self.at - start < self.steps:
                    g.step(self.at - start)
            self.at += 1

    def until(self, index):
        self.run(max(0, self.starts[index] + self.steps - self.at))


class Twin:
    def __init__(self, place, source, target, send_sem, recv_sem):
        self.place, self.source, self.target = place, source, target
        self.send_sem, self.recv_sem = send_sem, recv_sem

    def copy(self, slot):
        line = self.place.line
        group = slot // line
        there = slot + line * ((group % 2) - (group // 2))
        return remote(
            self.source(slot),
            self.target(there),
            self.send_sem.at[slot],
            self.recv_sem.at[there],
            self.place.twin(),
        )

    def start(self, slot):
        self.copy(slot).start()

    def take(self, slot):
        remote(
            self.source(slot),
            self.target(slot),
            self.send_sem.at[slot],
            self.recv_sem.at[slot],
            self.place.twin(),
        ).wait_recv()

    def wait_send(self, slot):
        self.copy(slot).wait_send()


class Reduce:
    def __init__(self, place, parts, from_b, from_a, from_z, send_sem, recv_sem, index=lambda slot: slot):
        self.place, self.parts, self.index = place, parts, index
        self.from_b, self.from_a, self.from_z = from_b, from_a, from_z
        self.send_sem, self.recv_sem = send_sem, recv_sem

    def _copy(self, source, target, sem, device):
        return remote(source, target, self.send_sem.at[sem], self.recv_sem.at[sem], device)

    def _to_b(self, k):
        line = self.place.line
        return self._copy(self.parts.at[self.index(2 * line + k)], self.from_b.at[k], k, self.place.beside_b())

    def _to_a(self, z):
        line = self.place.line
        block = self.parts.at[self.index(line + z)]
        return self._copy(block, self.from_a.at[z], 2 * line + z, self.place.beside_a())

    def _to_z(self, target):
        place, line = self.place, self.place.line
        return remote(
            self.parts.at[self.index(target)],
            self.from_z.at[place.z],
            self.send_sem.at[3 * line + target],
            self.recv_sem.at[3 * line + place.z],
            (place.me + 4 * (target - place.z), place.core),
        )

    def _add(self, slot, block):
        at = self.index(slot)
        self.parts[at] = (self.parts[at].astype(F32) + block.astype(F32)).astype(BF16)

    def send_b(self, k):
        self._to_b(k).start()

    def fold_b(self, k):
        self._to_b(k).wait_recv()
        self._add(k, self.from_b[k])

    def send_a(self, z):
        self._to_a(z).start()

    def fold_a(self, z):
        self._to_a(z).wait_recv()
        self._add(z, self.from_a[z])

    def fold_line_a(self):
        line = self.place.line
        for z in ends_first(line):
            self.fold_b(line + z)
            self.send_a(z)

    def fold_line_own(self):
        for z in ends_first(self.place.line):
            self.fold_b(z)

    def send_z(self, z):
        pl.when(self.place.z != z)(lambda: self._to_z(z).start())

    def finish_line(self):
        for z in ends_first(self.place.line):
            self.fold_a(z)
            self.send_z(z)

    def result(self, out):
        place, line = self.place, self.place.line
        out[...] = self.parts[self.index(place.z)].astype(F32)

        def add(z, carry):
            @pl.when(z != place.z)
            def _():
                remote(
                    self.from_z.at[z], self.from_z.at[z], self.send_sem.at[0], self.recv_sem.at[3 * line + z], place.up()
                ).wait_recv()
                out[...] += self.from_z[z].astype(F32)

            return carry

        lax.fori_loop(0, line, add, 0)

    def settle_b(self):
        def wait(k, carry):
            self._to_b(k).wait_send()
            return carry

        lax.fori_loop(0, 2 * self.place.line, wait, 0)

    def settle_hop_a(self):
        def wait(z, carry):
            self._to_a(z).wait_send()
            return carry

        lax.fori_loop(0, self.place.line, wait, 0)

    def settle_z(self):
        place = self.place

        def wait(z, carry):
            pl.when(place.z != z)(lambda: self._to_z(z).wait_send())
            return carry

        lax.fori_loop(0, place.line, wait, 0)

    def settle(self):
        self.settle_b()
        self.settle_hop_a()
        self.settle_z()


class PackedGather(Gather):
    def __init__(self, place, dense, packed, compact, picks, mine, send_sem, recv_sem, twin_sems):
        self.place, self.dense, self.packed, self.compact = place, dense, packed, compact
        self.own_pick, self.other_pick = picks
        self.mine, self.fixed = mine, False
        self.send_sem, self.recv_sem = send_sem, recv_sem
        view = lambda slot: compact.at[slot, :, mine]
        self.twin = Twin(place, view, view, twin_sems.at[0], twin_sems.at[1])

    def view(self, slot):
        return self.dense.at[slot]

    def _to_b(self, slot):
        line = self.place.line
        return remote(
            self.packed.at[slot],
            self.compact.at[2 * line + slot, :, self.mine],
            self.send_sem.at[3 * line + slot],
            self.recv_sem.at[2 * line + slot],
            self.place.beside_b(),
        )

    def take_compact(self, slot):
        line = self.place.line
        self._to_b(slot - 2 * line).wait_recv()
        self.twin.start(slot)

    def take(self, slot):
        self._copy(slot, slot, 0, self.place.beside_b()).wait_recv()

    def hand_on(self, slot):
        block = self.dense[slot]
        self.packed[slot] = jnp.dot(self.other_pick[slot], block, preferred_element_type=F32).astype(BF16)
        self._to_b(slot).start()
        self.compact[slot, :, self.mine] = jnp.dot(
            self.own_pick[slot], block, preferred_element_type=F32
        ).astype(BF16)
        self.twin.start(slot)


class PackedReduce(Reduce):
    def __init__(self, place, compact, picks, *rest):
        super().__init__(place, *rest)
        self.compact = compact
        self.own_pick, self.other_pick = picks

    def _to_b(self, k):
        line = self.place.line
        return self._copy(self.compact.at[2 * line + k], self.from_b.at[k], k, self.place.beside_b())

    def fold_b(self, k):
        self._to_b(k).wait_recv()
        own = contract_rows(self.own_pick[k], self.compact[k])
        self.parts[k] = (own + contract_rows(self.other_pick[k], self.from_b[k])).astype(BF16)


def selections(place, notes, own_pick, other_pick, gates=None):
    line = place.line
    cap, length = own_pick.shape[1:]
    rows = [notes[part_of(place, slot)][0:1, :] for slot in range(4 * line)]
    for slot in range(2 * line):
        note = notes[part_of(place, slot)]
        rows.append(jnp.where(place.core == 0, note[3:4, :], note[4:5, :]))
    before = lax.broadcasted_iota(jnp.int32, (length, length), 0) < lax.broadcasted_iota(
        jnp.int32, (length, length), 1
    )
    weights = jnp.concatenate(rows, axis=0)
    rank = jnp.dot(
        jnp.where(weights > 0.0, 1.0, 0.0).astype(BF16),
        jnp.where(before, 1.0, 0.0).astype(BF16),
        preferred_element_type=F32,
    )
    rank = jnp.where(weights > 0.0, rank, -1.0)
    number = lax.broadcasted_iota(jnp.int32, (cap, length), 0).astype(F32)
    for i in range(len(rows)):
        pick = jnp.where(rank[i : i + 1, :] == number, 1.0, 0.0)
        if i >= 4 * line:
            other_pick[i - 4 * line] = pick.astype(BF16)
            continue
        own_pick[i] = pick.astype(BF16)
        if gates is not None:
            gates[cap * i : cap * (i + 1), :] = jnp.sum(pick * rows[i], axis=1, keepdims=True)


AHEAD = 8


class Reductions:
    def __init__(self, reduces, finish):
        self.reduces, self.finish = reduces, finish
        self.at = self.sent = self.limit = 0
        line = self.line = reduces[0].place.line
        self.ks = [line + z for z in ends_first(line)] + ends_first(line)
        self.steps = [(i, k) for i in range(len(reduces)) for k in self.ks]

    def ready(self, number):
        self.limit = 2 * self.line * number
        self._send()

    def _send(self):
        while self.sent < min(self.at + AHEAD, self.limit):
            i, k = self.steps[self.sent]
            self.reduces[i].send_b(k)
            self.sent += 1

    def run(self, number):
        for _ in range(number):
            self._step()

    def _step(self):
        i, k = self.steps[self.at]
        self.at += 1
        self._send()
        self.reduces[i].fold_b(k)
        if k >= self.line:
            self.reduces[i].send_a(k - self.line)
        if k == self.ks[self.line - 1] and i > 0:
            self.reduces[i - 1].finish_line()
        if k == self.ks[-1] and i > 0:
            self.finish(i - 1)

    def complete(self):
        self.run(len(self.steps) - self.at)
        self.reduces[-1].finish_line()
        self.finish(len(self.reduces) - 1)


def reduce_scratch(line, block):
    return [
        pltpu.VMEM((2 * line, *block), BF16),
        pltpu.VMEM((line, *block), BF16),
        pltpu.VMEM((line, *block), BF16),
        pltpu.SemaphoreType.DMA((4 * line,)),
        pltpu.SemaphoreType.DMA((4 * line,)),
    ]


def ends_first(line):
    order = []
    for i in range((line + 1) // 2):
        order += [i] if i == line - 1 - i else [i, line - 1 - i]
    return order


def part_of(place, slot):
    line = place.line
    group, z = slot // line, slot % line
    flip_a, flip_b = group % 2, group // 2
    a = place.a + flip_a * (1 - 2 * place.a)
    b = place.b + flip_b * (1 - 2 * place.b)
    return place.part(z, a, b)


PIECES = 2


def pieces_of(place, width):
    piece = width // 2 // PIECES

    def spans(core):
        starts = [pl.multiple_of((core * PIECES + i) * piece, 128) for i in range(PIECES)]
        return [pl.ds(start, piece) for start in starts]

    return spans(place.core), spans(1 - place.core), piece


def halves(place, width):
    half = width // 2
    mine = pl.ds(pl.multiple_of(place.core * half, 128), half)
    theirs = pl.ds(pl.multiple_of((1 - place.core) * half, 128), half)
    return mine, theirs


def place_half(chunk, have, want, lane):
    chunk = chunk if have == want else pltpu.roll(chunk, HEAD_SIZE, 1)
    return jnp.where(lane // HEAD_SIZE == want, chunk, 0.0)


def rope_chunk(chunk, tables, sign):
    ahead = pltpu.roll(chunk, 128 - HEAD_SIZE // 2, 1)
    behind = pltpu.roll(chunk, HEAD_SIZE // 2, 1)
    return chunk * tables[0] + sign * (ahead * tables[1] + behind * tables[2])


def chunk_of(ref, j):
    return ref[:, 128 * j : 128 * (j + 1)]


def pair_of(ref, j, group_size, lane):
    both = []
    for half in (0, 1):
        group = (2 * j + half) // group_size
        both.append(place_half(chunk_of(ref, group // 2).astype(F32), group % 2, half, lane))
    return jnp.concatenate(both, axis=0).astype(BF16)


def spread_gains(notes, shard, width):
    total = jnp.zeros((8, width), F32)
    for p in range(notes.shape[0]):
        row = jnp.concatenate([notes[p], jnp.zeros((8, width - 128), F32)], axis=1)
        total += pltpu.roll(row, shard * p, 1) if p else row
    return total


def gate_table(logits, ids, experts):
    expo = jnp.exp(logits - jnp.max(logits, axis=0, keepdims=True))
    probs = expo / jnp.sum(expo, axis=0, keepdims=True)
    top, length = logits.shape
    expert = lax.broadcasted_iota(jnp.int32, (experts, length), 0)
    table = jnp.zeros((experts, length), F32)
    for c in range(top):
        table += jnp.where(ids[c : c + 1, :] == expert, probs[c : c + 1, :], 0.0)
    return table


def write_notes(note_ref, gates, gains):
    shard = gains[0].shape[1]
    row = lax.broadcasted_iota(jnp.int32, (8, 128), 0)
    pad = jnp.zeros((1, 128 - shard), F32)
    shared = jnp.zeros((8, 128), F32)
    for i, gain in enumerate(gains):
        shared = jnp.where(row == i + 1, jnp.concatenate([gain, pad], axis=1), shared)
    for p in range(note_ref.shape[0]):
        tile = shared
        for at, e in ((0, p), (3, p + 1 - 2 * (p % 2)), (4, p + 2 - 4 * (p // 2 % 2))):
            tile = jnp.where(row == at, gates[e : e + 1, :], tile)
        note_ref[p] = tile


def tree_tables(segments, parents, length):
    row = lax.broadcasted_iota(jnp.int32, (length, length), 0)
    lane = lax.broadcasted_iota(jnp.int32, (length, length), 1)

    def total(x):
        return jnp.sum(x.astype(F32), axis=1, keepdims=True)

    own_row = segments.astype(F32)
    own = total(jnp.where(row == lane, own_row, 0.0))
    kinds = parents.shape[1]
    kind = lax.broadcasted_iota(jnp.int32, (length, kinds), 1).astype(F32)
    above = parents.astype(F32)
    parent = total(jnp.where(kind == own, above, 0.0))
    grand = total(jnp.where(kind == parent, above, 0.0))
    in_parent, in_grand = own_row == parent, own_row == grand
    start = total(jnp.where(own_row < own, 1.0, 0.0))
    offset = jnp.where(own != 0.0, total(jnp.where(in_parent, 1.0, 0.0)), 0.0)
    offset += jnp.where(parent != 0.0, total(jnp.where(in_grand, 1.0, 0.0)), 0.0)
    place = lax.broadcasted_iota(jnp.int32, (length, 1), 0).astype(F32)
    linked = jnp.logical_or(own_row == own, jnp.logical_or(in_parent, in_grand))
    return place - start + offset, jnp.logical_and(linked, lane <= row)


def write_tables(tables_ref, position):
    lane = lax.broadcasted_iota(jnp.int32, (1, 128), 1)
    half = HEAD_SIZE // 2
    frequency = THETA ** ((lane % half).astype(F32) * (-2.0 / HEAD_SIZE))
    angles = position * frequency
    sine = jnp.sin(angles)
    first = lane % HEAD_SIZE < half
    tables_ref[0] = jnp.cos(angles)
    tables_ref[1] = jnp.where(first, -sine, 0.0)
    tables_ref[2] = jnp.where(first, 0.0, sine)


def forward_part(
    place,
    group_size,
    tokens_ref,
    query_ref,
    key_ref,
    value_ref,
    out_ref,
    cot_ref,
    gain_a_ref,
    gain_m_ref,
    logits_ref,
    ids_ref,
    segments_ref,
    parents_ref,
    moe_in_ref,
    hidden_ref,
    normed_ref,
    head_out_ref,
    queries_ref,
    keys_ref,
    values_ref,
    probs_ref,
    peak_ref,
    tables_ref,
    gains_ref,
    notes,
    query_keep,
    key_keep,
    value_keep,
    out_keep,
    query_all,
    key_all,
    value_all,
    out_all,
    cot_dense,
    cot_packed,
    cot_all,
    own_pick,
    other_pick,
    gates,
    mix_mine,
    mix_other,
    note_ref,
    sends,
    recvs,
    note_send,
    note_recv,
    cot_twins,
    local_sems,
    keep_sems,
    mix_sems,
    kept,
):
    line = place.line
    count = 4 * line
    length, width = tokens_ref.shape
    shard, q_cols = query_ref.shape
    chunks = q_cols // 128
    spans, _, piece = pieces_of(place, width)
    own = []
    blocks = ((query_ref, query_all), (key_ref, key_all), (value_ref, value_all), (out_ref, out_all))
    for i, (src, dst) in enumerate(blocks):
        own.append(pltpu.make_async_copy(src, dst.at[place.me], local_sems.at[i]))
    for i in range(PIECES):
        own.append(pltpu.make_async_copy(cot_ref.at[:, spans[i]], cot_dense.at[i, place.z], local_sems.at[4 + i]))
    for c in own:
        c.start()
    enter(place)
    note = Notes(place, note_ref, notes, note_send, note_recv, False)
    for c in own:
        c.wait()
    gathers = [
        Gather(place, lambda s, ref=ref: ref.at[part_of(place, s)], sends.at[i], recvs.at[i], True)
        for i, ref in enumerate((query_all, key_all, value_all, out_all))
    ]
    picks = (own_pick, other_pick)
    cots = [
        PackedGather(
            place,
            cot_dense.at[i],
            cot_packed.at[i],
            cot_all,
            picks,
            spans[i],
            sends.at[4 + i],
            recvs.at[4 + i],
            cot_twins.at[i],
        )
        for i in range(PIECES)
    ]
    out = gathers[3]
    pipeline = Pipeline([gathers[i] for i in (1, 2, 0, 3)] + cots, STARTS)
    pipeline.run(1)
    gains = [g[...].astype(F32) for g in (gain_a_ref, gain_m_ref)]
    write_notes(note_ref, gate_table(logits_ref[...], ids_ref[...], count), gains)
    note.start()
    inputs = tokens_ref[...].astype(F32)
    inv_attn = lax.rsqrt(jnp.mean(inputs * inputs, axis=1, keepdims=True) + EPSILON)
    pipeline.run(1)
    note.finish()
    gains_ref[...] = spread_gains(notes, shard, width)
    normed_ref[...] = (inputs * inv_attn * gains_ref[1:2, :]).astype(BF16)
    pipeline.run(1)
    position, allowed = tree_tables(segments_ref[...], parents_ref[...], length)
    write_tables(tables_ref, position)
    pipeline.run(1)
    selections(place, notes, own_pick, other_pick, gates)
    pipeline.until(2)
    for g in gathers[:3]:
        g.take_rest()
    normed = normed_ref[...]
    tables = [tables_ref[i] for i in range(3)]
    query_lin = jnp.dot(normed, query_all[...].reshape(width, q_cols), preferred_element_type=F32)
    for j in range(chunks):
        queries_ref[:, 128 * j : 128 * (j + 1)] = rope_chunk(
            query_lin[:, 128 * j : 128 * (j + 1)], tables, 1.0
        ).astype(BF16)
    kv_cols = key_ref.shape[1]
    key_lin = jnp.dot(normed, key_all[...].reshape(width, kv_cols), preferred_element_type=F32)
    for j in range(kv_cols // 128):
        keys_ref[:, 128 * j : 128 * (j + 1)] = rope_chunk(
            key_lin[:, 128 * j : 128 * (j + 1)], tables, 1.0
        ).astype(BF16)
    values_ref[...] = jnp.dot(
        normed, value_all[...].reshape(width, kv_cols), preferred_element_type=F32
    ).astype(BF16)
    lane = lax.broadcasted_iota(jnp.int32, (length, 128), 1)
    small_lane = lax.broadcasted_iota(jnp.int32, (8, 128), 1)
    peaks = jnp.zeros((8, 128), F32)
    pipeline.run(1)
    for j in range(chunks):
        both = contract_cols(chunk_of(queries_ref, j), pair_of(keys_ref, j, group_size, lane)) * SCORE_SCALE
        low = []
        for half in (0, 1):
            scores = jnp.where(allowed, both[:, length * half : length * (half + 1)], NEGATIVE)
            row_max = jnp.max(scores, axis=1, keepdims=True)
            peak = jnp.max(row_max, axis=0, keepdims=True)
            peaks = jnp.where(small_lane == 2 * j + half, peak, peaks)
            expo = jnp.exp(scores - row_max)
            prob = expo / jnp.sum(expo, axis=1, keepdims=True)
            probs_ref[j, :, length * half : length * (half + 1)] = prob
            low.append(prob.astype(BF16))
        mixed = jnp.dot(
            jnp.concatenate(low, axis=1),
            pair_of(values_ref, j, group_size, lane),
            preferred_element_type=F32,
        )
        head_out_ref[:, 128 * j : 128 * (j + 1)] = mixed.astype(BF16)
        pipeline.run(1)
    peak_ref[...] = peaks
    pairs = [(query_all, query_keep), (key_all, key_keep), (value_all, value_keep), *kept[:-1]]
    pairs += [(out_all, out_keep), kept[-1]]
    keeps = [pltpu.make_async_copy(src, dst, keep_sems.at[i]) for i, (src, dst) in enumerate(pairs)]
    for c in keeps[:-2]:
        c.start()
    out.take_rest()
    keeps[-2].start()
    mix_mine[...] = contract_cols(head_out_ref[...], out_all[...].reshape(width, q_cols))
    swap = remote(mix_mine, mix_other, mix_sems.at[0], mix_sems.at[1], place.twin())
    swap.start()
    swap.wait()
    hidden = tokens_ref[...].astype(F32) + RESIDUAL * (mix_mine[...] + mix_other[...])
    hidden_ref[...] = hidden
    keeps[-1].start()
    inv_moe = lax.rsqrt(jnp.mean(hidden * hidden, axis=1, keepdims=True) + EPSILON)
    moe_in_ref[...] = (hidden * inv_moe * gains_ref[2:3, :]).astype(BF16)

    pipeline.until(len(pipeline.gathers) - 1)

    def take_cots():
        def rest(slot, carry):
            for cot in cots:
                cot.take_compact(slot)
            return carry

        lax.fori_loop(2 * line, count, rest, 0)

    def take_twins(group):
        for slot in range(line * group, line * (group + 1)):
            for cot in cots:
                cot.twin.take(slot)
                cot.twin.wait_send(slot)

    def settle():
        for g in gathers + cots:
            g.settle()
        for c in keeps:
            c.wait()

    return take_cots, take_twins, settle


ANY = pl.BlockSpec(memory_space=pl.ANY)
IN_VMEM = pl.BlockSpec(memory_space=pltpu.VMEM)


def params(number):
    return pltpu.CompilerParams(
        collective_id=number, has_side_effects=True, vmem_limit_bytes=60 * 2**20
    )


def capacity_of(length, experts):
    most = 4 * (9 * length * TOP // (32 * experts))
    return min(-(-most // 16) * 16, length)


def experts_part(
    place,
    rows_ref,
    gate_ref,
    up_ref,
    down_ref,
    d_rows_ref,
    mix_ref,
    dense,
    packed,
    rows,
    cots,
    own_pick,
    other_pick,
    gates,
    active,
    d_gate,
    d_up,
    d_active,
    grad_stage,
    mix_stage,
    grad_compact,
    mix_compact,
    grad_dense,
    mix_dense,
    total,
    grad_from_b,
    mix_from_b,
    mix_from_a,
    from_a,
    from_z,
    reduce_sems,
    gather_send,
    gather_recv,
    row_twins,
    last_sems,
    store_sems,
    stored,
    take_cots,
    take_twins,
    settle_before,
):
    line = place.line
    count = 4 * line
    cap, width = rows.shape[1:]
    tile_rows = line * cap
    mine, _ = halves(place, width)
    spans, their_spans, piece = pieces_of(place, width)
    for i in range(PIECES):
        dense[i, place.z] = rows_ref[:, spans[i]]
    picks = (own_pick, other_pick)
    gathers = [
        PackedGather(
            place,
            dense.at[i],
            packed.at[i],
            rows,
            picks,
            spans[i],
            gather_send.at[i],
            gather_recv.at[i],
            row_twins.at[i],
        )
        for i in range(PIECES)
    ]
    grad_twins = [
        Twin(
            place,
            lambda s, i=i: grad_stage.at[s, :, their_spans[i]],
            lambda s, i=i: grad_compact.at[i, s],
            row_twins.at[PIECES + i, 0],
            row_twins.at[PIECES + i, 1],
        )
        for i in range(PIECES)
    ]
    mix_twin = Twin(
        place,
        lambda s: mix_stage.at[s, :, halves(place, width)[1]],
        lambda s: mix_compact.at[s],
        row_twins.at[2 * PIECES, 0],
        row_twins.at[2 * PIECES, 1],
    )
    reduces = [
        PackedReduce(
            place,
            grad_compact.at[i],
            picks,
            grad_dense.at[i],
            grad_from_b.at[i],
            from_a.at[i],
            from_z.at[i],
            reduce_sems.at[i, 0],
            reduce_sems.at[i, 1],
        )
        for i in range(PIECES)
    ]
    mix_reduce = PackedReduce(
        place,
        mix_compact,
        picks,
        mix_dense,
        mix_from_b,
        mix_from_a,
        None,
        reduce_sems.at[PIECES, 0],
        reduce_sems.at[PIECES, 1],
    )

    def group_of(group):
        first = pl.multiple_of(tile_rows * group, tile_rows)
        return pl.ds(line * group, line), pl.ds(first, tile_rows)

    def slots_of(group):
        return [line * group + z for z in range(line)]

    def ahead(group):
        some, flat = group_of(group)
        cot = cots[some].reshape(tile_rows, width).astype(F32)
        d_out = (gates[flat, :] * (RESIDUAL * cot)).astype(BF16)
        cots[some] = d_out.reshape(line, cap, width)
        d_active[flat, :] = jnp.dot(d_out, down_ref[...], preferred_element_type=F32)

    def work(group):
        some, flat = group_of(group)
        for slot in slots_of(group):
            for g in gathers:
                g.twin.take(slot)
        x = rows[some].reshape(tile_rows, width)
        gate_pre = jnp.dot(x, gate_ref[...], preferred_element_type=F32)
        up_pre = jnp.dot(x, up_ref[...], preferred_element_type=F32)
        sigmoid = 1.0 / (1.0 + jnp.exp(-gate_pre))
        silu = gate_pre * sigmoid
        active[flat, :] = (silu * up_pre).astype(BF16)
        d_act = d_active[flat, :]
        d_g = (d_act * up_pre * sigmoid * (1.0 + gate_pre * (1.0 - sigmoid))).astype(BF16)
        d_u = (d_act * silu).astype(BF16)
        d_gate[flat, :] = d_g
        d_up[flat, :] = d_u
        d_in = contract_cols(d_g, gate_ref[...]) + contract_cols(d_u, up_ref[...])
        grad_stage[some] = d_in.astype(BF16).reshape(line, cap, width)
        for twin in grad_twins:
            for slot in slots_of(group):
                twin.start(slot)

    def mix_work(group):
        some, flat = group_of(group)
        mix = gates[flat, :] * contract_cols(active[flat, :], down_ref[...])
        mix_stage[some] = mix.astype(BF16).reshape(line, cap, width)
        for slot in slots_of(group):
            mix_twin.start(slot)

    def fold(twin, stage, span, compact, group, send=None):
        def one(slot, carry):
            twin.take(slot)
            compact[slot] = (compact[slot].astype(F32) + stage[slot, :, span].astype(F32)).astype(BF16)
            if send is not None:
                send(slot - 2 * line)
            return carry

        lax.fori_loop(line * group, line * (group + 1), one, 0)

    def grad_fold(i, group, send=False):
        to_b = reduces[i].send_b if send else None
        fold(grad_twins[i], grad_stage, spans[i], grad_compact.at[i], group, to_b)

    def take_group(group):
        for slot in slots_of(group):
            for g in gathers:
                g.take_compact(slot)

    stores = []
    mix_fold = functools.partial(fold, mix_twin, mix_stage, mine, mix_compact)
    pipeline = Pipeline(gathers, [0] * PIECES)
    pipeline.run(1)
    take_cots()
    pipeline.run(2)
    for group in range(4):
        take_twins(group)

    def ahead_loop(group, carry):
        ahead(group)
        return carry

    lax.fori_loop(0, 4, ahead_loop, 0)
    pipeline.run(2)
    pipeline.until(PIECES - 1)
    work(0)
    take_group(2)
    work(2)
    work(1)
    take_group(3)
    order = ends_first(line)
    grad_fold(0, 2, True)
    for i in range(1, PIECES):
        grad_fold(i, 2)
    work(3)
    for i, (source, target) in enumerate(stored):
        stores.append(pltpu.make_async_copy(source, target, store_sems.at[i]))
        stores[-1].start()
    grad_fold(0, 3, True)
    for i in range(1, PIECES):
        for z in range(line):
            reduces[i].send_b(z)
        grad_fold(i, 3, True)
    mix_work(1)
    for i in range(PIECES):
        grad_fold(i, 1)
    mix_work(2)
    mix_fold(2, mix_reduce.send_b)
    for i in range(PIECES):
        grad_fold(i, 0)
    fillers = [
        lambda: mix_work(3),
        lambda: mix_fold(3, mix_reduce.send_b),
        lambda: mix_work(0),
        lambda: mix_fold(1),
        lambda: mix_fold(0),
    ]
    for i, r in enumerate(reduces):
        for z in order:
            r.fold_b(line + z)
            r.send_a(z)
        if fillers:
            fillers.pop(0)()
        for z in order:
            r.fold_b(z)
        if i > 0:
            reduces[i - 1].finish_line()
        if fillers:
            fillers.pop(0)()
    reduces[-1].finish_line()
    for filler in fillers:
        filler()
    for z in order:
        mix_reduce.fold_b(line + z)
        mix_reduce.send_a(z)
    for z in order:
        mix_reduce.fold_b(z)
    lasts = []
    for i, r in enumerate(reduces):
        r.result(total.at[i])
        d_rows_ref[:, spans[i]] = total[i]
        there = d_rows_ref.at[:, spans[i]]
        lasts.append(remote(total.at[i], there, last_sems.at[0, i], last_sems.at[1, i], place.twin()))
        lasts[-1].start()
    for z in order:
        mix_reduce.fold_a(z)
    stores.append(pltpu.make_async_copy(mix_dense.at[pl.ds(0, line)], mix_ref, store_sems.at[len(stored)]))
    stores[-1].start()
    for r in reduces:
        r.settle()
    mix_reduce.settle_b()
    mix_reduce.settle_hop_a()
    for g in gathers:
        g.settle()

    twins = [g.twin for g in gathers] + grad_twins + [mix_twin]

    def settle(slot, carry):
        for twin in twins:
            twin.wait_send(slot)
        return carry

    lax.fori_loop(0, count, settle, 0)
    for c in stores + lasts:
        c.wait()
    settle_before()


STARTS = (0, 1, 2, 3, 4, 5)
STARTS = (0, 1, 2, 3, 4, 5)


def taken(function, found):
    code = function.__code__
    return {name: found[name] for name in code.co_varnames[: code.co_argcount] if name in found}


def front_kernel(line, group_size, names, *refs):
    found = dict(zip(names, refs))
    r = types.SimpleNamespace(**found)
    place = Place(line)
    sources = (r.gate_hbm, r.up_hbm, r.down_hbm)
    loads = [
        pltpu.make_async_copy(source.at[0], target, r.load_sems.at[i])
        for i, (source, target) in enumerate(zip(sources, (r.gate_ref, r.up_ref, r.down_ref)))
    ]
    for c in loads:
        c.start()
    kept = (
        (r.normed_ref, r.normed_out),
        (r.head_out_ref, r.head_out_out),
        (r.queries_ref, r.queries_out),
        (r.keys_ref, r.keys_out),
        (r.values_ref, r.values_out),
        (r.probs_ref, r.probs_out),
        (r.hidden_ref, r.hidden_out),
    )
    rest = forward_part(place, group_size, kept=kept, **taken(forward_part, found))
    for c in loads:
        c.wait()
    stored = (
        (r.rows, r.rows_out),
        (r.cot_all, r.cots_out),
        (r.active, r.active_out),
        (r.d_gate, r.d_gate_out),
        (r.d_up, r.d_up_out),
    )
    experts_part(
        place,
        r.moe_in_ref,
        cots=r.cot_all,
        stored=stored,
        take_cots=rest[0],
        take_twins=rest[1],
        settle_before=rest[2],
        **taken(experts_part, found),
    )


def run_front(line, group_size, big, small, expert_weights):
    count = 4 * line
    tokens, query, key, value, out, cotangent = big
    length, width = tokens.shape
    q_cols, kv_cols = query.shape[1], key.shape[1]
    hidden = expert_weights[0].shape[2]
    half, cap = width // 2, capacity_of(length, count)
    piece, lines = half // PIECES, 2 * line
    inputs = dict(
        tokens_ref=(tokens, IN_VMEM),
        query_ref=(query, ANY),
        key_ref=(key, ANY),
        value_ref=(value, ANY),
        out_ref=(out, ANY),
        cot_ref=(cotangent, ANY),
        gain_a_ref=(small[0], IN_VMEM),
        gain_m_ref=(small[1], IN_VMEM),
        logits_ref=(small[2], IN_VMEM),
        ids_ref=(small[3], IN_VMEM),
        segments_ref=(small[4], IN_VMEM),
        parents_ref=(small[5], IN_VMEM),
        gate_hbm=(expert_weights[0], ANY),
        up_hbm=(expert_weights[1], ANY),
        down_hbm=(expert_weights[2], ANY),
    )
    rows, inner = (length, width), (count * cap, hidden)
    probs = (q_cols // 128, length, 2 * length)
    outputs = dict(
        hidden_out=(rows, F32, ANY),
        normed_out=(rows, BF16, ANY),
        head_out_out=((length, q_cols), BF16, ANY),
        queries_out=((length, q_cols), BF16, ANY),
        keys_out=((length, kv_cols), BF16, ANY),
        values_out=((length, kv_cols), BF16, ANY),
        probs_out=(probs, F32, ANY),
        peak_ref=((8, 128), F32, IN_VMEM),
        tables_ref=((3, length, 128), F32, IN_VMEM),
        gains_ref=((8, width), F32, IN_VMEM),
        query_keep=((count, *query.shape), BF16, ANY),
        key_keep=((count, *key.shape), BF16, ANY),
        value_keep=((count, *value.shape), BF16, ANY),
        out_keep=((count, *out.shape), BF16, ANY),
        d_rows_ref=(rows, F32, IN_VMEM),
        mix_ref=((line, length, half), BF16, ANY),
        rows_out=((count, cap, width), BF16, ANY),
        cots_out=((count, cap, width), BF16, ANY),
        active_out=(inner, BF16, ANY),
        d_gate_out=(inner, BF16, ANY),
        d_up_out=(inner, BF16, ANY),
    )
    vmem, dma = pltpu.VMEM, pltpu.SemaphoreType.DMA
    dense = vmem((PIECES, lines, length, piece), BF16)
    packed = vmem((PIECES, lines, cap, piece), BF16)
    one_line = vmem((PIECES, line, length, piece), BF16)
    compact = vmem((count, cap, width), BF16)
    scratch = dict(
        hidden_ref=vmem(rows, F32),
        normed_ref=vmem(rows, BF16),
        head_out_ref=vmem((length, q_cols), BF16),
        queries_ref=vmem((length, q_cols), BF16),
        keys_ref=vmem((length, kv_cols), BF16),
        values_ref=vmem((length, kv_cols), BF16),
        probs_ref=vmem(probs, F32),
        query_all=vmem((count, *query.shape), BF16),
        key_all=vmem((count, *key.shape), BF16),
        value_all=vmem((count, *value.shape), BF16),
        out_all=vmem((count, *out.shape), BF16),
        moe_in_ref=vmem(rows, BF16),
        notes=vmem((count, 8, 128), F32),
        note_ref=vmem((count, 8, 128), F32),
        cot_dense=dense,
        cot_packed=packed,
        cot_all=compact,
        own_pick=vmem((count, cap, length), BF16),
        other_pick=vmem((lines, cap, length), BF16),
        gates=vmem((count * cap, 1), F32),
        mix_mine=vmem(rows, F32),
        mix_other=vmem(rows, F32),
        dense=dense,
        packed=packed,
        rows=compact,
        active=vmem(inner, BF16),
        d_gate=vmem(inner, BF16),
        d_up=vmem(inner, BF16),
        d_active=vmem(inner, F32),
        grad_stage=compact,
        mix_stage=compact,
        grad_compact=vmem((PIECES, count, cap, piece), BF16),
        mix_compact=vmem((count, cap, half), BF16),
        grad_dense=dense,
        mix_dense=vmem((lines, length, half), BF16),
        total=vmem((PIECES, length, piece), F32),
        grad_from_b=packed,
        mix_from_b=vmem((lines, cap, half), BF16),
        mix_from_a=vmem((line, length, half), BF16),
        from_a=one_line,
        from_z=one_line,
        gate_ref=vmem((width, hidden), BF16),
        up_ref=vmem((width, hidden), BF16),
        down_ref=vmem((width, hidden), BF16),
        sends=dma((4 + PIECES, 5 * line)),
        recvs=dma((4 + PIECES, count)),
        note_send=dma((count,)),
        note_recv=dma((count,)),
        cot_twins=dma((PIECES, 2, count)),
        local_sems=dma((4 + PIECES,)),
        keep_sems=dma((11,)),
        mix_sems=dma((2,)),
        load_sems=dma((3,)),
        reduce_sems=dma((PIECES + 1, 2, 4 * line)),
        gather_send=dma((PIECES, 5 * line)),
        gather_recv=dma((PIECES, count)),
        row_twins=dma((2 * PIECES + 1, 2, count)),
        last_sems=dma((2, PIECES)),
        store_sems=dma((6,)),
    )
    names = [*inputs, *outputs, *scratch]
    results = pl.pallas_call(
        functools.partial(front_kernel, line, group_size, names),
        out_shape=[jax.ShapeDtypeStruct(shape, kind) for shape, kind, _ in outputs.values()],
        in_specs=[spec for _, spec in inputs.values()],
        out_specs=[spec for _, _, spec in outputs.values()],
        scratch_shapes=list(scratch.values()),
        compiler_params=params(0),
        name="run_front",
    )(*(x for x, _ in inputs.values()))
    return types.SimpleNamespace(**dict(zip(outputs, results)))


def backward_entry(line, group_size, number, *refs):
    targets, sems = refs[-number - 1 : -1], refs[-1]
    loads = [
        pltpu.make_async_copy(src, dst, sems.at[i]) for i, (src, dst) in enumerate(zip(refs[:number], targets))
    ]
    for c in loads:
        c.start()
    backward_kernel(line, group_size, loads, *targets, *refs[number : -number - 1])


def backward_kernel(
    line,
    group_size,
    loads,
    tokens_ref,
    hidden_ref,
    d_rows_ref,
    cot_ref,
    normed_ref,
    head_out_ref,
    queries_ref,
    keys_ref,
    values_ref,
    probs_ref,
    gains_ref,
    peak_ref,
    tables_ref,
    query_keep,
    key_keep,
    value_keep,
    out_keep,
    mix_ref,
    rows_hbm,
    cots_hbm,
    active_hbm,
    d_gate_hbm,
    d_up_hbm,
    input_grad_ref,
    output_ref,
    query_sum,
    key_sum,
    value_sum,
    out_sum,
    notes,
    grad_gate_ref,
    grad_up_ref,
    grad_down_ref,
    *scratch,
):
    place = Place(line)
    count = 4 * line
    length, width = tokens_ref.shape
    q_cols, kv_cols = queries_ref.shape[1], keys_ref.shape[1]
    shard = width // count
    chunks = q_cols // 128
    (query_all, key_all, value_all, out_all), work = scratch[:4], scratch[4:9]
    rest = scratch[9:34]
    (
        total,
        d_heads,
        d_query,
        d_key,
        d_value,
        part_mine,
        part_other,
        d_hidden_keep,
        mix_total,
        note,
        weight_sems,
        load_sems,
        last_sems,
        part_sems,
        note_sends,
        note_recvs,
        expert_rows,
        cots,
        active,
        d_gate,
        d_up,
        grads,
        expert_sems,
        store_sems,
    ) = scratch[34:]
    by_part = lambda slot: part_of(place, slot)
    reduces = [
        Reduce(place, work[i], *rest[5 * i : 5 * i + 5], *(() if i == 4 else (by_part,))) for i in range(5)
    ]

    def load(slot):
        return pltpu.make_async_copy(mix_ref.at[slot], work[4].at[slot], load_sems.at[slot])

    def begin(slot, carry):
        load(slot).start()
        return carry

    def loaded(slot, carry):
        load(slot).wait()
        return carry

    lax.fori_loop(0, line, begin, 0)
    weights = [
        pltpu.make_async_copy(src, dst, weight_sems.at[i])
        for i, (src, dst) in enumerate(
            ((out_keep, out_all), (query_keep, query_all), (key_keep, key_all), (value_keep, value_all))
        )
    ]
    for c in weights:
        c.start()
    experts = [
        pltpu.make_async_copy(src, dst, expert_sems.at[i])
        for i, (src, dst) in enumerate(
            ((rows_hbm, expert_rows), (cots_hbm, cots), (active_hbm, active), (d_gate_hbm, d_gate), (d_up_hbm, d_up))
        )
    ]
    for c in experts:
        c.start()
    stores = [
        pltpu.make_async_copy(grads.at[i], dst, store_sems.at[i])
        for i, dst in enumerate((grad_gate_ref, grad_up_ref, grad_down_ref))
    ]
    columns = width // 512

    def weight_grad(number):
        left, right = ((expert_rows, d_gate), (expert_rows, d_up), (cots, active))[number]
        left = left.reshape(left.shape[0] * left.shape[1], width)

        def some(i, carry):
            span = pl.ds(pl.multiple_of(512 * i, 512), 512)
            grads[number, span, :] = contract_rows(left[:, span], right[...])
            return carry

        lax.fori_loop(0, columns, some, 0)
        stores[number].start()

    enter(place)
    for c in loads:
        c.wait()
    lax.fori_loop(0, line, loaded, 0)
    mine, theirs = halves(place, width)
    outs = (query_sum, key_sum, value_sum, out_sum, total)
    order = (3, 0, 1, 2)
    mix = reduces[4]
    for z in ends_first(line):
        mix.send_z(z)
    last = remote(total, mix_total.at[:, mine], last_sems.at[0], last_sems.at[1], place.twin())

    def finish(at):
        i = order[at]
        reduces[i].result(outs[i])

    run = Reductions([reduces[i] for i in order], finish)
    hidden = hidden_ref[...]
    inv_moe = lax.rsqrt(jnp.mean(hidden * hidden, axis=1, keepdims=True) + EPSILON)
    unit_moe = hidden * inv_moe
    d_rows = d_rows_ref[...]
    scaled = d_rows * gains_ref[2:3, :]
    d_hidden = cot_ref[...].astype(F32) + inv_moe * (
        scaled - unit_moe * jnp.mean(scaled * unit_moe, axis=1, keepdims=True)
    )
    d_hidden_keep[...] = d_hidden
    moe_gain = jnp.sum(d_rows * unit_moe, axis=0, keepdims=True)
    d_attn = (RESIDUAL * d_hidden).astype(BF16)
    work[3][...] = contract_rows(d_attn, head_out_ref[...]).astype(BF16).reshape(count, shard, q_cols)
    run.ready(1)
    weights[0].wait()
    d_heads[...] = jnp.dot(
        d_attn, out_all[...].reshape(width, q_cols), preferred_element_type=F32
    ).astype(BF16)
    lane = lax.broadcasted_iota(jnp.int32, (length, 128), 1)
    d_key[...] = jnp.zeros_like(d_key)
    d_value[...] = jnp.zeros_like(d_value)
    tables = [tables_ref[i] for i in range(3)]
    for j in range(chunks):
        d_out = chunk_of(d_heads, j)
        keys = pair_of(keys_ref, j, group_size, lane)
        d_prob = contract_cols(d_out, pair_of(values_ref, j, group_size, lane))
        low, d_scores = [], []
        for half in (0, 1):
            side = slice(length * half, length * (half + 1))
            prob = probs_ref[j, :, side]
            grad = d_prob[:, side]
            inner = jnp.sum(prob * grad, axis=1, keepdims=True)
            d_scores.append((prob * (grad - inner)).astype(BF16))
            low.append(prob.astype(BF16))
        d_scores = jnp.concatenate(d_scores, axis=1)
        d_values = contract_rows(jnp.concatenate(low, axis=1), d_out)
        d_keys = contract_rows(d_scores, chunk_of(queries_ref, j)) * SCORE_SCALE
        turned = rope_chunk(
            jnp.dot(d_scores, keys, preferred_element_type=F32) * SCORE_SCALE, tables, -1.0
        )
        d_query[:, 128 * j : 128 * (j + 1)] = turned.astype(BF16)
        for half in (0, 1):
            group = (2 * j + half) // group_size
            side = slice(length * half, length * (half + 1))
            cols = slice(128 * (group // 2), 128 * (group // 2 + 1))
            d_key[:, cols] += place_half(d_keys[side], half, group % 2, lane)
            d_value[:, cols] += place_half(d_values[side], half, group % 2, lane)
        run.run(1)
    normed = normed_ref[...]
    work[0][...] = contract_rows(normed, d_query[...]).astype(BF16).reshape(count, shard, q_cols)
    run.ready(2)
    d_key_lin = jnp.concatenate(
        [rope_chunk(chunk_of(d_key, j), tables, -1.0) for j in range(kv_cols // 128)], axis=1
    ).astype(BF16)
    d_value_lin = d_value[...].astype(BF16)
    run.run(2)
    work[1][...] = contract_rows(normed, d_key_lin).astype(BF16).reshape(count, shard, kv_cols)
    work[2][...] = contract_rows(normed, d_value_lin).astype(BF16).reshape(count, shard, kv_cols)
    run.ready(4)
    run.run(2)
    mix.result(total)
    mix_total[:, mine] = total[...]
    last.start()
    for c in weights[1:]:
        c.wait()
    part_mine[...] = (
        contract_cols(d_query[...], query_all[...].reshape(width, q_cols))
        + contract_cols(d_key_lin, key_all[...].reshape(width, kv_cols))
        + contract_cols(d_value_lin, value_all[...].reshape(width, kv_cols))
    )
    swap = remote(part_mine, part_other, part_sems.at[0], part_sems.at[1], place.twin())
    swap.start()
    run.run(4)
    swap.wait()
    d_normed = part_mine[...] + part_other[...]
    inputs = tokens_ref[...].astype(F32)
    inv_attn = lax.rsqrt(jnp.mean(inputs * inputs, axis=1, keepdims=True) + EPSILON)
    unit_attn = inputs * inv_attn
    scaled = d_normed * gains_ref[1:2, :]
    input_grad_ref[...] = d_hidden_keep[...] + inv_attn * (
        scaled - unit_attn * jnp.mean(scaled * unit_attn, axis=1, keepdims=True)
    )
    attn_gain = jnp.sum(d_normed * unit_attn, axis=0, keepdims=True)
    rows = jnp.concatenate([attn_gain, moe_gain, jnp.zeros((6, width), F32)], axis=0)
    row = lax.broadcasted_iota(jnp.int32, (8, 128), 0)
    peaks = jnp.broadcast_to(peak_ref[0:1, :], (8, 128))
    for p in range(count):
        turned = pltpu.roll(rows, width - shard * p, 1) if p else rows
        note[p] = jnp.where(row == 2, peaks, turned[:, :128])
    exchange = Notes(place, note, notes, note_sends, note_recvs, False)
    exchange.start()
    for c in experts:
        c.wait()
    for number in range(3):
        weight_grad(number)
        run.run(6)
    run.complete()
    for r in reduces[:4]:
        r.settle()
    mix.settle_z()
    last.wait()
    output_ref[...] = (hidden_ref[...] + RESIDUAL * mix_total[...]).astype(BF16)
    exchange.finish()
    for c in stores:
        c.wait()


def run_backward(line, group_size, kept, keeps, mix, experts):
    count = 4 * line
    tokens, queries, keys = kept[0], kept[6], kept[7]
    length, width = tokens.shape
    q_cols, kv_cols = queries.shape[1], keys.shape[1]
    blocks = [x.shape[1:] for x in keeps] + [mix.shape[1:]]
    half = width // 2
    shape = jax.ShapeDtypeStruct
    outs = (
        [shape((length, width), F32), shape((length, width), BF16)]
        + [shape(s, F32) for s in blocks[:4]]
        + [shape((count, 8, 128), F32)]
    )
    kinds = [IN_VMEM] * len(outs) + [ANY] * 3
    hidden = experts[2].shape[1]
    outs += [shape((width, hidden), F32)] * 3
    return pl.pallas_call(
        functools.partial(backward_entry, line, group_size, len(kept)),
        out_shape=outs,
        in_specs=[ANY] * (len(kept) + 10),
        out_specs=kinds,
        scratch_shapes=[pltpu.VMEM(x.shape, BF16) for x in keeps]
        + [pltpu.VMEM((count, *s), BF16) for s in blocks[:4]]
        + [pltpu.VMEM(mix.shape, BF16)]
        + [x for s in blocks for x in reduce_scratch(line, s)]
        + [
            pltpu.VMEM((length, half), F32),
            pltpu.VMEM((length, q_cols), BF16),
            pltpu.VMEM((length, q_cols), BF16),
            pltpu.VMEM((length, kv_cols), F32),
            pltpu.VMEM((length, kv_cols), F32),
            pltpu.VMEM((length, width), F32),
            pltpu.VMEM((length, width), F32),
            pltpu.VMEM((length, width), F32),
            pltpu.VMEM((length, width), F32),
            pltpu.VMEM((count, 8, 128), F32),
            pltpu.SemaphoreType.DMA((4,)),
            pltpu.SemaphoreType.DMA((count,)),
            pltpu.SemaphoreType.DMA((2,)),
            pltpu.SemaphoreType.DMA((2,)),
            pltpu.SemaphoreType.DMA((count,)),
            pltpu.SemaphoreType.DMA((count,)),
        ]
        + [pltpu.VMEM(x.shape, BF16) for x in experts]
        + [
            pltpu.VMEM((3, width, hidden), F32),
            pltpu.SemaphoreType.DMA((5,)),
            pltpu.SemaphoreType.DMA((3,)),
        ]
        + [pltpu.VMEM(x.shape, x.dtype) for x in kept]
        + [pltpu.SemaphoreType.DMA((len(kept),))],
        compiler_params=params(3),
        name="run_backward",
    )(*kept, *keeps, mix, *experts)


def finish_kernel(
    group_size,
    output_in,
    input_grad_in,
    query_in,
    key_in,
    value_in,
    out_in,
    notes,
    query_ref,
    key_ref,
    gate_in,
    up_in,
    down_in,
    output,
    input_grad,
    grad_query,
    grad_key,
    grad_value,
    grad_out,
    gain_a,
    gain_m,
    clipped_query,
    clipped_key,
    grad_gate,
    grad_up,
    grad_down,
    stage,
    sems,
):
    pairs = ((gate_in, grad_gate), (up_in, grad_up), (down_in, grad_down))
    takes = [pltpu.make_async_copy(src, stage.at[i], sems.at[0, i]) for i, (src, _) in enumerate(pairs)]
    copies = [pltpu.make_async_copy(stage.at[i], dst.at[0], sems.at[1, i]) for i, (_, dst) in enumerate(pairs)]
    for c in takes:
        c.start()
    output[...] = output_in[...]
    input_grad[...] = input_grad_in[...]
    grad_query[...] = query_in[...]
    grad_key[...] = key_in[...]
    grad_value[...] = value_in[...]
    grad_out[...] = out_in[...]
    for take, c in zip(takes, copies):
        take.wait()
        c.start()
    total, peaks = notes[0], notes[0]
    for p in range(1, notes.shape[0]):
        total = total + notes[p]
        peaks = jnp.maximum(peaks, notes[p])
    shard = gain_a.shape[1]
    gain_a[...] = total[0:1, :shard]
    gain_m[...] = total[1:2, :shard]
    factor = CLIP_LIMIT / jnp.maximum(peaks, CLIP_LIMIT)
    root = jnp.sqrt(factor)
    lane = lax.broadcasted_iota(jnp.int32, (8, 128), 1)

    def scale(h):
        return jnp.max(jnp.where(lane == h, root, 0.0), axis=1, keepdims=True)[2:3, :]

    heads = query_ref.shape[1] // HEAD_SIZE
    wide = lax.broadcasted_iota(jnp.int32, (1, 128), 1)
    scales = [scale(h) for h in range(heads)]
    for j in range(heads // 2):
        row = jnp.where(wide < HEAD_SIZE, scales[2 * j], scales[2 * j + 1])
        cols = slice(128 * j, 128 * (j + 1))
        clipped_query[:, cols] = query_ref[:, cols].astype(F32) * row
    least = [
        functools.reduce(jnp.minimum, scales[group_size * g : group_size * (g + 1)])
        for g in range(heads // group_size)
    ]
    for j in range(len(least) // 2):
        row = jnp.where(wide < HEAD_SIZE, least[2 * j], least[2 * j + 1])
        cols = slice(128 * j, 128 * (j + 1))
        clipped_key[:, cols] = key_ref[:, cols].astype(F32) * row
    for c in copies:
        c.wait()


def finish(group_size, found, notes, query, key, expert_grads):
    shape = jax.ShapeDtypeStruct
    shard = query.shape[0]
    outs = [shape(x.shape, x.dtype) for x in found] + [
        shape((1, shard), F32),
        shape((1, shard), F32),
        shape(query.shape, F32),
        shape(key.shape, F32),
    ]
    return pl.pallas_call(
        functools.partial(finish_kernel, group_size),
        out_shape=outs + [shape((1, *g.shape), F32) for g in expert_grads],
        in_specs=[IN_VMEM] * 9 + [ANY] * 3,
        out_specs=[IN_VMEM] * 10 + [ANY] * 3,
        scratch_shapes=[
            pltpu.VMEM((3, *expert_grads[0].shape), F32),
            pltpu.SemaphoreType.DMA((2, 3)),
        ],
        compiler_params=pltpu.CompilerParams(vmem_limit_bytes=56 * 2**20),
        name="finish",
    )(*found, notes, query, key, *expert_grads)


def on_device_dense(
    tokens,
    attn_norm_gain,
    w_query,
    key_projection,
    value_projection,
    w_out,
    moe_norm_gain,
    w_gate,
    w_up,
    w_down,
    router_logits,
    expert_ids,
    segment_ids,
    parents,
    cotangent,
):
    length, model_width = tokens.shape
    q_cols, kv_cols = w_query.shape[1], key_projection.shape[1]
    q_heads, kv_heads = q_cols // HEAD_SIZE, kv_cols // HEAD_SIZE
    group_size = q_heads // kv_heads
    count = lax.axis_size("dp")
    line = count // 4
    shard = attn_norm_gain.shape[0]
    small = (
        attn_norm_gain[None],
        moe_norm_gain[None],
        router_logits.T,
        expert_ids.T,
        segment_ids,
        parents,
    )
    big = (tokens, w_query, key_projection, value_projection, w_out, cotangent)
    front = run_front(line, group_size, big, small, (w_gate, w_up, w_down))
    keeps = (front.query_keep, front.key_keep, front.value_keep, front.out_keep)
    experts = (front.rows_out, front.cots_out, front.active_out, front.d_gate_out, front.d_up_out)
    kept = (
        tokens,
        front.hidden_out,
        front.d_rows_ref,
        cotangent,
        front.normed_out,
        front.head_out_out,
        front.queries_out,
        front.keys_out,
        front.values_out,
        front.probs_out,
        front.gains_ref,
        front.peak_ref,
        front.tables_ref,
    )
    input_grad, output, *grads = run_backward(line, group_size, kept, keeps, front.mix_ref, experts)
    grads, sums, expert_grads = grads[:4], grads[4], grads[5:]
    output, input_grad, gq, gk, gv, go, gain_a, gain_m, clipped_query, clipped_key, gg, gu, gd = finish(
        group_size, (output, input_grad, *grads), sums, w_query, key_projection, expert_grads
    )
    return (
        output,
        input_grad,
        gain_a[0],
        gq,
        gk,
        gv,
        go,
        gain_m[0],
        gg,
        gu,
        gd,
        clipped_query,
        clipped_key,
    )


DENSE_BYTES = 8 * 2**20


def on_device(*args):
    tokens, w_gate = args[0], args[7]
    count, ranks = lax.axis_size("dp"), lax.axis_size("tensor")
    rows_bytes = count * tokens.shape[0] * tokens.shape[1] * 2
    whole_experts = w_gate.shape[2] * ranks == FFE
    dense = whole_experts and ranks == 2 and count % 8 == 0 and rows_bytes <= DENSE_BYTES
    return on_device_dense(*args) if dense else on_device_general(*args)


def solution(mesh):
    in_specs = (
        P("dp", None),
        P("dp"),
        P("dp", "tensor"),
        P("dp", "tensor"),
        P("dp", "tensor"),
        P("dp", "tensor"),
        P("dp"),
        P("dp", None, "tensor"),
        P("dp", None, "tensor"),
        P("dp", None, "tensor"),
        P("dp", None),
        P("dp", None),
        P("dp", None),
        P("dp", None),
        P("dp", None),
    )
    out_specs = (
        P("dp", None),
        P("dp", None),
        P("dp"),
        P("dp", "tensor"),
        P("dp", "tensor"),
        P("dp", "tensor"),
        P("dp", "tensor"),
        P("dp"),
        P("dp", None, "tensor"),
        P("dp", None, "tensor"),
        P("dp", None, "tensor"),
        P("dp", "tensor"),
        P("dp", "tensor"),
    )
    return jax.shard_map(
        on_device, mesh=mesh, in_specs=in_specs, out_specs=out_specs, check_vma=False
    )
```
